32 devices in a mesh: dp: 4 (over z), vocab: 8 (over y, x, core).
Axes of the slice: x: 2, y: 2, z: 4, core: 2. Of those that a mesh axis runs over, the one named last changes fastest.
Arguments:
- token_ids: int32 [32, 512], P(('dp', 'vocab')), may hold values from 0 to 15359, as said below
- lengths: int32 [32], P(('dp', 'vocab')), may hold values from 120 to 512
- mask_pos: int32 [32, 120], P(('dp', 'vocab')), may hold values from 0 to 511, as said below
- mask_count: int32 [32], P(('dp', 'vocab')), may hold values from 5 to 120
- owner_order: int32 [58624], replicated, may hold values from 0 to 58623, as said below
- step_count: int32 [1], replicated, may hold values from 1 to 20
- teacher_flat: bfloat16 [58624, 128], P(('dp', 'vocab')), may hold values from -4 to 4
- mentor_lexicon_weights: bfloat16 [15360, 768], P('vocab'), may hold values from -2 to 2
- student_flat: float32 [58624, 128], P(('dp', 'vocab')), may hold values from -4 to 4
- flat_first: float32 [58624, 128], P(('dp', 'vocab')), may hold values from -3.8146973e-06 to 3.8146973e-06
- flat_second: float32 [58624, 128], P(('dp', 'vocab')), may hold values from 1.0585976e-13 to 4.2343903e-13
- student_embed: float32 [15360, 768], P('vocab', 'dp'), may hold values from -2 to 2
- embed_first: float32 [15360, 768], P('vocab', 'dp'), may hold values from -3.8146973e-06 to 3.8146973e-06
- embed_second: float32 [15360, 768], P('vocab', 'dp'), may hold values from 1.0585976e-13 to 4.2343903e-13
Outputs:
- loss: float32 [], replicated
- grad_norm: float32 [], replicated
- new_flat: float32 [58624, 128], P(('dp', 'vocab'))
- new_flat_first: float32 [58624, 128], P(('dp', 'vocab'))
- new_flat_second: float32 [58624, 128], P(('dp', 'vocab'))
- new_embed: float32 [15360, 768], P('vocab', 'dp')
- new_embed_first: float32 [15360, 768], P('vocab', 'dp')
- new_embed_second: float32 [15360, 768], P('vocab', 'dp')
The draws below stay inside these ranges and needn't reach their ends.
Inputs may be any that keep to these rules, and one draw needn't show every extreme that they name: `token_ids`: ids of the vocabulary. `owner_order`: each stored tile holds a different tile of the vector. `mask_pos`: positions distinct within a row and less than that sequence's length.
All inputs are finite; a program needn't handle non-finite values.
Results may differ from the reference program's by a relative error of at most 0.002.
The reference program's roundings to bfloat16 on the way count: a program that leaves them out, or rounds other values in their place, can miss the bound.
Values may be sent and summed in bfloat16 or wider, within the bound.
No kernel may reach another device: no remote copies, remote signals or barrier semaphores. Data moves between devices by JAX's collectives and lax.ppermute only.
A program may use at most 256 MiB of HBM per device.

```python
import math
import jax
import jax.numpy as jnp
from jax import lax

D = 768
HEADS = 12
HEAD_DIM = 64
FF = 3072
LEN = 512
CAP = 120
TILE = 128
SEQS = 32
VOCAB = 15360
PARAMS = 7481856
NTILE = 58624


def tile_order(key):
    return jax.random.permutation(jax.random.fold_in(key, 11), NTILE).astype(jnp.int32)


def flat_values(key):
    subkeys = jax.random.split(key, 12)

    def normal(which_key, entries, spread):
        return jax.random.truncated_normal(subkeys[which_key], -4.0, 4.0, (entries,), jnp.float32) * spread
    out_fan = max(1, D // 128)
    gain_rows = jax.random.uniform(subkeys[6], (3, D), jnp.float32, 0.7, 1.3)
    shifts = normal(7, 3 * D, 0.2).reshape(3, D)
    biases = normal(5, 4 * D, 0.2).reshape(4, D)
    norm_rows = jnp.stack([gain_rows[0], shifts[0], gain_rows[1], shifts[1], gain_rows[2], shifts[2]])
    small_rows = jnp.concatenate([biases, norm_rows], axis=0).reshape(-1)
    pieces = [normal(0, 3 * D * D, D ** (-0.5)), normal(1, D * D, out_fan ** (-0.5)), normal(2, D * FF, D ** (-0.5)), normal(3, FF * D, FF ** (-0.5)), normal(4, LEN * D, 4.0 * D ** (-0.5)), small_rows, normal(8, FF, 0.2), normal(9, NTILE * TILE - PARAMS, 0.02)]
    return jnp.concatenate(pieces).reshape(NTILE, TILE)


def mask_layout(key):
    subkeys = jax.random.split(jax.random.fold_in(key, 7), 5)
    rows_index = jnp.arange(SEQS)
    shortest = max(CAP, LEN // 8)
    lengths = jax.random.randint(subkeys[0], (SEQS,), shortest, LEN + 1)
    lengths = jnp.where(rows_index == jax.random.randint(subkeys[1], (), 0, SEQS), LEN, lengths)
    counts = jax.random.randint(subkeys[2], (SEQS,), 5, CAP + 1)
    counts = jnp.where(rows_index == jax.random.randint(subkeys[3], (), 0, SEQS), CAP, counts)
    orders = jax.vmap(lambda sub: jax.random.permutation(sub, LEN))(jax.random.split(subkeys[4], SEQS))
    beyond = (orders >= lengths[:, None]).astype(jnp.int32)
    ranked = jnp.argsort(beyond, axis=1, stable=True)
    place_number = jnp.take_along_axis(orders, ranked[:, :CAP], axis=1)
    return (lengths.astype(jnp.int32), place_number.astype(jnp.int32), counts.astype(jnp.int32))


def draw_token_ids(key, part):
    subkeys = jax.random.split(jax.random.fold_in(key, 23), 5)
    levels = (VOCAB - 1).bit_length()
    spans = jax.random.randint(subkeys[0], (SEQS, LEN), 1, levels + 1)
    highs = jnp.minimum(jnp.left_shift(jnp.ones((SEQS, LEN), jnp.int32), spans.astype(jnp.int32)), VOCAB)
    ranks = jax.random.randint(subkeys[1], (SEQS, LEN), 0, highs)
    ranking = jax.random.permutation(subkeys[2], VOCAB).astype(jnp.int32)
    token_ids = ranking[ranks]
    rows_index = jnp.arange(SEQS)[:, None]
    cols_index = jnp.arange(LEN)[None, :]
    top_row = jax.random.randint(subkeys[3], (), 0, SEQS)
    top_col = jax.random.randint(subkeys[4], (), 0, LEN)
    token_ids = jnp.where((rows_index == top_row) & (cols_index == top_col), VOCAB - 1, token_ids)
    token_ids = jnp.where((rows_index == top_row) & (cols_index == (top_col + 1) % LEN), 0, token_ids)
    return token_ids.astype(jnp.int32)


def draw_owner_order(key, part):
    return tile_order(key)


def draw_teacher_flat(key, part):
    return flat_values(jax.random.fold_in(key, 1)).astype(jnp.bfloat16)


def draw_student_flat(key, part):
    return flat_values(jax.random.fold_in(key, 2))[tile_order(key)]


def draw_lengths(key, part):
    return mask_layout(key)[0]


def draw_mask_pos(key, part):
    return mask_layout(key)[1]


def draw_mask_count(key, part):
    return mask_layout(key)[2]


def steps_of(key, shape, shards, least, top_value):
    factor_of, own = 1.0, jax.random.fold_in(key, 6)
    for dim, blocks in shards:
        heights = jnp.exp(jax.random.uniform(jax.random.fold_in(own, dim), (blocks,), jnp.float32, least / len(shards), top_value / len(shards)))
        factor_of = factor_of * jnp.repeat(heights, shape[dim] // blocks).reshape([-1 if axis == dim else 1 for axis in range(len(shape))])
    return factor_of


def scatter_about(own_key, dims, deviation, reach, cuts=(), kind=jnp.bfloat16):
    level = steps_of(own_key, dims, cuts, -0.22, 0.18) if cuts else 1.0
    array = jax.random.normal(own_key, dims, jnp.float32) * deviation * level
    return jnp.minimum(jnp.maximum(array, -reach), reach).astype(kind)


def setup_inputs(seed: int = 0) -> dict:
    splits = jax.random.split(jax.random.key(seed), 15)
    return {
        "token_ids": draw_token_ids(jax.random.fold_in(splits[14], 71), 0),
        "lengths": draw_lengths(jax.random.fold_in(splits[14], 71), 0),
        "mask_pos": draw_mask_pos(jax.random.fold_in(splits[14], 71), 0),
        "mask_count": draw_mask_count(jax.random.fold_in(splits[14], 71), 0),
        "owner_order": draw_owner_order(jax.random.fold_in(splits[14], 71), 0),
        "step_count": jax.random.randint(splits[5], (1,), 1, 21).astype(jnp.int32),
        "teacher_flat": draw_teacher_flat(jax.random.fold_in(splits[14], 71), 0),
        "mentor_lexicon_weights": scatter_about(splits[7], (VOCAB, D), (4.0 / D ** 0.5), 2.0, ((0, 8),)),
        "student_flat": draw_student_flat(jax.random.fold_in(splits[14], 71), 0),
        "flat_first": scatter_about(splits[9], (NTILE, TILE), (0.00111 / (PARAMS + VOCAB * D) ** 0.5), 3.814697265625e-06, ((0, 32),), jnp.float32),
        "flat_second": jnp.clip(jnp.exp(math.log(4.234390344869804e-13) - 1.3862944 * jax.random.uniform(splits[10], (NTILE, TILE), jnp.float32) ** steps_of(splits[10], (NTILE, TILE), ((0, 32),), -0.2, 0.2)), 1.058597586217451e-13, 4.234390344869804e-13),
        "student_embed": scatter_about(splits[11], (VOCAB, D), (4.0 / D ** 0.5), 2.0, ((0, 8), (1, 4)), jnp.float32),
        "embed_first": scatter_about(splits[12], (VOCAB, D), (0.00111 / (PARAMS + VOCAB * D) ** 0.5), 3.814697265625e-06, ((0, 8), (1, 4)), jnp.float32),
        "embed_second": jnp.clip(jnp.exp(math.log(4.234390344869804e-13) - 1.3862944 * jax.random.uniform(splits[13], (VOCAB, D), jnp.float32) ** steps_of(splits[13], (VOCAB, D), ((0, 8), (1, 4)), -0.2, 0.2)), 1.058597586217451e-13, 4.234390344869804e-13),
    }


smoothing_heat_scale = 2.0
mixing_coefficient = 5.0
cosine_weight = 20.0
clip_norm = 0.01
beta_first = 0.9
beta_second = 0.98
adam_eps = 1e-08
weight_decay = 0.01
learn_rate = 0.1
norm_eps = 1e-12
cosine_eps = 1e-06

@jax.custom_vjp
def low(v):
    return lax.optimization_barrier(v.astype(jnp.bfloat16)).astype(jnp.float32)

@jax.custom_vjp
def low_back(v):
    return v

def low_keep(v):
    return (low(v), None)

def low_pass(kept, grad):
    return (grad,)

def back_keep(v):
    return (v, None)

def back_low(kept, grad):
    return (low(grad),)
low.defvjp(low_keep, low_pass)
low_back.defvjp(back_keep, back_low)

def both_ways(values):
    return low_back(low(values))

def array_multiply(left_side, right_side):
    return jnp.dot(left_side, right_side, precision=lax.Precision.HIGHEST, preferred_element_type=jnp.float32)

def unpack(vector):
    layout = [('qkv', (D, 3 * D)), ('out', (D, D)), ('up', (D, FF)), ('down', (FF, D)), ('place', (LEN, D)), ('small', (10, D)), ('upbias', (FF,))]
    pieces = {}
    offset = 0
    for piece_name, piece_dims in layout:
        entries = 1
        for extent in piece_dims:
            entries = entries * extent
        pieces[piece_name] = vector[offset:offset + entries].reshape(piece_dims)
        offset = offset + entries
    return pieces

def layer_norm(values, gain_row, shift_row):
    center = values - lax.optimization_barrier(jnp.mean(values, axis=-1, keepdims=True))
    inverse = lax.rsqrt(lax.optimization_barrier(jnp.mean(center * center, axis=-1, keepdims=True)) + norm_eps)
    return center * inverse * gain_row + shift_row

def encode(pieces, looked, length):
    small_rows = pieces['small']
    summed = low_back(looked) + pieces['place']
    first_norm = layer_norm(summed, small_rows[4], small_rows[5])
    qkv_bias = jnp.concatenate([small_rows[0], jnp.zeros((D,), jnp.float32), small_rows[1]])
    projected = both_ways(array_multiply(low(first_norm), pieces['qkv']) + qkv_bias).reshape(LEN, 3, HEADS, HEAD_DIM)
    scores = jnp.einsum('qhd,khd->hqk', projected[:, 0], projected[:, 1], precision=lax.Precision.HIGHEST)
    scores = low_back(scores * HEAD_DIM ** (-0.5))
    keep_keys = jnp.arange(LEN) < length
    scores = jnp.where(keep_keys[None, None, :], scores, -1000000000.0)
    probabilities = jax.nn.softmax(scores, axis=-1)
    context = jnp.einsum('hqk,khd->qhd', low(probabilities), projected[:, 2], precision=lax.Precision.HIGHEST).reshape(LEN, D)
    attended = low_back(array_multiply(both_ways(context), pieces['out']) + small_rows[2])
    middle = layer_norm(first_norm + attended, small_rows[6], small_rows[7])
    hidden = low_back(array_multiply(low(middle), pieces['up']) + pieces['upbias'])
    activated = low(jax.nn.gelu(hidden, approximate=False))
    output = low_back(array_multiply(activated, pieces['down']) + small_rows[3])
    return layer_norm(middle + output, small_rows[8], small_rows[9])

def adam_step(weight, first_moment, second, gradient, step_float):
    new_first = beta_first * first_moment + (1.0 - beta_first) * gradient
    new_second = beta_second * second + (1.0 - beta_second) * gradient * gradient
    fix_first = 1.0 - jnp.power(beta_first, step_float)
    fix_second = 1.0 - jnp.power(beta_second, step_float)
    update = new_first / fix_first / (jnp.sqrt(new_second / fix_second) + adam_eps)
    return (weight - learn_rate * (update + weight_decay * weight), new_first, new_second)

def reference(token_ids, lengths, mask_pos, mask_count, owner_order, step_count, teacher_flat, mentor_lexicon_weights, student_flat, flat_first, flat_second, student_embed, embed_first, embed_second):
    teacher_pieces = unpack(teacher_flat.astype(jnp.float32).reshape(-1))
    mentor_lexicon_array = mentor_lexicon_weights.astype(jnp.float32)
    logical = jnp.zeros_like(student_flat).at[owner_order].set(student_flat).reshape(-1)
    symbol_tally_overall = jnp.sum(lengths).astype(jnp.float32)
    hidden_slot_tally = jnp.sum(mask_count).astype(jnp.float32)
    teacher_final = lax.map(lambda inputs: encode(teacher_pieces, mentor_lexicon_array[inputs[0]], inputs[1]), (token_ids, lengths))

    def loss_of(vector, table_full):
        pieces = unpack(low(vector))
        narrow_lexicon_array = low(table_full)

        def one_sequence(running, inputs):
            ids_row, length, place_number, masked, mentor_activations = inputs
            final_lines = encode(pieces, narrow_lexicon_array[ids_row], length)
            student_logits = low_back(array_multiply(low(final_lines[place_number]), narrow_lexicon_array.T)) / smoothing_heat_scale
            teacher_logits = array_multiply(low(mentor_activations[place_number]), mentor_lexicon_array.T) / smoothing_heat_scale
            logsum_s = jax.nn.logsumexp(student_logits, axis=1)
            logsum_t = jax.nn.logsumexp(teacher_logits, axis=1)
            teacher_prob = jnp.exp(teacher_logits - logsum_t[:, None])
            diverge = lax.optimization_barrier(jnp.sum(teacher_prob * (teacher_logits - student_logits), axis=1)) - logsum_t + logsum_s
            live_slots = jnp.arange(CAP) < masked
            soft_sum = jnp.sum(jnp.where(live_slots, diverge, 0.0))
            inverse_s = lax.rsqrt(lax.optimization_barrier(jnp.sum(final_lines * final_lines, axis=1)) + cosine_eps)
            inverse_t = lax.rsqrt(lax.optimization_barrier(jnp.sum(mentor_activations * mentor_activations, axis=1)) + cosine_eps)
            cosine = lax.optimization_barrier(jnp.sum(final_lines * mentor_activations, axis=1)) * inverse_s * inverse_t
            live_rows = jnp.arange(LEN) < length
            spread = jnp.sum(jnp.where(live_rows, 1.0 - cosine, 0.0))
            return ((running[0] + soft_sum, running[1] + spread), None)
        initial = (jnp.zeros((), jnp.float32), jnp.zeros((), jnp.float32))
        sums = lax.scan(jax.checkpoint(one_sequence), initial, (token_ids, lengths, mask_pos, mask_count, teacher_final))[0]
        return mixing_coefficient * smoothing_heat_scale ** 2 * sums[0] / hidden_slot_tally + cosine_weight * sums[1] / symbol_tally_overall
    loss_value, pullback = jax.vjp(loss_of, logical, student_embed)
    grad_vector, grad_table = pullback(jnp.ones((), jnp.float32))
    grad_tiles = grad_vector.reshape(NTILE, TILE)[owner_order]
    grad_norm = jnp.sqrt(jnp.sum(grad_tiles * grad_tiles) + jnp.sum(grad_table * grad_table))
    factor = clip_norm / jnp.maximum(grad_norm, clip_norm)
    step_float = step_count[0].astype(jnp.float32)
    new_flat, new_flat_first, new_flat_second = adam_step(student_flat, flat_first, flat_second, grad_tiles * factor, step_float)
    new_embed, new_embed_first, new_embed_second = adam_step(student_embed, embed_first, embed_second, grad_table * factor, step_float)
    return (loss_value, grad_norm, new_flat, new_flat_first, new_flat_second, new_embed, new_embed_first, new_embed_second)
```

```python
import functools

import jax
import jax.numpy as jnp
from jax import lax
from jax.experimental import pallas as pl
from jax.experimental.pallas import tpu as pltpu
from jax.sharding import PartitionSpec as P

D = 768
HEADS = 12
HEAD_DIM = 64
FF = 3072
LEN = 512
CAP = 120
SLOTS = 128
TILE = 128

QKV = (0, D, 18)
OUT = (13824, D, 6)
UP = (18432, D, 24)
DOWN = (36864, FF, 6)
PLACE = (55296, LEN, 6)
MATRICES = (QKV, OUT, UP, DOWN, PLACE)
TAIL = 58368
TAIL_TILES = 88

VMEM_LIMIT = 60 * 1024 * 1024

smoothing_heat_scale = 2.0
mixing_coefficient = 5.0
cosine_weight = 20.0
clip_norm = 0.01
beta_first = 0.9
beta_second = 0.98
adam_eps = 1e-08
weight_decay = 0.01
learn_rate = 0.1
norm_eps = 1e-12
cosine_eps = 1e-06

CORE, ACROSS, DEEP = 1, 2, 4


def swap(value, bit):
    return lax.ppermute(value, "vocab", [(i, i ^ bit) for i in range(8)])


def shift(value, steps):
    size = lax.axis_size("dp")
    return lax.ppermute(value, "dp", [(i, (i + steps) % size) for i in range(size)])


def gather_near(value):
    value = value[None]
    for bit in (ACROSS, DEEP, CORE):
        value = jnp.concatenate([value, swap(value, bit)])
    return value


def scatter_near(value_far, value_near):
    half = value_near.shape[2] // 2
    value = value_near + swap(value_far, CORE)
    upper, lower = value[:, :, :half], value[:, :, half:]
    upper = upper[:, 0] + swap(upper[:, 1], ACROSS)
    lower = lower[0] + swap(lower[1], DEEP)
    upper = upper[0] + swap(upper[1], DEEP)
    lower = lower[0] + swap(lower[1], ACROSS)
    return jnp.concatenate([upper, lower])


def sum_everywhere(value):
    for bit in (CORE, ACROSS, DEEP):
        value = value + swap(value, bit)
    for step in (1, 2):
        value = value + lax.ppermute(value, "dp", [(i, i ^ step) for i in range(4)])
    return value


def relative_order(table, per_device):
    here = lax.axis_index("vocab")
    table = table.reshape(4, 2, 2, 2, per_device)
    for axis, bit in ((1, DEEP), (2, ACROSS), (3, CORE)):
        table = jnp.where((here & bit) != 0, jnp.flip(table, axis), table)
    return table


def rolled(table, downward):
    z = lax.axis_index("dp")
    order = (z - jnp.arange(4)) % 4 if downward else (z + jnp.arange(4)) % 4
    return jnp.stack([lax.dynamic_index_in_dim(table, order[k], keepdims=False) for k in range(4)])


def rows_of_tiles(tiles):
    rows = tiles
    for first, height, across in MATRICES:
        inside = (tiles >= first) & (tiles < first + height * across)
        at = tiles - first
        rows = jnp.where(inside, first + (at % across) * height + at // across, rows)
    return rows


def unpack_kernel(source, target, stage, *, across):
    stage[...] = source[...].astype(jnp.float32)

    def step(g, carry):
        for column in range(across):
            lines = stage[pl.ds(g * 16 * across + column, 16, stride=across), :]
            target[pl.ds(pl.multiple_of(g * 16, 16), 16), column * TILE : (column + 1) * TILE] = lines.astype(
                jnp.bfloat16
            )
        return carry

    lax.fori_loop(0, target.shape[0] // 16, step, 0)


def unpack_matrix(tiles, piece):
    first, height, across = piece
    lines = 64 if across > 6 else 128
    block = lines * across
    return pl.pallas_call(
        functools.partial(unpack_kernel, across=across),
        grid=(height // lines,),
        in_specs=[pl.BlockSpec((block, TILE), lambda i: (first // block + i, 0))],
        out_specs=pl.BlockSpec((lines, across * TILE), lambda i: (i, 0)),
        out_shape=jax.ShapeDtypeStruct((height, across * TILE), jnp.bfloat16),
        scratch_shapes=[pltpu.VMEM((block, TILE), jnp.float32)],
        name="unpack_matrix",
    )(tiles)


def place_kernel(rows, *refs, places, count, per):
    arrivals = refs[: len(places)]
    targets = refs[len(places) : len(places) + 5]
    tail = refs[len(places) + 5]
    landed, stage, full, packed, in_sems, out_sems, tail_sem = refs[len(places) + 6 :]
    copies = []
    for n, (arrival, place) in enumerate(zip(arrivals, places)):
        target = landed if place is None else landed.at[place[0], pl.ds(place[1], place[2])]
        copies.append(pltpu.make_async_copy(arrival, target, in_sems.at[n]))
    for copy in copies:
        copy.start()
    for copy in copies:
        copy.wait()

    def lines(block, start, size):
        stage[pl.ds(0, size), :] = landed[block, pl.ds(start, size), :].astype(jnp.float32)
        base = block * per + start
        for u in range(size):
            full[pl.ds(rows[base + u], 1), :] = stage[pl.ds(u, 1), :]

    whole, rest = divmod(per, 128)

    def one_block(block, carry):
        def one_step(i, inner):
            lines(block, pl.multiple_of(i * 128, 128), 128)
            return inner

        lax.fori_loop(0, whole, one_step, 0)
        if rest:
            lines(block, whole * 128, rest)
        return carry

    lax.fori_loop(0, count, one_block, 0)
    tail_copy = pltpu.make_async_copy(full.at[pl.ds(TAIL, TAIL_TILES)], tail, tail_sem)
    tail_copy.start()
    for target, (first, height, across) in zip(targets, MATRICES):
        size = min(height, D)
        parts = height // size

        def out_copy(n, slot, target=target, size=size, parts=parts):
            column, part = n // parts, n % parts
            return pltpu.make_async_copy(
                packed.at[slot, pl.ds(0, size)],
                target.at[
                    pl.ds(pl.multiple_of(part * size, 256), size),
                    pl.ds(pl.multiple_of(column * TILE, TILE), TILE),
                ],
                out_sems.at[slot],
            )

        def one_column(n, carry, first=first, size=size, out_copy=out_copy):
            slot = n % 2

            @pl.when(n >= 2)
            def _():
                out_copy(n - 2, slot).wait()

            packed[slot, pl.ds(0, size), :] = full[pl.ds(pl.multiple_of(first + n * size, 128), size), :].astype(
                jnp.bfloat16
            )
            out_copy(n, slot).start()
            return carry

        total = across * parts
        lax.fori_loop(0, total, one_column, 0)
        for n in (total - 2, total - 1):
            out_copy(n, n % 2).wait()
    tail_copy.wait()


def place_tiles(rows, arrivals, places, count, per):
    shapes = [jax.ShapeDtypeStruct((h, a * TILE), jnp.bfloat16) for _, h, a in MATRICES]
    return pl.pallas_call(
        functools.partial(place_kernel, places=places, count=count, per=per),
        in_specs=[pl.BlockSpec(memory_space=pltpu.SMEM)] + [pl.BlockSpec(memory_space=pl.ANY)] * len(arrivals),
        out_specs=[pl.BlockSpec(memory_space=pl.ANY)] * 6,
        out_shape=shapes + [jax.ShapeDtypeStruct((TAIL_TILES, TILE), jnp.float32)],
        scratch_shapes=[
            pltpu.VMEM((count, per, TILE), jnp.bfloat16),
            pltpu.VMEM((128, TILE), jnp.float32),
            pltpu.VMEM((count * per, TILE), jnp.float32),
            pltpu.VMEM((2, D, TILE), jnp.bfloat16),
            pltpu.SemaphoreType.DMA((len(arrivals),)),
            pltpu.SemaphoreType.DMA((2,)),
            pltpu.SemaphoreType.DMA,
        ],
        compiler_params=pltpu.CompilerParams(vmem_limit_bytes=VMEM_LIMIT),
        cost_estimate=pl.CostEstimate(flops=0, bytes_accessed=180_000_000, transcendentals=0),
        name="place_tiles",
    )(rows, *arrivals)


def step_size(rows):
    return max(n for n in range(8, 193, 8) if rows % n == 0)


def collect_kernel(rows, *refs, outs, blocks, per, begin):
    sources, targets = refs[:6], refs[6 : 6 + outs]
    full, sems = refs[6 + outs :]
    block = pl.program_id(0)

    @pl.when(block == 0)
    def _():
        copies = []
        for source, (first, height, across) in zip(sources, MATRICES):
            for column in range(across):
                copies.append(
                    pltpu.make_async_copy(
                        source.at[:, pl.ds(column * TILE, TILE)],
                        full.at[pl.ds(first + column * height, height)],
                        sems.at[len(copies)],
                    )
                )
        copies.append(pltpu.make_async_copy(sources[5], full.at[pl.ds(TAIL, TAIL_TILES)], sems.at[len(copies)]))
        for copy in copies:
            copy.start()
        unused = full.shape[0] - TAIL - TAIL_TILES
        full[pl.ds(TAIL + TAIL_TILES, unused), :] = jnp.zeros((unused, TILE), jnp.float32)
        for copy in copies:
            copy.wait()

    size = step_size(targets[0].shape[1])
    for n, target in enumerate(targets):
        base = (n * blocks + block) * per + begin

        def one_step(i, carry, target=target, base=base):
            start = pl.multiple_of(i * size, 8)
            for u in range(size):
                target[0, pl.ds(start + u, 1), :] = full[pl.ds(rows[base + start + u], 1), :]
            return carry

        lax.fori_loop(0, target.shape[1] // size, one_step, 0)


def collect_tiles(rows, sources, tiles_all, per, outs, begin, lines):
    blocks = tiles_all // per // outs
    return pl.pallas_call(
        functools.partial(collect_kernel, outs=outs, blocks=blocks, per=per, begin=begin),
        grid=(blocks,),
        in_specs=[pl.BlockSpec(memory_space=pltpu.SMEM)] + [pl.BlockSpec(memory_space=pl.ANY)] * 6,
        out_specs=[pl.BlockSpec((1, lines, TILE), lambda i: (i, 0, 0))] * outs,
        out_shape=[jax.ShapeDtypeStruct((blocks, lines, TILE), jnp.float32)] * outs,
        scratch_shapes=[pltpu.VMEM((tiles_all, TILE), jnp.float32), pltpu.SemaphoreType.DMA((61,))],
        compiler_params=pltpu.CompilerParams(vmem_limit_bytes=VMEM_LIMIT),
        cost_estimate=pl.CostEstimate(flops=0, bytes_accessed=80_000_000, transcendentals=0),
        name="collect_tiles",
    )(rows, *sources)


def array_multiply(left_side, right_side):
    return jnp.dot(left_side, right_side, preferred_element_type=jnp.float32)


def matmul_left(left_side, right_side):
    return lax.dot_general(
        left_side, right_side, (((0,), (0,)), ((), ())), preferred_element_type=jnp.float32
    )


def trailing_array_multiply(left_side, right_side):
    return lax.dot_general(
        left_side, right_side, (((1,), (1,)), ((), ())), preferred_element_type=jnp.float32
    )


def pieces_of(matrices, tail):
    qkv, out, up, down, place = matrices
    return {
        "qkv": qkv,
        "out": out,
        "up": up,
        "down": down,
        "place": place,
        "small": tail[:60].reshape(10, D),
        "upbias": tail[60:84].reshape(FF),
    }


def norm_forward(values, gain_row, shift_row):
    center = values - jnp.mean(values, axis=-1, keepdims=True)
    inverse = lax.rsqrt(jnp.mean(center * center, axis=-1, keepdims=True) + norm_eps)
    normed = center * inverse
    return (normed * gain_row + shift_row, normed, inverse)


def norm_backward(grad_out, normed, inverse, gain_row):
    scaled = grad_out * gain_row
    grad_in = inverse * (
        scaled
        - jnp.mean(scaled, axis=-1, keepdims=True)
        - normed * jnp.mean(scaled * normed, axis=-1, keepdims=True)
    )
    return (grad_in, jnp.sum(grad_out * normed, axis=0), jnp.sum(grad_out, axis=0))


def gelu_slope(values):
    return (
        0.5 * (1.0 + lax.erf(values * 0.7071067811865476))
        + values * jnp.exp(-0.5 * values * values) * 0.3989422804014327
    )


def key_scores(projected, lengths):
    seqs_count = lengths.shape[0]
    split_heads = projected.reshape(seqs_count, LEN, 3, HEADS, HEAD_DIM)
    scores = jnp.einsum(
        "sqhd,skhd->shqk",
        split_heads[:, :, 0],
        split_heads[:, :, 1],
        preferred_element_type=jnp.float32,
    ) * HEAD_DIM ** (-0.5)
    live_keys = jnp.arange(LEN)[None, :] < lengths[:, None]
    return (jnp.where(live_keys[:, None, None, :], scores, -1000000000.0), split_heads)


def layer_forward(pieces, looked, lengths):
    small_rows = pieces["small"].astype(jnp.float32)
    seqs_count = lengths.shape[0]
    rows_here = seqs_count * LEN
    summed = (
        looked.reshape(seqs_count, LEN, D) + pieces["place"].astype(jnp.float32)[None]
    ).reshape(rows_here, D)
    first_norm, normed_zero, inverse_zero = norm_forward(summed, small_rows[4], small_rows[5])
    inputs = first_norm.astype(jnp.bfloat16)
    qkv_bias = jnp.concatenate([small_rows[0], jnp.zeros((D,), jnp.float32), small_rows[1]])
    projected = (array_multiply(inputs, pieces["qkv"]) + qkv_bias).astype(jnp.bfloat16)
    scores, split_heads = key_scores(projected, lengths)
    peak = jnp.max(scores, axis=-1, keepdims=True)
    exps = jnp.exp(scores - peak)
    totals = jnp.sum(exps, axis=-1, keepdims=True)
    probabilities = (exps / totals).astype(jnp.bfloat16)
    logsum = peak + jnp.log(totals)
    context = jnp.einsum(
        "shqk,skhd->sqhd", probabilities, split_heads[:, :, 2], preferred_element_type=jnp.float32
    )
    context = context.reshape(rows_here, D).astype(jnp.bfloat16)
    attended = array_multiply(context, pieces["out"]) + small_rows[2]
    middle, normed_one, inverse_one = norm_forward(
        first_norm + attended, small_rows[6], small_rows[7]
    )
    middle_low = middle.astype(jnp.bfloat16)
    hidden = array_multiply(middle_low, pieces["up"]) + pieces["upbias"].astype(jnp.float32)
    activated = jax.nn.gelu(hidden, approximate=False).astype(jnp.bfloat16)
    output = array_multiply(activated, pieces["down"]) + small_rows[3]
    final_lines, normed_two, inverse_two = norm_forward(
        middle + output, small_rows[8], small_rows[9]
    )
    saved = {
        "inputs": inputs,
        "projected": projected,
        "logsum": logsum,
        "context": context,
        "middle_low": middle_low,
        "hidden": hidden,
        "activated": activated,
        "normed_zero": normed_zero,
        "inverse_zero": inverse_zero,
        "normed_one": normed_one,
        "inverse_one": inverse_one,
        "normed_two": normed_two,
        "inverse_two": inverse_two,
    }
    return (final_lines, saved)


def layer_backward(pieces, saved, grad_final, lengths):
    small_rows = pieces["small"].astype(jnp.float32)
    seqs_count = lengths.shape[0]
    rows_here = seqs_count * LEN
    grad_sum_two, grad_gain_two, grad_shift_two = norm_backward(
        grad_final, saved["normed_two"], saved["inverse_two"], small_rows[8]
    )
    grad_out = grad_sum_two.astype(jnp.bfloat16)
    grad_down = matmul_left(saved["activated"], grad_out)
    grad_act = trailing_array_multiply(grad_out, pieces["down"])
    grad_hidden = (grad_act * gelu_slope(saved["hidden"])).astype(jnp.bfloat16)
    grad_up = matmul_left(saved["middle_low"], grad_hidden)
    grad_middle = grad_sum_two + trailing_array_multiply(grad_hidden, pieces["up"])
    grad_sum_one, grad_gain_one, grad_shift_one = norm_backward(
        grad_middle, saved["normed_one"], saved["inverse_one"], small_rows[6]
    )
    grad_att = grad_sum_one.astype(jnp.bfloat16)
    grad_outw = matmul_left(saved["context"], grad_att)
    grad_context = (
        trailing_array_multiply(grad_att, pieces["out"])
        .astype(jnp.bfloat16)
        .reshape(seqs_count, LEN, HEADS, HEAD_DIM)
    )
    scores, split_heads = key_scores(saved["projected"], lengths)
    probabilities = jnp.exp(scores - saved["logsum"])
    grad_probs = jnp.einsum(
        "sqhd,skhd->shqk", grad_context, split_heads[:, :, 2], preferred_element_type=jnp.float32
    )
    grad_values = jnp.einsum(
        "shqk,sqhd->skhd",
        probabilities.astype(jnp.bfloat16),
        grad_context,
        preferred_element_type=jnp.float32,
    )
    grad_scores = probabilities * (
        grad_probs - jnp.sum(grad_probs * probabilities, axis=-1, keepdims=True)
    )
    grad_scores = grad_scores.astype(jnp.bfloat16)
    grad_queries = jnp.einsum(
        "shqk,skhd->sqhd", grad_scores, split_heads[:, :, 1], preferred_element_type=jnp.float32
    ) * HEAD_DIM ** (-0.5)
    grad_keys = jnp.einsum(
        "shqk,sqhd->skhd", grad_scores, split_heads[:, :, 0], preferred_element_type=jnp.float32
    ) * HEAD_DIM ** (-0.5)
    grad_proj = (
        jnp.stack([grad_queries, grad_keys, grad_values], axis=2)
        .reshape(rows_here, 3 * D)
        .astype(jnp.bfloat16)
    )
    grad_qkv = matmul_left(saved["inputs"], grad_proj)
    grad_bias_all = jnp.sum(grad_proj.astype(jnp.float32), axis=0)
    grad_first = grad_sum_one + trailing_array_multiply(grad_proj, pieces["qkv"])
    grad_embedded, grad_gain_zero, grad_shift_zero = norm_backward(
        grad_first, saved["normed_zero"], saved["inverse_zero"], small_rows[4]
    )
    grad_place = jnp.sum(grad_embedded.reshape(seqs_count, LEN, D), axis=0)
    grad_small = jnp.stack(
        [
            grad_bias_all[:D],
            grad_bias_all[2 * D :],
            jnp.sum(grad_att.astype(jnp.float32), axis=0),
            jnp.sum(grad_out.astype(jnp.float32), axis=0),
            grad_gain_zero,
            grad_shift_zero,
            grad_gain_one,
            grad_shift_one,
            grad_gain_two,
            grad_shift_two,
        ]
    )
    grad_upbias = jnp.sum(grad_hidden.astype(jnp.float32), axis=0)
    tail = jnp.concatenate(
        [grad_small.reshape(60, TILE), grad_upbias.reshape(24, TILE), jnp.zeros((4, TILE), jnp.float32)]
    )
    return ((grad_qkv, grad_outw, grad_up, grad_down, grad_place, tail), grad_embedded)


def combine_stats(earlier, later):
    peak_s = jnp.maximum(earlier[0], later[0])
    peak_t = jnp.maximum(earlier[2], later[2])
    factor_early = jnp.exp(earlier[0] - peak_s)
    factor_late = jnp.exp(later[0] - peak_s)
    teacher_early = jnp.exp(earlier[2] - peak_t)
    teacher_late = jnp.exp(later[2] - peak_t)
    return jnp.stack(
        [
            peak_s,
            earlier[1] * factor_early + later[1] * factor_late,
            peak_t,
            earlier[3] * teacher_early + later[3] * teacher_late,
            earlier[4] * teacher_early + later[4] * teacher_late,
        ]
    )


def adam_step(weight, first_moment, second, gradient, step_float):
    new_first = beta_first * first_moment + (1.0 - beta_first) * gradient
    new_second = beta_second * second + (1.0 - beta_second) * gradient * gradient
    fix_first = 1.0 - jnp.power(beta_first, step_float)
    fix_second = 1.0 - jnp.power(beta_second, step_float)
    update = new_first / fix_first / (jnp.sqrt(new_second / fix_second) + adam_eps)
    return (weight - learn_rate * (update + weight_decay * weight), new_first, new_second)


def gather_student(tiles):
    per = tiles.shape[0]
    half = per // 16 * 8
    arrivals, places = [], []

    def keep(value, plane, near, start):
        for core in (0, 1):
            arrivals.append(swap(value, CORE) if core else value)
            places.append((plane * 8 + near * 2 + core, start, value.shape[0]))

    for plane in range(4):
        across, deep = swap(tiles, ACROSS), swap(tiles, DEEP)
        keep(tiles, plane, 0, 0)
        keep(across, plane, 1, 0)
        keep(deep, plane, 2, 0)
        keep(swap(across[:half], DEEP), plane, 3, 0)
        keep(swap(deep[half:], ACROSS), plane, 3, half)
        if plane < 3:
            tiles = shift(tiles, 1)
    return arrivals, places


def reduce_chunk(mine, other):
    lines = mine.shape[1]
    value = (mine + swap(other, CORE)).reshape(4, 2, 2, lines, TILE)
    first, second = value[2:], value[:2]
    first = first[:, :, 0] + swap(first[:, :, 1], ACROSS)
    second = second[:, 0] + swap(second[:, 1], DEEP)
    first = first[:, 0] + swap(first[:, 1], DEEP)
    second = second[:, 0] + swap(second[:, 1], ACROSS)
    moving = shift(first[1], 1)
    moving = shift(first[0] + moving, 1)
    moving = shift(second[1] + moving, 1)
    return second[0] + moving


def on_device(
    near,
    token_ids,
    lengths,
    mask_pos,
    mask_count,
    owner_order,
    step_count,
    teacher_flat,
    mentor_lexicon_weights,
    student_flat,
    flat_first,
    flat_second,
    student_embed,
    embed_first,
    embed_second,
):
    per = student_flat.shape[0]
    tiles_all = owner_order.shape[0]
    vocab_rows, width_share = student_embed.shape
    planes = lax.axis_size("dp")
    group = lax.axis_size("vocab")
    here = lax.axis_index("vocab")

    facts = jnp.concatenate([token_ids.reshape(LEN), lengths, mask_count, jnp.zeros((TILE - 2,), jnp.int32)])
    target_rows = rows_of_tiles(owner_order)
    student_low = student_flat.astype(jnp.bfloat16)
    table_low = lax.all_gather(student_embed.T.astype(jnp.bfloat16), "dp", axis=0, tiled=True)
    teacher_tiles = lax.all_gather(teacher_flat, ("dp", "vocab"), axis=0, tiled=True)
    if near:
        plane_facts = gather_near(facts)
        by_plane = [facts, shift(facts, 1), shift(facts, 2), shift(facts, 3)]
        other_facts = gather_near(jnp.stack(by_plane[1:]))
        all_facts = jnp.concatenate([plane_facts[:, None], other_facts], axis=1)
        arrivals, places = gather_student(student_low)
        relative = relative_order(target_rows, per)
        downward = rolled(relative, True).reshape(-1)
        upward = rolled(relative.transpose(3, 0, 1, 2, 4).swapaxes(0, 1), False).swapaxes(0, 1).reshape(-1)
        matrices = place_tiles(downward, arrivals, tuple(places), planes * group, per)
    else:
        by_plane = lax.all_gather(facts, "dp", axis=0)
        all_facts = lax.all_gather(by_plane, "vocab", axis=0)
        plane_facts = lax.dynamic_index_in_dim(all_facts, lax.axis_index("dp"), 1, keepdims=False)
        student_tiles = lax.all_gather(student_low, ("dp", "vocab"), axis=0, tiled=True)
        matrices = place_tiles(
            target_rows, [student_tiles.reshape(planes * group, per, TILE)], (None,), planes * group, per
        )
    student = pieces_of(matrices[:5], matrices[5])
    teacher = pieces_of(
        [unpack_matrix(teacher_tiles, piece) for piece in MATRICES],
        teacher_tiles[TAIL : TAIL + TAIL_TILES].astype(jnp.float32),
    )
    token_total = jnp.sum(all_facts[:, :, LEN]).astype(jnp.float32)
    masked_total = jnp.sum(all_facts[:, :, LEN + 1]).astype(jnp.float32)

    words = jnp.arange(vocab_rows, dtype=jnp.int32)

    def chosen(ids):
        return (ids.reshape(-1, 1) - here * vocab_rows == words[None]).astype(jnp.bfloat16)

    def looked_up(multiply):
        if near:
            far = multiply(chosen(plane_facts[4:, :LEN])).astype(jnp.bfloat16)
            close = multiply(chosen(plane_facts[:4, :LEN])).astype(jnp.bfloat16)
            total = scatter_near(far.reshape(2, 2, LEN, D), close.reshape(2, 2, LEN, D))
        else:
            rows = multiply(chosen(plane_facts[:, :LEN])).astype(jnp.bfloat16)
            total = lax.psum_scatter(rows, "vocab", scatter_dimension=0, tiled=True)
        return total.astype(jnp.float32)

    looked_t = looked_up(lambda pick: array_multiply(pick, mentor_lexicon_weights))
    looked_s = looked_up(lambda pick: trailing_array_multiply(pick, table_low))
    final_s, saved = layer_forward(student, looked_s, lengths)
    final_t = layer_forward(teacher, looked_t, lengths)[0]

    offsets = jnp.concatenate([mask_pos.reshape(CAP), jnp.zeros((SLOTS - CAP,), jnp.int32)])
    picked_s = final_s[offsets].astype(jnp.bfloat16)
    picked_t = final_t[offsets].astype(jnp.bfloat16)
    if near:
        learner_picked = gather_near(picked_s).reshape(-1, D)
        mentor_picked = gather_near(picked_t).reshape(-1, D)
    else:
        learner_picked = lax.all_gather(picked_s, "vocab", axis=0, tiled=True)
        mentor_picked = lax.all_gather(picked_t, "vocab", axis=0, tiled=True)
    live_weighting = (
        (jnp.arange(SLOTS)[None] < plane_facts[:, LEN + 1, None]).astype(jnp.float32).reshape(-1)
    )
    learner_energy = array_multiply(learner_picked, table_low) / smoothing_heat_scale
    teacher_logit = (
        trailing_array_multiply(mentor_picked, mentor_lexicon_weights) / smoothing_heat_scale
    )
    peak_s = jnp.max(learner_energy, axis=1)
    peak_t = jnp.max(teacher_logit, axis=1)
    teacher_exps = jnp.exp(teacher_logit - peak_t[:, None])
    stats = jnp.stack(
        [
            peak_s,
            jnp.sum(jnp.exp(learner_energy - peak_s[:, None]), axis=1),
            peak_t,
            jnp.sum(teacher_exps, axis=1),
            jnp.sum(teacher_exps * (teacher_logit - learner_energy), axis=1),
        ]
    )
    if near:
        stats = stats.reshape(5, 2, 2, 2, SLOTS)
        for axis, bit in ((1, CORE), (2, DEEP), (3, ACROSS)):
            stats = combine_stats(stats, jnp.flip(swap(stats, bit), axis))
        stats = stats.reshape(5, -1)
    else:
        everything = lax.all_gather(stats, "vocab", axis=0)
        stats = everything[0]
        for k in range(1, group):
            stats = combine_stats(stats, everything[k])
    logsum_s = stats[0] + jnp.log(stats[1])
    logsum_t = stats[2] + jnp.log(stats[3])
    diverge = stats[4] / stats[3] - logsum_t + logsum_s
    mine = 0 if near else here * SLOTS
    divergence_part = jnp.sum(lax.dynamic_slice_in_dim(diverge * live_weighting, mine, SLOTS))
    student_probs = jnp.exp(learner_energy - logsum_s[:, None])
    teacher_probs = jnp.exp(teacher_logit - logsum_t[:, None])
    grad_logit = (
        mixing_coefficient
        * smoothing_heat_scale
        / masked_total
        * live_weighting[:, None]
        * (student_probs - teacher_probs)
    ).astype(jnp.bfloat16)
    if near:
        half = grad_logit.shape[0] // 2
        far = trailing_array_multiply(grad_logit[half:], table_low).reshape(2, 2, SLOTS, D)
        close = trailing_array_multiply(grad_logit[:half], table_low).reshape(2, 2, SLOTS, D)
        grad_rows = scatter_near(far, close)
    else:
        grad_rows = lax.psum_scatter(
            trailing_array_multiply(grad_logit, table_low), "vocab", scatter_dimension=0, tiled=True
        )
    head_part = lax.psum_scatter(
        matmul_left(learner_picked, grad_logit), "dp", scatter_dimension=0, tiled=True
    )
    products = jnp.sum(final_s * final_t, axis=1)
    inverse_s = lax.rsqrt(jnp.sum(final_s * final_s, axis=1) + cosine_eps)
    inverse_t = lax.rsqrt(jnp.sum(final_t * final_t, axis=1) + cosine_eps)
    live_rows = (jnp.arange(LEN)[None, :] < lengths[:, None]).reshape(-1)
    cosine = products * inverse_s * inverse_t
    cosine_term = jnp.sum(jnp.where(live_rows, 1.0 - cosine, 0.0))
    weighting = jnp.where(live_rows, -cosine_weight / token_total, 0.0) * inverse_s * inverse_t
    grad_final = weighting[:, None] * (
        final_t - (products * inverse_s * inverse_s)[:, None] * final_s
    )
    grad_final = grad_final.at[offsets].add(grad_rows)
    layer_grads, grad_embedded = layer_backward(student, saved, grad_final, lengths)

    shares = grad_embedded.astype(jnp.bfloat16).reshape(LEN, planes, width_share).transpose(1, 0, 2)
    if near:
        z = lax.axis_index("dp")
        own = [lax.dynamic_index_in_dim(shares, (z + k) % 4, keepdims=False) for k in range(4)]
        shares = jnp.stack([own[0]] + [shift(own[k], k) for k in (1, 2, 3)])
        ids = all_facts[:, :, :LEN].reshape(2, 2, 2, planes, LEN)
        for axis, bit in ((0, CORE), (1, DEEP), (2, ACROSS)):
            ids = jnp.where((here & bit) != 0, jnp.flip(ids, axis), ids)
        ids = ids.transpose(1, 2, 0, 3, 4)
    else:
        shares = lax.all_to_all(shares, "dp", 0, 0)
        ids = all_facts[:, :, :LEN]
    token_grads = lax.all_gather(shares.reshape(-1, width_share), "vocab", axis=0, tiled=True)
    token_part = matmul_left(token_grads, chosen(ids))
    table_grad = (head_part + token_part).T

    if near:
        split = per // 16 * 8
        parts = []
        for begin, end in ((0, split), (split, per)):
            own_tiles, other_tiles = collect_tiles(upward, layer_grads, tiles_all, per, 2, begin, end - begin)
            parts.append(reduce_chunk(own_tiles, other_tiles))
        flat_grad = jnp.concatenate(parts)
    else:
        (grad_tiles,) = collect_tiles(target_rows, layer_grads, tiles_all, per, 1, 0, per)
        flat_grad = lax.psum_scatter(
            grad_tiles.reshape(tiles_all, TILE), ("dp", "vocab"), scatter_dimension=0, tiled=True
        )
    loss_term = (
        mixing_coefficient * smoothing_heat_scale**2 * divergence_part / masked_total
        + cosine_weight * cosine_term / token_total
    )
    squares = jnp.sum(flat_grad * flat_grad) + jnp.sum(table_grad * table_grad)
    if near:
        squares, loss_value = sum_everywhere(jnp.stack([squares, loss_term]))
    else:
        squares, loss_value = lax.psum((squares, loss_term), ("dp", "vocab"))
    grad_norm = jnp.sqrt(squares)
    factor = clip_norm / jnp.maximum(grad_norm, clip_norm)
    step_float = step_count[0].astype(jnp.float32)
    new_flat, new_flat_first, new_flat_second = adam_step(
        student_flat, flat_first, flat_second, flat_grad * factor, step_float
    )
    new_embed, new_embed_first, new_embed_second = adam_step(
        student_embed, embed_first, embed_second, table_grad * factor, step_float
    )
    return (
        loss_value,
        grad_norm,
        new_flat,
        new_flat_first,
        new_flat_second,
        new_embed,
        new_embed_first,
        new_embed_second,
    )


def solution(mesh):
    near = mesh.shape["dp"] == 4 and mesh.shape["vocab"] == 8
    return jax.shard_map(
        functools.partial(on_device, near),
        mesh=mesh,
        in_specs=(
            P(("dp", "vocab"), None),
            P(("dp", "vocab")),
            P(("dp", "vocab"), None),
            P(("dp", "vocab")),
            P(),
            P(),
            P(("dp", "vocab"), None),
            P("vocab", None),
            P(("dp", "vocab"), None),
            P(("dp", "vocab"), None),
            P(("dp", "vocab"), None),
            P("vocab", "dp"),
            P("vocab", "dp"),
            P("vocab", "dp"),
        ),
        out_specs=(
            P(),
            P(),
            P(("dp", "vocab"), None),
            P(("dp", "vocab"), None),
            P(("dp", "vocab"), None),
            P("vocab", "dp"),
            P("vocab", "dp"),
            P("vocab", "dp"),
        ),
        check_vma=False,
    )
```

```python
import functools

import jax
import jax.numpy as jnp
from jax import lax
from jax.experimental import pallas as pl
from jax.experimental.pallas import tpu as pltpu
from jax.sharding import PartitionSpec as P

D = 768
HEADS = 12
HEAD_DIM = 64
FF = 3072
LEN = 512
CAP = 120
SLOTS = 128
TILE = 128

QKV = (0, D, 18)
OUT = (13824, D, 6)
UP = (18432, D, 24)
DOWN = (36864, FF, 6)
PLACE = (55296, LEN, 6)
MATRICES = (QKV, OUT, UP, DOWN, PLACE)
TAIL = 58368
TAIL_TILES = 88

VMEM_LIMIT = 60 * 1024 * 1024

smoothing_heat_scale = 2.0
mixing_coefficient = 5.0
cosine_weight = 20.0
clip_norm = 0.01
beta_first = 0.9
beta_second = 0.98
adam_eps = 1e-08
weight_decay = 0.01
learn_rate = 0.1
norm_eps = 1e-12
cosine_eps = 1e-06

CORE, ACROSS, DEEP = 1, 2, 4


def swap(value, bit):
    return lax.ppermute(value, "vocab", [(i, i ^ bit) for i in range(8)])


def shift(value, steps):
    size = lax.axis_size("dp")
    return lax.ppermute(value, "dp", [(i, (i + steps) % size) for i in range(size)])


def gather_near(value):
    value = value[None]
    for bit in (ACROSS, DEEP, CORE):
        value = jnp.concatenate([value, swap(value, bit)])
    return value


def scatter_near(value_far, value_near):
    half = value_near.shape[2] // 2
    value = value_near + swap(value_far, CORE)
    upper, lower = value[:, :, :half], value[:, :, half:]
    upper = upper[:, 0] + swap(upper[:, 1], ACROSS)
    lower = lower[0] + swap(lower[1], DEEP)
    upper = upper[0] + swap(upper[1], DEEP)
    lower = lower[0] + swap(lower[1], ACROSS)
    return jnp.concatenate([upper, lower])


def sum_everywhere(value):
    for bit in (CORE, ACROSS, DEEP):
        value = value + swap(value, bit)
    for step in (1, 2):
        value = value + lax.ppermute(value, "dp", [(i, i ^ step) for i in range(4)])
    return value


def relative_order(table, per_device):
    here = lax.axis_index("vocab")
    table = table.reshape(4, 2, 2, 2, per_device)
    for axis, bit in ((1, DEEP), (2, ACROSS), (3, CORE)):
        table = jnp.where((here & bit) != 0, jnp.flip(table, axis), table)
    return table


def rolled(table, downward):
    z = lax.axis_index("dp")
    order = (z - jnp.arange(4)) % 4 if downward else (z + jnp.arange(4)) % 4
    return jnp.stack([lax.dynamic_index_in_dim(table, order[k], keepdims=False) for k in range(4)])


def rows_of_tiles(tiles):
    rows = tiles
    for first, height, across in MATRICES:
        inside = (tiles >= first) & (tiles < first + height * across)
        at = tiles - first
        rows = jnp.where(inside, first + (at % across) * height + at // across, rows)
    return rows


def unpack_kernel(source, target, stage, *, across):
    stage[...] = source[...].astype(jnp.float32)

    def step(g, carry):
        for column in range(across):
            lines = stage[pl.ds(g * 16 * across + column, 16, stride=across), :]
            target[pl.ds(pl.multiple_of(g * 16, 16), 16), column * TILE : (column + 1) * TILE] = lines.astype(
                jnp.bfloat16
            )
        return carry

    lax.fori_loop(0, target.shape[0] // 16, step, 0)


def unpack_matrix(tiles, piece):
    first, height, across = piece
    lines = 64 if across > 6 else 128
    block = lines * across
    return pl.pallas_call(
        functools.partial(unpack_kernel, across=across),
        grid=(height // lines,),
        in_specs=[pl.BlockSpec((block, TILE), lambda i: (first // block + i, 0))],
        out_specs=pl.BlockSpec((lines, across * TILE), lambda i: (i, 0)),
        out_shape=jax.ShapeDtypeStruct((height, across * TILE), jnp.bfloat16),
        scratch_shapes=[pltpu.VMEM((block, TILE), jnp.float32)],
        name="unpack_matrix",
    )(tiles)


def place_kernel(rows, *refs, places, count, per):
    arrivals = refs[: len(places)]
    targets = refs[len(places) : len(places) + 5]
    tail = refs[len(places) + 5]
    landed, stage, full, packed, in_sems, out_sems, tail_sem = refs[len(places) + 6 :]
    copies = []
    for n, (arrival, place) in enumerate(zip(arrivals, places)):
        target = landed if place is None else landed.at[place[0], pl.ds(place[1], place[2])]
        copies.append(pltpu.make_async_copy(arrival, target, in_sems.at[n]))
    for copy in copies:
        copy.start()
    for copy in copies:
        copy.wait()

    def lines(block, start, size):
        stage[pl.ds(0, size), :] = landed[block, pl.ds(start, size), :].astype(jnp.float32)
        base = block * per + start
        for u in range(size):
            full[pl.ds(rows[base + u], 1), :] = stage[pl.ds(u, 1), :]

    whole, rest = divmod(per, 128)

    def one_block(block, carry):
        def one_step(i, inner):
            lines(block, pl.multiple_of(i * 128, 128), 128)
            return inner

        lax.fori_loop(0, whole, one_step, 0)
        if rest:
            lines(block, whole * 128, rest)
        return carry

    lax.fori_loop(0, count, one_block, 0)
    tail_copy = pltpu.make_async_copy(full.at[pl.ds(TAIL, TAIL_TILES)], tail, tail_sem)
    tail_copy.start()
    for target, (first, height, across) in zip(targets, MATRICES):
        size = min(height, D)
        parts = height // size

        def out_copy(n, slot, target=target, size=size, parts=parts):
            column, part = n // parts, n % parts
            return pltpu.make_async_copy(
                packed.at[slot, pl.ds(0, size)],
                target.at[
                    pl.ds(pl.multiple_of(part * size, 256), size),
                    pl.ds(pl.multiple_of(column * TILE, TILE), TILE),
                ],
                out_sems.at[slot],
            )

        def one_column(n, carry, first=first, size=size, out_copy=out_copy):
            slot = n % 2

            @pl.when(n >= 2)
            def _():
                out_copy(n - 2, slot).wait()

            packed[slot, pl.ds(0, size), :] = full[pl.ds(pl.multiple_of(first + n * size, 128), size), :].astype(
                jnp.bfloat16
            )
            out_copy(n, slot).start()
            return carry

        total = across * parts
        lax.fori_loop(0, total, one_column, 0)
        for n in (total - 2, total - 1):
            out_copy(n, n % 2).wait()
    tail_copy.wait()


def place_tiles(rows, arrivals, places, count, per):
    shapes = [jax.ShapeDtypeStruct((h, a * TILE), jnp.bfloat16) for _, h, a in MATRICES]
    return pl.pallas_call(
        functools.partial(place_kernel, places=places, count=count, per=per),
        in_specs=[pl.BlockSpec(memory_space=pltpu.SMEM)] + [pl.BlockSpec(memory_space=pl.ANY)] * len(arrivals),
        out_specs=[pl.BlockSpec(memory_space=pl.ANY)] * 6,
        out_shape=shapes + [jax.ShapeDtypeStruct((TAIL_TILES, TILE), jnp.float32)],
        scratch_shapes=[
            pltpu.VMEM((count, per, TILE), jnp.bfloat16),
            pltpu.VMEM((128, TILE), jnp.float32),
            pltpu.VMEM((count * per, TILE), jnp.float32),
            pltpu.VMEM((2, D, TILE), jnp.bfloat16),
            pltpu.SemaphoreType.DMA((len(arrivals),)),
            pltpu.SemaphoreType.DMA((2,)),
            pltpu.SemaphoreType.DMA,
        ],
        compiler_params=pltpu.CompilerParams(vmem_limit_bytes=VMEM_LIMIT),
        cost_estimate=pl.CostEstimate(flops=0, bytes_accessed=180_000_000, transcendentals=0),
        name="place_tiles",
    )(rows, *arrivals)


def step_size(rows):
    return max(n for n in range(8, 193, 8) if rows % n == 0)


def collect_kernel(rows, *refs, outs, blocks, per, begin):
    sources, targets = refs[:6], refs[6 : 6 + outs]
    full, sems = refs[6 + outs :]
    block = pl.program_id(0)

    @pl.when(block == 0)
    def _():
        copies = []
        for source, (first, height, across) in zip(sources, MATRICES):
            for column in range(across):
                copies.append(
                    pltpu.make_async_copy(
                        source.at[:, pl.ds(column * TILE, TILE)],
                        full.at[pl.ds(first + column * height, height)],
                        sems.at[len(copies)],
                    )
                )
        copies.append(pltpu.make_async_copy(sources[5], full.at[pl.ds(TAIL, TAIL_TILES)], sems.at[len(copies)]))
        for copy in copies:
            copy.start()
        unused = full.shape[0] - TAIL - TAIL_TILES
        full[pl.ds(TAIL + TAIL_TILES, unused), :] = jnp.zeros((unused, TILE), jnp.float32)
        for copy in copies:
            copy.wait()

    size = step_size(targets[0].shape[1])
    for n, target in enumerate(targets):
        base = (n * blocks + block) * per + begin

        def one_step(i, carry, target=target, base=base):
            start = pl.multiple_of(i * size, 8)
            for u in range(size):
                target[0, pl.ds(start + u, 1), :] = full[pl.ds(rows[base + start + u], 1), :]
            return carry

        lax.fori_loop(0, target.shape[1] // size, one_step, 0)


def collect_tiles(rows, sources, tiles_all, per, outs, begin, lines):
    blocks = tiles_all // per // outs
    return pl.pallas_call(
        functools.partial(collect_kernel, outs=outs, blocks=blocks, per=per, begin=begin),
        grid=(blocks,),
        in_specs=[pl.BlockSpec(memory_space=pltpu.SMEM)] + [pl.BlockSpec(memory_space=pl.ANY)] * 6,
        out_specs=[pl.BlockSpec((1, lines, TILE), lambda i: (i, 0, 0))] * outs,
        out_shape=[jax.ShapeDtypeStruct((blocks, lines, TILE), jnp.float32)] * outs,
        scratch_shapes=[pltpu.VMEM((tiles_all, TILE), jnp.float32), pltpu.SemaphoreType.DMA((61,))],
        compiler_params=pltpu.CompilerParams(vmem_limit_bytes=VMEM_LIMIT),
        cost_estimate=pl.CostEstimate(flops=0, bytes_accessed=80_000_000, transcendentals=0),
        name="collect_tiles",
    )(rows, *sources)


def array_multiply(left_side, right_side):
    return jnp.dot(left_side, right_side, preferred_element_type=jnp.float32)


def matmul_left(left_side, right_side):
    return lax.dot_general(
        left_side, right_side, (((0,), (0,)), ((), ())), preferred_element_type=jnp.float32
    )


def trailing_array_multiply(left_side, right_side):
    return lax.dot_general(
        left_side, right_side, (((1,), (1,)), ((), ())), preferred_element_type=jnp.float32
    )


def pieces_of(matrices, tail):
    qkv, out, up, down, place = matrices
    return {
        "qkv": qkv,
        "out": out,
        "up": up,
        "down": down,
        "place": place,
        "small": tail[:60].reshape(10, D),
        "upbias": tail[60:84].reshape(FF),
    }


def norm_forward(values, gain_row, shift_row):
    center = values - jnp.mean(values, axis=-1, keepdims=True)
    inverse = lax.rsqrt(jnp.mean(center * center, axis=-1, keepdims=True) + norm_eps)
    normed = center * inverse
    return (normed * gain_row + shift_row, normed, inverse)


def norm_backward(grad_out, normed, inverse, gain_row):
    scaled = grad_out * gain_row
    grad_in = inverse * (
        scaled
        - jnp.mean(scaled, axis=-1, keepdims=True)
        - normed * jnp.mean(scaled * normed, axis=-1, keepdims=True)
    )
    return (grad_in, jnp.sum(grad_out * normed, axis=0), jnp.sum(grad_out, axis=0))


def gelu_slope(values):
    return (
        0.5 * (1.0 + lax.erf(values * 0.7071067811865476))
        + values * jnp.exp(-0.5 * values * values) * 0.3989422804014327
    )


def key_scores(projected, lengths):
    seqs_count = lengths.shape[0]
    split_heads = projected.reshape(seqs_count, LEN, 3, HEADS, HEAD_DIM)
    scores = jnp.einsum(
        "sqhd,skhd->shqk",
        split_heads[:, :, 0],
        split_heads[:, :, 1],
        preferred_element_type=jnp.float32,
    ) * HEAD_DIM ** (-0.5)
    live_keys = jnp.arange(LEN)[None, :] < lengths[:, None]
    return (jnp.where(live_keys[:, None, None, :], scores, -1000000000.0), split_heads)


def layer_forward(pieces, looked, lengths):
    small_rows = pieces["small"].astype(jnp.float32)
    seqs_count = lengths.shape[0]
    rows_here = seqs_count * LEN
    summed = (
        looked.reshape(seqs_count, LEN, D) + pieces["place"].astype(jnp.float32)[None]
    ).reshape(rows_here, D)
    first_norm, normed_zero, inverse_zero = norm_forward(summed, small_rows[4], small_rows[5])
    inputs = first_norm.astype(jnp.bfloat16)
    qkv_bias = jnp.concatenate([small_rows[0], jnp.zeros((D,), jnp.float32), small_rows[1]])
    projected = (array_multiply(inputs, pieces["qkv"]) + qkv_bias).astype(jnp.bfloat16)
    scores, split_heads = key_scores(projected, lengths)
    peak = jnp.max(scores, axis=-1, keepdims=True)
    exps = jnp.exp(scores - peak)
    totals = jnp.sum(exps, axis=-1, keepdims=True)
    probabilities = (exps / totals).astype(jnp.bfloat16)
    logsum = peak + jnp.log(totals)
    context = jnp.einsum(
        "shqk,skhd->sqhd", probabilities, split_heads[:, :, 2], preferred_element_type=jnp.float32
    )
    context = context.reshape(rows_here, D).astype(jnp.bfloat16)
    attended = array_multiply(context, pieces["out"]) + small_rows[2]
    middle, normed_one, inverse_one = norm_forward(
        first_norm + attended, small_rows[6], small_rows[7]
    )
    middle_low = middle.astype(jnp.bfloat16)
    hidden = array_multiply(middle_low, pieces["up"]) + pieces["upbias"].astype(jnp.float32)
    activated = jax.nn.gelu(hidden, approximate=False).astype(jnp.bfloat16)
    output = array_multiply(activated, pieces["down"]) + small_rows[3]
    final_lines, normed_two, inverse_two = norm_forward(
        middle + output, small_rows[8], small_rows[9]
    )
    saved = {
        "inputs": inputs,
        "projected": projected,
        "logsum": logsum,
        "context": context,
        "middle_low": middle_low,
        "hidden": hidden,
        "activated": activated,
        "normed_zero": normed_zero,
        "inverse_zero": inverse_zero,
        "normed_one": normed_one,
        "inverse_one": inverse_one,
        "normed_two": normed_two,
        "inverse_two": inverse_two,
    }
    return (final_lines, saved)


def layer_backward(pieces, saved, grad_final, lengths):
    small_rows = pieces["small"].astype(jnp.float32)
    seqs_count = lengths.shape[0]
    rows_here = seqs_count * LEN
    grad_sum_two, grad_gain_two, grad_shift_two = norm_backward(
        grad_final, saved["normed_two"], saved["inverse_two"], small_rows[8]
    )
    grad_out = grad_sum_two.astype(jnp.bfloat16)
    grad_down = matmul_left(saved["activated"], grad_out)
    grad_act = trailing_array_multiply(grad_out, pieces["down"])
    grad_hidden = (grad_act * gelu_slope(saved["hidden"])).astype(jnp.bfloat16)
    grad_up = matmul_left(saved["middle_low"], grad_hidden)
    grad_middle = grad_sum_two + trailing_array_multiply(grad_hidden, pieces["up"])
    grad_sum_one, grad_gain_one, grad_shift_one = norm_backward(
        grad_middle, saved["normed_one"], saved["inverse_one"], small_rows[6]
    )
    grad_att = grad_sum_one.astype(jnp.bfloat16)
    grad_outw = matmul_left(saved["context"], grad_att)
    grad_context = (
        trailing_array_multiply(grad_att, pieces["out"])
        .astype(jnp.bfloat16)
        .reshape(seqs_count, LEN, HEADS, HEAD_DIM)
    )
    scores, split_heads = key_scores(saved["projected"], lengths)
    probabilities = jnp.exp(scores - saved["logsum"])
    grad_probs = jnp.einsum(
        "sqhd,skhd->shqk", grad_context, split_heads[:, :, 2], preferred_element_type=jnp.float32
    )
    grad_values = jnp.einsum(
        "shqk,sqhd->skhd",
        probabilities.astype(jnp.bfloat16),
        grad_context,
        preferred_element_type=jnp.float32,
    )
    grad_scores = probabilities * (
        grad_probs - jnp.sum(grad_probs * probabilities, axis=-1, keepdims=True)
    )
    grad_scores = grad_scores.astype(jnp.bfloat16)
    grad_queries = jnp.einsum(
        "shqk,skhd->sqhd", grad_scores, split_heads[:, :, 1], preferred_element_type=jnp.float32
    ) * HEAD_DIM ** (-0.5)
    grad_keys = jnp.einsum(
        "shqk,sqhd->skhd", grad_scores, split_heads[:, :, 0], preferred_element_type=jnp.float32
    ) * HEAD_DIM ** (-0.5)
    grad_proj = (
        jnp.stack([grad_queries, grad_keys, grad_values], axis=2)
        .reshape(rows_here, 3 * D)
        .astype(jnp.bfloat16)
    )
    grad_qkv = matmul_left(saved["inputs"], grad_proj)
    grad_bias_all = jnp.sum(grad_proj.astype(jnp.float32), axis=0)
    grad_first = grad_sum_one + trailing_array_multiply(grad_proj, pieces["qkv"])
    grad_embedded, grad_gain_zero, grad_shift_zero = norm_backward(
        grad_first, saved["normed_zero"], saved["inverse_zero"], small_rows[4]
    )
    grad_place = jnp.sum(grad_embedded.reshape(seqs_count, LEN, D), axis=0)
    grad_small = jnp.stack(
        [
            grad_bias_all[:D],
            grad_bias_all[2 * D :],
            jnp.sum(grad_att.astype(jnp.float32), axis=0),
            jnp.sum(grad_out.astype(jnp.float32), axis=0),
            grad_gain_zero,
            grad_shift_zero,
            grad_gain_one,
            grad_shift_one,
            grad_gain_two,
            grad_shift_two,
        ]
    )
    grad_upbias = jnp.sum(grad_hidden.astype(jnp.float32), axis=0)
    tail = jnp.concatenate(
        [grad_small.reshape(60, TILE), grad_upbias.reshape(24, TILE), jnp.zeros((4, TILE), jnp.float32)]
    )
    return ((grad_qkv, grad_outw, grad_up, grad_down, grad_place, tail), grad_embedded)


def combine_stats(earlier, later):
    peak_s = jnp.maximum(earlier[0], later[0])
    peak_t = jnp.maximum(earlier[2], later[2])
    factor_early = jnp.exp(earlier[0] - peak_s)
    factor_late = jnp.exp(later[0] - peak_s)
    teacher_early = jnp.exp(earlier[2] - peak_t)
    teacher_late = jnp.exp(later[2] - peak_t)
    return jnp.stack(
        [
            peak_s,
            earlier[1] * factor_early + later[1] * factor_late,
            peak_t,
            earlier[3] * teacher_early + later[3] * teacher_late,
            earlier[4] * teacher_early + later[4] * teacher_late,
        ]
    )


def adam_step(weight, first_moment, second, gradient, step_float):
    new_first = beta_first * first_moment + (1.0 - beta_first) * gradient
    new_second = beta_second * second + (1.0 - beta_second) * gradient * gradient
    fix_first = 1.0 - jnp.power(beta_first, step_float)
    fix_second = 1.0 - jnp.power(beta_second, step_float)
    update = new_first / fix_first / (jnp.sqrt(new_second / fix_second) + adam_eps)
    return (weight - learn_rate * (update + weight_decay * weight), new_first, new_second)


def gather_student(tiles):
    per = tiles.shape[0]
    half = per // 16 * 8
    arrivals, places = [], []

    def keep(value, plane, near, start):
        for core in (0, 1):
            arrivals.append(swap(value, CORE) if core else value)
            places.append((plane * 8 + near * 2 + core, start, value.shape[0]))

    for plane in range(4):
        across, deep = swap(tiles, ACROSS), swap(tiles, DEEP)
        keep(tiles, plane, 0, 0)
        keep(across, plane, 1, 0)
        keep(deep, plane, 2, 0)
        keep(swap(across[:half], DEEP), plane, 3, 0)
        keep(swap(deep[half:], ACROSS), plane, 3, half)
        if plane < 3:
            tiles = shift(tiles, 1)
    return arrivals, places


def sent_low(value, bit):
    return swap(value.astype(jnp.bfloat16), bit).astype(jnp.float32)


def reduce_chunk(value):
    lines = value.shape[1]
    value = value.reshape(4, 2, 2, lines, TILE)
    first, second = value[2:], value[:2]
    first = first[:, :, 0] + sent_low(first[:, :, 1], ACROSS)
    second = second[:, 0] + sent_low(second[:, 1], DEEP)
    first = first[:, 0] + sent_low(first[:, 1], DEEP)
    second = second[:, 0] + sent_low(second[:, 1], ACROSS)
    moving = shift(first[1], 1)
    moving = shift(first[0] + moving, 1)
    moving = shift(second[1] + moving, 1)
    return second[0] + moving


def on_device(
    near,
    token_ids,
    lengths,
    mask_pos,
    mask_count,
    owner_order,
    step_count,
    teacher_flat,
    mentor_lexicon_weights,
    student_flat,
    flat_first,
    flat_second,
    student_embed,
    embed_first,
    embed_second,
):
    per = student_flat.shape[0]
    tiles_all = owner_order.shape[0]
    vocab_rows, width_share = student_embed.shape
    planes = lax.axis_size("dp")
    group = lax.axis_size("vocab")
    here = lax.axis_index("vocab")

    facts = jnp.concatenate([token_ids.reshape(LEN), lengths, mask_count, jnp.zeros((TILE - 2,), jnp.int32)])
    target_rows = rows_of_tiles(owner_order)
    student_low = student_flat.astype(jnp.bfloat16)
    table_low = lax.all_gather(student_embed.T.astype(jnp.bfloat16), "dp", axis=0, tiled=True)
    teacher_tiles = lax.all_gather(teacher_flat, ("dp", "vocab"), axis=0, tiled=True)
    if near:
        plane_facts = gather_near(facts)
        by_plane = [facts, shift(facts, 1), shift(facts, 2), shift(facts, 3)]
        other_facts = gather_near(jnp.stack(by_plane[1:]))
        all_facts = jnp.concatenate([plane_facts[:, None], other_facts], axis=1)
        relative = relative_order(target_rows, per)
        downward = rolled(relative, True).reshape(-1)
        upward = rolled(relative.transpose(3, 0, 1, 2, 4).swapaxes(0, 1), False).swapaxes(0, 1).reshape(-1)
    else:
        by_plane = lax.all_gather(facts, "dp", axis=0)
        all_facts = lax.all_gather(by_plane, "vocab", axis=0)
        plane_facts = lax.dynamic_index_in_dim(all_facts, lax.axis_index("dp"), 1, keepdims=False)
        student_tiles = lax.all_gather(student_low, ("dp", "vocab"), axis=0, tiled=True)
    token_total = jnp.sum(all_facts[:, :, LEN]).astype(jnp.float32)
    masked_total = jnp.sum(all_facts[:, :, LEN + 1]).astype(jnp.float32)

    words = jnp.arange(vocab_rows, dtype=jnp.int32)

    def chosen(ids):
        return (ids.reshape(-1, 1) - here * vocab_rows == words[None]).astype(jnp.bfloat16)

    def looked_up(multiply):
        if near:
            far = multiply(chosen(plane_facts[4:, :LEN])).astype(jnp.bfloat16)
            close = multiply(chosen(plane_facts[:4, :LEN])).astype(jnp.bfloat16)
            total = scatter_near(far.reshape(2, 2, LEN, D), close.reshape(2, 2, LEN, D))
        else:
            rows = multiply(chosen(plane_facts[:, :LEN])).astype(jnp.bfloat16)
            total = lax.psum_scatter(rows, "vocab", scatter_dimension=0, tiled=True)
        return total.astype(jnp.float32)

    looked_t = looked_up(lambda pick: array_multiply(pick, mentor_lexicon_weights))
    looked_s = looked_up(lambda pick: trailing_array_multiply(pick, table_low))
    if near:
        arrivals, places = gather_student(student_low)
        arrivals, looked_t, looked_s = lax.optimization_barrier((arrivals, looked_t, looked_s))
        matrices = place_tiles(downward, arrivals, tuple(places), planes * group, per)
    else:
        matrices = place_tiles(
            target_rows, [student_tiles.reshape(planes * group, per, TILE)], (None,), planes * group, per
        )
    student = pieces_of(matrices[:5], matrices[5])
    teacher = pieces_of(
        [unpack_matrix(teacher_tiles, piece) for piece in MATRICES],
        teacher_tiles[TAIL : TAIL + TAIL_TILES].astype(jnp.float32),
    )
    final_s, saved = layer_forward(student, looked_s, lengths)
    final_t = layer_forward(teacher, looked_t, lengths)[0]

    offsets = jnp.concatenate([mask_pos.reshape(CAP), jnp.zeros((SLOTS - CAP,), jnp.int32)])
    picked_s = final_s[offsets].astype(jnp.bfloat16)
    picked_t = final_t[offsets].astype(jnp.bfloat16)
    if near:
        learner_picked = gather_near(picked_s).reshape(-1, D)
        mentor_picked = gather_near(picked_t).reshape(-1, D)
    else:
        learner_picked = lax.all_gather(picked_s, "vocab", axis=0, tiled=True)
        mentor_picked = lax.all_gather(picked_t, "vocab", axis=0, tiled=True)
    live_weighting = (
        (jnp.arange(SLOTS)[None] < plane_facts[:, LEN + 1, None]).astype(jnp.float32).reshape(-1)
    )
    learner_energy = array_multiply(learner_picked, table_low) / smoothing_heat_scale
    teacher_logit = (
        trailing_array_multiply(mentor_picked, mentor_lexicon_weights) / smoothing_heat_scale
    )
    peak_s = jnp.max(learner_energy, axis=1)
    peak_t = jnp.max(teacher_logit, axis=1)
    teacher_exps = jnp.exp(teacher_logit - peak_t[:, None])
    stats = jnp.stack(
        [
            peak_s,
            jnp.sum(jnp.exp(learner_energy - peak_s[:, None]), axis=1),
            peak_t,
            jnp.sum(teacher_exps, axis=1),
            jnp.sum(teacher_exps * (teacher_logit - learner_energy), axis=1),
        ]
    )
    if near:
        stats = stats.reshape(5, 2, 2, 2, SLOTS)
        for axis, bit in ((1, CORE), (2, DEEP), (3, ACROSS)):
            stats = combine_stats(stats, jnp.flip(swap(stats, bit), axis))
        stats = stats.reshape(5, -1)
    else:
        everything = lax.all_gather(stats, "vocab", axis=0)
        stats = everything[0]
        for k in range(1, group):
            stats = combine_stats(stats, everything[k])
    logsum_s = stats[0] + jnp.log(stats[1])
    logsum_t = stats[2] + jnp.log(stats[3])
    diverge = stats[4] / stats[3] - logsum_t + logsum_s
    mine = 0 if near else here * SLOTS
    divergence_part = jnp.sum(lax.dynamic_slice_in_dim(diverge * live_weighting, mine, SLOTS))
    student_probs = jnp.exp(learner_energy - logsum_s[:, None])
    teacher_probs = jnp.exp(teacher_logit - logsum_t[:, None])
    grad_logit = (
        mixing_coefficient
        * smoothing_heat_scale
        / masked_total
        * live_weighting[:, None]
        * (student_probs - teacher_probs)
    ).astype(jnp.bfloat16)
    if near:
        half = grad_logit.shape[0] // 2
        far = trailing_array_multiply(grad_logit[half:], table_low).reshape(2, 2, SLOTS, D)
        close = trailing_array_multiply(grad_logit[:half], table_low).reshape(2, 2, SLOTS, D)
        grad_rows = scatter_near(far, close)
    else:
        grad_rows = lax.psum_scatter(
            trailing_array_multiply(grad_logit, table_low), "vocab", scatter_dimension=0, tiled=True
        )
    head_grad = matmul_left(learner_picked, grad_logit)
    head_grad, grad_rows = lax.optimization_barrier((head_grad, grad_rows))
    head_part = lax.psum_scatter(head_grad, "dp", scatter_dimension=0, tiled=True)
    products = jnp.sum(final_s * final_t, axis=1)
    inverse_s = lax.rsqrt(jnp.sum(final_s * final_s, axis=1) + cosine_eps)
    inverse_t = lax.rsqrt(jnp.sum(final_t * final_t, axis=1) + cosine_eps)
    live_rows = (jnp.arange(LEN)[None, :] < lengths[:, None]).reshape(-1)
    cosine = products * inverse_s * inverse_t
    cosine_term = jnp.sum(jnp.where(live_rows, 1.0 - cosine, 0.0))
    weighting = jnp.where(live_rows, -cosine_weight / token_total, 0.0) * inverse_s * inverse_t
    grad_final = weighting[:, None] * (
        final_t - (products * inverse_s * inverse_s)[:, None] * final_s
    )
    grad_final = grad_final.at[offsets].add(grad_rows)
    layer_grads, grad_embedded = layer_backward(student, saved, grad_final, lengths)
    layer_grads, head_part = lax.optimization_barrier((layer_grads, head_part))

    shares = grad_embedded.astype(jnp.bfloat16).reshape(LEN, planes, width_share).transpose(1, 0, 2)
    if near:
        z = lax.axis_index("dp")
        own = [lax.dynamic_index_in_dim(shares, (z + k) % 4, keepdims=False) for k in range(4)]
        shares = jnp.stack([own[0]] + [shift(own[k], k) for k in (1, 2, 3)])
        ids = all_facts[:, :, :LEN].reshape(2, 2, 2, planes, LEN)
        for axis, bit in ((0, CORE), (1, DEEP), (2, ACROSS)):
            ids = jnp.where((here & bit) != 0, jnp.flip(ids, axis), ids)
        ids = ids.transpose(1, 2, 0, 3, 4)
    else:
        shares = lax.all_to_all(shares, "dp", 0, 0)
        ids = all_facts[:, :, :LEN]
    token_grads = lax.all_gather(shares.reshape(-1, width_share), "vocab", axis=0, tiled=True)
    if near:
        split = per // 16 * 8
        sums = []
        for begin, end in ((0, split), (split, per)):
            own_tiles, other_tiles = collect_tiles(upward, layer_grads, tiles_all, per, 2, begin, end - begin)
            chip = own_tiles + swap(other_tiles, CORE)
            chip, upward, token_grads = lax.optimization_barrier((chip, upward, token_grads))
            sums.append(reduce_chunk(chip))
        flat_grad = jnp.concatenate(sums)
    else:
        (grad_tiles,) = collect_tiles(target_rows, layer_grads, tiles_all, per, 1, 0, per)
        flat_grad = lax.psum_scatter(
            grad_tiles.reshape(tiles_all, TILE), ("dp", "vocab"), scatter_dimension=0, tiled=True
        )
    token_part = matmul_left(token_grads, chosen(ids))
    table_grad = (head_part + token_part).T
    loss_term = (
        mixing_coefficient * smoothing_heat_scale**2 * divergence_part / masked_total
        + cosine_weight * cosine_term / token_total
    )
    squares = jnp.sum(flat_grad * flat_grad) + jnp.sum(table_grad * table_grad)
    if near:
        squares, loss_value = sum_everywhere(jnp.stack([squares, loss_term]))
    else:
        squares, loss_value = lax.psum((squares, loss_term), ("dp", "vocab"))
    grad_norm = jnp.sqrt(squares)
    factor = clip_norm / jnp.maximum(grad_norm, clip_norm)
    step_float = step_count[0].astype(jnp.float32)
    new_flat, new_flat_first, new_flat_second = adam_step(
        student_flat, flat_first, flat_second, flat_grad * factor, step_float
    )
    new_embed, new_embed_first, new_embed_second = adam_step(
        student_embed, embed_first, embed_second, table_grad * factor, step_float
    )
    return (
        loss_value,
        grad_norm,
        new_flat,
        new_flat_first,
        new_flat_second,
        new_embed,
        new_embed_first,
        new_embed_second,
    )


def solution(mesh):
    near = mesh.shape["dp"] == 4 and mesh.shape["vocab"] == 8
    return jax.shard_map(
        functools.partial(on_device, near),
        mesh=mesh,
        in_specs=(
            P(("dp", "vocab"), None),
            P(("dp", "vocab")),
            P(("dp", "vocab"), None),
            P(("dp", "vocab")),
            P(),
            P(),
            P(("dp", "vocab"), None),
            P("vocab", None),
            P(("dp", "vocab"), None),
            P(("dp", "vocab"), None),
            P(("dp", "vocab"), None),
            P("vocab", "dp"),
            P("vocab", "dp"),
            P("vocab", "dp"),
        ),
        out_specs=(
            P(),
            P(),
            P(("dp", "vocab"), None),
            P(("dp", "vocab"), None),
            P(("dp", "vocab"), None),
            P("vocab", "dp"),
            P("vocab", "dp"),
            P("vocab", "dp"),
        ),
        check_vma=False,
    )
```

```python
import functools

import jax
import jax.numpy as jnp
from jax import lax
from jax.experimental import pallas as pl
from jax.experimental.pallas import tpu as pltpu
from jax.sharding import PartitionSpec as P

D = 768
HEADS = 12
HEAD_DIM = 64
FF = 3072
LEN = 512
CAP = 120
SLOTS = 128
TILE = 128

QKV = (0, D, 18)
OUT = (13824, D, 6)
UP = (18432, D, 24)
DOWN = (36864, FF, 6)
PLACE = (55296, LEN, 6)
MATRICES = (QKV, OUT, UP, DOWN, PLACE)
TAIL = 58368
TAIL_TILES = 88

VMEM_LIMIT = 60 * 1024 * 1024

smoothing_heat_scale = 2.0
mixing_coefficient = 5.0
cosine_weight = 20.0
clip_norm = 0.01
beta_first = 0.9
beta_second = 0.98
adam_eps = 1e-08
weight_decay = 0.01
learn_rate = 0.1
norm_eps = 1e-12
cosine_eps = 1e-06

CORE, ACROSS, DEEP = 1, 2, 4


def swap(value, bit):
    return lax.ppermute(value, "vocab", [(i, i ^ bit) for i in range(8)])


def shift(value, steps):
    size = lax.axis_size("dp")
    return lax.ppermute(value, "dp", [(i, (i + steps) % size) for i in range(size)])


def gather_near(value):
    value = value[None]
    for bit in (ACROSS, DEEP, CORE):
        value = jnp.concatenate([value, swap(value, bit)])
    return value


def plane_hop(value):
    half = value.shape[2] // 2
    upper, lower = value[:, :, :half], value[:, :, half:]
    return upper[:, 0] + swap(upper[:, 1], ACROSS), lower[0] + swap(lower[1], DEEP)


def plane_end(upper, lower):
    return jnp.concatenate([upper[0] + swap(upper[1], DEEP), lower[0] + swap(lower[1], ACROSS)])


def together(*values):
    return lax.optimization_barrier(values)


def ring_sum(value):
    moving = shift(value[3], 1)
    moving = shift(value[2] + moving, 1)
    moving = shift(value[1] + moving, 1)
    return value[0] + moving


def sum_everywhere(value):
    for bit in (CORE, ACROSS, DEEP):
        value = value + swap(value, bit)
    for step in (1, 2):
        value = value + lax.ppermute(value, "dp", [(i, i ^ step) for i in range(4)])
    return value


def relative_order(table, per_device):
    here = lax.axis_index("vocab")
    table = table.reshape(4, 2, 2, 2, per_device)
    for axis, bit in ((1, DEEP), (2, ACROSS), (3, CORE)):
        table = jnp.where((here & bit) != 0, jnp.flip(table, axis), table)
    return table


def rolled(table, downward):
    z = lax.axis_index("dp")
    order = (z - jnp.arange(4)) % 4 if downward else (z + jnp.arange(4)) % 4
    return [lax.dynamic_index_in_dim(table, order[k], keepdims=False) for k in range(4)]


def rows_of_tiles(tiles):
    rows = tiles
    for first, height, across in MATRICES:
        inside = (tiles >= first) & (tiles < first + height * across)
        at = tiles - first
        rows = jnp.where(inside, first + (at % across) * height + at // across, rows)
    return rows


def unpack_kernel(source, target, stage, *, across):
    stage[...] = source[...].astype(jnp.float32)

    def step(g, carry):
        for column in range(across):
            lines = stage[pl.ds(g * 16 * across + column, 16, stride=across), :]
            target[pl.ds(pl.multiple_of(g * 16, 16), 16), column * TILE : (column + 1) * TILE] = lines.astype(
                jnp.bfloat16
            )
        return carry

    lax.fori_loop(0, target.shape[0] // 16, step, 0)


def unpack_matrix(tiles, piece):
    first, height, across = piece
    lines = min(height, 384 if across > 6 else 768)
    block = lines * across
    return pl.pallas_call(
        functools.partial(unpack_kernel, across=across),
        grid=(height // lines,),
        in_specs=[pl.BlockSpec((block, TILE), lambda i: (first // block + i, 0))],
        out_specs=pl.BlockSpec((lines, across * TILE), lambda i: (i, 0)),
        out_shape=jax.ShapeDtypeStruct((height, across * TILE), jnp.bfloat16),
        scratch_shapes=[pltpu.VMEM((block, TILE), jnp.float32)],
        name="unpack_matrix",
    )(tiles)


def place_kernel(rows, *refs, places, count, per):
    arrivals = refs[: len(places)]
    targets = refs[len(places) : len(places) + 5]
    tail = refs[len(places) + 5]
    landed, stage, full, packed, in_sems, out_sems, tail_sem = refs[len(places) + 6 :]
    slots = packed.shape[0]
    copies = []
    for n, (arrival, place) in enumerate(zip(arrivals, places)):
        target = landed if place is None else landed.at[place[0], pl.ds(place[1], place[2])]
        copies.append(pltpu.make_async_copy(arrival, target, in_sems.at[n]))
    for copy in copies:
        copy.start()
    for copy in copies:
        copy.wait()

    def lines(block, start, size):
        stage[pl.ds(0, size), :] = landed[block, pl.ds(start, size), :].astype(jnp.float32)
        base = block * per + start
        for u in range(size):
            full[pl.ds(rows[base + u], 1), :] = stage[pl.ds(u, 1), :]

    whole, rest = divmod(per, 128)

    def one_block(block, carry):
        def one_step(i, inner):
            lines(block, pl.multiple_of(i * 128, 128), 128)
            return inner

        lax.fori_loop(0, whole, one_step, 0)
        if rest:
            lines(block, whole * 128, rest)
        return carry

    lax.fori_loop(0, count, one_block, 0)
    tail_copy = pltpu.make_async_copy(full.at[pl.ds(TAIL, TAIL_TILES)], tail, tail_sem)
    tail_copy.start()
    for target, (first, height, across) in zip(targets, MATRICES):
        size = min(height, D)
        parts = height // size

        def out_copy(n, slot, target=target, size=size, parts=parts):
            column, part = n // parts, n % parts
            return pltpu.make_async_copy(
                packed.at[slot, pl.ds(0, size)],
                target.at[
                    pl.ds(pl.multiple_of(part * size, 256), size),
                    pl.ds(pl.multiple_of(column * TILE, TILE), TILE),
                ],
                out_sems.at[slot],
            )

        def one_column(n, carry, first=first, size=size, out_copy=out_copy):
            slot = n % slots

            @pl.when(n >= slots)
            def _():
                out_copy(n - slots, slot).wait()

            packed[slot, pl.ds(0, size), :] = full[pl.ds(pl.multiple_of(first + n * size, 128), size), :].astype(
                jnp.bfloat16
            )
            out_copy(n, slot).start()
            return carry

        total = across * parts
        lax.fori_loop(0, total, one_column, 0)
        for n in range(total - slots, total):
            out_copy(n, n % slots).wait()
    tail_copy.wait()


def place_tiles(rows, arrivals, places, count, per):
    shapes = [jax.ShapeDtypeStruct((h, a * TILE), jnp.bfloat16) for _, h, a in MATRICES]
    return pl.pallas_call(
        functools.partial(place_kernel, places=places, count=count, per=per),
        in_specs=[pl.BlockSpec(memory_space=pltpu.SMEM)] + [pl.BlockSpec(memory_space=pl.ANY)] * len(arrivals),
        out_specs=[pl.BlockSpec(memory_space=pl.ANY)] * 6,
        out_shape=shapes + [jax.ShapeDtypeStruct((TAIL_TILES, TILE), jnp.float32)],
        scratch_shapes=[
            pltpu.VMEM((count, per, TILE), jnp.bfloat16),
            pltpu.VMEM((128, TILE), jnp.float32),
            pltpu.VMEM((count * per, TILE), jnp.float32),
            pltpu.VMEM((6, D, TILE), jnp.bfloat16),
            pltpu.SemaphoreType.DMA((len(arrivals),)),
            pltpu.SemaphoreType.DMA((6,)),
            pltpu.SemaphoreType.DMA,
        ],
        compiler_params=pltpu.CompilerParams(vmem_limit_bytes=VMEM_LIMIT),
        cost_estimate=pl.CostEstimate(flops=0, bytes_accessed=180_000_000, transcendentals=0),
        name="place_tiles",
    )(rows, *arrivals)


def step_size(rows):
    return max(n for n in range(8, 193, 8) if rows % n == 0)


def collect_kernel(rows, *refs, outs, blocks, per, begin):
    sources, targets = refs[:6], refs[6 : 6 + outs]
    full, sems = refs[6 + outs :]
    block = pl.program_id(0)

    @pl.when(block == 0)
    def _():
        copies = []
        for source, (first, height, across) in zip(sources, MATRICES):
            for column in range(across):
                copies.append(
                    pltpu.make_async_copy(
                        source.at[:, pl.ds(column * TILE, TILE)],
                        full.at[pl.ds(first + column * height, height)],
                        sems.at[len(copies)],
                    )
                )
        copies.append(pltpu.make_async_copy(sources[5], full.at[pl.ds(TAIL, TAIL_TILES)], sems.at[len(copies)]))
        for copy in copies:
            copy.start()
        unused = full.shape[0] - TAIL - TAIL_TILES
        full[pl.ds(TAIL + TAIL_TILES, unused), :] = jnp.zeros((unused, TILE), jnp.float32)
        for copy in copies:
            copy.wait()

    size = step_size(targets[0].shape[1])
    for n, target in enumerate(targets):
        base = (n * blocks + block) * per + begin

        def one_step(i, carry, target=target, base=base):
            start = pl.multiple_of(i * size, 8)
            for u in range(size):
                target[0, pl.ds(start + u, 1), :] = full[pl.ds(rows[base + start + u], 1), :]
            return carry

        lax.fori_loop(0, target.shape[1] // size, one_step, 0)


def collect_tiles(rows, sources, tiles_all, per, outs, begin, lines):
    blocks = tiles_all // per // outs
    return pl.pallas_call(
        functools.partial(collect_kernel, outs=outs, blocks=blocks, per=per, begin=begin),
        grid=(blocks,),
        in_specs=[pl.BlockSpec(memory_space=pltpu.SMEM)] + [pl.BlockSpec(memory_space=pl.ANY)] * 6,
        out_specs=[pl.BlockSpec((1, lines, TILE), lambda i: (i, 0, 0))] * outs,
        out_shape=[jax.ShapeDtypeStruct((blocks, lines, TILE), jnp.float32)] * outs,
        scratch_shapes=[pltpu.VMEM((tiles_all, TILE), jnp.float32), pltpu.SemaphoreType.DMA((61,))],
        compiler_params=pltpu.CompilerParams(vmem_limit_bytes=VMEM_LIMIT),
        cost_estimate=pl.CostEstimate(flops=0, bytes_accessed=80_000_000, transcendentals=0),
        name="collect_tiles",
    )(rows, *sources)


def array_multiply(left_side, right_side):
    return jnp.dot(left_side, right_side, preferred_element_type=jnp.float32)


def matmul_left(left_side, right_side):
    return lax.dot_general(
        left_side, right_side, (((0,), (0,)), ((), ())), preferred_element_type=jnp.float32
    )


def trailing_array_multiply(left_side, right_side):
    return lax.dot_general(
        left_side, right_side, (((1,), (1,)), ((), ())), preferred_element_type=jnp.float32
    )


def pieces_of(matrices, tail):
    qkv, out, up, down, place = matrices
    return {
        "qkv": qkv,
        "out": out,
        "up": up,
        "down": down,
        "place": place,
        "small": tail[:60].reshape(10, D),
        "upbias": tail[60:84].reshape(FF),
    }


def norm_forward(values, gain_row, shift_row):
    center = values - jnp.mean(values, axis=-1, keepdims=True)
    inverse = lax.rsqrt(jnp.mean(center * center, axis=-1, keepdims=True) + norm_eps)
    normed = center * inverse
    return (normed * gain_row + shift_row, normed, inverse)


def norm_backward(grad_out, normed, inverse, gain_row):
    scaled = grad_out * gain_row
    grad_in = inverse * (
        scaled
        - jnp.mean(scaled, axis=-1, keepdims=True)
        - normed * jnp.mean(scaled * normed, axis=-1, keepdims=True)
    )
    return (grad_in, jnp.sum(grad_out * normed, axis=0), jnp.sum(grad_out, axis=0))


def gelu_slope(values):
    return (
        0.5 * (1.0 + lax.erf(values * 0.7071067811865476))
        + values * jnp.exp(-0.5 * values * values) * 0.3989422804014327
    )


def key_scores(projected, lengths):
    seqs_count = lengths.shape[0]
    split_heads = projected.reshape(seqs_count, LEN, 3, HEADS, HEAD_DIM)
    scores = jnp.einsum(
        "sqhd,skhd->shqk",
        split_heads[:, :, 0],
        split_heads[:, :, 1],
        preferred_element_type=jnp.float32,
    ) * HEAD_DIM ** (-0.5)
    live_keys = jnp.arange(LEN)[None, :] < lengths[:, None]
    return (jnp.where(live_keys[:, None, None, :], scores, -1000000000.0), split_heads)


def layer_forward(pieces, looked, lengths):
    small_rows = pieces["small"].astype(jnp.float32)
    seqs_count = lengths.shape[0]
    rows_here = seqs_count * LEN
    summed = (
        looked.reshape(seqs_count, LEN, D) + pieces["place"].astype(jnp.float32)[None]
    ).reshape(rows_here, D)
    first_norm, normed_zero, inverse_zero = norm_forward(summed, small_rows[4], small_rows[5])
    inputs = first_norm.astype(jnp.bfloat16)
    qkv_bias = jnp.concatenate([small_rows[0], jnp.zeros((D,), jnp.float32), small_rows[1]])
    projected = (array_multiply(inputs, pieces["qkv"]) + qkv_bias).astype(jnp.bfloat16)
    scores, split_heads = key_scores(projected, lengths)
    peak = jnp.max(scores, axis=-1, keepdims=True)
    exps = jnp.exp(scores - peak)
    totals = jnp.sum(exps, axis=-1, keepdims=True)
    probabilities = (exps / totals).astype(jnp.bfloat16)
    logsum = peak + jnp.log(totals)
    context = jnp.einsum(
        "shqk,skhd->sqhd", probabilities, split_heads[:, :, 2], preferred_element_type=jnp.float32
    )
    context = context.reshape(rows_here, D).astype(jnp.bfloat16)
    attended = array_multiply(context, pieces["out"]) + small_rows[2]
    middle, normed_one, inverse_one = norm_forward(
        first_norm + attended, small_rows[6], small_rows[7]
    )
    middle_low = middle.astype(jnp.bfloat16)
    hidden = array_multiply(middle_low, pieces["up"]) + pieces["upbias"].astype(jnp.float32)
    activated = jax.nn.gelu(hidden, approximate=False).astype(jnp.bfloat16)
    output = array_multiply(activated, pieces["down"]) + small_rows[3]
    final_lines, normed_two, inverse_two = norm_forward(
        middle + output, small_rows[8], small_rows[9]
    )
    saved = {
        "inputs": inputs,
        "projected": projected,
        "logsum": logsum,
        "context": context,
        "middle_low": middle_low,
        "hidden": hidden,
        "activated": activated,
        "normed_zero": normed_zero,
        "inverse_zero": inverse_zero,
        "normed_one": normed_one,
        "inverse_one": inverse_one,
        "normed_two": normed_two,
        "inverse_two": inverse_two,
    }
    return (final_lines, saved)


def feed_backward(pieces, saved, grad_final):
    small_rows = pieces["small"]
    grad_sum_two, grad_gain_two, grad_shift_two = norm_backward(
        grad_final, saved["normed_two"], saved["inverse_two"], small_rows[8]
    )
    grad_out = grad_sum_two.astype(jnp.bfloat16)
    grad_down = matmul_left(saved["activated"], grad_out)
    grad_act = trailing_array_multiply(grad_out, pieces["down"])
    grad_hidden = (grad_act * gelu_slope(saved["hidden"])).astype(jnp.bfloat16)
    grad_up = matmul_left(saved["middle_low"], grad_hidden)
    grad_middle = grad_sum_two + trailing_array_multiply(grad_hidden, pieces["up"])
    grad_sum_one, grad_gain_one, grad_shift_one = norm_backward(
        grad_middle, saved["normed_one"], saved["inverse_one"], small_rows[6]
    )
    grad_small = [jnp.sum(grad_out.astype(jnp.float32), axis=0), grad_gain_one, grad_shift_one, grad_gain_two, grad_shift_two]
    grad_upbias = jnp.sum(grad_hidden.astype(jnp.float32), axis=0)
    return grad_sum_one, (grad_up, grad_down, grad_small, grad_upbias)


def attention_backward(pieces, saved, grad_sum_one, feed_grads, lengths):
    small_rows = pieces["small"]
    seqs_count = lengths.shape[0]
    rows_here = seqs_count * LEN
    grad_up, grad_down, grad_small, grad_upbias = feed_grads
    grad_att = grad_sum_one.astype(jnp.bfloat16)
    grad_outw = matmul_left(saved["context"], grad_att)
    grad_context = (
        trailing_array_multiply(grad_att, pieces["out"])
        .astype(jnp.bfloat16)
        .reshape(seqs_count, LEN, HEADS, HEAD_DIM)
    )
    scores, split_heads = key_scores(saved["projected"], lengths)
    probabilities = jnp.exp(scores - saved["logsum"])
    grad_probs = jnp.einsum(
        "sqhd,skhd->shqk", grad_context, split_heads[:, :, 2], preferred_element_type=jnp.float32
    )
    grad_values = jnp.einsum(
        "shqk,sqhd->skhd",
        probabilities.astype(jnp.bfloat16),
        grad_context,
        preferred_element_type=jnp.float32,
    )
    grad_scores = probabilities * (
        grad_probs - jnp.sum(grad_probs * probabilities, axis=-1, keepdims=True)
    )
    grad_scores = grad_scores.astype(jnp.bfloat16)
    grad_queries = jnp.einsum(
        "shqk,skhd->sqhd", grad_scores, split_heads[:, :, 1], preferred_element_type=jnp.float32
    ) * HEAD_DIM ** (-0.5)
    grad_keys = jnp.einsum(
        "shqk,sqhd->skhd", grad_scores, split_heads[:, :, 0], preferred_element_type=jnp.float32
    ) * HEAD_DIM ** (-0.5)
    grad_proj = (
        jnp.stack([grad_queries, grad_keys, grad_values], axis=2)
        .reshape(rows_here, 3 * D)
        .astype(jnp.bfloat16)
    )
    grad_qkv = matmul_left(saved["inputs"], grad_proj)
    grad_bias_all = jnp.sum(grad_proj.astype(jnp.float32), axis=0)
    grad_first = grad_sum_one + trailing_array_multiply(grad_proj, pieces["qkv"])
    grad_embedded, grad_gain_zero, grad_shift_zero = norm_backward(
        grad_first, saved["normed_zero"], saved["inverse_zero"], small_rows[4]
    )
    grad_place = jnp.sum(grad_embedded.reshape(seqs_count, LEN, D), axis=0)
    grad_small = jnp.stack(
        [
            grad_bias_all[:D],
            grad_bias_all[2 * D :],
            jnp.sum(grad_att.astype(jnp.float32), axis=0),
            grad_small[0],
            grad_gain_zero,
            grad_shift_zero,
            *grad_small[1:],
        ]
    )
    tail = jnp.concatenate(
        [grad_small.reshape(60, TILE), grad_upbias.reshape(24, TILE), jnp.zeros((4, TILE), jnp.float32)]
    )
    return ((grad_qkv, grad_outw, grad_up, grad_down, grad_place, tail), grad_embedded)


def combine_stats(earlier, later):
    peak_s = jnp.maximum(earlier[0], later[0])
    peak_t = jnp.maximum(earlier[2], later[2])
    factor_early = jnp.exp(earlier[0] - peak_s)
    factor_late = jnp.exp(later[0] - peak_s)
    teacher_early = jnp.exp(earlier[2] - peak_t)
    teacher_late = jnp.exp(later[2] - peak_t)
    return jnp.stack(
        [
            peak_s,
            earlier[1] * factor_early + later[1] * factor_late,
            peak_t,
            earlier[3] * teacher_early + later[3] * teacher_late,
            earlier[4] * teacher_early + later[4] * teacher_late,
        ]
    )


def adam_step(weight, first_moment, second, gradient, step_float):
    new_first = beta_first * first_moment + (1.0 - beta_first) * gradient
    new_second = beta_second * second + (1.0 - beta_second) * gradient * gradient
    fix_first = 1.0 - jnp.power(beta_first, step_float)
    fix_second = 1.0 - jnp.power(beta_second, step_float)
    update = new_first / fix_first / (jnp.sqrt(new_second / fix_second) + adam_eps)
    return (weight - learn_rate * (update + weight_decay * weight), new_first, new_second)


def gather_student(tiles):
    per = tiles.shape[0]
    half = per // 16 * 8
    arrivals, places = [], []

    def keep(value, plane, near, start):
        for core in (0, 1):
            arrivals.append(swap(value, CORE) if core else value)
            places.append((plane * 8 + near * 2 + core, start, value.shape[0]))

    for plane in range(4):
        across, deep = swap(tiles, ACROSS), swap(tiles, DEEP)
        keep(tiles, plane, 0, 0)
        keep(across, plane, 1, 0)
        keep(deep, plane, 2, 0)
        keep(swap(across[:half], DEEP), plane, 3, 0)
        keep(swap(deep[half:], ACROSS), plane, 3, half)
        if plane < 3:
            tiles = shift(tiles, 1)
    return arrivals, places


def sent_low(value, bit):
    return swap(value.astype(jnp.bfloat16), bit).astype(jnp.float32)


def plane_first(value):
    value = value.reshape(4, 2, 2, value.shape[1], TILE)
    first, second = value[2:], value[:2]
    first = first[:, :, 0] + sent_low(first[:, :, 1], ACROSS)
    second = second[:, 0] + sent_low(second[:, 1], DEEP)
    return first, second


def plane_second(first, second):
    first = first[:, 0] + sent_low(first[:, 1], DEEP)
    second = second[:, 0] + sent_low(second[:, 1], ACROSS)
    return [second[0], second[1], first[0], first[1]]


def on_device(
    near,
    token_ids,
    lengths,
    mask_pos,
    mask_count,
    owner_order,
    step_count,
    teacher_flat,
    mentor_lexicon_weights,
    student_flat,
    flat_first,
    flat_second,
    student_embed,
    embed_first,
    embed_second,
):
    per = student_flat.shape[0]
    tiles_all = owner_order.shape[0]
    vocab_rows, width_share = student_embed.shape
    planes = lax.axis_size("dp")
    group = lax.axis_size("vocab")
    here = lax.axis_index("vocab")

    facts = jnp.concatenate([token_ids.reshape(LEN), lengths, mask_count, jnp.zeros((TILE - 2,), jnp.int32)])
    target_rows = rows_of_tiles(owner_order)
    student_low = student_flat.astype(jnp.bfloat16)
    table_low = lax.all_gather(student_embed.T.astype(jnp.bfloat16), "dp", axis=0, tiled=True)
    words = jnp.arange(vocab_rows, dtype=jnp.int32)

    def chosen(ids):
        return (ids.reshape(-1, 1) - here * vocab_rows == words[None]).astype(jnp.bfloat16)

    def rows_t(ids):
        return array_multiply(chosen(ids), mentor_lexicon_weights).astype(jnp.bfloat16)

    def rows_s(ids):
        return trailing_array_multiply(chosen(ids), table_low).astype(jnp.bfloat16)

    if near:
        plane_facts = gather_near(facts)
        by_plane = [facts, shift(facts, 1), shift(facts, 2), shift(facts, 3)]
        other_facts = gather_near(jnp.stack(by_plane[1:]))
        all_facts = jnp.concatenate([plane_facts[:, None], other_facts], axis=1)
        relative = relative_order(target_rows, per)
        downward = jnp.stack(rolled(relative, True)).reshape(-1)
        upward = jnp.stack(rolled(relative.transpose(0, 3, 1, 2, 4), False), axis=1).reshape(-1)
        arrivals, places = gather_student(student_low)
        far_ids, close_ids = plane_facts[4:, :LEN], plane_facts[:4, :LEN]
        shape = (2, 2, LEN, D)
        looked_t = rows_t(close_ids).reshape(shape) + swap(rows_t(far_ids).reshape(shape), CORE)
        looked_s = rows_s(close_ids).reshape(shape) + swap(rows_s(far_ids).reshape(shape), CORE)
        arrivals, teacher_flat, looked_t, looked_s = lax.optimization_barrier(
            (arrivals, teacher_flat, looked_t, looked_s)
        )
        teacher_tiles = lax.all_gather(teacher_flat, ("dp", "vocab"), axis=0, tiled=True)
        looked_t, looked_s = plane_hop(looked_t), plane_hop(looked_s)
        matrices = place_tiles(downward, arrivals, tuple(places), planes * group, per)
        matrices, looked_t, looked_s = together(matrices, looked_t, looked_s)
        looked_s = plane_end(*looked_s).astype(jnp.float32)
        looked_t = plane_end(*looked_t).astype(jnp.float32)
    else:
        by_plane = lax.all_gather(facts, "dp", axis=0)
        all_facts = lax.all_gather(by_plane, "vocab", axis=0)
        plane_facts = lax.dynamic_index_in_dim(all_facts, lax.axis_index("dp"), 1, keepdims=False)
        teacher_tiles = lax.all_gather(teacher_flat, ("dp", "vocab"), axis=0, tiled=True)
        student_tiles = lax.all_gather(student_low, ("dp", "vocab"), axis=0, tiled=True)
        plane_ids = plane_facts[:, :LEN]
        looked_t, looked_s = (
            lax.psum_scatter(rows, "vocab", scatter_dimension=0, tiled=True).astype(jnp.float32)
            for rows in (rows_t(plane_ids), rows_s(plane_ids))
        )
        matrices = place_tiles(
            target_rows, [student_tiles.reshape(planes * group, per, TILE)], (None,), planes * group, per
        )
    student = pieces_of(matrices[:5], matrices[5])
    final_s, saved = layer_forward(student, looked_s, lengths)
    final_s, teacher_tiles, looked_t, all_facts = together(final_s, teacher_tiles, looked_t, all_facts)
    teacher = pieces_of(
        [unpack_matrix(teacher_tiles, piece) for piece in MATRICES],
        teacher_tiles[TAIL : TAIL + TAIL_TILES].astype(jnp.float32),
    )
    token_total = jnp.sum(all_facts[:, :, LEN]).astype(jnp.float32)
    masked_total = jnp.sum(all_facts[:, :, LEN + 1]).astype(jnp.float32)

    offsets = jnp.concatenate([mask_pos.reshape(CAP), jnp.zeros((SLOTS - CAP,), jnp.int32)])
    picked_s = final_s[offsets].astype(jnp.bfloat16)
    if near:
        learner_picked = gather_near(picked_s).reshape(-1, D)
    final_t = layer_forward(teacher, looked_t, lengths)[0]
    if near:
        final_t, learner_picked = together(final_t, learner_picked)

    picked_t = final_t[offsets].astype(jnp.bfloat16)
    if near:
        mentor_picked = gather_near(picked_t).reshape(-1, D)
    else:
        learner_picked = lax.all_gather(picked_s, "vocab", axis=0, tiled=True)
        mentor_picked = lax.all_gather(picked_t, "vocab", axis=0, tiled=True)
    live_weighting = (
        (jnp.arange(SLOTS)[None] < plane_facts[:, LEN + 1, None]).astype(jnp.float32).reshape(-1)
    )
    learner_energy = array_multiply(learner_picked, table_low) / smoothing_heat_scale
    teacher_logit = (
        trailing_array_multiply(mentor_picked, mentor_lexicon_weights) / smoothing_heat_scale
    )
    peak_s = jnp.max(learner_energy, axis=1)
    peak_t = jnp.max(teacher_logit, axis=1)
    teacher_exps = jnp.exp(teacher_logit - peak_t[:, None])
    stats = jnp.stack(
        [
            peak_s,
            jnp.sum(jnp.exp(learner_energy - peak_s[:, None]), axis=1),
            peak_t,
            jnp.sum(teacher_exps, axis=1),
            jnp.sum(teacher_exps * (teacher_logit - learner_energy), axis=1),
        ]
    )
    if near:
        stats = stats.reshape(5, 2, 2, 2, SLOTS)
        for axis, bit in ((1, CORE), (2, DEEP), (3, ACROSS)):
            stats = combine_stats(stats, jnp.flip(swap(stats, bit), axis))
        stats = stats.reshape(5, -1)
    else:
        everything = lax.all_gather(stats, "vocab", axis=0)
        stats = everything[0]
        for k in range(1, group):
            stats = combine_stats(stats, everything[k])
    logsum_s = stats[0] + jnp.log(stats[1])
    logsum_t = stats[2] + jnp.log(stats[3])
    diverge = stats[4] / stats[3] - logsum_t + logsum_s
    mine = 0 if near else here * SLOTS
    divergence_part = jnp.sum(lax.dynamic_slice_in_dim(diverge * live_weighting, mine, SLOTS))
    student_probs = jnp.exp(learner_energy - logsum_s[:, None])
    teacher_probs = jnp.exp(teacher_logit - logsum_t[:, None])
    grad_logit = (
        mixing_coefficient
        * smoothing_heat_scale
        / masked_total
        * live_weighting[:, None]
        * (student_probs - teacher_probs)
    ).astype(jnp.bfloat16)
    if near:
        half = grad_logit.shape[0] // 2
        far = trailing_array_multiply(grad_logit[half:], table_low).reshape(2, 2, SLOTS, D)
        close = trailing_array_multiply(grad_logit[:half], table_low).reshape(2, 2, SLOTS, D)
        grad_rows = plane_end(*plane_hop(close + swap(far, CORE)))
    else:
        grad_rows = lax.psum_scatter(
            trailing_array_multiply(grad_logit, table_low), "vocab", scatter_dimension=0, tiled=True
        )
    head_grad = matmul_left(learner_picked, grad_logit)
    head_grad, grad_rows = together(head_grad, grad_rows)
    if not near:
        head_part = lax.psum_scatter(head_grad, "dp", scatter_dimension=0, tiled=True)
    products = jnp.sum(final_s * final_t, axis=1)
    inverse_s = lax.rsqrt(jnp.sum(final_s * final_s, axis=1) + cosine_eps)
    inverse_t = lax.rsqrt(jnp.sum(final_t * final_t, axis=1) + cosine_eps)
    live_rows = (jnp.arange(LEN)[None, :] < lengths[:, None]).reshape(-1)
    cosine = products * inverse_s * inverse_t
    cosine_term = jnp.sum(jnp.where(live_rows, 1.0 - cosine, 0.0))
    weighting = jnp.where(live_rows, -cosine_weight / token_total, 0.0) * inverse_s * inverse_t
    grad_final = weighting[:, None] * (
        final_t - (products * inverse_s * inverse_s)[:, None] * final_s
    )
    grad_final = grad_final.at[offsets].add(grad_rows)
    if near:
        heads = rolled(head_grad.reshape(4, width_share, vocab_rows), False)
        moving = shift(heads[3], 1)
        grad_sum_one, feed_grads = feed_backward(student, saved, grad_final)
        grad_sum_one, moving = together(grad_sum_one, moving)
        moving = shift(heads[2] + moving, 1)
        layer_grads, grad_embedded = attention_backward(student, saved, grad_sum_one, feed_grads, lengths)
        grad_embedded, moving = together(grad_embedded, moving)
        moving = shift(heads[1] + moving, 1)
    else:
        grad_sum_one, feed_grads = feed_backward(student, saved, grad_final)
        layer_grads, grad_embedded = attention_backward(student, saved, grad_sum_one, feed_grads, lengths)

    shares = grad_embedded.astype(jnp.bfloat16).reshape(LEN, planes, width_share).transpose(1, 0, 2)
    if near:
        own = rolled(shares, False)
        shares = jnp.stack([own[0]] + [shift(own[k], k) for k in (1, 2, 3)])
        ids = all_facts[:, :, :LEN].reshape(2, 2, 2, planes, LEN)
        for axis, bit in ((0, CORE), (1, DEEP), (2, ACROSS)):
            ids = jnp.where((here & bit) != 0, jnp.flip(ids, axis), ids)
        ids = ids.transpose(1, 2, 0, 3, 4)
    else:
        shares = lax.all_to_all(shares, "dp", 0, 0)
        ids = all_facts[:, :, :LEN]
    token_grads = lax.all_gather(shares.reshape(-1, width_share), "vocab", axis=0, tiled=True)
    if near:
        step = per // 32 * 8
        edges = (0, step, 2 * step, 3 * step, per)

        def collect(n):
            return collect_tiles(upward, layer_grads, tiles_all, per, 2, edges[n], edges[n + 1] - edges[n])

        one = collect(0)
        one, moving, shares = together(one, moving, shares)
        token_grads = lax.all_gather(shares.reshape(-1, width_share), "vocab", axis=0, tiled=True)
        head_part = heads[0] + moving
        chip_one = one[0] + swap(one[1], CORE)
        chip_one, two = together(chip_one, collect(1))
        first_one = plane_first(chip_one)
        chip_two = two[0] + swap(two[1], CORE)
        first_one, chip_two, three = together(first_one, chip_two, collect(2))
        blocks_one = plane_second(*first_one)
        first_two = plane_first(chip_two)
        chip_three = three[0] + swap(three[1], CORE)
        blocks_one, first_two, chip_three, token_grads, four = together(
            blocks_one, first_two, chip_three, token_grads, collect(3)
        )
        token_part = matmul_left(token_grads, chosen(ids))
        blocks_two = plane_second(*first_two)
        first_three = plane_first(chip_three)
        chip_four = four[0] + swap(four[1], CORE)
        blocks_two, first_three, chip_four, token_part = together(blocks_two, first_three, chip_four, token_part)
        blocks_three = plane_second(*first_three)
        blocks_four = plane_second(*plane_first(chip_four))
        sums = [ring_sum(blocks) for blocks in (blocks_one, blocks_two, blocks_three, blocks_four)]
        flat_grad = jnp.concatenate(sums)
    else:
        token_grads = lax.all_gather(shares.reshape(-1, width_share), "vocab", axis=0, tiled=True)
        token_part = matmul_left(token_grads, chosen(ids))
        (grad_tiles,) = collect_tiles(target_rows, layer_grads, tiles_all, per, 1, 0, per)
        flat_grad = lax.psum_scatter(
            grad_tiles.reshape(tiles_all, TILE), ("dp", "vocab"), scatter_dimension=0, tiled=True
        )
    table_grad = (head_part + token_part).T
    loss_term = (
        mixing_coefficient * smoothing_heat_scale**2 * divergence_part / masked_total
        + cosine_weight * cosine_term / token_total
    )
    squares = jnp.sum(flat_grad * flat_grad) + jnp.sum(table_grad * table_grad)
    if near:
        squares, loss_value = sum_everywhere(jnp.stack([squares, loss_term]))
    else:
        squares, loss_value = lax.psum((squares, loss_term), ("dp", "vocab"))
    grad_norm = jnp.sqrt(squares)
    factor = clip_norm / jnp.maximum(grad_norm, clip_norm)
    step_float = step_count[0].astype(jnp.float32)
    new_flat, new_flat_first, new_flat_second = adam_step(
        student_flat, flat_first, flat_second, flat_grad * factor, step_float
    )
    new_embed, new_embed_first, new_embed_second = adam_step(
        student_embed, embed_first, embed_second, table_grad * factor, step_float
    )
    return (
        loss_value,
        grad_norm,
        new_flat,
        new_flat_first,
        new_flat_second,
        new_embed,
        new_embed_first,
        new_embed_second,
    )


def solution(mesh):
    near = mesh.shape["dp"] == 4 and mesh.shape["vocab"] == 8
    return jax.shard_map(
        functools.partial(on_device, near),
        mesh=mesh,
        in_specs=(
            P(("dp", "vocab"), None),
            P(("dp", "vocab")),
            P(("dp", "vocab"), None),
            P(("dp", "vocab")),
            P(),
            P(),
            P(("dp", "vocab"), None),
            P("vocab", None),
            P(("dp", "vocab"), None),
            P(("dp", "vocab"), None),
            P(("dp", "vocab"), None),
            P("vocab", "dp"),
            P("vocab", "dp"),
            P("vocab", "dp"),
        ),
        out_specs=(
            P(),
            P(),
            P(("dp", "vocab"), None),
            P(("dp", "vocab"), None),
            P(("dp", "vocab"), None),
            P("vocab", "dp"),
            P("vocab", "dp"),
            P("vocab", "dp"),
        ),
        check_vma=False,
    )
```

```python
import functools

import jax
import jax.numpy as jnp
from jax import lax
from jax.experimental import pallas as pl
from jax.experimental.pallas import tpu as pltpu
from jax.sharding import PartitionSpec as P

D = 768
HEADS = 12
HEAD_DIM = 64
FF = 3072
LEN = 512
CAP = 120
SLOTS = 128
TILE = 128

QKV = (0, D, 18)
OUT = (13824, D, 6)
UP = (18432, D, 24)
DOWN = (36864, FF, 6)
PLACE = (55296, LEN, 6)
MATRICES = (QKV, OUT, UP, DOWN, PLACE)
TAIL = 58368
TAIL_TILES = 88

VMEM_LIMIT = 60 * 1024 * 1024

smoothing_heat_scale = 2.0
mixing_coefficient = 5.0
cosine_weight = 20.0
clip_norm = 0.01
beta_first = 0.9
beta_second = 0.98
adam_eps = 1e-08
weight_decay = 0.01
learn_rate = 0.1
norm_eps = 1e-12
cosine_eps = 1e-06

CORE, ACROSS, DEEP = 1, 2, 4


def swap(value, bit):
    return lax.ppermute(value, "vocab", [(i, i ^ bit) for i in range(8)])


def shift(value, steps):
    size = lax.axis_size("dp")
    return lax.ppermute(value, "dp", [(i, (i + steps) % size) for i in range(size)])


def gather_near(value):
    value = value[None]
    for bit in (ACROSS, DEEP, CORE):
        value = jnp.concatenate([value, swap(value, bit)])
    return value


def plane_hop(value):
    half = value.shape[2] // 2
    upper, lower = value[:, :, :half], value[:, :, half:]
    return upper[:, 0] + swap(upper[:, 1], ACROSS), lower[0] + swap(lower[1], DEEP)


def plane_end(upper, lower):
    return jnp.concatenate([upper[0] + swap(upper[1], DEEP), lower[0] + swap(lower[1], ACROSS)])


def together(*values):
    return lax.optimization_barrier(values)


def ring_sum(value):
    moving = shift(value[3], 1)
    moving = shift(value[2] + moving, 1)
    moving = shift(value[1] + moving, 1)
    return value[0] + moving


def sum_everywhere(value):
    for bit in (CORE, ACROSS, DEEP):
        value = value + swap(value, bit)
    for step in (1, 2):
        value = value + lax.ppermute(value, "dp", [(i, i ^ step) for i in range(4)])
    return value


def upward(table):
    z = lax.axis_index("dp")
    return [lax.dynamic_index_in_dim(table, (z + k) % 4, keepdims=False) for k in range(4)]


def rows_of_tiles(tiles):
    rows = tiles
    for first, height, across in MATRICES:
        inside = (tiles >= first) & (tiles < first + height * across)
        at = tiles - first
        rows = jnp.where(inside, first + (at % across) * height + at // across, rows)
    return rows


def unpack_kernel(source, target, stage, *, across):
    stage[...] = source[...].astype(jnp.float32)

    def step(g, carry):
        for column in range(across):
            lines = stage[pl.ds(g * 16 * across + column, 16, stride=across), :]
            target[pl.ds(pl.multiple_of(g * 16, 16), 16), column * TILE : (column + 1) * TILE] = lines.astype(
                jnp.bfloat16
            )
        return carry

    lax.fori_loop(0, target.shape[0] // 16, step, 0)


def unpack_matrix(tiles, piece):
    first, height, across = piece
    lines = min(height, 384 if across > 6 else 768)
    block = lines * across
    return pl.pallas_call(
        functools.partial(unpack_kernel, across=across),
        grid=(height // lines,),
        in_specs=[pl.BlockSpec((block, TILE), lambda i: (first // block + i, 0))],
        out_specs=pl.BlockSpec((lines, across * TILE), lambda i: (i, 0)),
        out_shape=jax.ShapeDtypeStruct((height, across * TILE), jnp.bfloat16),
        scratch_shapes=[pltpu.VMEM((block, TILE), jnp.float32)],
        name="unpack_matrix",
    )(tiles)


def place_kernel(spot, rows, *refs, places, count, per):
    arrivals = refs[: len(places)]
    targets = refs[len(places) : len(places) + 5]
    tail = refs[len(places) + 5]
    landed, stage, full, packed, in_sems, out_sems, tail_sem = refs[len(places) + 6 :]
    slots = packed.shape[0]
    copies = []
    for n, (arrival, place) in enumerate(zip(arrivals, places)):
        target = landed if place is None else landed.at[place[0], pl.ds(place[1], place[2])]
        copies.append(pltpu.make_async_copy(arrival, target, in_sems.at[n]))
    for copy in copies:
        copy.start()
    for copy in copies:
        copy.wait()

    def lines(block, start, size):
        stage[pl.ds(0, size), :] = landed[block, pl.ds(start, size), :].astype(jnp.float32)
        if places[0] is None:
            owner = block
        else:
            owner = ((spot[0] + 4 - block // 8) % 4) * 8 + (spot[1] ^ (block % 8))
        base = owner * per + start
        for u in range(size):
            full[pl.ds(rows[base + u], 1), :] = stage[pl.ds(u, 1), :]

    whole, rest = divmod(per, 128)

    def one_block(block, carry):
        def one_step(i, inner):
            lines(block, pl.multiple_of(i * 128, 128), 128)
            return inner

        lax.fori_loop(0, whole, one_step, 0)
        if rest:
            lines(block, whole * 128, rest)
        return carry

    lax.fori_loop(0, count, one_block, 0)
    tail_copy = pltpu.make_async_copy(full.at[pl.ds(TAIL, TAIL_TILES)], tail, tail_sem)
    tail_copy.start()
    for target, (first, height, across) in zip(targets, MATRICES):
        size = min(height, D)
        parts = height // size

        def out_copy(n, slot, target=target, size=size, parts=parts):
            column, part = n // parts, n % parts
            return pltpu.make_async_copy(
                packed.at[slot, pl.ds(0, size)],
                target.at[
                    pl.ds(pl.multiple_of(part * size, 256), size),
                    pl.ds(pl.multiple_of(column * TILE, TILE), TILE),
                ],
                out_sems.at[slot],
            )

        def one_column(n, carry, first=first, size=size, out_copy=out_copy):
            slot = n % slots

            @pl.when(n >= slots)
            def _():
                out_copy(n - slots, slot).wait()

            packed[slot, pl.ds(0, size), :] = full[pl.ds(pl.multiple_of(first + n * size, 128), size), :].astype(
                jnp.bfloat16
            )
            out_copy(n, slot).start()
            return carry

        total = across * parts
        lax.fori_loop(0, total, one_column, 0)
        for n in range(total - slots, total):
            out_copy(n, n % slots).wait()
    tail_copy.wait()


def place_tiles(spot, rows, arrivals, places, count, per):
    shapes = [jax.ShapeDtypeStruct((h, a * TILE), jnp.bfloat16) for _, h, a in MATRICES]
    return pl.pallas_call(
        functools.partial(place_kernel, places=places, count=count, per=per),
        in_specs=[pl.BlockSpec(memory_space=pltpu.SMEM)] * 2 + [pl.BlockSpec(memory_space=pl.ANY)] * len(arrivals),
        out_specs=[pl.BlockSpec(memory_space=pl.ANY)] * 6,
        out_shape=shapes + [jax.ShapeDtypeStruct((TAIL_TILES, TILE), jnp.float32)],
        scratch_shapes=[
            pltpu.VMEM((count, per, TILE), jnp.bfloat16),
            pltpu.VMEM((128, TILE), jnp.float32),
            pltpu.VMEM((count * per, TILE), jnp.float32),
            pltpu.VMEM((6, D, TILE), jnp.bfloat16),
            pltpu.SemaphoreType.DMA((len(arrivals),)),
            pltpu.SemaphoreType.DMA((6,)),
            pltpu.SemaphoreType.DMA,
        ],
        compiler_params=pltpu.CompilerParams(vmem_limit_bytes=VMEM_LIMIT),
        cost_estimate=pl.CostEstimate(flops=0, bytes_accessed=180_000_000, transcendentals=0),
        name="place_tiles",
    )(spot, rows, *arrivals)


def step_size(rows):
    return max(n for n in range(8, 193, 8) if rows % n == 0)


def collect_kernel(spot, rows, *refs, outs, blocks, per, begin):
    sources, targets = refs[:6], refs[6 : 6 + outs]
    full, sems = refs[6 + outs :]
    block = pl.program_id(0)

    @pl.when(block == 0)
    def _():
        copies = []
        for source, (first, height, across) in zip(sources, MATRICES):
            for column in range(across):
                copies.append(
                    pltpu.make_async_copy(
                        source.at[:, pl.ds(column * TILE, TILE)],
                        full.at[pl.ds(first + column * height, height)],
                        sems.at[len(copies)],
                    )
                )
        copies.append(pltpu.make_async_copy(sources[5], full.at[pl.ds(TAIL, TAIL_TILES)], sems.at[len(copies)]))
        for copy in copies:
            copy.start()
        unused = full.shape[0] - TAIL - TAIL_TILES
        full[pl.ds(TAIL + TAIL_TILES, unused), :] = jnp.zeros((unused, TILE), jnp.float32)
        for copy in copies:
            copy.wait()

    size = step_size(targets[0].shape[1])
    for n, target in enumerate(targets):
        if outs == 1:
            owner = block
        else:
            owner = ((spot[0] + block // 4) % 4) * 8 + (spot[1] ^ ((block % 4) * 2 + n))
        base = owner * per + begin

        def one_step(i, carry, target=target, base=base):
            start = pl.multiple_of(i * size, 8)
            for u in range(size):
                target[0, pl.ds(start + u, 1), :] = full[pl.ds(rows[base + start + u], 1), :]
            return carry

        lax.fori_loop(0, target.shape[1] // size, one_step, 0)


def collect_tiles(spot, rows, sources, tiles_all, per, outs, begin, lines):
    blocks = tiles_all // per // outs
    return pl.pallas_call(
        functools.partial(collect_kernel, outs=outs, blocks=blocks, per=per, begin=begin),
        grid=(blocks,),
        in_specs=[pl.BlockSpec(memory_space=pltpu.SMEM)] * 2 + [pl.BlockSpec(memory_space=pl.ANY)] * 6,
        out_specs=[pl.BlockSpec((1, lines, TILE), lambda i: (i, 0, 0))] * outs,
        out_shape=[jax.ShapeDtypeStruct((blocks, lines, TILE), jnp.float32)] * outs,
        scratch_shapes=[pltpu.VMEM((tiles_all, TILE), jnp.float32), pltpu.SemaphoreType.DMA((61,))],
        compiler_params=pltpu.CompilerParams(vmem_limit_bytes=VMEM_LIMIT),
        cost_estimate=pl.CostEstimate(flops=0, bytes_accessed=80_000_000, transcendentals=0),
        name="collect_tiles",
    )(spot, rows, *sources)


def array_multiply(left_side, right_side):
    return jnp.dot(left_side, right_side, preferred_element_type=jnp.float32)


def matmul_left(left_side, right_side):
    return lax.dot_general(
        left_side, right_side, (((0,), (0,)), ((), ())), preferred_element_type=jnp.float32
    )


def trailing_array_multiply(left_side, right_side):
    return lax.dot_general(
        left_side, right_side, (((1,), (1,)), ((), ())), preferred_element_type=jnp.float32
    )


def pieces_of(matrices, tail):
    qkv, out, up, down, place = matrices
    return {
        "qkv": qkv,
        "out": out,
        "up": up,
        "down": down,
        "place": place,
        "small": tail[:60].reshape(10, D),
        "upbias": tail[60:84].reshape(FF),
    }


def norm_forward(values, gain_row, shift_row):
    center = values - jnp.mean(values, axis=-1, keepdims=True)
    inverse = lax.rsqrt(jnp.mean(center * center, axis=-1, keepdims=True) + norm_eps)
    normed = center * inverse
    return (normed * gain_row + shift_row, normed, inverse)


def norm_backward(grad_out, normed, inverse, gain_row):
    scaled = grad_out * gain_row
    grad_in = inverse * (
        scaled
        - jnp.mean(scaled, axis=-1, keepdims=True)
        - normed * jnp.mean(scaled * normed, axis=-1, keepdims=True)
    )
    return (grad_in, jnp.sum(grad_out * normed, axis=0), jnp.sum(grad_out, axis=0))


def gelu_slope(values):
    return (
        0.5 * (1.0 + lax.erf(values * 0.7071067811865476))
        + values * jnp.exp(-0.5 * values * values) * 0.3989422804014327
    )


def key_scores(projected, lengths):
    seqs_count = lengths.shape[0]
    split_heads = projected.reshape(seqs_count, LEN, 3, HEADS, HEAD_DIM)
    scores = jnp.einsum(
        "sqhd,skhd->shqk",
        split_heads[:, :, 0],
        split_heads[:, :, 1],
        preferred_element_type=jnp.float32,
    ) * HEAD_DIM ** (-0.5)
    live_keys = jnp.arange(LEN)[None, :] < lengths[:, None]
    return (jnp.where(live_keys[:, None, None, :], scores, -1000000000.0), split_heads)


def layer_forward(pieces, looked, lengths):
    small_rows = pieces["small"].astype(jnp.float32)
    seqs_count = lengths.shape[0]
    rows_here = seqs_count * LEN
    summed = (
        looked.reshape(seqs_count, LEN, D) + pieces["place"].astype(jnp.float32)[None]
    ).reshape(rows_here, D)
    first_norm, normed_zero, inverse_zero = norm_forward(summed, small_rows[4], small_rows[5])
    inputs = first_norm.astype(jnp.bfloat16)
    qkv_bias = jnp.concatenate([small_rows[0], jnp.zeros((D,), jnp.float32), small_rows[1]])
    projected = (array_multiply(inputs, pieces["qkv"]) + qkv_bias).astype(jnp.bfloat16)
    scores, split_heads = key_scores(projected, lengths)
    peak = jnp.max(scores, axis=-1, keepdims=True)
    exps = jnp.exp(scores - peak)
    totals = jnp.sum(exps, axis=-1, keepdims=True)
    probabilities = (exps / totals).astype(jnp.bfloat16)
    logsum = peak + jnp.log(totals)
    context = jnp.einsum(
        "shqk,skhd->sqhd", probabilities, split_heads[:, :, 2], preferred_element_type=jnp.float32
    )
    context = context.reshape(rows_here, D).astype(jnp.bfloat16)
    attended = array_multiply(context, pieces["out"]) + small_rows[2]
    middle, normed_one, inverse_one = norm_forward(
        first_norm + attended, small_rows[6], small_rows[7]
    )
    middle_low = middle.astype(jnp.bfloat16)
    hidden = array_multiply(middle_low, pieces["up"]) + pieces["upbias"].astype(jnp.float32)
    activated = jax.nn.gelu(hidden, approximate=False).astype(jnp.bfloat16)
    output = array_multiply(activated, pieces["down"]) + small_rows[3]
    final_lines, normed_two, inverse_two = norm_forward(
        middle + output, small_rows[8], small_rows[9]
    )
    saved = {
        "inputs": inputs,
        "projected": projected,
        "logsum": logsum,
        "context": context,
        "middle_low": middle_low,
        "hidden": hidden,
        "activated": activated,
        "normed_zero": normed_zero,
        "inverse_zero": inverse_zero,
        "normed_one": normed_one,
        "inverse_one": inverse_one,
        "normed_two": normed_two,
        "inverse_two": inverse_two,
    }
    return (final_lines, saved)


def feed_backward(pieces, saved, grad_final):
    small_rows = pieces["small"]
    grad_sum_two, grad_gain_two, grad_shift_two = norm_backward(
        grad_final, saved["normed_two"], saved["inverse_two"], small_rows[8]
    )
    grad_out = grad_sum_two.astype(jnp.bfloat16)
    grad_down = matmul_left(saved["activated"], grad_out)
    grad_act = trailing_array_multiply(grad_out, pieces["down"])
    grad_hidden = (grad_act * gelu_slope(saved["hidden"])).astype(jnp.bfloat16)
    grad_up = matmul_left(saved["middle_low"], grad_hidden)
    grad_middle = grad_sum_two + trailing_array_multiply(grad_hidden, pieces["up"])
    grad_sum_one, grad_gain_one, grad_shift_one = norm_backward(
        grad_middle, saved["normed_one"], saved["inverse_one"], small_rows[6]
    )
    grad_small = [jnp.sum(grad_out.astype(jnp.float32), axis=0), grad_gain_one, grad_shift_one, grad_gain_two, grad_shift_two]
    grad_upbias = jnp.sum(grad_hidden.astype(jnp.float32), axis=0)
    return grad_sum_one, (grad_up, grad_down, grad_small, grad_upbias)


def attention_backward(pieces, saved, grad_sum_one, feed_grads, lengths):
    small_rows = pieces["small"]
    seqs_count = lengths.shape[0]
    rows_here = seqs_count * LEN
    grad_up, grad_down, grad_small, grad_upbias = feed_grads
    grad_att = grad_sum_one.astype(jnp.bfloat16)
    grad_outw = matmul_left(saved["context"], grad_att)
    grad_context = (
        trailing_array_multiply(grad_att, pieces["out"])
        .astype(jnp.bfloat16)
        .reshape(seqs_count, LEN, HEADS, HEAD_DIM)
    )
    scores, split_heads = key_scores(saved["projected"], lengths)
    probabilities = jnp.exp(scores - saved["logsum"])
    grad_probs = jnp.einsum(
        "sqhd,skhd->shqk", grad_context, split_heads[:, :, 2], preferred_element_type=jnp.float32
    )
    grad_values = jnp.einsum(
        "shqk,sqhd->skhd",
        probabilities.astype(jnp.bfloat16),
        grad_context,
        preferred_element_type=jnp.float32,
    )
    grad_scores = probabilities * (
        grad_probs - jnp.sum(grad_probs * probabilities, axis=-1, keepdims=True)
    )
    grad_scores = grad_scores.astype(jnp.bfloat16)
    grad_queries = jnp.einsum(
        "shqk,skhd->sqhd", grad_scores, split_heads[:, :, 1], preferred_element_type=jnp.float32
    ) * HEAD_DIM ** (-0.5)
    grad_keys = jnp.einsum(
        "shqk,sqhd->skhd", grad_scores, split_heads[:, :, 0], preferred_element_type=jnp.float32
    ) * HEAD_DIM ** (-0.5)
    grad_proj = (
        jnp.stack([grad_queries, grad_keys, grad_values], axis=2)
        .reshape(rows_here, 3 * D)
        .astype(jnp.bfloat16)
    )
    grad_qkv = matmul_left(saved["inputs"], grad_proj)
    grad_bias_all = jnp.sum(grad_proj.astype(jnp.float32), axis=0)
    grad_first = grad_sum_one + trailing_array_multiply(grad_proj, pieces["qkv"])
    grad_embedded, grad_gain_zero, grad_shift_zero = norm_backward(
        grad_first, saved["normed_zero"], saved["inverse_zero"], small_rows[4]
    )
    grad_place = jnp.sum(grad_embedded.reshape(seqs_count, LEN, D), axis=0)
    grad_small = jnp.stack(
        [
            grad_bias_all[:D],
            grad_bias_all[2 * D :],
            jnp.sum(grad_att.astype(jnp.float32), axis=0),
            grad_small[0],
            grad_gain_zero,
            grad_shift_zero,
            *grad_small[1:],
        ]
    )
    tail = jnp.concatenate(
        [grad_small.reshape(60, TILE), grad_upbias.reshape(24, TILE), jnp.zeros((4, TILE), jnp.float32)]
    )
    return ((grad_qkv, grad_outw, grad_up, grad_down, grad_place, tail), grad_embedded)


def combine_stats(earlier, later):
    peak_s = jnp.maximum(earlier[0], later[0])
    peak_t = jnp.maximum(earlier[2], later[2])
    factor_early = jnp.exp(earlier[0] - peak_s)
    factor_late = jnp.exp(later[0] - peak_s)
    teacher_early = jnp.exp(earlier[2] - peak_t)
    teacher_late = jnp.exp(later[2] - peak_t)
    return jnp.stack(
        [
            peak_s,
            earlier[1] * factor_early + later[1] * factor_late,
            peak_t,
            earlier[3] * teacher_early + later[3] * teacher_late,
            earlier[4] * teacher_early + later[4] * teacher_late,
        ]
    )


def adam_step(weight, first_moment, second, gradient, step_float):
    new_first = beta_first * first_moment + (1.0 - beta_first) * gradient
    new_second = beta_second * second + (1.0 - beta_second) * gradient * gradient
    fix_first = 1.0 - jnp.power(beta_first, step_float)
    fix_second = 1.0 - jnp.power(beta_second, step_float)
    update = new_first / fix_first / (jnp.sqrt(new_second / fix_second) + adam_eps)
    return (weight - learn_rate * (update + weight_decay * weight), new_first, new_second)


def gather_student(tiles, beside):
    per = tiles.shape[0]
    half = per // 16 * 8
    arrivals, places = [], []

    def keep(value, plane, near, start):
        for core in (0, 1):
            arrivals.append(swap(value, CORE) if core else value)
            places.append((plane * 8 + near * 2 + core, start, value.shape[0]))

    for plane in range(4):
        across, deep = swap(tiles, ACROSS), swap(tiles, DEEP)
        if plane == 3:
            across, deep, beside = together(across, deep, beside)
        keep(tiles, plane, 0, 0)
        keep(across, plane, 1, 0)
        keep(deep, plane, 2, 0)
        keep(swap(across[:half], DEEP), plane, 3, 0)
        keep(swap(deep[half:], ACROSS), plane, 3, half)
        if plane < 3:
            tiles = shift(tiles, 1)
    return arrivals, places, beside


def sent_low(value, bit):
    return swap(value.astype(jnp.bfloat16), bit).astype(jnp.float32)


def plane_first(value):
    value = value.reshape(4, 2, 2, value.shape[1], TILE)
    first, second = value[2:], value[:2]
    first = first[:, :, 0] + sent_low(first[:, :, 1], ACROSS)
    second = second[:, 0] + sent_low(second[:, 1], DEEP)
    return first, second


def plane_second(first, second):
    first = first[:, 0] + sent_low(first[:, 1], DEEP)
    second = second[:, 0] + sent_low(second[:, 1], ACROSS)
    return [second[0], second[1], first[0], first[1]]


def on_device(
    near,
    token_ids,
    lengths,
    mask_pos,
    mask_count,
    owner_order,
    step_count,
    teacher_flat,
    mentor_lexicon_weights,
    student_flat,
    flat_first,
    flat_second,
    student_embed,
    embed_first,
    embed_second,
):
    per = student_flat.shape[0]
    tiles_all = owner_order.shape[0]
    vocab_rows, width_share = student_embed.shape
    planes = lax.axis_size("dp")
    group = lax.axis_size("vocab")
    here = lax.axis_index("vocab")
    spot = jnp.stack([lax.axis_index("dp"), here]).astype(jnp.int32)

    facts = jnp.concatenate([token_ids.reshape(LEN), lengths, mask_count, jnp.zeros((TILE - 2,), jnp.int32)])
    target_rows = rows_of_tiles(owner_order)
    student_low = student_flat.astype(jnp.bfloat16)
    table_low = lax.all_gather(student_embed.T.astype(jnp.bfloat16), "dp", axis=0, tiled=True)
    words = jnp.arange(vocab_rows, dtype=jnp.int32)

    def chosen(ids):
        return (ids.reshape(-1, 1) - here * vocab_rows == words[None]).astype(jnp.bfloat16)

    def rows_t(ids):
        return array_multiply(chosen(ids), mentor_lexicon_weights).astype(jnp.bfloat16)

    def rows_s(ids):
        return trailing_array_multiply(chosen(ids), table_low).astype(jnp.bfloat16)

    if near:
        plane_facts = gather_near(facts)
        far_ids, close_ids = plane_facts[4:, :LEN], plane_facts[:4, :LEN]
        shape = (2, 2, LEN, D)
        beside = [
            rows_t(close_ids).reshape(shape) + swap(rows_t(far_ids).reshape(shape), CORE),
            rows_s(close_ids).reshape(shape),
            rows_s(far_ids).reshape(shape),
        ]
        arrivals, places, beside = gather_student(student_low, beside)
        looked_t = beside[0]
        looked_s = beside[1] + swap(beside[2], CORE)
        arrivals, teacher_flat, looked_t, looked_s, target_rows = together(
            arrivals, teacher_flat, looked_t, looked_s, target_rows
        )
        teacher_tiles = lax.all_gather(teacher_flat, ("dp", "vocab"), axis=0, tiled=True)
        looked_t, looked_s = plane_hop(looked_t), plane_hop(looked_s)
        matrices = place_tiles(spot, target_rows, arrivals, tuple(places), planes * group, per)
        matrices, looked_t, looked_s, facts = together(matrices, looked_t, looked_s, facts)
        other_facts = gather_near(jnp.stack([shift(facts, 1), shift(facts, 2), shift(facts, 3)]))
        all_facts = jnp.concatenate([plane_facts[:, None], other_facts], axis=1)
        looked_s = plane_end(*looked_s).astype(jnp.float32)
        looked_t = plane_end(*looked_t).astype(jnp.float32)
    else:
        by_plane = lax.all_gather(facts, "dp", axis=0)
        all_facts = lax.all_gather(by_plane, "vocab", axis=0)
        plane_facts = lax.dynamic_index_in_dim(all_facts, lax.axis_index("dp"), 1, keepdims=False)
        teacher_tiles = lax.all_gather(teacher_flat, ("dp", "vocab"), axis=0, tiled=True)
        student_tiles = lax.all_gather(student_low, ("dp", "vocab"), axis=0, tiled=True)
        plane_ids = plane_facts[:, :LEN]
        looked_t, looked_s = (
            lax.psum_scatter(rows, "vocab", scatter_dimension=0, tiled=True).astype(jnp.float32)
            for rows in (rows_t(plane_ids), rows_s(plane_ids))
        )
        matrices = place_tiles(
            spot, target_rows, [student_tiles.reshape(planes * group, per, TILE)], (None,), planes * group, per
        )
    student = pieces_of(matrices[:5], matrices[5])
    final_s, saved = layer_forward(student, looked_s, lengths)
    final_s, teacher_tiles, looked_t, all_facts = together(final_s, teacher_tiles, looked_t, all_facts)
    teacher = pieces_of(
        [unpack_matrix(teacher_tiles, piece) for piece in MATRICES],
        teacher_tiles[TAIL : TAIL + TAIL_TILES].astype(jnp.float32),
    )
    token_total = jnp.sum(all_facts[:, :, LEN]).astype(jnp.float32)
    masked_total = jnp.sum(all_facts[:, :, LEN + 1]).astype(jnp.float32)

    offsets = jnp.concatenate([mask_pos.reshape(CAP), jnp.zeros((SLOTS - CAP,), jnp.int32)])
    picked_s = final_s[offsets].astype(jnp.bfloat16)
    if near:
        learner_picked = gather_near(picked_s).reshape(-1, D)
    final_t = layer_forward(teacher, looked_t, lengths)[0]
    if near:
        final_t, learner_picked = together(final_t, learner_picked)

    picked_t = final_t[offsets].astype(jnp.bfloat16)
    if near:
        mentor_picked = gather_near(picked_t).reshape(-1, D)
    else:
        learner_picked = lax.all_gather(picked_s, "vocab", axis=0, tiled=True)
        mentor_picked = lax.all_gather(picked_t, "vocab", axis=0, tiled=True)
    live_weighting = (
        (jnp.arange(SLOTS)[None] < plane_facts[:, LEN + 1, None]).astype(jnp.float32).reshape(-1)
    )
    learner_energy = array_multiply(learner_picked, table_low) / smoothing_heat_scale
    teacher_logit = (
        trailing_array_multiply(mentor_picked, mentor_lexicon_weights) / smoothing_heat_scale
    )
    peak_s = jnp.max(learner_energy, axis=1)
    peak_t = jnp.max(teacher_logit, axis=1)
    teacher_exps = jnp.exp(teacher_logit - peak_t[:, None])
    stats = jnp.stack(
        [
            peak_s,
            jnp.sum(jnp.exp(learner_energy - peak_s[:, None]), axis=1),
            peak_t,
            jnp.sum(teacher_exps, axis=1),
            jnp.sum(teacher_exps * (teacher_logit - learner_energy), axis=1),
        ]
    )
    if near:
        stats = stats.reshape(5, 2, 2, 2, SLOTS)
        for axis, bit in ((1, CORE), (2, DEEP), (3, ACROSS)):
            stats = combine_stats(stats, jnp.flip(swap(stats, bit), axis))
        stats = stats.reshape(5, -1)
    else:
        everything = lax.all_gather(stats, "vocab", axis=0)
        stats = everything[0]
        for k in range(1, group):
            stats = combine_stats(stats, everything[k])
    logsum_s = stats[0] + jnp.log(stats[1])
    logsum_t = stats[2] + jnp.log(stats[3])
    diverge = stats[4] / stats[3] - logsum_t + logsum_s
    mine = 0 if near else here * SLOTS
    divergence_part = jnp.sum(lax.dynamic_slice_in_dim(diverge * live_weighting, mine, SLOTS))
    student_probs = jnp.exp(learner_energy - logsum_s[:, None])
    teacher_probs = jnp.exp(teacher_logit - logsum_t[:, None])
    grad_logit = (
        mixing_coefficient
        * smoothing_heat_scale
        / masked_total
        * live_weighting[:, None]
        * (student_probs - teacher_probs)
    ).astype(jnp.bfloat16)
    if near:
        half = grad_logit.shape[0] // 2
        far = trailing_array_multiply(grad_logit[half:], table_low).reshape(2, 2, SLOTS, D)
        close = trailing_array_multiply(grad_logit[:half], table_low).reshape(2, 2, SLOTS, D)
        grad_rows = plane_end(*plane_hop(close + swap(far, CORE)))
    else:
        grad_rows = lax.psum_scatter(
            trailing_array_multiply(grad_logit, table_low), "vocab", scatter_dimension=0, tiled=True
        )
    head_grad = matmul_left(learner_picked, grad_logit)
    head_grad, grad_rows = together(head_grad, grad_rows)
    if not near:
        head_part = lax.psum_scatter(head_grad, "dp", scatter_dimension=0, tiled=True)
    products = jnp.sum(final_s * final_t, axis=1)
    inverse_s = lax.rsqrt(jnp.sum(final_s * final_s, axis=1) + cosine_eps)
    inverse_t = lax.rsqrt(jnp.sum(final_t * final_t, axis=1) + cosine_eps)
    live_rows = (jnp.arange(LEN)[None, :] < lengths[:, None]).reshape(-1)
    cosine = products * inverse_s * inverse_t
    cosine_term = jnp.sum(jnp.where(live_rows, 1.0 - cosine, 0.0))
    weighting = jnp.where(live_rows, -cosine_weight / token_total, 0.0) * inverse_s * inverse_t
    grad_final = weighting[:, None] * (
        final_t - (products * inverse_s * inverse_s)[:, None] * final_s
    )
    grad_final = grad_final.at[offsets].add(grad_rows)
    if near:
        heads = upward(head_grad.reshape(4, width_share, vocab_rows))
        moving = shift(heads[3], 1)
        grad_sum_one, feed_grads = feed_backward(student, saved, grad_final)
        layer_grads, grad_embedded = attention_backward(student, saved, grad_sum_one, feed_grads, lengths)
        grad_embedded, moving = together(grad_embedded, moving)
    else:
        grad_sum_one, feed_grads = feed_backward(student, saved, grad_final)
        layer_grads, grad_embedded = attention_backward(student, saved, grad_sum_one, feed_grads, lengths)

    shares = grad_embedded.astype(jnp.bfloat16).reshape(LEN, planes, width_share).transpose(1, 0, 2)
    if near:
        own = upward(shares)
        shares = jnp.stack([own[0]] + [shift(own[k], k) for k in (1, 2, 3)])
        ids = all_facts[:, :, :LEN].reshape(2, 2, 2, planes, LEN)
        for axis, bit in ((0, CORE), (1, DEEP), (2, ACROSS)):
            ids = jnp.where((here & bit) != 0, jnp.flip(ids, axis), ids)
        ids = ids.transpose(1, 2, 0, 3, 4)
    else:
        shares = lax.all_to_all(shares, "dp", 0, 0)
        ids = all_facts[:, :, :LEN]
    token_grads = lax.all_gather(shares.reshape(-1, width_share), "vocab", axis=0, tiled=True)
    if near:
        edges = (0, 640, 1256, per)

        def collect(n):
            return collect_tiles(spot, target_rows, layer_grads, tiles_all, per, 2, edges[n], edges[n + 1] - edges[n])

        one, shares = together(collect(0), shares)
        moving = shift(heads[2] + moving, 1)
        token_grads = lax.all_gather(shares.reshape(-1, width_share), "vocab", axis=0, tiled=True)
        chip_one = one[0] + swap(one[1], CORE)
        chip_one, two, moving = together(chip_one, collect(1), moving)
        moving = shift(heads[1] + moving, 1)
        first_one = plane_first(chip_one)
        chip_two = two[0] + swap(two[1], CORE)
        first_one, chip_two, three, token_grads = together(first_one, chip_two, collect(2), token_grads)
        token_part = matmul_left(token_grads, chosen(ids))
        blocks_one = plane_second(*first_one)
        first_two = plane_first(chip_two)
        chip_three = three[0] + swap(three[1], CORE)
        blocks_one, first_two, chip_three, token_part, moving = together(
            blocks_one, first_two, chip_three, token_part, moving
        )
        head_part = heads[0] + moving
        blocks_two = plane_second(*first_two)
        blocks_three = plane_second(*plane_first(chip_three))
        sums = [ring_sum(blocks) for blocks in (blocks_one, blocks_two, blocks_three)]
        flat_grad = jnp.concatenate(sums)
    else:
        token_grads = lax.all_gather(shares.reshape(-1, width_share), "vocab", axis=0, tiled=True)
        token_part = matmul_left(token_grads, chosen(ids))
        (grad_tiles,) = collect_tiles(spot, target_rows, layer_grads, tiles_all, per, 1, 0, per)
        flat_grad = lax.psum_scatter(
            grad_tiles.reshape(tiles_all, TILE), ("dp", "vocab"), scatter_dimension=0, tiled=True
        )
    table_grad = (head_part + token_part).T
    loss_term = (
        mixing_coefficient * smoothing_heat_scale**2 * divergence_part / masked_total
        + cosine_weight * cosine_term / token_total
    )
    squares = jnp.sum(flat_grad * flat_grad) + jnp.sum(table_grad * table_grad)
    if near:
        squares, loss_value = sum_everywhere(jnp.stack([squares, loss_term]))
    else:
        squares, loss_value = lax.psum((squares, loss_term), ("dp", "vocab"))
    grad_norm = jnp.sqrt(squares)
    factor = clip_norm / jnp.maximum(grad_norm, clip_norm)
    step_float = step_count[0].astype(jnp.float32)
    new_flat, new_flat_first, new_flat_second = adam_step(
        student_flat, flat_first, flat_second, flat_grad * factor, step_float
    )
    new_embed, new_embed_first, new_embed_second = adam_step(
        student_embed, embed_first, embed_second, table_grad * factor, step_float
    )
    return (
        loss_value,
        grad_norm,
        new_flat,
        new_flat_first,
        new_flat_second,
        new_embed,
        new_embed_first,
        new_embed_second,
    )


def solution(mesh):
    near = mesh.shape["dp"] == 4 and mesh.shape["vocab"] == 8
    return jax.shard_map(
        functools.partial(on_device, near),
        mesh=mesh,
        in_specs=(
            P(("dp", "vocab"), None),
            P(("dp", "vocab")),
            P(("dp", "vocab"), None),
            P(("dp", "vocab")),
            P(),
            P(),
            P(("dp", "vocab"), None),
            P("vocab", None),
            P(("dp", "vocab"), None),
            P(("dp", "vocab"), None),
            P(("dp", "vocab"), None),
            P("vocab", "dp"),
            P("vocab", "dp"),
            P("vocab", "dp"),
        ),
        out_specs=(
            P(),
            P(),
            P(("dp", "vocab"), None),
            P(("dp", "vocab"), None),
            P(("dp", "vocab"), None),
            P("vocab", "dp"),
            P("vocab", "dp"),
            P("vocab", "dp"),
        ),
        check_vma=False,
    )
```

```python
import functools
import math

import jax
import jax.numpy as jnp
from jax import lax
from jax.experimental import pallas as pl
from jax.experimental.pallas import tpu as pltpu
from jax.sharding import PartitionSpec as P

D = 768
HEADS = 12
HEAD_DIM = 64
FF = 3072
LEN = 512
CAP = 120
SLOTS = 128
TILE = 128

QKV = (0, D, 18)
OUT = (13824, D, 6)
UP = (18432, D, 24)
DOWN = (36864, FF, 6)
PLACE = (55296, LEN, 6)
MATRICES = (QKV, OUT, UP, DOWN, PLACE)
TAIL = 58368
TAIL_TILES = 88
HOME_ORDER = (UP, DOWN, QKV, OUT, PLACE)

VMEM_LIMIT = 60 * 1024 * 1024

smoothing_heat_scale = 2.0
mixing_coefficient = 5.0
cosine_weight = 20.0
clip_norm = 0.01
beta_first = 0.9
beta_second = 0.98
adam_eps = 1e-08
weight_decay = 0.01
learn_rate = 0.1
norm_eps = 1e-12
cosine_eps = 1e-06

CORE, ACROSS, DEEP = 1, 2, 4


def swap(value, bit):
    return lax.ppermute(value, "vocab", [(i, i ^ bit) for i in range(8)])


def shift(value, steps):
    size = lax.axis_size("dp")
    return lax.ppermute(value, "dp", [(i, (i + steps) % size) for i in range(size)])


def gather_near(value):
    value = value[None]
    for bit in (ACROSS, DEEP, CORE):
        value = jnp.concatenate([value, swap(value, bit)])
    return value


def plane_hop(value):
    half = value.shape[2] // 2
    upper, lower = value[:, :, :half], value[:, :, half:]
    return upper[:, 0] + swap(upper[:, 1], ACROSS), lower[0] + swap(lower[1], DEEP)


def plane_end(upper, lower):
    return jnp.concatenate([upper[0] + swap(upper[1], DEEP), lower[0] + swap(lower[1], ACROSS)])


def together(*values):
    return lax.optimization_barrier(values)


def ring_hop(blocks):
    moving = shift(blocks[-1], 1)
    return [*blocks[:-2], blocks[-2] + moving]


def sum_everywhere(value):
    for bit in (CORE, ACROSS, DEEP):
        value = value + swap(value, bit)
    for step in (1, 2):
        value = value + lax.ppermute(value, "dp", [(i, i ^ step) for i in range(4)])
    return value


def upward(table):
    z = lax.axis_index("dp")
    return [lax.dynamic_index_in_dim(table, (z + k) % 4, keepdims=False) for k in range(4)]


def shares_of(tiles_all, devices):
    sizes = [height * across // devices for _, height, across in HOME_ORDER]
    sizes.append((tiles_all - TAIL) // devices)
    starts = [sum(sizes[:n]) for n in range(len(sizes))]
    return sizes, starts


def homes_of(tiles, tiles_all, devices):
    per = tiles_all // devices
    sizes, starts = shares_of(tiles_all, devices)
    homes = ((tiles - TAIL) // sizes[-1]) * per + starts[-1] + (tiles - TAIL) % sizes[-1]
    for (first, height, across), size, start in zip(HOME_ORDER, sizes, starts):
        at = tiles - first
        line = (at % across) * height + at // across
        inside = (at >= 0) & (at < height * across)
        homes = jnp.where(inside, (line // size) * per + start + line % size, homes)
    return homes


def room(per, devices):
    mean = per / devices
    return int(-(-(mean + 5.0 * mean**0.5) // 8) * 8)


def row_steps(total, size, step):
    whole, rest = divmod(total, size)

    def body(i, carry):
        step(i * size, size)
        return carry

    lax.fori_loop(0, whole, body, 0)
    if rest:
        step(whole * size, rest)


def send_kernel(slots, lines, tiles, packed, index, stage, *, per):
    slot_count = packed.shape[0]

    def clear(start, size):
        for u in range(size):
            index[start + u] = per

    row_steps(slot_count + 8, 64, clear)
    stage[...] = jnp.zeros_like(stage)

    def place(start, size):
        for u in range(size):
            slot = slots[start + u]
            stage[pl.ds(slot, 1), :] = tiles[pl.ds(start + u, 1), :]
            index[slot] = lines[start + u]

    row_steps(per, 64, place)
    packed[...] = stage[pl.ds(0, slot_count), :].astype(packed.dtype)


def send_tiles(slots, lines, tiles, slot_count):
    per = tiles.shape[0]
    return pl.pallas_call(
        functools.partial(send_kernel, per=per),
        in_specs=[pl.BlockSpec(memory_space=pltpu.SMEM)] * 2 + [pl.BlockSpec(memory_space=pltpu.VMEM)],
        out_specs=[pl.BlockSpec(memory_space=pltpu.VMEM), pl.BlockSpec(memory_space=pltpu.SMEM)],
        out_shape=[
            jax.ShapeDtypeStruct((slot_count, TILE), jnp.bfloat16),
            jax.ShapeDtypeStruct((slot_count + 8,), jnp.int32),
        ],
        scratch_shapes=[pltpu.VMEM((slot_count + 8, TILE), jnp.float32)],
        name="send_tiles",
    )(slots, lines, tiles)


def land_kernel(index, packed, tiles, stage, full):
    stage[...] = packed[...].astype(jnp.float32)

    def place(start, size):
        for u in range(size):
            full[pl.ds(index[start + u], 1), :] = stage[pl.ds(start + u, 1), :]

    row_steps(packed.shape[0], 128, place)
    tiles[...] = full[pl.ds(0, tiles.shape[0]), :].astype(tiles.dtype)


def land_tiles(index, packed, per):
    slot_count = packed.shape[0]
    return pl.pallas_call(
        land_kernel,
        in_specs=[pl.BlockSpec(memory_space=pltpu.SMEM), pl.BlockSpec(memory_space=pltpu.VMEM)],
        out_specs=pl.BlockSpec(memory_space=pltpu.VMEM),
        out_shape=jax.ShapeDtypeStruct((per, TILE), jnp.bfloat16),
        scratch_shapes=[pltpu.VMEM((slot_count, TILE), jnp.float32), pltpu.VMEM((per + 8, TILE), jnp.float32)],
        name="land_tiles",
    )(index, packed)


def pick_kernel(index, source, target, *, count):
    def pick(start, size):
        for u in range(size):
            target[pl.ds(start + u, 1), :] = source[pl.ds(index[start + u], 1), :]

    row_steps(count, 128, pick)


def pick_tiles(index, source, count):
    return pl.pallas_call(
        functools.partial(pick_kernel, count=count),
        in_specs=[pl.BlockSpec(memory_space=pltpu.SMEM), pl.BlockSpec(memory_space=pltpu.VMEM)],
        out_specs=pl.BlockSpec(memory_space=pltpu.VMEM),
        out_shape=jax.ShapeDtypeStruct((count, TILE), source.dtype),
        name="pick_tiles",
    )(index, source)


def assemble_kernel(spot, *refs, places, sizes, starts):
    arrivals = refs[: len(places)]
    targets = refs[len(places) : len(places) + 5]
    tail = refs[len(places) + 5]
    landed, sems = refs[len(places) + 6 :]
    copies = []
    for n, (arrival, place) in enumerate(zip(arrivals, places)):
        target = landed.at[place[0], pl.ds(place[1], place[2])]
        copies.append(pltpu.make_async_copy(arrival, target, sems.at[n]))
    for copy in copies:
        copy.start()
    for copy in copies:
        copy.wait()

    def one_device(block, carry):
        owner = ((spot[0] + 4 - block // 8) % 4) * 8 + (spot[1] ^ (block % 8))
        for target, (_, height, _), size, start in zip(targets, HOME_ORDER, sizes, starts):
            unit = math.gcd(size, height)
            for part in range(size // unit):
                line = owner * size + part * unit
                column = line // height
                target[
                    pl.ds(pl.multiple_of(line - column * height, 16), unit),
                    pl.ds(pl.multiple_of(column * TILE, TILE), TILE),
                ] = landed[block, pl.ds(start + part * unit, unit), :]
        tail[owner] = landed[block, pl.ds(starts[-1], sizes[-1]), :].astype(jnp.float32)
        return carry

    lax.fori_loop(0, landed.shape[0], one_device, 0)


def assemble_layer(spot, arrivals, places, tiles_all, devices):
    sizes, starts = shares_of(tiles_all, devices)
    return pl.pallas_call(
        functools.partial(assemble_kernel, places=places, sizes=sizes, starts=starts),
        in_specs=[pl.BlockSpec(memory_space=pltpu.SMEM)] + [pl.BlockSpec(memory_space=pl.ANY)] * len(arrivals),
        out_specs=[pl.BlockSpec(memory_space=pltpu.VMEM)] * 6,
        out_shape=[jax.ShapeDtypeStruct((h, a * TILE), jnp.bfloat16) for _, h, a in HOME_ORDER]
        + [jax.ShapeDtypeStruct((devices, sizes[-1], TILE), jnp.float32)],
        scratch_shapes=[
            pltpu.VMEM((devices, tiles_all // devices, TILE), jnp.bfloat16),
            pltpu.SemaphoreType.DMA((len(arrivals),)),
        ],
        compiler_params=pltpu.CompilerParams(vmem_limit_bytes=VMEM_LIMIT),
        cost_estimate=pl.CostEstimate(flops=0, bytes_accessed=60_000_000, transcendentals=0),
        name="assemble_layer",
    )(spot, *arrivals)


def split_kernel(spot, *refs, count, sizes):
    near, far = refs[2 * count :]
    start = 0
    for n in range(count):
        near[0, pl.ds(start, sizes[n]), :] = refs[n][0]
        far[0, pl.ds(start, sizes[n]), :] = refs[count + n][0]
        start += sizes[n]


def split_cores(spot, parts):
    sizes = [part.shape[1] for part in parts]
    total = sum(sizes)

    def owner(block, spot, core):
        return ((spot[0] + block // 4) % 4) * 8 + (spot[1] ^ ((block % 4) * 2 + core))

    specs = [
        pl.BlockSpec((1, size, TILE), lambda i, spot, core=core: (owner(i, spot, core), 0, 0))
        for core in (0, 1)
        for size in sizes
    ]
    return pl.pallas_call(
        functools.partial(split_kernel, count=len(parts), sizes=sizes),
        grid_spec=pltpu.PrefetchScalarGridSpec(
            num_scalar_prefetch=1,
            grid=(16,),
            in_specs=specs,
            out_specs=[pl.BlockSpec((1, total, TILE), lambda i, spot: (i, 0, 0))] * 2,
        ),
        out_shape=[jax.ShapeDtypeStruct((16, total, TILE), jnp.float32)] * 2,
        cost_estimate=pl.CostEstimate(flops=0, bytes_accessed=32 * total * TILE * 8, transcendentals=0),
        name="split_cores",
    )(spot, *parts, *parts)


def weight_grad_kernel(left, right, target):
    product = lax.dot_general(
        left[...], right[...], (((0,), (0,)), ((), ())), preferred_element_type=jnp.float32
    )
    for column in range(target.shape[0]):
        target[column] = product[:, column * TILE : (column + 1) * TILE]


def weight_grad(left, right, columns):
    rows, height = left.shape
    across = right.shape[1] // TILE
    return pl.pallas_call(
        weight_grad_kernel,
        grid=(height // D, across // columns),
        in_specs=[
            pl.BlockSpec((rows, D), lambda i, j: (0, i)),
            pl.BlockSpec((rows, columns * TILE), lambda i, j: (0, j)),
        ],
        out_specs=pl.BlockSpec((columns, D, TILE), lambda i, j: (j, i, 0)),
        out_shape=jax.ShapeDtypeStruct((across, height, TILE), jnp.float32),
        cost_estimate=pl.CostEstimate(
            flops=2 * rows * height * across * TILE,
            bytes_accessed=rows * (height + across * TILE) * 2 + height * across * TILE * 4,
            transcendentals=0,
        ),
        name="weight_grad",
    )(left, right)


def unpack_kernel(source, target, stage, *, across):
    stage[...] = source[...].astype(jnp.float32)

    def step(g, carry):
        for column in range(across):
            lines = stage[pl.ds(g * 16 * across + column, 16, stride=across), :]
            target[pl.ds(pl.multiple_of(g * 16, 16), 16), column * TILE : (column + 1) * TILE] = lines.astype(
                jnp.bfloat16
            )
        return carry

    lax.fori_loop(0, target.shape[0] // 16, step, 0)


def unpack_matrix(tiles, piece):
    first, height, across = piece
    lines = min(height, 384 if across > 6 else 768)
    block = lines * across
    return pl.pallas_call(
        functools.partial(unpack_kernel, across=across),
        grid=(height // lines,),
        in_specs=[pl.BlockSpec((block, TILE), lambda i: (first // block + i, 0))],
        out_specs=pl.BlockSpec((lines, across * TILE), lambda i: (i, 0)),
        out_shape=jax.ShapeDtypeStruct((height, across * TILE), jnp.bfloat16),
        scratch_shapes=[pltpu.VMEM((block, TILE), jnp.float32)],
        name="unpack_matrix",
    )(tiles)


def array_multiply(left_side, right_side):
    return jnp.dot(left_side, right_side, preferred_element_type=jnp.float32)


def matmul_left(left_side, right_side):
    return lax.dot_general(
        left_side, right_side, (((0,), (0,)), ((), ())), preferred_element_type=jnp.float32
    )


def trailing_array_multiply(left_side, right_side):
    return lax.dot_general(
        left_side, right_side, (((1,), (1,)), ((), ())), preferred_element_type=jnp.float32
    )


def pieces_of(matrices, tail):
    qkv, out, up, down, place = matrices
    return {
        "qkv": qkv,
        "out": out,
        "up": up,
        "down": down,
        "place": place,
        "small": tail[:60].reshape(10, D),
        "upbias": tail[60:84].reshape(FF),
    }


def norm_forward(values, gain_row, shift_row):
    center = values - jnp.mean(values, axis=-1, keepdims=True)
    inverse = lax.rsqrt(jnp.mean(center * center, axis=-1, keepdims=True) + norm_eps)
    normed = center * inverse
    return (normed * gain_row + shift_row, normed, inverse)


def norm_backward(grad_out, normed, inverse, gain_row):
    scaled = grad_out * gain_row
    grad_in = inverse * (
        scaled
        - jnp.mean(scaled, axis=-1, keepdims=True)
        - normed * jnp.mean(scaled * normed, axis=-1, keepdims=True)
    )
    return (grad_in, jnp.sum(grad_out * normed, axis=0), jnp.sum(grad_out, axis=0))


def gelu_slope(values):
    return (
        0.5 * (1.0 + lax.erf(values * 0.7071067811865476))
        + values * jnp.exp(-0.5 * values * values) * 0.3989422804014327
    )


def key_scores(projected, lengths):
    seqs_count = lengths.shape[0]
    split_heads = projected.reshape(seqs_count, LEN, 3, HEADS, HEAD_DIM)
    scores = jnp.einsum(
        "sqhd,skhd->shqk",
        split_heads[:, :, 0],
        split_heads[:, :, 1],
        preferred_element_type=jnp.float32,
    ) * HEAD_DIM ** (-0.5)
    live_keys = jnp.arange(LEN)[None, :] < lengths[:, None]
    return (jnp.where(live_keys[:, None, None, :], scores, -1000000000.0), split_heads)


def layer_forward(pieces, looked, lengths):
    small_rows = pieces["small"].astype(jnp.float32)
    seqs_count = lengths.shape[0]
    rows_here = seqs_count * LEN
    summed = (
        looked.reshape(seqs_count, LEN, D) + pieces["place"].astype(jnp.float32)[None]
    ).reshape(rows_here, D)
    first_norm, normed_zero, inverse_zero = norm_forward(summed, small_rows[4], small_rows[5])
    inputs = first_norm.astype(jnp.bfloat16)
    qkv_bias = jnp.concatenate([small_rows[0], jnp.zeros((D,), jnp.float32), small_rows[1]])
    projected = (array_multiply(inputs, pieces["qkv"]) + qkv_bias).astype(jnp.bfloat16)
    scores, split_heads = key_scores(projected, lengths)
    peak = jnp.max(scores, axis=-1, keepdims=True)
    exps = jnp.exp(scores - peak)
    totals = jnp.sum(exps, axis=-1, keepdims=True)
    probabilities = (exps / totals).astype(jnp.bfloat16)
    logsum = peak + jnp.log(totals)
    context = jnp.einsum(
        "shqk,skhd->sqhd", probabilities, split_heads[:, :, 2], preferred_element_type=jnp.float32
    )
    context = context.reshape(rows_here, D).astype(jnp.bfloat16)
    attended = array_multiply(context, pieces["out"]) + small_rows[2]
    middle, normed_one, inverse_one = norm_forward(
        first_norm + attended, small_rows[6], small_rows[7]
    )
    middle_low = middle.astype(jnp.bfloat16)
    hidden = array_multiply(middle_low, pieces["up"]) + pieces["upbias"].astype(jnp.float32)
    activated = jax.nn.gelu(hidden, approximate=False).astype(jnp.bfloat16)
    output = array_multiply(activated, pieces["down"]) + small_rows[3]
    final_lines, normed_two, inverse_two = norm_forward(
        middle + output, small_rows[8], small_rows[9]
    )
    saved = {
        "inputs": inputs,
        "projected": projected,
        "logsum": logsum,
        "context": context,
        "middle_low": middle_low,
        "hidden": hidden,
        "activated": activated,
        "normed_zero": normed_zero,
        "inverse_zero": inverse_zero,
        "normed_one": normed_one,
        "inverse_one": inverse_one,
        "normed_two": normed_two,
        "inverse_two": inverse_two,
    }
    return (final_lines, saved)


def feed_backward(pieces, saved, grad_final, flow):
    small_rows = pieces["small"]
    grad_sum_two, grad_gain_two, grad_shift_two = norm_backward(
        grad_final, saved["normed_two"], saved["inverse_two"], small_rows[8]
    )
    grad_out = grad_sum_two.astype(jnp.bfloat16)
    flow.add(weight_grad(saved["activated"], grad_out, 6))
    grad_act = trailing_array_multiply(grad_out, pieces["down"])
    grad_hidden = (grad_act * gelu_slope(saved["hidden"])).astype(jnp.bfloat16)
    (grad_hidden,) = flow.advance(grad_hidden)
    flow.add(weight_grad(saved["middle_low"], grad_hidden, 6))
    grad_middle = grad_sum_two + trailing_array_multiply(grad_hidden, pieces["up"])
    grad_sum_one, grad_gain_one, grad_shift_one = norm_backward(
        grad_middle, saved["normed_one"], saved["inverse_one"], small_rows[6]
    )
    grad_upbias = jnp.sum(grad_hidden.astype(jnp.float32), axis=0)
    (grad_sum_one,) = flow.advance(grad_sum_one)
    return (
        grad_sum_one,
        [jnp.sum(grad_out.astype(jnp.float32), axis=0), grad_gain_one, grad_shift_one, grad_gain_two, grad_shift_two],
        grad_upbias,
    )


def attention_backward(pieces, saved, grad_sum_one, grad_small, grad_upbias, lengths, tail_rows, flow):
    small_rows = pieces["small"]
    seqs_count = lengths.shape[0]
    rows_here = seqs_count * LEN
    grad_att = grad_sum_one.astype(jnp.bfloat16)
    grad_outw = weight_grad(saved["context"], grad_att, 6)
    grad_context = (
        trailing_array_multiply(grad_att, pieces["out"])
        .astype(jnp.bfloat16)
        .reshape(seqs_count, LEN, HEADS, HEAD_DIM)
    )
    scores, split_heads = key_scores(saved["projected"], lengths)
    probabilities = jnp.exp(scores - saved["logsum"])
    grad_probs = jnp.einsum(
        "sqhd,skhd->shqk", grad_context, split_heads[:, :, 2], preferred_element_type=jnp.float32
    )
    grad_values = jnp.einsum(
        "shqk,sqhd->skhd",
        probabilities.astype(jnp.bfloat16),
        grad_context,
        preferred_element_type=jnp.float32,
    )
    grad_values, grad_probs = flow.advance(grad_values, grad_probs)
    grad_scores = probabilities * (
        grad_probs - jnp.sum(grad_probs * probabilities, axis=-1, keepdims=True)
    )
    (grad_scores,) = flow.advance(grad_scores.astype(jnp.bfloat16))
    grad_queries = jnp.einsum(
        "shqk,skhd->sqhd", grad_scores, split_heads[:, :, 1], preferred_element_type=jnp.float32
    ) * HEAD_DIM ** (-0.5)
    grad_keys = jnp.einsum(
        "shqk,sqhd->skhd", grad_scores, split_heads[:, :, 0], preferred_element_type=jnp.float32
    ) * HEAD_DIM ** (-0.5)
    grad_proj = (
        jnp.stack([grad_queries, grad_keys, grad_values], axis=2)
        .reshape(rows_here, 3 * D)
        .astype(jnp.bfloat16)
    )
    (grad_proj,) = flow.advance(grad_proj)
    grad_qkv = weight_grad(saved["inputs"], grad_proj, 6)
    grad_bias_all = jnp.sum(grad_proj.astype(jnp.float32), axis=0)
    grad_first = grad_sum_one + trailing_array_multiply(grad_proj, pieces["qkv"])
    grad_embedded, grad_gain_zero, grad_shift_zero = norm_backward(
        grad_first, saved["normed_zero"], saved["inverse_zero"], small_rows[4]
    )
    grad_place = jnp.sum(grad_embedded.reshape(seqs_count, LEN, D), axis=0)
    grad_small = jnp.stack(
        [
            grad_bias_all[:D],
            grad_bias_all[2 * D :],
            jnp.sum(grad_att.astype(jnp.float32), axis=0),
            grad_small[0],
            grad_gain_zero,
            grad_shift_zero,
            *grad_small[1:],
        ]
    )
    tail = jnp.concatenate(
        [
            grad_small.reshape(60, TILE),
            grad_upbias.reshape(24, TILE),
            jnp.zeros((tail_rows - 84, TILE), jnp.float32),
        ]
    )
    (grad_embedded,) = flow.advance(grad_embedded)
    flow.add(grad_qkv, grad_outw, grad_place.reshape(LEN, 6, TILE).transpose(1, 0, 2), tail)
    return grad_embedded


def combine_stats(earlier, later):
    peak_s = jnp.maximum(earlier[0], later[0])
    peak_t = jnp.maximum(earlier[2], later[2])
    factor_early = jnp.exp(earlier[0] - peak_s)
    factor_late = jnp.exp(later[0] - peak_s)
    teacher_early = jnp.exp(earlier[2] - peak_t)
    teacher_late = jnp.exp(later[2] - peak_t)
    return jnp.stack(
        [
            peak_s,
            earlier[1] * factor_early + later[1] * factor_late,
            peak_t,
            earlier[3] * teacher_early + later[3] * teacher_late,
            earlier[4] * teacher_early + later[4] * teacher_late,
        ]
    )


def adam_step(weight, first_moment, second, gradient, step_float):
    new_first = beta_first * first_moment + (1.0 - beta_first) * gradient
    new_second = beta_second * second + (1.0 - beta_second) * gradient * gradient
    fix_first = 1.0 - jnp.power(beta_first, step_float)
    fix_second = 1.0 - jnp.power(beta_second, step_float)
    update = new_first / fix_first / (jnp.sqrt(new_second / fix_second) + adam_eps)
    return (weight - learn_rate * (update + weight_decay * weight), new_first, new_second)


def gather_layer(tiles, fillers):
    per = tiles.shape[0]
    half = per // 16 * 8
    arrivals, places = [], []
    waiting = [(tiles, 0, 0, 0)]
    crossed = None
    done = []
    for stage in range(6):
        moved = []
        for value, plane, near, start in waiting:
            arrivals.append(value)
            places.append((plane * 8 + near * 2, start, value.shape[0]))
            moved.append((swap(value, CORE), plane, near, start))
        landed = []
        if crossed is not None:
            across, deep, plane = crossed
            landed.append((swap(across[:half], DEEP), plane, 3, 0))
            landed.append((swap(deep[half:], ACROSS), plane, 3, half))
            crossed = None
        if stage < 4:
            across, deep = swap(tiles, ACROSS), swap(tiles, DEEP)
            landed.append((across, stage, 1, 0))
            landed.append((deep, stage, 2, 0))
            crossed = (across, deep, stage)
        ahead = shift(tiles, 1) if stage < 3 else tiles
        extra = fillers[stage](done) if stage < len(fillers) else []
        values, landed_values, ahead, extra = together(
            [entry[0] for entry in moved], [entry[0] for entry in landed], ahead, extra
        )
        done = done + list(extra)
        for value, (_, plane, near, start) in zip(values, moved):
            arrivals.append(value)
            places.append((plane * 8 + near * 2 + 1, start, value.shape[0]))
        landed = [(value, *entry[1:]) for value, entry in zip(landed_values, landed)]
        if stage < 4:
            crossed = (landed_values[-2], landed_values[-1], stage)
        waiting = landed
        if stage < 3:
            tiles = ahead
            waiting = waiting + [(tiles, stage + 1, 0, 0)]
    return arrivals, places, done


def reduce_steps(near, far):
    chip = yield [near + swap(far, CORE)]
    first, second = yield list(plane_first(chip[0]))
    blocks = yield plane_second(first, second)
    for _ in range(3):
        blocks = yield ring_hop(blocks)
    return blocks[0]


class Flow:
    def __init__(self, spot, devices):
        self.spot, self.devices = spot, devices
        self.lines, self.waiting, self.sums = [], [], []

    def add(self, *parts):
        near, far = split_cores(self.spot, [part.reshape(self.devices, -1, TILE) for part in parts])
        self.lines.append(reduce_steps(near, far))
        self.waiting.append(next(self.lines[-1]))
        self.sums.append(None)

    def advance(self, *values):
        tied, values = together([moved for moved in self.waiting if moved is not None], list(values))
        tied = list(tied)
        for n, moved in enumerate(self.waiting):
            if moved is not None:
                try:
                    self.waiting[n] = self.lines[n].send(tied.pop(0))
                except StopIteration as stop:
                    self.waiting[n], self.sums[n] = None, stop.value
        return values


class PlainFlow:
    def __init__(self, devices):
        self.devices, self.sums = devices, []

    def add(self, *parts):
        whole = jnp.concatenate([part.reshape(self.devices, -1, TILE) for part in parts], axis=1)
        self.sums.append(lax.psum_scatter(whole, ("dp", "vocab"), scatter_dimension=0, tiled=False))

    def advance(self, *values):
        return values


def sent_low(value, bit):
    return swap(value.astype(jnp.bfloat16), bit).astype(jnp.float32)


def plane_first(value):
    value = value.reshape(4, 2, 2, value.shape[1], TILE)
    first, second = value[2:], value[:2]
    first = first[:, :, 0] + sent_low(first[:, :, 1], ACROSS)
    second = second[:, 0] + sent_low(second[:, 1], DEEP)
    return first, second


def plane_second(first, second):
    first = first[:, 0] + sent_low(first[:, 1], DEEP)
    second = second[:, 0] + sent_low(second[:, 1], ACROSS)
    return [second[0], second[1], first[0], first[1]]


def on_device(
    near,
    token_ids,
    lengths,
    mask_pos,
    mask_count,
    owner_order,
    step_count,
    teacher_flat,
    mentor_lexicon_weights,
    student_flat,
    flat_first,
    flat_second,
    student_embed,
    embed_first,
    embed_second,
):
    per = student_flat.shape[0]
    tiles_all = owner_order.shape[0]
    vocab_rows, width_share = student_embed.shape
    planes = lax.axis_size("dp")
    group = lax.axis_size("vocab")
    here = lax.axis_index("vocab")
    spot = jnp.stack([lax.axis_index("dp"), here]).astype(jnp.int32)
    devices = planes * group
    everywhere = ("dp", "vocab")
    device = lax.axis_index(everywhere)
    capacity = room(per, devices)
    slot_count = devices * capacity

    facts = jnp.concatenate([token_ids.reshape(LEN), lengths, mask_count, jnp.zeros((TILE - 2,), jnp.int32)])
    table_low = lax.all_gather(student_embed.T.astype(jnp.bfloat16), "dp", axis=0, tiled=True)

    homes = homes_of(owner_order, tiles_all, devices)
    one_of = jnp.arange(devices, dtype=jnp.int32)
    pairs = jnp.sum((homes.reshape(devices, per, 1) // per == one_of).astype(jnp.int32), axis=1)
    crowded = jnp.max(pairs) > capacity
    own_homes = lax.dynamic_slice_in_dim(homes, device * per, per)
    own_target = own_homes // per
    chosen_target = (own_target[:, None] == one_of).astype(jnp.bfloat16)
    lines = jnp.arange(per, dtype=jnp.int32)
    earlier = (lines[None] < lines[:, None]).astype(jnp.bfloat16)
    rank = jnp.sum(array_multiply(earlier, chosen_target) * chosen_target.astype(jnp.float32), axis=1)
    rank = rank.astype(jnp.int32)
    slots = jnp.where(rank < capacity, own_target * capacity + rank, slot_count)
    packed, home_line = send_tiles(slots, own_homes % per, student_flat, slot_count)
    packed = lax.all_to_all(packed.reshape(devices, capacity, TILE), everywhere, 0, 0)
    home_line = lax.all_to_all(home_line[:slot_count].reshape(devices, 1, capacity), everywhere, 0, 0)
    home_line = home_line.reshape(slot_count)
    home_tiles = land_tiles(home_line, packed.reshape(slot_count, TILE), per)

    def every_tile(tiles):
        stored = lax.all_gather(student_flat.astype(jnp.bfloat16), everywhere, axis=0, tiled=True)
        sources = jnp.zeros((tiles_all,), jnp.int32).at[homes].set(jnp.arange(tiles_all, dtype=jnp.int32))
        return stored[lax.dynamic_slice_in_dim(sources, device * per, per)]

    home_tiles = lax.cond(crowded, every_tile, lambda tiles: tiles, home_tiles)

    words = jnp.arange(vocab_rows, dtype=jnp.int32)

    def chosen(ids):
        return (ids.reshape(-1, 1) - here * vocab_rows == words[None]).astype(jnp.bfloat16)

    def rows_t(ids):
        return array_multiply(chosen(ids), mentor_lexicon_weights).astype(jnp.bfloat16)

    def rows_s(ids):
        return trailing_array_multiply(chosen(ids), table_low).astype(jnp.bfloat16)

    if near:
        plane_facts = gather_near(facts)
        shape = (2, 2, LEN, D)

        def ids(far):
            return plane_facts[4:, :LEN] if far else plane_facts[:4, :LEN]

        fillers = [
            lambda done: [],
            lambda done: [rows_t(ids(True)).reshape(shape)],
            lambda done: [rows_t(ids(False)).reshape(shape), swap(done[0], CORE)],
            lambda done: [done[1] + done[2], rows_s(ids(True)).reshape(shape)],
            lambda done: [rows_s(ids(False)).reshape(shape), swap(done[4], CORE)],
            lambda done: [done[5] + done[6], *plane_hop(done[3])],
        ]
        teacher_flat, plane_facts = together(teacher_flat, plane_facts)
        teacher_tiles = lax.all_gather(teacher_flat, everywhere, axis=0, tiled=True)
        arrivals, places, done = gather_layer(home_tiles, fillers)
        looked_s, looked_t = done[7], (done[8], done[9])
        looked_s = plane_hop(looked_s)
        matrices = assemble_layer(spot, arrivals, tuple(places), tiles_all, devices)
        matrices, looked_s, facts = together(matrices, looked_s, facts)
        other_facts = gather_near(jnp.stack([shift(facts, 1), shift(facts, 2), shift(facts, 3)]))
        all_facts = jnp.concatenate([plane_facts[:, None], other_facts], axis=1)
        looked_s = plane_end(*looked_s).astype(jnp.float32)
        looked_t = plane_end(*looked_t).astype(jnp.float32)
    else:
        by_plane = lax.all_gather(facts, "dp", axis=0)
        all_facts = lax.all_gather(by_plane, "vocab", axis=0)
        plane_facts = lax.dynamic_index_in_dim(all_facts, lax.axis_index("dp"), 1, keepdims=False)
        teacher_tiles = lax.all_gather(teacher_flat, everywhere, axis=0, tiled=True)
        layer = lax.all_gather(home_tiles, everywhere, axis=0)
        sizes, starts = shares_of(tiles_all, devices)
        matrices = [
            layer[:, start : start + size].reshape(across, height, TILE).transpose(1, 0, 2).reshape(height, -1)
            for (_, height, across), size, start in zip(HOME_ORDER, sizes, starts)
        ]
        matrices.append(layer[:, starts[-1] :].astype(jnp.float32))
        plane_ids = plane_facts[:, :LEN]
        looked_t, looked_s = (
            lax.psum_scatter(rows, "vocab", scatter_dimension=0, tiled=True).astype(jnp.float32)
            for rows in (rows_t(plane_ids), rows_s(plane_ids))
        )
    up, down, qkv, out, place = matrices[:5]
    student = pieces_of((qkv, out, up, down, place), matrices[5].reshape(-1, TILE))
    final_s, saved = layer_forward(student, looked_s, lengths)
    final_s, teacher_tiles, looked_t, all_facts = together(final_s, teacher_tiles, looked_t, all_facts)
    teacher = pieces_of(
        [unpack_matrix(teacher_tiles, piece) for piece in MATRICES],
        teacher_tiles[TAIL : TAIL + TAIL_TILES].astype(jnp.float32),
    )
    token_total = jnp.sum(all_facts[:, :, LEN]).astype(jnp.float32)
    masked_total = jnp.sum(all_facts[:, :, LEN + 1]).astype(jnp.float32)

    offsets = jnp.concatenate([mask_pos.reshape(CAP), jnp.zeros((SLOTS - CAP,), jnp.int32)])
    picked_s = final_s[offsets].astype(jnp.bfloat16)
    if near:
        learner_picked = gather_near(picked_s).reshape(-1, D)
    final_t = layer_forward(teacher, looked_t, lengths)[0]
    if near:
        final_t, learner_picked = together(final_t, learner_picked)

    picked_t = final_t[offsets].astype(jnp.bfloat16)
    if near:
        mentor_picked = gather_near(picked_t).reshape(-1, D)
    else:
        learner_picked = lax.all_gather(picked_s, "vocab", axis=0, tiled=True)
        mentor_picked = lax.all_gather(picked_t, "vocab", axis=0, tiled=True)
    live_weighting = (
        (jnp.arange(SLOTS)[None] < plane_facts[:, LEN + 1, None]).astype(jnp.float32).reshape(-1)
    )
    learner_energy = array_multiply(learner_picked, table_low) / smoothing_heat_scale
    teacher_logit = (
        trailing_array_multiply(mentor_picked, mentor_lexicon_weights) / smoothing_heat_scale
    )
    peak_s = jnp.max(learner_energy, axis=1)
    peak_t = jnp.max(teacher_logit, axis=1)
    teacher_exps = jnp.exp(teacher_logit - peak_t[:, None])
    stats = jnp.stack(
        [
            peak_s,
            jnp.sum(jnp.exp(learner_energy - peak_s[:, None]), axis=1),
            peak_t,
            jnp.sum(teacher_exps, axis=1),
            jnp.sum(teacher_exps * (teacher_logit - learner_energy), axis=1),
        ]
    )
    if near:
        stats = stats.reshape(5, 2, 2, 2, SLOTS)
        for axis, bit in ((1, CORE), (2, DEEP), (3, ACROSS)):
            stats = combine_stats(stats, jnp.flip(swap(stats, bit), axis))
        stats = stats.reshape(5, -1)
    else:
        everything = lax.all_gather(stats, "vocab", axis=0)
        stats = everything[0]
        for k in range(1, group):
            stats = combine_stats(stats, everything[k])
    logsum_s = stats[0] + jnp.log(stats[1])
    logsum_t = stats[2] + jnp.log(stats[3])
    diverge = stats[4] / stats[3] - logsum_t + logsum_s
    mine = 0 if near else here * SLOTS
    divergence_part = jnp.sum(lax.dynamic_slice_in_dim(diverge * live_weighting, mine, SLOTS))
    student_probs = jnp.exp(learner_energy - logsum_s[:, None])
    teacher_probs = jnp.exp(teacher_logit - logsum_t[:, None])
    grad_logit = (
        mixing_coefficient
        * smoothing_heat_scale
        / masked_total
        * live_weighting[:, None]
        * (student_probs - teacher_probs)
    ).astype(jnp.bfloat16)
    if near:
        half = grad_logit.shape[0] // 2
        far = trailing_array_multiply(grad_logit[half:], table_low).reshape(2, 2, SLOTS, D)
        close = trailing_array_multiply(grad_logit[:half], table_low).reshape(2, 2, SLOTS, D)
        grad_rows = plane_end(*plane_hop(close + swap(far, CORE)))
    else:
        grad_rows = lax.psum_scatter(
            trailing_array_multiply(grad_logit, table_low), "vocab", scatter_dimension=0, tiled=True
        )
    head_grad = matmul_left(learner_picked, grad_logit)
    head_grad, grad_rows = together(head_grad, grad_rows)
    head_part = lax.psum_scatter(head_grad, "dp", scatter_dimension=0, tiled=True)
    products = jnp.sum(final_s * final_t, axis=1)
    inverse_s = lax.rsqrt(jnp.sum(final_s * final_s, axis=1) + cosine_eps)
    inverse_t = lax.rsqrt(jnp.sum(final_t * final_t, axis=1) + cosine_eps)
    live_rows = (jnp.arange(LEN)[None, :] < lengths[:, None]).reshape(-1)
    cosine = products * inverse_s * inverse_t
    cosine_term = jnp.sum(jnp.where(live_rows, 1.0 - cosine, 0.0))
    weighting = jnp.where(live_rows, -cosine_weight / token_total, 0.0) * inverse_s * inverse_t
    grad_final = weighting[:, None] * (
        final_t - (products * inverse_s * inverse_s)[:, None] * final_s
    )
    grad_final = grad_final.at[offsets].add(grad_rows)
    flow = Flow(spot, devices) if near else PlainFlow(devices)
    grad_sum_one, grad_small, grad_upbias = feed_backward(student, saved, grad_final, flow)
    grad_embedded = attention_backward(
        student, saved, grad_sum_one, grad_small, grad_upbias, lengths, tiles_all - TAIL, flow
    )

    shares = grad_embedded.astype(jnp.bfloat16).reshape(LEN, planes, width_share).transpose(1, 0, 2)
    if near:
        own = upward(shares)
        shares = jnp.stack([own[0]] + [shift(own[k], k) for k in (1, 2, 3)])
        ids = all_facts[:, :, :LEN].reshape(2, 2, 2, planes, LEN)
        for axis, bit in ((0, CORE), (1, DEEP), (2, ACROSS)):
            ids = jnp.where((here & bit) != 0, jnp.flip(ids, axis), ids)
        ids = ids.transpose(1, 2, 0, 3, 4)
    else:
        shares = lax.all_to_all(shares, "dp", 0, 0)
        ids = all_facts[:, :, :LEN]
    token_grads = lax.all_gather(shares.reshape(-1, width_share), "vocab", axis=0, tiled=True)
    def token_sum(n):
        third = token_grads.shape[0] // 8 * 3
        begin, end = (n * third, (n + 1) * third) if n < 2 else (n * third, token_grads.shape[0])
        return matmul_left(token_grads[begin:end], chosen(ids.reshape(-1)[begin:end]))

    shares, head_part = flow.advance(shares, head_part)
    token_grads = lax.all_gather(shares.reshape(-1, width_share), "vocab", axis=0, tiled=True)
    flow.advance()
    flow.advance()
    (token_grads,) = flow.advance(token_grads)
    (token_part,) = flow.advance(token_sum(0))
    flow.advance()
    sum_down, sum_up, sum_rest = flow.sums
    home_grads = jnp.concatenate([sum_up, sum_down, sum_rest])
    returned = pick_tiles(jnp.minimum(home_line, per - 1), home_grads, slot_count)
    returned = lax.all_to_all(returned.reshape(devices, capacity, TILE), everywhere, 0, 0)
    flat_grad = pick_tiles(jnp.minimum(slots, slot_count - 1), returned.reshape(slot_count, TILE), per)
    flat_grad = lax.cond(
        crowded,
        lambda grads: lax.all_gather(home_grads, everywhere, axis=0, tiled=True)[own_homes],
        lambda grads: grads,
        flat_grad,
    )
    token_part = token_part + token_sum(1) + token_sum(2)
    table_grad = (head_part + token_part).T
    loss_term = (
        mixing_coefficient * smoothing_heat_scale**2 * divergence_part / masked_total
        + cosine_weight * cosine_term / token_total
    )
    squares = jnp.sum(flat_grad * flat_grad) + jnp.sum(table_grad * table_grad)
    if near:
        squares, loss_value = sum_everywhere(jnp.stack([squares, loss_term]))
    else:
        squares, loss_value = lax.psum((squares, loss_term), ("dp", "vocab"))
    grad_norm = jnp.sqrt(squares)
    factor = clip_norm / jnp.maximum(grad_norm, clip_norm)
    step_float = step_count[0].astype(jnp.float32)
    new_flat, new_flat_first, new_flat_second = adam_step(
        student_flat, flat_first, flat_second, flat_grad * factor, step_float
    )
    new_embed, new_embed_first, new_embed_second = adam_step(
        student_embed, embed_first, embed_second, table_grad * factor, step_float
    )
    return (
        loss_value,
        grad_norm,
        new_flat,
        new_flat_first,
        new_flat_second,
        new_embed,
        new_embed_first,
        new_embed_second,
    )


def solution(mesh):
    near = mesh.shape["dp"] == 4 and mesh.shape["vocab"] == 8
    return jax.shard_map(
        functools.partial(on_device, near),
        mesh=mesh,
        in_specs=(
            P(("dp", "vocab"), None),
            P(("dp", "vocab")),
            P(("dp", "vocab"), None),
            P(("dp", "vocab")),
            P(),
            P(),
            P(("dp", "vocab"), None),
            P("vocab", None),
            P(("dp", "vocab"), None),
            P(("dp", "vocab"), None),
            P(("dp", "vocab"), None),
            P("vocab", "dp"),
            P("vocab", "dp"),
            P("vocab", "dp"),
        ),
        out_specs=(
            P(),
            P(),
            P(("dp", "vocab"), None),
            P(("dp", "vocab"), None),
            P(("dp", "vocab"), None),
            P("vocab", "dp"),
            P("vocab", "dp"),
            P("vocab", "dp"),
        ),
        check_vma=False,
    )
```

```python
import functools

import jax
import jax.numpy as jnp
from jax import lax
from jax.experimental import pallas as pl
from jax.experimental.pallas import tpu as pltpu
from jax.sharding import PartitionSpec as P

D = 768
HEADS = 12
HEAD_DIM = 64
FF = 3072
LEN = 512
CAP = 120
SLOTS = 128
TILE = 128

QKV = (0, D, 18)
OUT = (13824, D, 6)
UP = (18432, D, 24)
DOWN = (36864, FF, 6)
PLACE = (55296, LEN, 6)
MATRICES = (QKV, OUT, UP, DOWN, PLACE)
TAIL = 58368
TAIL_TILES = 88
HOME_ORDER = (UP, DOWN, QKV, OUT, PLACE)

VMEM_LIMIT = 60 * 1024 * 1024

smoothing_heat_scale = 2.0
mixing_coefficient = 5.0
cosine_weight = 20.0
clip_norm = 0.01
beta_first = 0.9
beta_second = 0.98
adam_eps = 1e-08
weight_decay = 0.01
learn_rate = 0.1
norm_eps = 1e-12
cosine_eps = 1e-06

CHIPS = 16
SLABS = ((0, 48, 1, 12, 0), (48, 48, 4, 3, 0), (96, 48, 1, 9, 0), (96, 48, 1, 3, 9), (144, 16, 2, 3, 0))
SHARE = (160, 1536)
TAIL_AT = (144, 6)
CORE, ACROSS, DEEP = 1, 2, 4


def swap(value, bit):
    return lax.ppermute(value, "vocab", [(i, i ^ bit) for i in range(8)])


def shift(value, steps):
    size = lax.axis_size("dp")
    return lax.ppermute(value, "dp", [(i, (i + steps) % size) for i in range(size)])


def gather_near(value):
    value = value[None]
    for bit in (ACROSS, DEEP, CORE):
        value = jnp.concatenate([value, swap(value, bit)])
    return value


def plane_hop(value):
    half = value.shape[2] // 2
    upper, lower = value[:, :, :half], value[:, :, half:]
    return upper[:, 0] + swap(upper[:, 1], ACROSS), lower[0] + swap(lower[1], DEEP)


def plane_end(upper, lower):
    return jnp.concatenate([upper[0] + swap(upper[1], DEEP), lower[0] + swap(lower[1], ACROSS)])


def together(*values):
    return lax.optimization_barrier(values)


def ring_hop(blocks):
    moving = shift(blocks[-1], 1)
    return [*blocks[:-2], blocks[-2] + moving]


def sum_everywhere(value):
    for bit in (CORE, ACROSS, DEEP):
        value = value + swap(value, bit)
    for step in (1, 2):
        value = value + lax.ppermute(value, "dp", [(i, i ^ step) for i in range(4)])
    return value


def upward(table):
    z = lax.axis_index("dp")
    return [lax.dynamic_index_in_dim(table, (z + k) % 4, keepdims=False) for k in range(4)]


def shares_of(tiles_all, devices):
    sizes = [height * across // devices for _, height, across in HOME_ORDER]
    sizes.append((tiles_all - TAIL) // devices)
    starts = [sum(sizes[:n]) for n in range(len(sizes))]
    return sizes, starts


def homes_of(tiles, tiles_all, devices, near):
    per = tiles_all // devices
    sizes, starts = shares_of(tiles_all, devices)
    homes = ((tiles - TAIL) // sizes[-1]) * per + starts[-1] + (tiles - TAIL) % sizes[-1]
    for (first, height, across), size, start in zip(HOME_ORDER, sizes, starts):
        at = tiles - first
        inside = (at >= 0) & (at < height * across)
        if near:
            row, column = at // across, at % across
            slab, half = height // CHIPS, across // 2
            owner = row // slab * 2 + column // half
            line = column % half * slab + row % slab
        else:
            owner, line = at // size, at % size
        homes = jnp.where(inside, owner * per + start + line, homes)
    return homes


def room(per, devices):
    mean = per / devices
    return int(-(-(mean + 5.0 * mean**0.5) // 8) * 8)


def row_steps(total, size, step):
    whole, rest = divmod(total, size)

    def body(i, carry):
        step(i * size, size)
        return carry

    lax.fori_loop(0, whole, body, 0)
    if rest:
        step(whole * size, rest)


def send_kernel(slots, lines, tiles, packed, index, stage, *, per):
    slot_count = packed.shape[0]

    def clear(start, size):
        for u in range(size):
            index[start + u] = per

    row_steps(slot_count + 8, 64, clear)
    stage[...] = jnp.zeros_like(stage)

    def place(start, size):
        for u in range(size):
            slot = slots[start + u]
            stage[pl.ds(slot, 1), :] = tiles[pl.ds(start + u, 1), :]
            index[slot] = lines[start + u]

    row_steps(per, 64, place)
    packed[...] = stage[pl.ds(0, slot_count), :].astype(packed.dtype)


def send_tiles(slots, lines, tiles, slot_count):
    per = tiles.shape[0]
    return pl.pallas_call(
        functools.partial(send_kernel, per=per),
        in_specs=[pl.BlockSpec(memory_space=pltpu.SMEM)] * 2 + [pl.BlockSpec(memory_space=pltpu.VMEM)],
        out_specs=[pl.BlockSpec(memory_space=pltpu.VMEM), pl.BlockSpec(memory_space=pltpu.SMEM)],
        out_shape=[
            jax.ShapeDtypeStruct((slot_count, TILE), jnp.bfloat16),
            jax.ShapeDtypeStruct((slot_count + 8,), jnp.int32),
        ],
        scratch_shapes=[pltpu.VMEM((slot_count + 8, TILE), jnp.float32)],
        name="send_tiles",
    )(slots, lines, tiles)


def slab_pieces(starts):
    for (row, lines, groups, columns, offset), start in zip(SLABS, starts):
        for column in range(columns):
            for part in range(groups):
                yield row, offset + part * columns + column, lines, start + (column * groups + part) * lines


def land_kernel(index, packed, tiles, stage, full, *, starts):
    stage[...] = packed[...].astype(jnp.float32)

    def place(start, size):
        for u in range(size):
            full[pl.ds(index[start + u], 1), :] = stage[pl.ds(start + u, 1), :]

    row_steps(packed.shape[0], 128, place)
    if starts is None:
        tiles[...] = full[pl.ds(0, tiles.shape[0]), :].astype(tiles.dtype)
    else:
        tiles[...] = jnp.zeros_like(tiles)
        for row, column, lines, line in (*slab_pieces(starts), (*TAIL_AT, 16, starts[-1])):
            tiles[pl.ds(row, lines), column * TILE : (column + 1) * TILE] = full[pl.ds(line, lines), :].astype(
                tiles.dtype
            )


def land_tiles(index, packed, per, starts):
    slot_count = packed.shape[0]
    return pl.pallas_call(
        functools.partial(land_kernel, starts=starts),
        in_specs=[pl.BlockSpec(memory_space=pltpu.SMEM), pl.BlockSpec(memory_space=pltpu.VMEM)],
        out_specs=pl.BlockSpec(memory_space=pltpu.VMEM),
        out_shape=jax.ShapeDtypeStruct((per, TILE) if starts is None else SHARE, jnp.bfloat16),
        scratch_shapes=[pltpu.VMEM((slot_count, TILE), jnp.float32), pltpu.VMEM((per + 8, TILE), jnp.float32)],
        name="land_tiles",
    )(index, packed)


def share_lines_kernel(up, down, qkv, rest, lines, *, starts):
    slabs = (up, down, qkv, rest, rest)
    first = (0, 0, 0, 0, 48)
    for n, (source, (_, _, _, columns, _), begin, start) in enumerate(zip(slabs, SLABS, first, starts)):
        height = HOME_ORDER[n][1] // CHIPS
        for column in range(columns):
            lines[pl.ds(start + column * height, height), :] = source[
                pl.ds(begin, height), column * TILE : (column + 1) * TILE
            ]
    lines[pl.ds(starts[-1], 8), :] = rest[pl.ds(80, 8), :TILE]


def share_lines(up, down, qkv, rest, per, starts):
    return pl.pallas_call(
        functools.partial(share_lines_kernel, starts=starts),
        in_specs=[pl.BlockSpec(memory_space=pltpu.VMEM)] * 4,
        out_specs=pl.BlockSpec(memory_space=pltpu.VMEM),
        out_shape=jax.ShapeDtypeStruct((per, TILE), jnp.float32),
        name="share_lines",
    )(up, down, qkv, rest)


def pick_kernel(index, source, target, *, count):
    def pick(start, size):
        for u in range(size):
            target[pl.ds(start + u, 1), :] = source[pl.ds(index[start + u], 1), :]

    row_steps(count, 128, pick)


def pick_tiles(index, source, count):
    return pl.pallas_call(
        functools.partial(pick_kernel, count=count),
        in_specs=[pl.BlockSpec(memory_space=pltpu.SMEM), pl.BlockSpec(memory_space=pltpu.VMEM)],
        out_specs=pl.BlockSpec(memory_space=pltpu.VMEM),
        out_shape=jax.ShapeDtypeStruct((count, TILE), source.dtype),
        name="pick_tiles",
    )(index, source)


def assemble_kernel(spot, *refs, places):
    arrivals = refs[: len(places)]
    up, down, qkv, out, place, tail, landed, sems = refs[len(places) :]
    copies = []
    for n, (arrival, where) in enumerate(zip(arrivals, places)):
        target = landed.at[where[0], pl.ds(where[1], where[2])]
        copies.append(pltpu.make_async_copy(arrival, target, sems.at[n]))
    for copy in copies:
        copy.start()
    for copy in copies:
        copy.wait()

    def one_device(block, carry):
        owner = ((spot[0] + 4 - block // 8) % 4) * 8 + (spot[1] ^ (block % 8))
        chip, core = owner // 2, owner % 2

        def put(target, row, lines, width, source_row, source_column):
            target[
                pl.ds(pl.multiple_of(row, 16), lines), pl.ds(pl.multiple_of(core * width, TILE), width)
            ] = landed[block, pl.ds(source_row, lines), source_column : source_column + width]

        put(up, chip * 48, 48, 1536, 0, 0)
        for part in range(4):
            put(down, chip * 192 + part * 48, 48, 384, 48, part * 384)
        put(qkv, chip * 48, 48, 1152, 96, 0)
        put(out, chip * 48, 48, 384, 96, 1152)
        for part in range(2):
            put(place, chip * 32 + part * 16, 16, 384, 144, part * 384)
        tail[owner] = landed[block, pl.ds(TAIL_AT[0], 16), TAIL_AT[1] * TILE : (TAIL_AT[1] + 1) * TILE].astype(
            jnp.float32
        )[:8]
        return carry

    lax.fori_loop(0, landed.shape[0], one_device, 0)


def assemble_layer(spot, arrivals, places, devices):
    return pl.pallas_call(
        functools.partial(assemble_kernel, places=places),
        in_specs=[pl.BlockSpec(memory_space=pltpu.SMEM)] + [pl.BlockSpec(memory_space=pl.ANY)] * len(arrivals),
        out_specs=[pl.BlockSpec(memory_space=pltpu.VMEM)] * 6,
        out_shape=[jax.ShapeDtypeStruct((h, a * TILE), jnp.bfloat16) for _, h, a in HOME_ORDER]
        + [jax.ShapeDtypeStruct((devices, 8, TILE), jnp.float32)],
        scratch_shapes=[
            pltpu.VMEM((devices, *SHARE), jnp.bfloat16),
            pltpu.SemaphoreType.DMA((len(arrivals),)),
        ],
        compiler_params=pltpu.CompilerParams(vmem_limit_bytes=VMEM_LIMIT),
        cost_estimate=pl.CostEstimate(flops=0, bytes_accessed=60_000_000, transcendentals=0),
        name="assemble_layer",
    )(spot, *arrivals)


def unpack_kernel(source, target, stage, *, across):
    stage[...] = source[...].astype(jnp.float32)

    def step(g, carry):
        for column in range(across):
            lines = stage[pl.ds(g * 16 * across + column, 16, stride=across), :]
            target[pl.ds(pl.multiple_of(g * 16, 16), 16), column * TILE : (column + 1) * TILE] = lines.astype(
                jnp.bfloat16
            )
        return carry

    lax.fori_loop(0, target.shape[0] // 16, step, 0)


def unpack_matrix(tiles, piece):
    first, height, across = piece
    lines = min(height, 384 if across > 6 else 768)
    block = lines * across
    return pl.pallas_call(
        functools.partial(unpack_kernel, across=across),
        grid=(height // lines,),
        in_specs=[pl.BlockSpec((block, TILE), lambda i: (first // block + i, 0))],
        out_specs=pl.BlockSpec((lines, across * TILE), lambda i: (i, 0)),
        out_shape=jax.ShapeDtypeStruct((height, across * TILE), jnp.bfloat16),
        scratch_shapes=[pltpu.VMEM((block, TILE), jnp.float32)],
        name="unpack_matrix",
    )(tiles)


def array_multiply(left_side, right_side):
    return jnp.dot(left_side, right_side, preferred_element_type=jnp.float32)


def matmul_left(left_side, right_side):
    return lax.dot_general(
        left_side, right_side, (((0,), (0,)), ((), ())), preferred_element_type=jnp.float32
    )


def trailing_array_multiply(left_side, right_side):
    return lax.dot_general(
        left_side, right_side, (((1,), (1,)), ((), ())), preferred_element_type=jnp.float32
    )


def pieces_of(matrices, tail):
    qkv, out, up, down, place = matrices
    return {
        "qkv": qkv,
        "out": out,
        "up": up,
        "down": down,
        "place": place,
        "small": tail[:60].reshape(10, D),
        "upbias": tail[60:84].reshape(FF),
    }


def norm_forward(values, gain_row, shift_row):
    center = values - jnp.mean(values, axis=-1, keepdims=True)
    inverse = lax.rsqrt(jnp.mean(center * center, axis=-1, keepdims=True) + norm_eps)
    normed = center * inverse
    return (normed * gain_row + shift_row, normed, inverse)


def norm_backward(grad_out, normed, inverse, gain_row):
    scaled = grad_out * gain_row
    grad_in = inverse * (
        scaled
        - jnp.mean(scaled, axis=-1, keepdims=True)
        - normed * jnp.mean(scaled * normed, axis=-1, keepdims=True)
    )
    return (grad_in, jnp.sum(grad_out * normed, axis=0), jnp.sum(grad_out, axis=0))


def gelu_slope(values):
    return (
        0.5 * (1.0 + lax.erf(values * 0.7071067811865476))
        + values * jnp.exp(-0.5 * values * values) * 0.3989422804014327
    )


def key_scores(projected, lengths):
    seqs_count = lengths.shape[0]
    split_heads = projected.reshape(seqs_count, LEN, 3, HEADS, HEAD_DIM)
    scores = jnp.einsum(
        "sqhd,skhd->shqk",
        split_heads[:, :, 0],
        split_heads[:, :, 1],
        preferred_element_type=jnp.float32,
    ) * HEAD_DIM ** (-0.5)
    live_keys = jnp.arange(LEN)[None, :] < lengths[:, None]
    return (jnp.where(live_keys[:, None, None, :], scores, -1000000000.0), split_heads)


def layer_forward(pieces, looked, lengths):
    small_rows = pieces["small"].astype(jnp.float32)
    seqs_count = lengths.shape[0]
    rows_here = seqs_count * LEN
    summed = (
        looked.reshape(seqs_count, LEN, D) + pieces["place"].astype(jnp.float32)[None]
    ).reshape(rows_here, D)
    first_norm, normed_zero, inverse_zero = norm_forward(summed, small_rows[4], small_rows[5])
    inputs = first_norm.astype(jnp.bfloat16)
    qkv_bias = jnp.concatenate([small_rows[0], jnp.zeros((D,), jnp.float32), small_rows[1]])
    projected = (array_multiply(inputs, pieces["qkv"]) + qkv_bias).astype(jnp.bfloat16)
    scores, split_heads = key_scores(projected, lengths)
    peak = jnp.max(scores, axis=-1, keepdims=True)
    exps = jnp.exp(scores - peak)
    totals = jnp.sum(exps, axis=-1, keepdims=True)
    probabilities = (exps / totals).astype(jnp.bfloat16)
    logsum = peak + jnp.log(totals)
    context = jnp.einsum(
        "shqk,skhd->sqhd", probabilities, split_heads[:, :, 2], preferred_element_type=jnp.float32
    )
    context = context.reshape(rows_here, D).astype(jnp.bfloat16)
    attended = array_multiply(context, pieces["out"]) + small_rows[2]
    middle, normed_one, inverse_one = norm_forward(
        first_norm + attended, small_rows[6], small_rows[7]
    )
    middle_low = middle.astype(jnp.bfloat16)
    hidden = array_multiply(middle_low, pieces["up"]) + pieces["upbias"].astype(jnp.float32)
    activated = jax.nn.gelu(hidden, approximate=False).astype(jnp.bfloat16)
    output = array_multiply(activated, pieces["down"]) + small_rows[3]
    final_lines, normed_two, inverse_two = norm_forward(
        middle + output, small_rows[8], small_rows[9]
    )
    saved = {
        "inputs": inputs,
        "projected": projected,
        "logsum": logsum,
        "context": context,
        "middle_low": middle_low,
        "hidden": hidden,
        "activated": activated,
        "normed_zero": normed_zero,
        "inverse_zero": inverse_zero,
        "normed_one": normed_one,
        "inverse_one": inverse_one,
        "normed_two": normed_two,
        "inverse_two": inverse_two,
    }
    return (final_lines, saved)


def feed_backward(pieces, saved, grad_final, flow):
    small_rows = pieces["small"]
    grad_sum_two, grad_gain_two, grad_shift_two = norm_backward(
        grad_final, saved["normed_two"], saved["inverse_two"], small_rows[8]
    )
    grad_out = grad_sum_two.astype(jnp.bfloat16)
    flow.add_product(saved["activated"], grad_out)
    grad_act = trailing_array_multiply(grad_out, pieces["down"])
    grad_hidden = (grad_act * gelu_slope(saved["hidden"])).astype(jnp.bfloat16)
    (grad_hidden,) = flow.advance(grad_hidden)
    flow.add_product(saved["middle_low"], grad_hidden)
    grad_middle = grad_sum_two + trailing_array_multiply(grad_hidden, pieces["up"])
    grad_sum_one, grad_gain_one, grad_shift_one = norm_backward(
        grad_middle, saved["normed_one"], saved["inverse_one"], small_rows[6]
    )
    grad_upbias = jnp.sum(grad_hidden.astype(jnp.float32), axis=0)
    (grad_sum_one,) = flow.advance(grad_sum_one)
    return (
        grad_sum_one,
        [jnp.sum(grad_out.astype(jnp.float32), axis=0), grad_gain_one, grad_shift_one, grad_gain_two, grad_shift_two],
        grad_upbias,
    )


def attention_backward(pieces, saved, grad_sum_one, grad_small, grad_upbias, lengths, tail_rows, flow):
    small_rows = pieces["small"]
    seqs_count = lengths.shape[0]
    rows_here = seqs_count * LEN
    grad_att = grad_sum_one.astype(jnp.bfloat16)
    grad_outw = matmul_left(saved["context"], grad_att)
    grad_context = (
        trailing_array_multiply(grad_att, pieces["out"])
        .astype(jnp.bfloat16)
        .reshape(seqs_count, LEN, HEADS, HEAD_DIM)
    )
    scores, split_heads = key_scores(saved["projected"], lengths)
    probabilities = jnp.exp(scores - saved["logsum"])
    grad_probs = jnp.einsum(
        "sqhd,skhd->shqk", grad_context, split_heads[:, :, 2], preferred_element_type=jnp.float32
    )
    grad_values = jnp.einsum(
        "shqk,sqhd->skhd",
        probabilities.astype(jnp.bfloat16),
        grad_context,
        preferred_element_type=jnp.float32,
    )
    grad_values, grad_probs = flow.advance(grad_values, grad_probs)
    grad_scores = probabilities * (
        grad_probs - jnp.sum(grad_probs * probabilities, axis=-1, keepdims=True)
    )
    (grad_scores,) = flow.advance(grad_scores.astype(jnp.bfloat16))
    grad_queries = jnp.einsum(
        "shqk,skhd->sqhd", grad_scores, split_heads[:, :, 1], preferred_element_type=jnp.float32
    ) * HEAD_DIM ** (-0.5)
    grad_keys = jnp.einsum(
        "shqk,sqhd->skhd", grad_scores, split_heads[:, :, 0], preferred_element_type=jnp.float32
    ) * HEAD_DIM ** (-0.5)
    grad_proj = (
        jnp.stack([grad_queries, grad_keys, grad_values], axis=2)
        .reshape(rows_here, 3 * D)
        .astype(jnp.bfloat16)
    )
    (grad_proj,) = flow.advance(grad_proj)
    flow.add_product(saved["inputs"], grad_proj)
    grad_bias_all = jnp.sum(grad_proj.astype(jnp.float32), axis=0)
    grad_first = grad_sum_one + trailing_array_multiply(grad_proj, pieces["qkv"])
    grad_embedded, grad_gain_zero, grad_shift_zero = norm_backward(
        grad_first, saved["normed_zero"], saved["inverse_zero"], small_rows[4]
    )
    grad_place = jnp.sum(grad_embedded.reshape(seqs_count, LEN, D), axis=0)
    grad_small = jnp.stack(
        [
            grad_bias_all[:D],
            grad_bias_all[2 * D :],
            jnp.sum(grad_att.astype(jnp.float32), axis=0),
            grad_small[0],
            grad_gain_zero,
            grad_shift_zero,
            *grad_small[1:],
        ]
    )
    tail = jnp.concatenate(
        [
            grad_small.reshape(60, TILE),
            grad_upbias.reshape(24, TILE),
            jnp.zeros((tail_rows - 84, TILE), jnp.float32),
        ]
    )
    (grad_embedded,) = flow.advance(grad_embedded)
    flow.add_rest(grad_outw, grad_place, tail)
    return grad_embedded


def combine_stats(earlier, later):
    peak_s = jnp.maximum(earlier[0], later[0])
    peak_t = jnp.maximum(earlier[2], later[2])
    factor_early = jnp.exp(earlier[0] - peak_s)
    factor_late = jnp.exp(later[0] - peak_s)
    teacher_early = jnp.exp(earlier[2] - peak_t)
    teacher_late = jnp.exp(later[2] - peak_t)
    return jnp.stack(
        [
            peak_s,
            earlier[1] * factor_early + later[1] * factor_late,
            peak_t,
            earlier[3] * teacher_early + later[3] * teacher_late,
            earlier[4] * teacher_early + later[4] * teacher_late,
        ]
    )


def adam_step(weight, first_moment, second, gradient, step_float):
    new_first = beta_first * first_moment + (1.0 - beta_first) * gradient
    new_second = beta_second * second + (1.0 - beta_second) * gradient * gradient
    fix_first = 1.0 - jnp.power(beta_first, step_float)
    fix_second = 1.0 - jnp.power(beta_second, step_float)
    update = new_first / fix_first / (jnp.sqrt(new_second / fix_second) + adam_eps)
    return (weight - learn_rate * (update + weight_decay * weight), new_first, new_second)


def gather_layer(tiles, fillers):
    per = tiles.shape[0]
    half = per // 16 * 8
    arrivals, places = [], []
    waiting = [(tiles, 0, 0, 0)]
    crossed = None
    done = []
    for stage in range(6):
        moved = []
        for value, plane, near, start in waiting:
            arrivals.append(value)
            places.append((plane * 8 + near * 2, start, value.shape[0]))
            moved.append((swap(value, CORE), plane, near, start))
        landed = []
        if crossed is not None:
            across, deep, plane = crossed
            landed.append((swap(across[:half], DEEP), plane, 3, 0))
            landed.append((swap(deep[half:], ACROSS), plane, 3, half))
            crossed = None
        if stage < 4:
            across, deep = swap(tiles, ACROSS), swap(tiles, DEEP)
            landed.append((across, stage, 1, 0))
            landed.append((deep, stage, 2, 0))
            crossed = (across, deep, stage)
        ahead = shift(tiles, 1) if stage < 3 else tiles
        extra = fillers[stage](done) if stage < len(fillers) else []
        values, landed_values, ahead, extra = together(
            [entry[0] for entry in moved], [entry[0] for entry in landed], ahead, extra
        )
        done = done + list(extra)
        for value, (_, plane, near, start) in zip(values, moved):
            arrivals.append(value)
            places.append((plane * 8 + near * 2 + 1, start, value.shape[0]))
        landed = [(value, *entry[1:]) for value, entry in zip(landed_values, landed)]
        if stage < 4:
            crossed = (landed_values[-2], landed_values[-1], stage)
        waiting = landed
        if stage < 3:
            tiles = ahead
            waiting = waiting + [(tiles, stage + 1, 0, 0)]
    return arrivals, places, done


def at(value, index, axis):
    return lax.dynamic_index_in_dim(value, index, axis, keepdims=False)


def sent_low(value, bit):
    return swap(value.astype(jnp.bfloat16), bit).astype(jnp.float32)


def bit_of(bit):
    return lax.axis_index("vocab") // bit % 2


def halved(value, axis, bit):
    mine = bit_of(bit)
    return at(value, mine, axis) + sent_low(at(value, 1 - mine, axis), bit)


def reduce_steps(near, far):
    (chip,) = yield [near + swap(far, CORE)]
    chip = chip.reshape(4, 2, 2, chip.shape[0] // CHIPS, chip.shape[1])
    first, second = yield [halved(chip[:2], 2, ACROSS), halved(chip[2:], 1, DEEP)]
    first, second = yield [halved(first, 1, DEEP), halved(second, 1, ACROSS)]
    z = lax.axis_index("dp")
    blocks = [
        jnp.where((z + k) % 4 < 2, at(first, (z + k) % 2, 0), at(second, (z + k) % 2, 0)) for k in range(4)
    ]
    for _ in range(3):
        blocks = yield ring_hop(blocks)
    return blocks[0]


class Flow:
    def __init__(self):
        self.lines, self.waiting, self.sums = [], [], []

    def add(self, near, far):
        self.lines.append(reduce_steps(near, far))
        self.waiting.append(next(self.lines[-1]))
        self.sums.append(None)

    def add_product(self, left, right):
        width = right.shape[1] // 2
        core = bit_of(CORE)
        far = matmul_left(left, lax.dynamic_slice_in_dim(right, (1 - core) * width, width, 1))
        near = matmul_left(left, lax.dynamic_slice_in_dim(right, core * width, width, 1))
        self.add(near, far)

    def add_rest(self, out, place, tail):
        def half(core):
            columns = [
                lax.dynamic_slice_in_dim(whole, core * 384, 384, 1).reshape(CHIPS, -1, 384) for whole in (out, place)
            ]
            ends = jnp.pad(at(tail.reshape(CHIPS, 2, 8, TILE), core, 1), ((0, 0), (0, 0), (0, 256)))
            return jnp.concatenate([*columns, ends], axis=1).reshape(-1, 384)

        self.add(half(bit_of(CORE)), half(1 - bit_of(CORE)))

    def advance(self, *values):
        tied, values = together([moved for moved in self.waiting if moved is not None], list(values))
        tied = list(tied)
        for n, moved in enumerate(self.waiting):
            if moved is not None:
                try:
                    self.waiting[n] = self.lines[n].send(tied.pop(0))
                except StopIteration as stop:
                    self.waiting[n], self.sums[n] = None, stop.value
        return values


class PlainFlow:
    def __init__(self, devices):
        self.devices, self.sums = devices, []

    def add_product(self, left, right):
        parts = matmul_left(left, right).reshape(self.devices, -1, TILE)
        self.sums.append(lax.psum_scatter(parts, ("dp", "vocab"), scatter_dimension=0, tiled=False))

    def add_rest(self, out, place, tail):
        parts = [part.reshape(self.devices, -1, TILE) for part in (out, place, tail)]
        parts = jnp.concatenate(parts, axis=1)
        self.sums.append(lax.psum_scatter(parts, ("dp", "vocab"), scatter_dimension=0, tiled=False))

    def advance(self, *values):
        return values


def on_device(
    near,
    token_ids,
    lengths,
    mask_pos,
    mask_count,
    owner_order,
    step_count,
    teacher_flat,
    mentor_lexicon_weights,
    student_flat,
    flat_first,
    flat_second,
    student_embed,
    embed_first,
    embed_second,
):
    per = student_flat.shape[0]
    tiles_all = owner_order.shape[0]
    vocab_rows, width_share = student_embed.shape
    planes = lax.axis_size("dp")
    group = lax.axis_size("vocab")
    here = lax.axis_index("vocab")
    spot = jnp.stack([lax.axis_index("dp"), here]).astype(jnp.int32)
    devices = planes * group
    everywhere = ("dp", "vocab")
    device = lax.axis_index(everywhere)
    capacity = room(per, devices)
    slot_count = devices * capacity

    facts = jnp.concatenate([token_ids.reshape(LEN), lengths, mask_count, jnp.zeros((TILE - 2,), jnp.int32)])
    table_low = lax.all_gather(student_embed.T.astype(jnp.bfloat16), "dp", axis=0, tiled=True)

    homes = homes_of(owner_order, tiles_all, devices, near)
    sizes, starts = shares_of(tiles_all, devices)
    one_of = jnp.arange(devices, dtype=jnp.int32)
    pairs = jnp.sum((homes.reshape(devices, per, 1) // per == one_of).astype(jnp.int32), axis=1)
    crowded = jnp.max(pairs) > capacity
    own_homes = lax.dynamic_slice_in_dim(homes, device * per, per)
    own_target = own_homes // per
    chosen_target = (own_target[:, None] == one_of).astype(jnp.bfloat16)
    lines = jnp.arange(per, dtype=jnp.int32)
    earlier = (lines[None] < lines[:, None]).astype(jnp.bfloat16)
    rank = jnp.sum(array_multiply(earlier, chosen_target) * chosen_target.astype(jnp.float32), axis=1)
    rank = rank.astype(jnp.int32)
    slots = jnp.where(rank < capacity, own_target * capacity + rank, slot_count)
    packed, home_line = send_tiles(slots, own_homes % per, student_flat, slot_count)
    packed = lax.all_to_all(packed.reshape(devices, capacity, TILE), everywhere, 0, 0)
    home_line = lax.all_to_all(home_line[:slot_count].reshape(devices, 1, capacity), everywhere, 0, 0)
    home_line = home_line.reshape(slot_count)
    home_tiles = land_tiles(home_line, packed.reshape(slot_count, TILE), per, starts if near else None)
    home_tiles, table_low = together(home_tiles, table_low)

    def every_tile(tiles):
        stored = lax.all_gather(student_flat.astype(jnp.bfloat16), everywhere, axis=0, tiled=True)
        sources = jnp.zeros((tiles_all,), jnp.int32).at[homes].set(jnp.arange(tiles_all, dtype=jnp.int32))
        stored = stored[lax.dynamic_slice_in_dim(sources, device * per, per)]
        if near:
            return land_tiles(lines, stored, per, starts)
        return stored

    home_tiles = lax.cond(crowded, every_tile, lambda tiles: tiles, home_tiles)

    words = jnp.arange(vocab_rows, dtype=jnp.int32)

    def chosen(ids):
        return (ids.reshape(-1, 1) - here * vocab_rows == words[None]).astype(jnp.bfloat16)

    def rows_t(ids):
        return array_multiply(chosen(ids), mentor_lexicon_weights).astype(jnp.bfloat16)

    def rows_s(ids):
        return trailing_array_multiply(chosen(ids), table_low).astype(jnp.bfloat16)

    if near:
        plane_facts = gather_near(facts)
        shape = (2, 2, LEN, D)

        def ids(far):
            return plane_facts[4:, :LEN] if far else plane_facts[:4, :LEN]

        fillers = [
            lambda done: [],
            lambda done: [rows_t(ids(True)).reshape(shape)],
            lambda done: [rows_t(ids(False)).reshape(shape), swap(done[0], CORE)],
            lambda done: [done[1] + done[2], rows_s(ids(True)).reshape(shape)],
            lambda done: [rows_s(ids(False)).reshape(shape), swap(done[4], CORE)],
            lambda done: [done[5] + done[6], *plane_hop(done[3])],
        ]
        teacher_flat, plane_facts = together(teacher_flat, plane_facts)
        teacher_tiles = lax.all_gather(teacher_flat, everywhere, axis=0, tiled=True)
        arrivals, places, done = gather_layer(home_tiles, fillers)
        looked_s, looked_t = done[7], (done[8], done[9])
        looked_s = plane_hop(looked_s)
        matrices = assemble_layer(spot, arrivals, tuple(places), devices)
        matrices, looked_s, facts = together(matrices, looked_s, facts)
        other_facts = gather_near(jnp.stack([shift(facts, 1), shift(facts, 2), shift(facts, 3)]))
        all_facts = jnp.concatenate([plane_facts[:, None], other_facts], axis=1)
        looked_s = plane_end(*looked_s).astype(jnp.float32)
        looked_t = plane_end(*looked_t).astype(jnp.float32)
    else:
        by_plane = lax.all_gather(facts, "dp", axis=0)
        all_facts = lax.all_gather(by_plane, "vocab", axis=0)
        plane_facts = lax.dynamic_index_in_dim(all_facts, lax.axis_index("dp"), 1, keepdims=False)
        teacher_tiles = lax.all_gather(teacher_flat, everywhere, axis=0, tiled=True)
        layer = lax.all_gather(home_tiles, everywhere, axis=0)
        matrices = [
            layer[:, start : start + size].reshape(height, across * TILE)
            for (_, height, across), size, start in zip(HOME_ORDER, sizes, starts)
        ]
        matrices.append(layer[:, starts[-1] :].astype(jnp.float32))
        plane_ids = plane_facts[:, :LEN]
        looked_t, looked_s = (
            lax.psum_scatter(rows, "vocab", scatter_dimension=0, tiled=True).astype(jnp.float32)
            for rows in (rows_t(plane_ids), rows_s(plane_ids))
        )
    up, down, qkv, out, place = matrices[:5]
    student = pieces_of((qkv, out, up, down, place), matrices[5].reshape(-1, TILE))
    final_s, saved = layer_forward(student, looked_s, lengths)
    final_s, teacher_tiles, looked_t, all_facts = together(final_s, teacher_tiles, looked_t, all_facts)
    teacher = pieces_of(
        [unpack_matrix(teacher_tiles, piece) for piece in MATRICES],
        teacher_tiles[TAIL : TAIL + TAIL_TILES].astype(jnp.float32),
    )
    token_total = jnp.sum(all_facts[:, :, LEN]).astype(jnp.float32)
    masked_total = jnp.sum(all_facts[:, :, LEN + 1]).astype(jnp.float32)

    offsets = jnp.concatenate([mask_pos.reshape(CAP), jnp.zeros((SLOTS - CAP,), jnp.int32)])
    picked_s = final_s[offsets].astype(jnp.bfloat16)
    if near:
        learner_picked = gather_near(picked_s).reshape(-1, D)
    final_t = layer_forward(teacher, looked_t, lengths)[0]
    if near:
        final_t, learner_picked = together(final_t, learner_picked)

    picked_t = final_t[offsets].astype(jnp.bfloat16)
    if near:
        mentor_picked = gather_near(picked_t).reshape(-1, D)
    else:
        learner_picked = lax.all_gather(picked_s, "vocab", axis=0, tiled=True)
        mentor_picked = lax.all_gather(picked_t, "vocab", axis=0, tiled=True)
    live_weighting = (
        (jnp.arange(SLOTS)[None] < plane_facts[:, LEN + 1, None]).astype(jnp.float32).reshape(-1)
    )
    learner_energy = array_multiply(learner_picked, table_low) / smoothing_heat_scale
    teacher_logit = (
        trailing_array_multiply(mentor_picked, mentor_lexicon_weights) / smoothing_heat_scale
    )
    peak_s = jnp.max(learner_energy, axis=1)
    peak_t = jnp.max(teacher_logit, axis=1)
    teacher_exps = jnp.exp(teacher_logit - peak_t[:, None])
    stats = jnp.stack(
        [
            peak_s,
            jnp.sum(jnp.exp(learner_energy - peak_s[:, None]), axis=1),
            peak_t,
            jnp.sum(teacher_exps, axis=1),
            jnp.sum(teacher_exps * (teacher_logit - learner_energy), axis=1),
        ]
    )
    if near:
        stats = stats.reshape(5, 2, 2, 2, SLOTS)
        for axis, bit in ((1, CORE), (2, DEEP), (3, ACROSS)):
            stats = combine_stats(stats, jnp.flip(swap(stats, bit), axis))
        stats = stats.reshape(5, -1)
    else:
        everything = lax.all_gather(stats, "vocab", axis=0)
        stats = everything[0]
        for k in range(1, group):
            stats = combine_stats(stats, everything[k])
    logsum_s = stats[0] + jnp.log(stats[1])
    logsum_t = stats[2] + jnp.log(stats[3])
    diverge = stats[4] / stats[3] - logsum_t + logsum_s
    mine = 0 if near else here * SLOTS
    divergence_part = jnp.sum(lax.dynamic_slice_in_dim(diverge * live_weighting, mine, SLOTS))
    student_probs = jnp.exp(learner_energy - logsum_s[:, None])
    teacher_probs = jnp.exp(teacher_logit - logsum_t[:, None])
    grad_logit = (
        mixing_coefficient
        * smoothing_heat_scale
        / masked_total
        * live_weighting[:, None]
        * (student_probs - teacher_probs)
    ).astype(jnp.bfloat16)
    if near:
        half = grad_logit.shape[0] // 2
        far = trailing_array_multiply(grad_logit[half:], table_low).reshape(2, 2, SLOTS, D)
        close = trailing_array_multiply(grad_logit[:half], table_low).reshape(2, 2, SLOTS, D)
        grad_rows = plane_end(*plane_hop(close + swap(far, CORE)))
    else:
        grad_rows = lax.psum_scatter(
            trailing_array_multiply(grad_logit, table_low), "vocab", scatter_dimension=0, tiled=True
        )
    head_grad = matmul_left(learner_picked, grad_logit)
    head_grad, grad_rows = together(head_grad, grad_rows)
    head_part = lax.psum_scatter(head_grad, "dp", scatter_dimension=0, tiled=True)
    products = jnp.sum(final_s * final_t, axis=1)
    inverse_s = lax.rsqrt(jnp.sum(final_s * final_s, axis=1) + cosine_eps)
    inverse_t = lax.rsqrt(jnp.sum(final_t * final_t, axis=1) + cosine_eps)
    live_rows = (jnp.arange(LEN)[None, :] < lengths[:, None]).reshape(-1)
    cosine = products * inverse_s * inverse_t
    cosine_term = jnp.sum(jnp.where(live_rows, 1.0 - cosine, 0.0))
    weighting = jnp.where(live_rows, -cosine_weight / token_total, 0.0) * inverse_s * inverse_t
    grad_final = weighting[:, None] * (
        final_t - (products * inverse_s * inverse_s)[:, None] * final_s
    )
    grad_final = grad_final.at[offsets].add(grad_rows)
    flow = Flow() if near else PlainFlow(devices)
    grad_sum_one, grad_small, grad_upbias = feed_backward(student, saved, grad_final, flow)
    grad_embedded = attention_backward(
        student, saved, grad_sum_one, grad_small, grad_upbias, lengths, tiles_all - TAIL, flow
    )

    shares = grad_embedded.astype(jnp.bfloat16).reshape(LEN, planes, width_share).transpose(1, 0, 2)
    if near:
        own = upward(shares)
        shares = jnp.stack([own[0]] + [shift(own[k], k) for k in (1, 2, 3)])
        ids = all_facts[:, :, :LEN].reshape(2, 2, 2, planes, LEN)
        for axis, bit in ((0, CORE), (1, DEEP), (2, ACROSS)):
            ids = jnp.where((here & bit) != 0, jnp.flip(ids, axis), ids)
        ids = ids.transpose(1, 2, 0, 3, 4)
    else:
        shares = lax.all_to_all(shares, "dp", 0, 0)
        ids = all_facts[:, :, :LEN]
    token_grads = lax.all_gather(shares.reshape(-1, width_share), "vocab", axis=0, tiled=True)
    def token_sum(n):
        third = token_grads.shape[0] // 8 * 3
        begin, end = (n * third, (n + 1) * third) if n < 2 else (n * third, token_grads.shape[0])
        return matmul_left(token_grads[begin:end], chosen(ids.reshape(-1)[begin:end]))

    shares, head_part = flow.advance(shares, head_part)
    token_grads = lax.all_gather(shares.reshape(-1, width_share), "vocab", axis=0, tiled=True)
    flow.advance()
    flow.advance()
    (token_grads,) = flow.advance(token_grads)
    (token_part,) = flow.advance(token_sum(0))
    flow.advance()
    sum_down, sum_up, sum_qkv, sum_rest = flow.sums
    if near:
        home_grads = share_lines(sum_up, sum_down, sum_qkv, sum_rest, per, starts)
    else:
        home_grads = jnp.concatenate([sum_up, sum_down, sum_qkv, sum_rest])
    returned = pick_tiles(jnp.minimum(home_line, per - 1), home_grads, slot_count)
    returned = lax.all_to_all(returned.reshape(devices, capacity, TILE), everywhere, 0, 0)
    flat_grad = pick_tiles(jnp.minimum(slots, slot_count - 1), returned.reshape(slot_count, TILE), per)
    flat_grad = lax.cond(
        crowded,
        lambda grads: lax.all_gather(home_grads, everywhere, axis=0, tiled=True)[own_homes],
        lambda grads: grads,
        flat_grad,
    )
    token_part = token_part + token_sum(1) + token_sum(2)
    table_grad = (head_part + token_part).T
    loss_term = (
        mixing_coefficient * smoothing_heat_scale**2 * divergence_part / masked_total
        + cosine_weight * cosine_term / token_total
    )
    squares = jnp.sum(flat_grad * flat_grad) + jnp.sum(table_grad * table_grad)
    if near:
        squares, loss_value = sum_everywhere(jnp.stack([squares, loss_term]))
    else:
        squares, loss_value = lax.psum((squares, loss_term), ("dp", "vocab"))
    grad_norm = jnp.sqrt(squares)
    factor = clip_norm / jnp.maximum(grad_norm, clip_norm)
    step_float = step_count[0].astype(jnp.float32)
    new_flat, new_flat_first, new_flat_second = adam_step(
        student_flat, flat_first, flat_second, flat_grad * factor, step_float
    )
    new_embed, new_embed_first, new_embed_second = adam_step(
        student_embed, embed_first, embed_second, table_grad * factor, step_float
    )
    return (
        loss_value,
        grad_norm,
        new_flat,
        new_flat_first,
        new_flat_second,
        new_embed,
        new_embed_first,
        new_embed_second,
    )


def solution(mesh):
    near = mesh.shape["dp"] == 4 and mesh.shape["vocab"] == 8
    return jax.shard_map(
        functools.partial(on_device, near),
        mesh=mesh,
        in_specs=(
            P(("dp", "vocab"), None),
            P(("dp", "vocab")),
            P(("dp", "vocab"), None),
            P(("dp", "vocab")),
            P(),
            P(),
            P(("dp", "vocab"), None),
            P("vocab", None),
            P(("dp", "vocab"), None),
            P(("dp", "vocab"), None),
            P(("dp", "vocab"), None),
            P("vocab", "dp"),
            P("vocab", "dp"),
            P("vocab", "dp"),
        ),
        out_specs=(
            P(),
            P(),
            P(("dp", "vocab"), None),
            P(("dp", "vocab"), None),
            P(("dp", "vocab"), None),
            P("vocab", "dp"),
            P("vocab", "dp"),
            P("vocab", "dp"),
        ),
        check_vma=False,
    )
```

```python
import functools

import jax
import jax.numpy as jnp
from jax import lax
from jax.experimental import pallas as pl
from jax.experimental.pallas import tpu as pltpu
from jax.sharding import PartitionSpec as P

D = 768
HEADS = 12
HEAD_DIM = 64
FF = 3072
LEN = 512
CAP = 120
SLOTS = 128
TILE = 128

QKV = (0, D, 18)
OUT = (13824, D, 6)
UP = (18432, D, 24)
DOWN = (36864, FF, 6)
PLACE = (55296, LEN, 6)
MATRICES = (QKV, OUT, UP, DOWN, PLACE)
TAIL = 58368
TAIL_TILES = 88
HOME_ORDER = (UP, DOWN, QKV, OUT, PLACE)

VMEM_LIMIT = 60 * 1024 * 1024

smoothing_heat_scale = 2.0
mixing_coefficient = 5.0
cosine_weight = 20.0
clip_norm = 0.01
beta_first = 0.9
beta_second = 0.98
adam_eps = 1e-08
weight_decay = 0.01
learn_rate = 0.1
norm_eps = 1e-12
cosine_eps = 1e-06

CHIPS = 16
SLABS = ((0, 48, 1, 12, 0), (48, 48, 4, 3, 0), (96, 48, 1, 9, 0), (96, 48, 1, 3, 9), (144, 16, 2, 3, 0))
SHARE = (160, 1536)
TAIL_AT = (144, 6)
CORE, ACROSS, DEEP = 1, 2, 4


def swap(value, bit):
    return lax.ppermute(value, "vocab", [(i, i ^ bit) for i in range(8)])


def shift(value, steps):
    size = lax.axis_size("dp")
    return lax.ppermute(value, "dp", [(i, (i + steps) % size) for i in range(size)])


def gather_near(value):
    value = value[None]
    for bit in (ACROSS, DEEP, CORE):
        value = jnp.concatenate([value, swap(value, bit)])
    return value


def plane_hop(value):
    half = value.shape[2] // 2
    upper, lower = value[:, :, :half], value[:, :, half:]
    return upper[:, 0] + swap(upper[:, 1], ACROSS), lower[0] + swap(lower[1], DEEP)


def plane_end(upper, lower):
    return jnp.concatenate([upper[0] + swap(upper[1], DEEP), lower[0] + swap(lower[1], ACROSS)])


def together(*values):
    return lax.optimization_barrier(values)


def sum_everywhere(value):
    for bit in (CORE, ACROSS, DEEP):
        value = value + swap(value, bit)
    for step in (1, 2):
        value = value + lax.ppermute(value, "dp", [(i, i ^ step) for i in range(4)])
    return value


def upward(table):
    z = lax.axis_index("dp")
    return [lax.dynamic_index_in_dim(table, (z + k) % 4, keepdims=False) for k in range(4)]


def shares_of(tiles_all, devices):
    sizes = [height * across // devices for _, height, across in HOME_ORDER]
    sizes.append((tiles_all - TAIL) // devices)
    starts = [sum(sizes[:n]) for n in range(len(sizes))]
    return sizes, starts


def homes_of(tiles, tiles_all, devices, near):
    per = tiles_all // devices
    sizes, starts = shares_of(tiles_all, devices)
    homes = ((tiles - TAIL) // sizes[-1]) * per + starts[-1] + (tiles - TAIL) % sizes[-1]
    for (first, height, across), size, start in zip(HOME_ORDER, sizes, starts):
        at = tiles - first
        inside = (at >= 0) & (at < height * across)
        if near:
            row, column = at // across, at % across
            slab, half = height // CHIPS, across // 2
            owner = row // slab * 2 + column // half
            line = column % half * slab + row % slab
        else:
            owner, line = at // size, at % size
        homes = jnp.where(inside, owner * per + start + line, homes)
    return homes


def room(per, devices):
    mean = per / devices
    return int(-(-(mean + 5.0 * mean**0.5) // 8) * 8)


def row_steps(total, size, step):
    whole, rest = divmod(total, size)

    def body(i, carry):
        step(i * size, size)
        return carry

    lax.fori_loop(0, whole, body, 0)
    if rest:
        step(whole * size, rest)


def send_kernel(slots, lines, tiles, packed, index, stage, *, per):
    slot_count = packed.shape[0]

    def clear(start, size):
        for u in range(size):
            index[start + u] = per

    row_steps(slot_count + 8, 64, clear)
    stage[...] = jnp.zeros_like(stage)

    def place(start, size):
        for u in range(size):
            slot = slots[start + u]
            stage[pl.ds(slot, 1), :] = tiles[pl.ds(start + u, 1), :]
            index[slot] = lines[start + u]

    row_steps(per, 64, place)
    packed[...] = stage[pl.ds(0, slot_count), :].astype(packed.dtype)


def send_tiles(slots, lines, tiles, slot_count):
    per = tiles.shape[0]
    return pl.pallas_call(
        functools.partial(send_kernel, per=per),
        in_specs=[pl.BlockSpec(memory_space=pltpu.SMEM)] * 2 + [pl.BlockSpec(memory_space=pltpu.VMEM)],
        out_specs=[pl.BlockSpec(memory_space=pltpu.VMEM), pl.BlockSpec(memory_space=pltpu.SMEM)],
        out_shape=[
            jax.ShapeDtypeStruct((slot_count, TILE), jnp.bfloat16),
            jax.ShapeDtypeStruct((slot_count + 8,), jnp.int32),
        ],
        scratch_shapes=[pltpu.VMEM((slot_count + 8, TILE), jnp.float32)],
        name="send_tiles",
    )(slots, lines, tiles)


def slab_pieces(starts):
    for (row, lines, groups, columns, offset), start in zip(SLABS, starts):
        for column in range(columns):
            for part in range(groups):
                yield row, offset + part * columns + column, lines, start + (column * groups + part) * lines


def land_kernel(index, packed, tiles, stage, full, *, starts):
    stage[...] = packed[...].astype(jnp.float32)

    def place(start, size):
        for u in range(size):
            full[pl.ds(index[start + u], 1), :] = stage[pl.ds(start + u, 1), :]

    row_steps(packed.shape[0], 128, place)
    if starts is None:
        tiles[...] = full[pl.ds(0, tiles.shape[0]), :].astype(tiles.dtype)
    else:
        tiles[...] = jnp.zeros_like(tiles)
        for row, column, lines, line in (*slab_pieces(starts), (*TAIL_AT, 16, starts[-1])):
            tiles[pl.ds(row, lines), column * TILE : (column + 1) * TILE] = full[pl.ds(line, lines), :].astype(
                tiles.dtype
            )


def land_tiles(index, packed, per, starts):
    slot_count = packed.shape[0]
    return pl.pallas_call(
        functools.partial(land_kernel, starts=starts),
        in_specs=[pl.BlockSpec(memory_space=pltpu.SMEM), pl.BlockSpec(memory_space=pltpu.VMEM)],
        out_specs=pl.BlockSpec(memory_space=pltpu.VMEM),
        out_shape=jax.ShapeDtypeStruct((per, TILE) if starts is None else SHARE, jnp.bfloat16),
        scratch_shapes=[pltpu.VMEM((slot_count, TILE), jnp.float32), pltpu.VMEM((per + 8, TILE), jnp.float32)],
        name="land_tiles",
    )(index, packed)


def share_lines_kernel(up, down, qkv, rest, lines, *, starts):
    slabs = (up, down, qkv, rest, rest)
    first = (0, 0, 0, 0, 48)
    for n, (source, (_, _, _, columns, _), begin, start) in enumerate(zip(slabs, SLABS, first, starts)):
        height = HOME_ORDER[n][1] // CHIPS
        for column in range(columns):
            lines[pl.ds(start + column * height, height), :] = source[
                pl.ds(begin, height), column * TILE : (column + 1) * TILE
            ]
    lines[pl.ds(starts[-1], 8), :] = rest[pl.ds(80, 8), :TILE]


def share_lines(up, down, qkv, rest, per, starts):
    return pl.pallas_call(
        functools.partial(share_lines_kernel, starts=starts),
        in_specs=[pl.BlockSpec(memory_space=pltpu.VMEM)] * 4,
        out_specs=pl.BlockSpec(memory_space=pltpu.VMEM),
        out_shape=jax.ShapeDtypeStruct((per, TILE), jnp.float32),
        name="share_lines",
    )(up, down, qkv, rest)


def pick_kernel(index, source, target, *, count):
    def pick(start, size):
        for u in range(size):
            target[pl.ds(start + u, 1), :] = source[pl.ds(index[start + u], 1), :]

    row_steps(count, 128, pick)


def pick_tiles(index, source, count):
    return pl.pallas_call(
        functools.partial(pick_kernel, count=count),
        in_specs=[pl.BlockSpec(memory_space=pltpu.SMEM), pl.BlockSpec(memory_space=pltpu.VMEM)],
        out_specs=pl.BlockSpec(memory_space=pltpu.VMEM),
        out_shape=jax.ShapeDtypeStruct((count, TILE), source.dtype),
        name="pick_tiles",
    )(index, source)


def assemble_kernel(arrived, up, down, qkv, out, place, tail, landed, sem):
    copy = pltpu.make_async_copy(arrived, landed, sem)
    copy.start()
    copy.wait()

    def one_device(block, carry):
        chip, core = block // 2, block % 2

        def put(target, row, lines, width, source_row, source_column):
            target[
                pl.ds(pl.multiple_of(row, 16), lines), pl.ds(pl.multiple_of(core * width, TILE), width)
            ] = landed[block, pl.ds(source_row, lines), source_column : source_column + width]

        put(up, chip * 48, 48, 1536, 0, 0)
        for part in range(4):
            put(down, chip * 192 + part * 48, 48, 384, 48, part * 384)
        put(qkv, chip * 48, 48, 1152, 96, 0)
        put(out, chip * 48, 48, 384, 96, 1152)
        for part in range(2):
            put(place, chip * 32 + part * 16, 16, 384, 144, part * 384)
        tail[block] = landed[block, pl.ds(TAIL_AT[0], 16), TAIL_AT[1] * TILE : (TAIL_AT[1] + 1) * TILE].astype(
            jnp.float32
        )[:8]
        return carry

    lax.fori_loop(0, landed.shape[0], one_device, 0)


def assemble_layer(arrived):
    devices = arrived.shape[0]
    return pl.pallas_call(
        assemble_kernel,
        in_specs=[pl.BlockSpec(memory_space=pl.ANY)],
        out_specs=[pl.BlockSpec(memory_space=pltpu.VMEM)] * 6,
        out_shape=[jax.ShapeDtypeStruct((h, a * TILE), jnp.bfloat16) for _, h, a in HOME_ORDER]
        + [jax.ShapeDtypeStruct((devices, 8, TILE), jnp.float32)],
        scratch_shapes=[
            pltpu.VMEM((devices, *SHARE), jnp.bfloat16),
            pltpu.SemaphoreType.DMA,
        ],
        compiler_params=pltpu.CompilerParams(vmem_limit_bytes=VMEM_LIMIT),
        cost_estimate=pl.CostEstimate(flops=0, bytes_accessed=60_000_000, transcendentals=0),
        name="assemble_layer",
    )(arrived)


def unpack_kernel(source, target, stage, *, across):
    stage[...] = source[...].astype(jnp.float32)

    def step(g, carry):
        for column in range(across):
            lines = stage[pl.ds(g * 16 * across + column, 16, stride=across), :]
            target[pl.ds(pl.multiple_of(g * 16, 16), 16), column * TILE : (column + 1) * TILE] = lines.astype(
                jnp.bfloat16
            )
        return carry

    lax.fori_loop(0, target.shape[0] // 16, step, 0)


def unpack_matrix(tiles, piece):
    first, height, across = piece
    lines = min(height, 384 if across > 6 else 768)
    block = lines * across
    return pl.pallas_call(
        functools.partial(unpack_kernel, across=across),
        grid=(height // lines,),
        in_specs=[pl.BlockSpec((block, TILE), lambda i: (first // block + i, 0))],
        out_specs=pl.BlockSpec((lines, across * TILE), lambda i: (i, 0)),
        out_shape=jax.ShapeDtypeStruct((height, across * TILE), jnp.bfloat16),
        scratch_shapes=[pltpu.VMEM((block, TILE), jnp.float32)],
        name="unpack_matrix",
    )(tiles)


def array_multiply(left_side, right_side):
    return jnp.dot(left_side, right_side, preferred_element_type=jnp.float32)


def matmul_left(left_side, right_side):
    return lax.dot_general(
        left_side, right_side, (((0,), (0,)), ((), ())), preferred_element_type=jnp.float32
    )


def trailing_array_multiply(left_side, right_side):
    return lax.dot_general(
        left_side, right_side, (((1,), (1,)), ((), ())), preferred_element_type=jnp.float32
    )


def pieces_of(matrices, tail):
    qkv, out, up, down, place = matrices
    return {
        "qkv": qkv,
        "out": out,
        "up": up,
        "down": down,
        "place": place,
        "small": tail[:60].reshape(10, D),
        "upbias": tail[60:84].reshape(FF),
    }


def norm_forward(values, gain_row, shift_row):
    center = values - jnp.mean(values, axis=-1, keepdims=True)
    inverse = lax.rsqrt(jnp.mean(center * center, axis=-1, keepdims=True) + norm_eps)
    normed = center * inverse
    return (normed * gain_row + shift_row, normed, inverse)


def norm_backward(grad_out, normed, inverse, gain_row):
    scaled = grad_out * gain_row
    grad_in = inverse * (
        scaled
        - jnp.mean(scaled, axis=-1, keepdims=True)
        - normed * jnp.mean(scaled * normed, axis=-1, keepdims=True)
    )
    return (grad_in, jnp.sum(grad_out * normed, axis=0), jnp.sum(grad_out, axis=0))


def gelu_slope(values):
    return (
        0.5 * (1.0 + lax.erf(values * 0.7071067811865476))
        + values * jnp.exp(-0.5 * values * values) * 0.3989422804014327
    )


def key_scores(projected, lengths):
    seqs_count = lengths.shape[0]
    split_heads = projected.reshape(seqs_count, LEN, 3, HEADS, HEAD_DIM)
    scores = jnp.einsum(
        "sqhd,skhd->shqk",
        split_heads[:, :, 0],
        split_heads[:, :, 1],
        preferred_element_type=jnp.float32,
    ) * HEAD_DIM ** (-0.5)
    live_keys = jnp.arange(LEN)[None, :] < lengths[:, None]
    return (jnp.where(live_keys[:, None, None, :], scores, -1000000000.0), split_heads)


def attention_forward(pieces, looked, lengths):
    small_rows = pieces["small"].astype(jnp.float32)
    seqs_count = lengths.shape[0]
    rows_here = seqs_count * LEN
    summed = (
        looked.reshape(seqs_count, LEN, D) + pieces["place"].astype(jnp.float32)[None]
    ).reshape(rows_here, D)
    first_norm, normed_zero, inverse_zero = norm_forward(summed, small_rows[4], small_rows[5])
    inputs = first_norm.astype(jnp.bfloat16)
    qkv_bias = jnp.concatenate([small_rows[0], jnp.zeros((D,), jnp.float32), small_rows[1]])
    projected = (array_multiply(inputs, pieces["qkv"]) + qkv_bias).astype(jnp.bfloat16)
    scores, split_heads = key_scores(projected, lengths)
    peak = jnp.max(scores, axis=-1, keepdims=True)
    exps = jnp.exp(scores - peak)
    totals = jnp.sum(exps, axis=-1, keepdims=True)
    probabilities = (exps / totals).astype(jnp.bfloat16)
    logsum = peak + jnp.log(totals)
    context = jnp.einsum(
        "shqk,skhd->sqhd", probabilities, split_heads[:, :, 2], preferred_element_type=jnp.float32
    )
    context = context.reshape(rows_here, D).astype(jnp.bfloat16)
    attended = array_multiply(context, pieces["out"]) + small_rows[2]
    middle, normed_one, inverse_one = norm_forward(
        first_norm + attended, small_rows[6], small_rows[7]
    )
    saved = {
        "inputs": inputs,
        "projected": projected,
        "logsum": logsum,
        "context": context,
        "normed_zero": normed_zero,
        "inverse_zero": inverse_zero,
        "normed_one": normed_one,
        "inverse_one": inverse_one,
    }
    return middle, saved


def feed_forward(pieces, middle, saved):
    small_rows = pieces["small"]
    middle_low = middle.astype(jnp.bfloat16)
    hidden = array_multiply(middle_low, pieces["up"]) + pieces["upbias"].astype(jnp.float32)
    activated = jax.nn.gelu(hidden, approximate=False).astype(jnp.bfloat16)
    output = array_multiply(activated, pieces["down"]) + small_rows[3]
    final_lines, normed_two, inverse_two = norm_forward(
        middle + output, small_rows[8], small_rows[9]
    )
    saved = {
        **saved,
        "middle_low": middle_low,
        "hidden": hidden,
        "activated": activated,
        "normed_two": normed_two,
        "inverse_two": inverse_two,
    }
    return (final_lines, saved)


def feed_backward(pieces, saved, grad_final, flow):
    small_rows = pieces["small"]
    grad_sum_two, grad_gain_two, grad_shift_two = norm_backward(
        grad_final, saved["normed_two"], saved["inverse_two"], small_rows[8]
    )
    grad_out = grad_sum_two.astype(jnp.bfloat16)
    flow.add_product(saved["activated"], grad_out)
    grad_act = trailing_array_multiply(grad_out, pieces["down"])
    grad_hidden = (grad_act * gelu_slope(saved["hidden"])).astype(jnp.bfloat16)
    flow.add_product(saved["middle_low"], grad_hidden)
    grad_middle = grad_sum_two + trailing_array_multiply(grad_hidden, pieces["up"])
    grad_sum_one, grad_gain_one, grad_shift_one = norm_backward(
        grad_middle, saved["normed_one"], saved["inverse_one"], small_rows[6]
    )
    grad_upbias = jnp.sum(grad_hidden.astype(jnp.float32), axis=0)
    (grad_sum_one,) = flow.advance(grad_sum_one)
    return (
        grad_sum_one,
        [jnp.sum(grad_out.astype(jnp.float32), axis=0), grad_gain_one, grad_shift_one, grad_gain_two, grad_shift_two],
        grad_upbias,
    )


def attention_backward(pieces, saved, grad_sum_one, grad_small, grad_upbias, lengths, tail_rows, flow, head_part):
    small_rows = pieces["small"]
    seqs_count = lengths.shape[0]
    rows_here = seqs_count * LEN
    grad_att = grad_sum_one.astype(jnp.bfloat16)
    grad_outw = matmul_left(saved["context"], grad_att)
    grad_context = (
        trailing_array_multiply(grad_att, pieces["out"])
        .astype(jnp.bfloat16)
        .reshape(seqs_count, LEN, HEADS, HEAD_DIM)
    )
    scores, split_heads = key_scores(saved["projected"], lengths)
    probabilities = jnp.exp(scores - saved["logsum"])
    grad_probs = jnp.einsum(
        "sqhd,skhd->shqk", grad_context, split_heads[:, :, 2], preferred_element_type=jnp.float32
    )
    grad_values = jnp.einsum(
        "shqk,sqhd->skhd",
        probabilities.astype(jnp.bfloat16),
        grad_context,
        preferred_element_type=jnp.float32,
    )
    grad_scores = probabilities * (
        grad_probs - jnp.sum(grad_probs * probabilities, axis=-1, keepdims=True)
    )
    (grad_scores,) = flow.advance(grad_scores.astype(jnp.bfloat16))
    grad_queries = jnp.einsum(
        "shqk,skhd->sqhd", grad_scores, split_heads[:, :, 1], preferred_element_type=jnp.float32
    ) * HEAD_DIM ** (-0.5)
    grad_keys = jnp.einsum(
        "shqk,sqhd->skhd", grad_scores, split_heads[:, :, 0], preferred_element_type=jnp.float32
    ) * HEAD_DIM ** (-0.5)
    grad_proj = (
        jnp.stack([grad_queries, grad_keys, grad_values], axis=2)
        .reshape(rows_here, 3 * D)
        .astype(jnp.bfloat16)
    )
    grad_bias_all = jnp.sum(grad_proj.astype(jnp.float32), axis=0)
    grad_first = grad_sum_one + trailing_array_multiply(grad_proj, pieces["qkv"])
    grad_embedded, grad_gain_zero, grad_shift_zero = norm_backward(
        grad_first, saved["normed_zero"], saved["inverse_zero"], small_rows[4]
    )
    grad_place = jnp.sum(grad_embedded.reshape(seqs_count, LEN, D), axis=0)
    grad_small = jnp.stack(
        [
            grad_bias_all[:D],
            grad_bias_all[2 * D :],
            jnp.sum(grad_att.astype(jnp.float32), axis=0),
            grad_small[0],
            grad_gain_zero,
            grad_shift_zero,
            *grad_small[1:],
        ]
    )
    tail = jnp.concatenate(
        [
            grad_small.reshape(60, TILE),
            grad_upbias.reshape(24, TILE),
            jnp.zeros((tail_rows - 84, TILE), jnp.float32),
        ]
    )
    grad_embedded, head_part = flow.advance(grad_embedded, head_part)
    flow.add_product(saved["inputs"], grad_proj)
    flow.add_rest(grad_outw, grad_place, tail)
    return grad_embedded, head_part


def combine_stats(earlier, later):
    peak_s = jnp.maximum(earlier[0], later[0])
    peak_t = jnp.maximum(earlier[2], later[2])
    factor_early = jnp.exp(earlier[0] - peak_s)
    factor_late = jnp.exp(later[0] - peak_s)
    teacher_early = jnp.exp(earlier[2] - peak_t)
    teacher_late = jnp.exp(later[2] - peak_t)
    return jnp.stack(
        [
            peak_s,
            earlier[1] * factor_early + later[1] * factor_late,
            peak_t,
            earlier[3] * teacher_early + later[3] * teacher_late,
            earlier[4] * teacher_early + later[4] * teacher_late,
        ]
    )


def adam_step(weight, first_moment, second, gradient, step_float):
    new_first = beta_first * first_moment + (1.0 - beta_first) * gradient
    new_second = beta_second * second + (1.0 - beta_second) * gradient * gradient
    fix_first = 1.0 - jnp.power(beta_first, step_float)
    fix_second = 1.0 - jnp.power(beta_second, step_float)
    update = new_first / fix_first / (jnp.sqrt(new_second / fix_second) + adam_eps)
    return (weight - learn_rate * (update + weight_decay * weight), new_first, new_second)


def at(value, index, axis):
    return lax.dynamic_index_in_dim(value, index, axis, keepdims=False)


def sent_low(value, bit):
    return swap(value.astype(jnp.bfloat16), bit).astype(jnp.float32)


def bit_of(bit):
    return lax.axis_index("vocab") // bit % 2


def halved(value, axis, bit):
    mine = bit_of(bit)
    return at(value, mine, axis) + sent_low(at(value, 1 - mine, axis), bit)


def reduce_steps(near, far):
    (chip,) = yield [near + swap(far, CORE)]
    chip = chip.reshape(4, 2, 2, chip.shape[0] // CHIPS, chip.shape[1])
    first, second = yield [halved(chip[:2], 2, ACROSS), halved(chip[2:], 1, DEEP)]
    first, second = yield [halved(first, 1, DEEP), halved(second, 1, ACROSS)]
    z = lax.axis_index("dp")
    blocks = [
        jnp.where((z + k) % 4 < 2, at(first, (z + k) % 2, 0), at(second, (z + k) % 2, 0)) for k in range(4)
    ]
    blocks = yield [blocks[0], *(shift(blocks[k], k) for k in (1, 2, 3))]
    return blocks[0] + blocks[1] + blocks[2] + blocks[3]


class Flow:
    def __init__(self):
        self.lines, self.waiting, self.sums = [], [], []

    def add(self, near, far):
        self.lines.append(reduce_steps(near, far))
        self.waiting.append(next(self.lines[-1]))
        self.sums.append(None)

    def add_product(self, left, right):
        width = right.shape[1] // 2
        core = bit_of(CORE)
        far = matmul_left(left, lax.dynamic_slice_in_dim(right, (1 - core) * width, width, 1))
        near = matmul_left(left, lax.dynamic_slice_in_dim(right, core * width, width, 1))
        self.add(near, far)

    def add_rest(self, out, place, tail):
        def half(core):
            columns = [
                lax.dynamic_slice_in_dim(whole, core * 384, 384, 1).reshape(CHIPS, -1, 384) for whole in (out, place)
            ]
            ends = jnp.pad(at(tail.reshape(CHIPS, 2, 8, TILE), core, 1), ((0, 0), (0, 0), (0, 256)))
            return jnp.concatenate([*columns, ends], axis=1).reshape(-1, 384)

        self.add(half(bit_of(CORE)), half(1 - bit_of(CORE)))

    def advance(self, *values):
        tied, values = together([moved for moved in self.waiting if moved is not None], list(values))
        tied = list(tied)
        for n, moved in enumerate(self.waiting):
            if moved is not None:
                try:
                    self.waiting[n] = self.lines[n].send(tied.pop(0))
                except StopIteration as stop:
                    self.waiting[n], self.sums[n] = None, stop.value
        return values


class PlainFlow:
    def __init__(self, devices):
        self.devices, self.sums = devices, []

    def add_product(self, left, right):
        parts = matmul_left(left, right).reshape(self.devices, -1, TILE)
        self.sums.append(lax.psum_scatter(parts, ("dp", "vocab"), scatter_dimension=0, tiled=False))

    def add_rest(self, out, place, tail):
        parts = [part.reshape(self.devices, -1, TILE) for part in (out, place, tail)]
        parts = jnp.concatenate(parts, axis=1)
        self.sums.append(lax.psum_scatter(parts, ("dp", "vocab"), scatter_dimension=0, tiled=False))

    def advance(self, *values):
        return values


def on_device(
    near,
    token_ids,
    lengths,
    mask_pos,
    mask_count,
    owner_order,
    step_count,
    teacher_flat,
    mentor_lexicon_weights,
    student_flat,
    flat_first,
    flat_second,
    student_embed,
    embed_first,
    embed_second,
):
    per = student_flat.shape[0]
    tiles_all = owner_order.shape[0]
    vocab_rows, width_share = student_embed.shape
    planes = lax.axis_size("dp")
    group = lax.axis_size("vocab")
    here = lax.axis_index("vocab")
    spot = jnp.stack([lax.axis_index("dp"), here]).astype(jnp.int32)
    devices = planes * group
    everywhere = ("dp", "vocab")
    device = lax.axis_index(everywhere)
    capacity = room(per, devices)
    slot_count = devices * capacity

    facts = jnp.concatenate([token_ids.reshape(LEN), lengths, mask_count, jnp.zeros((TILE - 2,), jnp.int32)])
    columns_low = student_embed.T.astype(jnp.bfloat16)
    words = jnp.arange(vocab_rows, dtype=jnp.int32)

    def chosen(ids):
        return (ids.reshape(-1, 1) - here * vocab_rows == words[None]).astype(jnp.bfloat16)

    def rows_t(ids):
        return array_multiply(chosen(ids), mentor_lexicon_weights).astype(jnp.bfloat16)

    def rows_s(ids, table):
        return trailing_array_multiply(chosen(ids), table).astype(jnp.bfloat16)

    def teacher_pieces(tiles):
        return pieces_of(
            [unpack_matrix(tiles, piece) for piece in MATRICES],
            tiles[TAIL : TAIL + TAIL_TILES].astype(jnp.float32),
        )

    homes = homes_of(owner_order, tiles_all, devices, near)
    sizes, starts = shares_of(tiles_all, devices)
    one_of = jnp.arange(devices, dtype=jnp.int32)
    pairs = jnp.sum((homes.reshape(devices, per, 1) // per == one_of).astype(jnp.int32), axis=1)
    crowded = jnp.max(pairs) > capacity
    own_homes = lax.dynamic_slice_in_dim(homes, device * per, per)
    own_target = own_homes // per
    chosen_target = (own_target[:, None] == one_of).astype(jnp.bfloat16)
    lines = jnp.arange(per, dtype=jnp.int32)
    earlier = (lines[None] < lines[:, None]).astype(jnp.bfloat16)
    rank = jnp.sum(array_multiply(earlier, chosen_target) * chosen_target.astype(jnp.float32), axis=1)
    rank = rank.astype(jnp.int32)
    slots = jnp.where(rank < capacity, own_target * capacity + rank, slot_count)
    packed, home_line = send_tiles(slots, own_homes % per, student_flat, slot_count)
    if near:
        teacher_tiles = lax.all_gather(teacher_flat, everywhere, axis=0, tiled=True)
        plane_facts = gather_near(facts)
        shape = (2, 2, LEN, D)
        far = rows_t(plane_facts[4:, :LEN]).reshape(shape)
        columns = [columns_low, shift(columns_low, 1)]
        packed, home_line, far, columns = together(packed, home_line, far, columns)
    packed = lax.all_to_all(packed.reshape(devices, capacity, TILE), everywhere, 0, 0)
    home_line = lax.all_to_all(home_line[:slot_count].reshape(devices, 1, capacity), everywhere, 0, 0)
    home_line = home_line.reshape(slot_count)
    if near:
        looked_t = rows_t(plane_facts[:4, :LEN]).reshape(shape) + swap(far, CORE)
        packed, home_line, looked_t, ahead = together(packed, home_line, looked_t, shift(columns[1], 1))
        columns = [*columns, ahead]
    home_tiles = land_tiles(home_line, packed.reshape(slot_count, TILE), per, starts if near else None)
    if near:
        home_tiles, looked_t, ahead = together(home_tiles, plane_hop(looked_t), shift(columns[2], 1))
        columns = [*columns, ahead]

    def from_everywhere(part):
        copies = jnp.broadcast_to(part[None], (devices, *part.shape))
        return lax.all_to_all(copies, everywhere, 0, 0).reshape(-1, TILE)

    def every_tile(tiles):
        stored = from_everywhere(student_flat.astype(jnp.bfloat16))
        sources = jnp.zeros((tiles_all,), jnp.int32).at[homes].set(jnp.arange(tiles_all, dtype=jnp.int32))
        stored = stored[lax.dynamic_slice_in_dim(sources, device * per, per)]
        if near:
            return land_tiles(lines, stored, per, starts)
        return stored

    home_tiles = lax.cond(crowded, every_tile, lambda tiles: tiles, home_tiles)

    if near:
        layer = lax.all_gather(home_tiles, everywhere, axis=0)
        z = lax.axis_index("dp")
        table_low = jnp.zeros((D, vocab_rows), jnp.bfloat16)
        for k, part in enumerate(columns):
            table_low = lax.dynamic_update_slice(table_low, part, ((z + 4 - k) % 4 * width_share, 0))
        far = rows_s(plane_facts[4:, :LEN], table_low).reshape(shape)
        looked_t, far = together(plane_end(*looked_t).astype(jnp.float32), far)
        close = rows_s(plane_facts[:4, :LEN], table_low).reshape(shape)
        looked_s, teacher_tiles = together(close + swap(far, CORE), teacher_tiles)
        teacher = teacher_pieces(teacher_tiles)
        teacher, looked_s = together(teacher, plane_hop(looked_s))
        middle, _ = attention_forward(teacher, looked_t, lengths)
        middle, looked_s = together(middle, plane_end(*looked_s).astype(jnp.float32))
        final_t = feed_forward(teacher, middle, {})[0]
        final_t, layer = together(final_t, layer)
        matrices = assemble_layer(layer)
        matrices, facts = together(matrices, facts)
        other_facts = gather_near(jnp.stack([shift(facts, 1), shift(facts, 2), shift(facts, 3)]))
        all_facts = jnp.concatenate([plane_facts[:, None], other_facts], axis=1)
    else:
        table_low = lax.all_gather(columns_low, "dp", axis=0, tiled=True)
        by_plane = lax.all_gather(facts, "dp", axis=0)
        all_facts = lax.all_gather(by_plane, "vocab", axis=0)
        plane_facts = lax.dynamic_index_in_dim(all_facts, lax.axis_index("dp"), 1, keepdims=False)
        teacher_tiles = lax.all_gather(teacher_flat, everywhere, axis=0, tiled=True)
        layer = lax.all_gather(home_tiles, everywhere, axis=0)
        matrices = [
            layer[:, start : start + size].reshape(height, across * TILE)
            for (_, height, across), size, start in zip(HOME_ORDER, sizes, starts)
        ]
        matrices.append(layer[:, starts[-1] :].astype(jnp.float32))
        plane_ids = plane_facts[:, :LEN]
        looked_t, looked_s = (
            lax.psum_scatter(rows, "vocab", scatter_dimension=0, tiled=True).astype(jnp.float32)
            for rows in (rows_t(plane_ids), rows_s(plane_ids, table_low))
        )
        teacher = teacher_pieces(teacher_tiles)
        middle, _ = attention_forward(teacher, looked_t, lengths)
        final_t = feed_forward(teacher, middle, {})[0]
    up, down, qkv, out, place = matrices[:5]
    student = pieces_of((qkv, out, up, down, place), matrices[5].reshape(-1, TILE))
    middle, saved = attention_forward(student, looked_s, lengths)
    final_s, saved = feed_forward(student, middle, saved)

    offsets = jnp.concatenate([mask_pos.reshape(CAP), jnp.zeros((SLOTS - CAP,), jnp.int32)])
    picked_t = final_t[offsets].astype(jnp.bfloat16)
    if near:
        mentor_picked = gather_near(picked_t).reshape(-1, D)
        final_s, mentor_picked, all_facts = together(final_s, mentor_picked, all_facts)
    else:
        mentor_picked = lax.all_gather(picked_t, "vocab", axis=0, tiled=True)
    token_total = jnp.sum(all_facts[:, :, LEN]).astype(jnp.float32)
    masked_total = jnp.sum(all_facts[:, :, LEN + 1]).astype(jnp.float32)
    teacher_logit = (
        trailing_array_multiply(mentor_picked, mentor_lexicon_weights) / smoothing_heat_scale
    )
    peak_t = jnp.max(teacher_logit, axis=1)
    picked_s = final_s[offsets].astype(jnp.bfloat16)
    if near:
        learner_picked = gather_near(picked_s).reshape(-1, D)
        learner_picked, teacher_logit, peak_t = together(learner_picked, teacher_logit, peak_t)
    else:
        learner_picked = lax.all_gather(picked_s, "vocab", axis=0, tiled=True)
    live_weighting = (
        (jnp.arange(SLOTS)[None] < plane_facts[:, LEN + 1, None]).astype(jnp.float32).reshape(-1)
    )
    learner_energy = array_multiply(learner_picked, table_low) / smoothing_heat_scale
    peak_s = jnp.max(learner_energy, axis=1)
    teacher_exps = jnp.exp(teacher_logit - peak_t[:, None])
    stats = jnp.stack(
        [
            peak_s,
            jnp.sum(jnp.exp(learner_energy - peak_s[:, None]), axis=1),
            peak_t,
            jnp.sum(teacher_exps, axis=1),
            jnp.sum(teacher_exps * (teacher_logit - learner_energy), axis=1),
        ]
    )
    if near:
        stats = stats.reshape(5, 2, 2, 2, SLOTS)
        for axis, bit in ((1, CORE), (2, DEEP), (3, ACROSS)):
            stats = combine_stats(stats, jnp.flip(swap(stats, bit), axis))
        stats = stats.reshape(5, -1)
    else:
        everything = lax.all_gather(stats, "vocab", axis=0)
        stats = everything[0]
        for k in range(1, group):
            stats = combine_stats(stats, everything[k])
    logsum_s = stats[0] + jnp.log(stats[1])
    logsum_t = stats[2] + jnp.log(stats[3])
    diverge = stats[4] / stats[3] - logsum_t + logsum_s
    mine = 0 if near else here * SLOTS
    divergence_part = jnp.sum(lax.dynamic_slice_in_dim(diverge * live_weighting, mine, SLOTS))
    student_probs = jnp.exp(learner_energy - logsum_s[:, None])
    teacher_probs = jnp.exp(teacher_logit - logsum_t[:, None])
    grad_logit = (
        mixing_coefficient
        * smoothing_heat_scale
        / masked_total
        * live_weighting[:, None]
        * (student_probs - teacher_probs)
    ).astype(jnp.bfloat16)
    if near:
        half = grad_logit.shape[0] // 2
        far = trailing_array_multiply(grad_logit[half:], table_low).reshape(2, 2, SLOTS, D)
        close = trailing_array_multiply(grad_logit[:half], table_low).reshape(2, 2, SLOTS, D)
        grad_rows = plane_end(*plane_hop(close + swap(far, CORE)))
    else:
        grad_rows = lax.psum_scatter(
            trailing_array_multiply(grad_logit, table_low), "vocab", scatter_dimension=0, tiled=True
        )
    head_grad = matmul_left(learner_picked, grad_logit)
    head_grad, grad_rows = together(head_grad, grad_rows)
    head_part = lax.psum_scatter(head_grad, "dp", scatter_dimension=0, tiled=True)
    products = jnp.sum(final_s * final_t, axis=1)
    inverse_s = lax.rsqrt(jnp.sum(final_s * final_s, axis=1) + cosine_eps)
    inverse_t = lax.rsqrt(jnp.sum(final_t * final_t, axis=1) + cosine_eps)
    live_rows = (jnp.arange(LEN)[None, :] < lengths[:, None]).reshape(-1)
    cosine = products * inverse_s * inverse_t
    cosine_term = jnp.sum(jnp.where(live_rows, 1.0 - cosine, 0.0))
    weighting = jnp.where(live_rows, -cosine_weight / token_total, 0.0) * inverse_s * inverse_t
    grad_final = weighting[:, None] * (
        final_t - (products * inverse_s * inverse_s)[:, None] * final_s
    )
    grad_final = grad_final.at[offsets].add(grad_rows)
    flow = Flow() if near else PlainFlow(devices)
    grad_sum_one, grad_small, grad_upbias = feed_backward(student, saved, grad_final, flow)
    grad_embedded, head_part = attention_backward(
        student, saved, grad_sum_one, grad_small, grad_upbias, lengths, tiles_all - TAIL, flow, head_part
    )

    shares = grad_embedded.astype(jnp.bfloat16).reshape(LEN, planes, width_share).transpose(1, 0, 2)
    if near:
        own = upward(shares)
        shares = jnp.stack([own[0]] + [shift(own[k], k) for k in (1, 2, 3)])
        ids = all_facts[:, :, :LEN].reshape(2, 2, 2, planes, LEN)
        for axis, bit in ((0, CORE), (1, DEEP), (2, ACROSS)):
            ids = jnp.where((here & bit) != 0, jnp.flip(ids, axis), ids)
        ids = ids.transpose(1, 2, 0, 3, 4)
    else:
        shares = lax.all_to_all(shares, "dp", 0, 0)
        ids = all_facts[:, :, :LEN]
    token_grads = lax.all_gather(shares.reshape(-1, width_share), "vocab", axis=0, tiled=True)
    (shares,) = flow.advance(shares)
    token_grads = lax.all_gather(shares.reshape(-1, width_share), "vocab", axis=0, tiled=True)
    flow.advance()
    flow.advance()
    (token_grads,) = flow.advance(token_grads)
    sum_down, sum_up, sum_qkv, sum_rest = flow.sums
    if near:
        home_grads = share_lines(sum_up, sum_down, sum_qkv, sum_rest, per, starts)
    else:
        home_grads = jnp.concatenate([sum_up, sum_down, sum_qkv, sum_rest])
    returned = pick_tiles(jnp.minimum(home_line, per - 1), home_grads, slot_count)
    returned = lax.all_to_all(returned.reshape(devices, capacity, TILE), everywhere, 0, 0)
    token_part = matmul_left(token_grads, chosen(ids))
    returned, token_part = together(returned, token_part)
    flat_grad = pick_tiles(jnp.minimum(slots, slot_count - 1), returned.reshape(slot_count, TILE), per)
    flat_grad = lax.cond(
        crowded,
        lambda grads: from_everywhere(home_grads)[own_homes],
        lambda grads: grads,
        flat_grad,
    )
    table_grad = (head_part + token_part).T
    loss_term = (
        mixing_coefficient * smoothing_heat_scale**2 * divergence_part / masked_total
        + cosine_weight * cosine_term / token_total
    )
    squares = jnp.sum(flat_grad * flat_grad) + jnp.sum(table_grad * table_grad)
    if near:
        squares, loss_value = sum_everywhere(jnp.stack([squares, loss_term]))
    else:
        squares, loss_value = lax.psum((squares, loss_term), ("dp", "vocab"))
    grad_norm = jnp.sqrt(squares)
    factor = clip_norm / jnp.maximum(grad_norm, clip_norm)
    step_float = step_count[0].astype(jnp.float32)
    new_flat, new_flat_first, new_flat_second = adam_step(
        student_flat, flat_first, flat_second, flat_grad * factor, step_float
    )
    new_embed, new_embed_first, new_embed_second = adam_step(
        student_embed, embed_first, embed_second, table_grad * factor, step_float
    )
    return (
        loss_value,
        grad_norm,
        new_flat,
        new_flat_first,
        new_flat_second,
        new_embed,
        new_embed_first,
        new_embed_second,
    )


def solution(mesh):
    near = mesh.shape["dp"] == 4 and mesh.shape["vocab"] == 8
    return jax.shard_map(
        functools.partial(on_device, near),
        mesh=mesh,
        in_specs=(
            P(("dp", "vocab"), None),
            P(("dp", "vocab")),
            P(("dp", "vocab"), None),
            P(("dp", "vocab")),
            P(),
            P(),
            P(("dp", "vocab"), None),
            P("vocab", None),
            P(("dp", "vocab"), None),
            P(("dp", "vocab"), None),
            P(("dp", "vocab"), None),
            P("vocab", "dp"),
            P("vocab", "dp"),
            P("vocab", "dp"),
        ),
        out_specs=(
            P(),
            P(),
            P(("dp", "vocab"), None),
            P(("dp", "vocab"), None),
            P(("dp", "vocab"), None),
            P("vocab", "dp"),
            P("vocab", "dp"),
            P("vocab", "dp"),
        ),
        check_vma=False,
    )
```

```python
import functools

import jax
import jax.numpy as jnp
from jax import lax
from jax.experimental import pallas as pl
from jax.experimental.pallas import tpu as pltpu
from jax.sharding import PartitionSpec as P

D = 768
HEADS = 12
HEAD_DIM = 64
FF = 3072
LEN = 512
CAP = 120
SLOTS = 128
TILE = 128

QKV = (0, D, 18)
OUT = (13824, D, 6)
UP = (18432, D, 24)
DOWN = (36864, FF, 6)
PLACE = (55296, LEN, 6)
MATRICES = (QKV, OUT, UP, DOWN, PLACE)
TAIL = 58368
TAIL_TILES = 88
HOME_ORDER = (UP, DOWN, QKV, OUT, PLACE)

VMEM_LIMIT = 60 * 1024 * 1024

smoothing_heat_scale = 2.0
mixing_coefficient = 5.0
cosine_weight = 20.0
clip_norm = 0.01
beta_first = 0.9
beta_second = 0.98
adam_eps = 1e-08
weight_decay = 0.01
learn_rate = 0.1
norm_eps = 1e-12
cosine_eps = 1e-06

CHIPS = 16
SLABS = ((0, 48, 1, 12, 0), (48, 48, 4, 3, 0), (96, 48, 1, 9, 0), (96, 48, 1, 3, 9), (144, 16, 2, 3, 0))
SHARE = (160, 1536)
TAIL_AT = (144, 6)
CORE, ACROSS, DEEP = 1, 2, 4


def swap(value, bit):
    return lax.ppermute(value, "vocab", [(i, i ^ bit) for i in range(8)])


def shift(value, steps):
    size = lax.axis_size("dp")
    return lax.ppermute(value, "dp", [(i, (i + steps) % size) for i in range(size)])


def gather_near(value):
    value = value[None]
    for bit in (ACROSS, DEEP, CORE):
        value = jnp.concatenate([value, swap(value, bit)])
    return value


def gather_split(value):
    half = value.shape[0] // 2
    across, deep = swap(value, ACROSS), swap(value, DEEP)
    diagonal = [swap(across[:half], DEEP), swap(deep[half:], ACROSS)]
    plane = jnp.concatenate([value, across, deep, *diagonal])
    return jnp.concatenate([plane, swap(plane, CORE)])


def plane_hop(value):
    half = value.shape[2] // 2
    upper, lower = value[:, :, :half], value[:, :, half:]
    return upper[:, 0] + swap(upper[:, 1], ACROSS), lower[0] + swap(lower[1], DEEP)


def plane_end(upper, lower):
    return jnp.concatenate([upper[0] + swap(upper[1], DEEP), lower[0] + swap(lower[1], ACROSS)])


def together(*values):
    return lax.optimization_barrier(values)


def sum_everywhere(value):
    for bit in (CORE, ACROSS, DEEP):
        value = value + swap(value, bit)
    for step in (1, 2):
        value = value + lax.ppermute(value, "dp", [(i, i ^ step) for i in range(4)])
    return value


def upward(table):
    z = lax.axis_index("dp")
    return [lax.dynamic_index_in_dim(table, (z + k) % 4, keepdims=False) for k in range(4)]


def shares_of(tiles_all, devices):
    sizes = [height * across // devices for _, height, across in HOME_ORDER]
    sizes.append((tiles_all - TAIL) // devices)
    starts = [sum(sizes[:n]) for n in range(len(sizes))]
    return sizes, starts


def homes_of(tiles, tiles_all, devices, near):
    per = tiles_all // devices
    sizes, starts = shares_of(tiles_all, devices)
    homes = ((tiles - TAIL) // sizes[-1]) * per + starts[-1] + (tiles - TAIL) % sizes[-1]
    for (first, height, across), size, start in zip(HOME_ORDER, sizes, starts):
        at = tiles - first
        inside = (at >= 0) & (at < height * across)
        if near:
            row, column = at // across, at % across
            slab, half = height // CHIPS, across // 2
            owner = row // slab * 2 + column // half
            line = column % half * slab + row % slab
        else:
            owner, line = at // size, at % size
        homes = jnp.where(inside, owner * per + start + line, homes)
    return homes


def room(per, devices):
    mean = per / devices
    return int(-(-(mean + 5.0 * mean**0.5) // 8) * 8)


def row_steps(total, size, step):
    whole, rest = divmod(total, size)

    def body(i, carry):
        step(i * size, size)
        return carry

    lax.fori_loop(0, whole, body, 0)
    if rest:
        step(whole * size, rest)


def send_kernel(slots, lines, tiles, packed, index, stage, *, per):
    slot_count = packed.shape[0]

    def clear(start, size):
        for u in range(size):
            index[start + u] = per

    row_steps(slot_count + 8, 64, clear)
    stage[...] = jnp.zeros_like(stage)

    def place(start, size):
        for u in range(size):
            slot = slots[start + u]
            stage[pl.ds(slot, 1), :] = tiles[pl.ds(start + u, 1), :]
            index[slot] = lines[start + u]

    row_steps(per, 64, place)
    packed[...] = stage[pl.ds(0, slot_count), :].astype(packed.dtype)


def send_tiles(slots, lines, tiles, slot_count):
    per = tiles.shape[0]
    return pl.pallas_call(
        functools.partial(send_kernel, per=per),
        in_specs=[pl.BlockSpec(memory_space=pltpu.SMEM)] * 2 + [pl.BlockSpec(memory_space=pltpu.VMEM)],
        out_specs=[pl.BlockSpec(memory_space=pltpu.VMEM), pl.BlockSpec(memory_space=pltpu.SMEM)],
        out_shape=[
            jax.ShapeDtypeStruct((slot_count, TILE), jnp.bfloat16),
            jax.ShapeDtypeStruct((slot_count + 8,), jnp.int32),
        ],
        scratch_shapes=[pltpu.VMEM((slot_count + 8, TILE), jnp.float32)],
        name="send_tiles",
    )(slots, lines, tiles)


def slab_pieces(starts):
    for (row, lines, groups, columns, offset), start in zip(SLABS, starts):
        for column in range(columns):
            for part in range(groups):
                yield row, offset + part * columns + column, lines, start + (column * groups + part) * lines


def land_kernel(index, packed, tiles, stage, full, *, starts):
    stage[...] = packed[...].astype(jnp.float32)

    def place(start, size):
        for u in range(size):
            full[pl.ds(index[start + u], 1), :] = stage[pl.ds(start + u, 1), :]

    row_steps(packed.shape[0], 128, place)
    if starts is None:
        tiles[...] = full[pl.ds(0, tiles.shape[0]), :].astype(tiles.dtype)
    else:
        tiles[...] = jnp.zeros_like(tiles)
        for row, column, lines, line in (*slab_pieces(starts), (*TAIL_AT, 16, starts[-1])):
            tiles[pl.ds(row, lines), column * TILE : (column + 1) * TILE] = full[pl.ds(line, lines), :].astype(
                tiles.dtype
            )


def land_tiles(index, packed, per, starts):
    slot_count = packed.shape[0]
    return pl.pallas_call(
        functools.partial(land_kernel, starts=starts),
        in_specs=[pl.BlockSpec(memory_space=pltpu.SMEM), pl.BlockSpec(memory_space=pltpu.VMEM)],
        out_specs=pl.BlockSpec(memory_space=pltpu.VMEM),
        out_shape=jax.ShapeDtypeStruct((per, TILE) if starts is None else SHARE, jnp.bfloat16),
        scratch_shapes=[pltpu.VMEM((slot_count, TILE), jnp.float32), pltpu.VMEM((per + 8, TILE), jnp.float32)],
        name="land_tiles",
    )(index, packed)


def share_lines_kernel(up, down, qkv, rest, lines, *, starts):
    slabs = (up, down, qkv, rest, rest)
    first = (0, 0, 0, 0, 48)
    for n, (source, (_, _, _, columns, _), begin, start) in enumerate(zip(slabs, SLABS, first, starts)):
        height = HOME_ORDER[n][1] // CHIPS
        for column in range(columns):
            lines[pl.ds(start + column * height, height), :] = source[
                pl.ds(begin, height), column * TILE : (column + 1) * TILE
            ]
    lines[pl.ds(starts[-1], 8), :] = rest[pl.ds(80, 8), :TILE]


def share_lines(up, down, qkv, rest, per, starts):
    return pl.pallas_call(
        functools.partial(share_lines_kernel, starts=starts),
        in_specs=[pl.BlockSpec(memory_space=pltpu.VMEM)] * 4,
        out_specs=pl.BlockSpec(memory_space=pltpu.VMEM),
        out_shape=jax.ShapeDtypeStruct((per, TILE), jnp.float32),
        name="share_lines",
    )(up, down, qkv, rest)


def pick_kernel(index, source, target, *, count):
    def pick(start, size):
        for u in range(size):
            target[pl.ds(start + u, 1), :] = source[pl.ds(index[start + u], 1), :]

    row_steps(count, 128, pick)


def pick_tiles(index, source, count):
    return pl.pallas_call(
        functools.partial(pick_kernel, count=count),
        in_specs=[pl.BlockSpec(memory_space=pltpu.SMEM), pl.BlockSpec(memory_space=pltpu.VMEM)],
        out_specs=pl.BlockSpec(memory_space=pltpu.VMEM),
        out_shape=jax.ShapeDtypeStruct((count, TILE), source.dtype),
        name="pick_tiles",
    )(index, source)


def assemble_kernel(arrived, up, down, qkv, out, place, tail, landed, sem):
    copy = pltpu.make_async_copy(arrived, landed, sem)
    copy.start()
    copy.wait()

    def one_device(block, carry):
        chip, core = block // 2, block % 2

        def put(target, row, lines, width, source_row, source_column):
            target[
                pl.ds(pl.multiple_of(row, 16), lines), pl.ds(pl.multiple_of(core * width, TILE), width)
            ] = landed[block, pl.ds(source_row, lines), source_column : source_column + width]

        put(up, chip * 48, 48, 1536, 0, 0)
        for part in range(4):
            put(down, chip * 192 + part * 48, 48, 384, 48, part * 384)
        put(qkv, chip * 48, 48, 1152, 96, 0)
        put(out, chip * 48, 48, 384, 96, 1152)
        for part in range(2):
            put(place, chip * 32 + part * 16, 16, 384, 144, part * 384)
        tail[block] = landed[block, pl.ds(TAIL_AT[0], 16), TAIL_AT[1] * TILE : (TAIL_AT[1] + 1) * TILE].astype(
            jnp.float32
        )[:8]
        return carry

    lax.fori_loop(0, landed.shape[0], one_device, 0)


def assemble_layer(arrived):
    devices = arrived.shape[0]
    return pl.pallas_call(
        assemble_kernel,
        in_specs=[pl.BlockSpec(memory_space=pl.ANY)],
        out_specs=[pl.BlockSpec(memory_space=pltpu.VMEM)] * 6,
        out_shape=[jax.ShapeDtypeStruct((h, a * TILE), jnp.bfloat16) for _, h, a in HOME_ORDER]
        + [jax.ShapeDtypeStruct((devices, 8, TILE), jnp.float32)],
        scratch_shapes=[
            pltpu.VMEM((devices, *SHARE), jnp.bfloat16),
            pltpu.SemaphoreType.DMA,
        ],
        compiler_params=pltpu.CompilerParams(vmem_limit_bytes=VMEM_LIMIT),
        cost_estimate=pl.CostEstimate(flops=0, bytes_accessed=60_000_000, transcendentals=0),
        name="assemble_layer",
    )(arrived)


def unpack_kernel(source, target, stage, *, across):
    stage[...] = source[...].astype(jnp.float32)

    def step(g, carry):
        for column in range(across):
            lines = stage[pl.ds(g * 16 * across + column, 16, stride=across), :]
            target[pl.ds(pl.multiple_of(g * 16, 16), 16), column * TILE : (column + 1) * TILE] = lines.astype(
                jnp.bfloat16
            )
        return carry

    lax.fori_loop(0, target.shape[0] // 16, step, 0)


def unpack_matrix(tiles, piece):
    first, height, across = piece
    lines = min(height, 384 if across > 6 else 768)
    block = lines * across
    return pl.pallas_call(
        functools.partial(unpack_kernel, across=across),
        grid=(height // lines,),
        in_specs=[pl.BlockSpec((block, TILE), lambda i: (first // block + i, 0))],
        out_specs=pl.BlockSpec((lines, across * TILE), lambda i: (i, 0)),
        out_shape=jax.ShapeDtypeStruct((height, across * TILE), jnp.bfloat16),
        scratch_shapes=[pltpu.VMEM((block, TILE), jnp.float32)],
        name="unpack_matrix",
    )(tiles)


def array_multiply(left_side, right_side):
    return jnp.dot(left_side, right_side, preferred_element_type=jnp.float32)


def matmul_left(left_side, right_side):
    return lax.dot_general(
        left_side, right_side, (((0,), (0,)), ((), ())), preferred_element_type=jnp.float32
    )


def trailing_array_multiply(left_side, right_side):
    return lax.dot_general(
        left_side, right_side, (((1,), (1,)), ((), ())), preferred_element_type=jnp.float32
    )


def pieces_of(matrices, tail):
    qkv, out, up, down, place = matrices
    return {
        "qkv": qkv,
        "out": out,
        "up": up,
        "down": down,
        "place": place,
        "small": tail[:60].reshape(10, D),
        "upbias": tail[60:84].reshape(FF),
    }


def norm_forward(values, gain_row, shift_row):
    center = values - jnp.mean(values, axis=-1, keepdims=True)
    inverse = lax.rsqrt(jnp.mean(center * center, axis=-1, keepdims=True) + norm_eps)
    normed = center * inverse
    return (normed * gain_row + shift_row, normed, inverse)


def norm_backward(grad_out, normed, inverse, gain_row):
    scaled = grad_out * gain_row
    grad_in = inverse * (
        scaled
        - jnp.mean(scaled, axis=-1, keepdims=True)
        - normed * jnp.mean(scaled * normed, axis=-1, keepdims=True)
    )
    return (grad_in, jnp.sum(grad_out * normed, axis=0), jnp.sum(grad_out, axis=0))


def gelu_slope(values):
    return (
        0.5 * (1.0 + lax.erf(values * 0.7071067811865476))
        + values * jnp.exp(-0.5 * values * values) * 0.3989422804014327
    )


def key_scores(projected, lengths):
    seqs_count = lengths.shape[0]
    split_heads = projected.reshape(seqs_count, LEN, 3, HEADS, HEAD_DIM)
    scores = jnp.einsum(
        "sqhd,skhd->shqk",
        split_heads[:, :, 0],
        split_heads[:, :, 1],
        preferred_element_type=jnp.float32,
    ) * HEAD_DIM ** (-0.5)
    live_keys = jnp.arange(LEN)[None, :] < lengths[:, None]
    return (jnp.where(live_keys[:, None, None, :], scores, -1000000000.0), split_heads)


def attention_forward(pieces, looked, lengths):
    small_rows = pieces["small"].astype(jnp.float32)
    seqs_count = lengths.shape[0]
    rows_here = seqs_count * LEN
    summed = (
        looked.reshape(seqs_count, LEN, D) + pieces["place"].astype(jnp.float32)[None]
    ).reshape(rows_here, D)
    first_norm, normed_zero, inverse_zero = norm_forward(summed, small_rows[4], small_rows[5])
    inputs = first_norm.astype(jnp.bfloat16)
    qkv_bias = jnp.concatenate([small_rows[0], jnp.zeros((D,), jnp.float32), small_rows[1]])
    projected = (array_multiply(inputs, pieces["qkv"]) + qkv_bias).astype(jnp.bfloat16)
    scores, split_heads = key_scores(projected, lengths)
    peak = jnp.max(scores, axis=-1, keepdims=True)
    exps = jnp.exp(scores - peak)
    totals = jnp.sum(exps, axis=-1, keepdims=True)
    probabilities = (exps / totals).astype(jnp.bfloat16)
    logsum = peak + jnp.log(totals)
    context = jnp.einsum(
        "shqk,skhd->sqhd", probabilities, split_heads[:, :, 2], preferred_element_type=jnp.float32
    )
    context = context.reshape(rows_here, D).astype(jnp.bfloat16)
    attended = array_multiply(context, pieces["out"]) + small_rows[2]
    middle, normed_one, inverse_one = norm_forward(
        first_norm + attended, small_rows[6], small_rows[7]
    )
    saved = {
        "inputs": inputs,
        "projected": projected,
        "logsum": logsum,
        "context": context,
        "normed_zero": normed_zero,
        "inverse_zero": inverse_zero,
        "normed_one": normed_one,
        "inverse_one": inverse_one,
    }
    return middle, saved


def feed_forward(pieces, middle, saved):
    small_rows = pieces["small"]
    middle_low = middle.astype(jnp.bfloat16)
    hidden = array_multiply(middle_low, pieces["up"]) + pieces["upbias"].astype(jnp.float32)
    activated = jax.nn.gelu(hidden, approximate=False).astype(jnp.bfloat16)
    output = array_multiply(activated, pieces["down"]) + small_rows[3]
    final_lines, normed_two, inverse_two = norm_forward(
        middle + output, small_rows[8], small_rows[9]
    )
    saved = {
        **saved,
        "middle_low": middle_low,
        "hidden": hidden,
        "activated": activated,
        "normed_two": normed_two,
        "inverse_two": inverse_two,
    }
    return (final_lines, saved)


def feed_backward(pieces, saved, grad_final, flow):
    small_rows = pieces["small"]
    grad_sum_two, grad_gain_two, grad_shift_two = norm_backward(
        grad_final, saved["normed_two"], saved["inverse_two"], small_rows[8]
    )
    grad_out = grad_sum_two.astype(jnp.bfloat16)
    flow.add_product(saved["activated"], grad_out)
    grad_act = trailing_array_multiply(grad_out, pieces["down"])
    grad_hidden = (grad_act * gelu_slope(saved["hidden"])).astype(jnp.bfloat16)
    flow.add_product(saved["middle_low"], grad_hidden)
    grad_middle = grad_sum_two + trailing_array_multiply(grad_hidden, pieces["up"])
    grad_sum_one, grad_gain_one, grad_shift_one = norm_backward(
        grad_middle, saved["normed_one"], saved["inverse_one"], small_rows[6]
    )
    grad_upbias = jnp.sum(grad_hidden.astype(jnp.float32), axis=0)
    (grad_sum_one,) = flow.advance(grad_sum_one)
    return (
        grad_sum_one,
        [jnp.sum(grad_out.astype(jnp.float32), axis=0), grad_gain_one, grad_shift_one, grad_gain_two, grad_shift_two],
        grad_upbias,
    )


def attention_backward(pieces, saved, grad_sum_one, grad_small, grad_upbias, lengths, tail_rows, flow, head_part):
    small_rows = pieces["small"]
    seqs_count = lengths.shape[0]
    rows_here = seqs_count * LEN
    grad_att = grad_sum_one.astype(jnp.bfloat16)
    grad_outw = matmul_left(saved["context"], grad_att)
    grad_context = (
        trailing_array_multiply(grad_att, pieces["out"])
        .astype(jnp.bfloat16)
        .reshape(seqs_count, LEN, HEADS, HEAD_DIM)
    )
    scores, split_heads = key_scores(saved["projected"], lengths)
    probabilities = jnp.exp(scores - saved["logsum"])
    grad_probs = jnp.einsum(
        "sqhd,skhd->shqk", grad_context, split_heads[:, :, 2], preferred_element_type=jnp.float32
    )
    grad_values = jnp.einsum(
        "shqk,sqhd->skhd",
        probabilities.astype(jnp.bfloat16),
        grad_context,
        preferred_element_type=jnp.float32,
    )
    grad_values, grad_probs = flow.advance(grad_values, grad_probs)
    grad_scores = probabilities * (
        grad_probs - jnp.sum(grad_probs * probabilities, axis=-1, keepdims=True)
    )
    (grad_scores,) = flow.advance(grad_scores.astype(jnp.bfloat16))
    grad_queries = jnp.einsum(
        "shqk,skhd->sqhd", grad_scores, split_heads[:, :, 1], preferred_element_type=jnp.float32
    ) * HEAD_DIM ** (-0.5)
    grad_keys = jnp.einsum(
        "shqk,sqhd->skhd", grad_scores, split_heads[:, :, 0], preferred_element_type=jnp.float32
    ) * HEAD_DIM ** (-0.5)
    grad_proj = (
        jnp.stack([grad_queries, grad_keys, grad_values], axis=2)
        .reshape(rows_here, 3 * D)
        .astype(jnp.bfloat16)
    )
    if flow.near:
        grad_proj, head_part = together(grad_proj, head_part)
    flow.add_product(saved["inputs"], grad_proj)
    grad_bias_all = jnp.sum(grad_proj.astype(jnp.float32), axis=0)
    grad_first = grad_sum_one + trailing_array_multiply(grad_proj, pieces["qkv"])
    grad_embedded, grad_gain_zero, grad_shift_zero = norm_backward(
        grad_first, saved["normed_zero"], saved["inverse_zero"], small_rows[4]
    )
    grad_place = jnp.sum(grad_embedded.reshape(seqs_count, LEN, D), axis=0)
    grad_small = jnp.stack(
        [
            grad_bias_all[:D],
            grad_bias_all[2 * D :],
            jnp.sum(grad_att.astype(jnp.float32), axis=0),
            grad_small[0],
            grad_gain_zero,
            grad_shift_zero,
            *grad_small[1:],
        ]
    )
    tail = jnp.concatenate(
        [
            grad_small.reshape(60, TILE),
            grad_upbias.reshape(24, TILE),
            jnp.zeros((tail_rows - 84, TILE), jnp.float32),
        ]
    )
    (grad_embedded,) = flow.advance(grad_embedded)
    flow.add_rest(grad_outw, grad_place, tail)
    return grad_embedded, head_part


def combine_stats(earlier, later):
    peak_s = jnp.maximum(earlier[0], later[0])
    peak_t = jnp.maximum(earlier[2], later[2])
    factor_early = jnp.exp(earlier[0] - peak_s)
    factor_late = jnp.exp(later[0] - peak_s)
    teacher_early = jnp.exp(earlier[2] - peak_t)
    teacher_late = jnp.exp(later[2] - peak_t)
    return jnp.stack(
        [
            peak_s,
            earlier[1] * factor_early + later[1] * factor_late,
            peak_t,
            earlier[3] * teacher_early + later[3] * teacher_late,
            earlier[4] * teacher_early + later[4] * teacher_late,
        ]
    )


def adam_step(weight, first_moment, second, gradient, step_float):
    new_first = beta_first * first_moment + (1.0 - beta_first) * gradient
    new_second = beta_second * second + (1.0 - beta_second) * gradient * gradient
    fix_first = 1.0 - jnp.power(beta_first, step_float)
    fix_second = 1.0 - jnp.power(beta_second, step_float)
    update = new_first / fix_first / (jnp.sqrt(new_second / fix_second) + adam_eps)
    return (weight - learn_rate * (update + weight_decay * weight), new_first, new_second)


def at(value, index, axis):
    return lax.dynamic_index_in_dim(value, index, axis, keepdims=False)


def sent_low(value, bit):
    return swap(value.astype(jnp.bfloat16), bit).astype(jnp.float32)


def bit_of(bit):
    return lax.axis_index("vocab") // bit % 2


def halved(value, axis, bit):
    mine = bit_of(bit)
    return at(value, mine, axis) + sent_low(at(value, 1 - mine, axis), bit)


def reduce_steps(near, far):
    (chip,) = yield [near + swap(far, CORE)]
    chip = chip.reshape(4, 2, 2, chip.shape[0] // CHIPS, chip.shape[1])
    first, second = yield [halved(chip[:2], 2, ACROSS), halved(chip[2:], 1, DEEP)]
    first, second = yield [halved(first, 1, DEEP), halved(second, 1, ACROSS)]
    z = lax.axis_index("dp")
    blocks = [
        jnp.where((z + k) % 4 < 2, at(first, (z + k) % 2, 0), at(second, (z + k) % 2, 0)) for k in range(4)
    ]
    blocks = yield [blocks[0], *(shift(blocks[k], k) for k in (1, 2, 3))]
    return blocks[0] + blocks[1] + blocks[2] + blocks[3]


class Flow:
    near = True

    def __init__(self):
        self.lines, self.waiting, self.sums = [], [], []

    def add(self, near, far):
        self.lines.append(reduce_steps(near, far))
        self.waiting.append(next(self.lines[-1]))
        self.sums.append(None)

    def add_product(self, left, right):
        width = right.shape[1] // 2
        core = bit_of(CORE)
        far = matmul_left(left, lax.dynamic_slice_in_dim(right, (1 - core) * width, width, 1))
        near = matmul_left(left, lax.dynamic_slice_in_dim(right, core * width, width, 1))
        self.add(near, far)

    def add_rest(self, out, place, tail):
        def half(core):
            columns = [
                lax.dynamic_slice_in_dim(whole, core * 384, 384, 1).reshape(CHIPS, -1, 384) for whole in (out, place)
            ]
            ends = jnp.pad(at(tail.reshape(CHIPS, 2, 8, TILE), core, 1), ((0, 0), (0, 0), (0, 256)))
            return jnp.concatenate([*columns, ends], axis=1).reshape(-1, 384)

        self.add(half(bit_of(CORE)), half(1 - bit_of(CORE)))

    def advance(self, *values):
        tied, values = together([moved for moved in self.waiting if moved is not None], list(values))
        tied = list(tied)
        for n, moved in enumerate(self.waiting):
            if moved is not None:
                try:
                    self.waiting[n] = self.lines[n].send(tied.pop(0))
                except StopIteration as stop:
                    self.waiting[n], self.sums[n] = None, stop.value
        return values


class PlainFlow:
    near = False

    def __init__(self, devices):
        self.devices, self.sums = devices, []

    def add_product(self, left, right):
        parts = matmul_left(left, right).reshape(self.devices, -1, TILE)
        self.sums.append(lax.psum_scatter(parts, ("dp", "vocab"), scatter_dimension=0, tiled=False))

    def add_rest(self, out, place, tail):
        parts = [part.reshape(self.devices, -1, TILE) for part in (out, place, tail)]
        parts = jnp.concatenate(parts, axis=1)
        self.sums.append(lax.psum_scatter(parts, ("dp", "vocab"), scatter_dimension=0, tiled=False))

    def advance(self, *values):
        return values


def on_device(
    near,
    token_ids,
    lengths,
    mask_pos,
    mask_count,
    owner_order,
    step_count,
    teacher_flat,
    mentor_lexicon_weights,
    student_flat,
    flat_first,
    flat_second,
    student_embed,
    embed_first,
    embed_second,
):
    per = student_flat.shape[0]
    tiles_all = owner_order.shape[0]
    vocab_rows, width_share = student_embed.shape
    planes = lax.axis_size("dp")
    group = lax.axis_size("vocab")
    here = lax.axis_index("vocab")
    spot = jnp.stack([lax.axis_index("dp"), here]).astype(jnp.int32)
    devices = planes * group
    everywhere = ("dp", "vocab")
    device = lax.axis_index(everywhere)
    capacity = room(per, devices)
    slot_count = devices * capacity

    facts = jnp.concatenate([token_ids.reshape(LEN), lengths, mask_count, jnp.zeros((TILE - 2,), jnp.int32)])
    columns_low = student_embed.T.astype(jnp.bfloat16)
    words = jnp.arange(vocab_rows, dtype=jnp.int32)

    def chosen(ids):
        return (ids.reshape(-1, 1) - here * vocab_rows == words[None]).astype(jnp.bfloat16)

    def rows_t(ids):
        return array_multiply(chosen(ids), mentor_lexicon_weights).astype(jnp.bfloat16)

    def rows_s(ids, table):
        return trailing_array_multiply(chosen(ids), table).astype(jnp.bfloat16)

    def teacher_pieces(tiles):
        return pieces_of(
            [unpack_matrix(tiles, piece) for piece in MATRICES],
            tiles[TAIL : TAIL + TAIL_TILES].astype(jnp.float32),
        )

    homes = homes_of(owner_order, tiles_all, devices, near)
    sizes, starts = shares_of(tiles_all, devices)
    one_of = jnp.arange(devices, dtype=jnp.int32)
    pairs = jnp.sum((homes.reshape(devices, per, 1) // per == one_of).astype(jnp.int32), axis=1)
    crowded = jnp.max(pairs) > capacity
    own_homes = lax.dynamic_slice_in_dim(homes, device * per, per)
    own_target = own_homes // per
    chosen_target = (own_target[:, None] == one_of).astype(jnp.bfloat16)
    lines = jnp.arange(per, dtype=jnp.int32)
    earlier = (lines[None] < lines[:, None]).astype(jnp.bfloat16)
    rank = jnp.sum(array_multiply(earlier, chosen_target) * chosen_target.astype(jnp.float32), axis=1)
    rank = rank.astype(jnp.int32)
    slots = jnp.where(rank < capacity, own_target * capacity + rank, slot_count)
    packed, home_line = send_tiles(slots, own_homes % per, student_flat, slot_count)
    if near:
        teacher_tiles = lax.all_gather(teacher_flat, everywhere, axis=0, tiled=True)
        plane_facts = gather_near(facts)
        shape = (2, 2, LEN, D)
        far = rows_t(plane_facts[4:, :LEN]).reshape(shape)
        columns = [columns_low, shift(columns_low, 1)]
        packed, home_line, far, columns = together(packed, home_line, far, columns)
    packed = lax.all_to_all(packed.reshape(devices, capacity, TILE), everywhere, 0, 0)
    home_line = lax.all_to_all(home_line[:slot_count].reshape(devices, 1, capacity), everywhere, 0, 0)
    home_line = home_line.reshape(slot_count)
    if near:
        looked_t = rows_t(plane_facts[:4, :LEN]).reshape(shape) + swap(far, CORE)
        packed, home_line, looked_t, ahead = together(packed, home_line, looked_t, shift(columns[1], 1))
        columns = [*columns, ahead]
    home_tiles = land_tiles(home_line, packed.reshape(slot_count, TILE), per, starts if near else None)
    if near:
        home_tiles, looked_t, ahead = together(home_tiles, plane_hop(looked_t), shift(columns[2], 1))
        columns = [*columns, ahead]

    def from_everywhere(part):
        copies = jnp.broadcast_to(part[None], (devices, *part.shape))
        return lax.all_to_all(copies, everywhere, 0, 0).reshape(-1, TILE)

    def every_tile(tiles):
        stored = from_everywhere(student_flat.astype(jnp.bfloat16))
        sources = jnp.zeros((tiles_all,), jnp.int32).at[homes].set(jnp.arange(tiles_all, dtype=jnp.int32))
        stored = stored[lax.dynamic_slice_in_dim(sources, device * per, per)]
        if near:
            return land_tiles(lines, stored, per, starts)
        return stored

    home_tiles = lax.cond(crowded, every_tile, lambda tiles: tiles, home_tiles)

    if near:
        layer = lax.all_gather(home_tiles, everywhere, axis=0)
        z = lax.axis_index("dp")
        table_low = jnp.zeros((D, vocab_rows), jnp.bfloat16)
        for k, part in enumerate(columns):
            table_low = lax.dynamic_update_slice(table_low, part, ((z + 4 - k) % 4 * width_share, 0))
        far = rows_s(plane_facts[4:, :LEN], table_low).reshape(shape)
        looked_t, far = together(plane_end(*looked_t).astype(jnp.float32), far)
        close = rows_s(plane_facts[:4, :LEN], table_low).reshape(shape)
        other_facts = gather_near(jnp.stack([shift(facts, 1), shift(facts, 2), shift(facts, 3)]))
        all_facts = jnp.concatenate([plane_facts[:, None], other_facts], axis=1)
        looked_s, teacher_tiles, all_facts = together(close + swap(far, CORE), teacher_tiles, all_facts)
        teacher = teacher_pieces(teacher_tiles)
        teacher, looked_s = together(teacher, plane_hop(looked_s))
        middle, _ = attention_forward(teacher, looked_t, lengths)
        middle, looked_s = together(middle, plane_end(*looked_s).astype(jnp.float32))
        final_t = feed_forward(teacher, middle, {})[0]
        final_t, layer = together(final_t, layer)
        matrices = assemble_layer(layer)
    else:
        table_low = lax.all_gather(columns_low, "dp", axis=0, tiled=True)
        by_plane = lax.all_gather(facts, "dp", axis=0)
        all_facts = lax.all_gather(by_plane, "vocab", axis=0)
        plane_facts = lax.dynamic_index_in_dim(all_facts, lax.axis_index("dp"), 1, keepdims=False)
        teacher_tiles = lax.all_gather(teacher_flat, everywhere, axis=0, tiled=True)
        layer = lax.all_gather(home_tiles, everywhere, axis=0)
        matrices = [
            layer[:, start : start + size].reshape(height, across * TILE)
            for (_, height, across), size, start in zip(HOME_ORDER, sizes, starts)
        ]
        matrices.append(layer[:, starts[-1] :].astype(jnp.float32))
        plane_ids = plane_facts[:, :LEN]
        looked_t, looked_s = (
            lax.psum_scatter(rows, "vocab", scatter_dimension=0, tiled=True).astype(jnp.float32)
            for rows in (rows_t(plane_ids), rows_s(plane_ids, table_low))
        )
        teacher = teacher_pieces(teacher_tiles)
        middle, _ = attention_forward(teacher, looked_t, lengths)
        final_t = feed_forward(teacher, middle, {})[0]
    up, down, qkv, out, place = matrices[:5]
    student = pieces_of((qkv, out, up, down, place), matrices[5].reshape(-1, TILE))
    middle, saved = attention_forward(student, looked_s, lengths)
    offsets = jnp.concatenate([mask_pos.reshape(CAP), jnp.zeros((SLOTS - CAP,), jnp.int32)])
    picked_t = final_t[offsets].astype(jnp.bfloat16)
    if near:
        middle, mentor_picked = together(middle, gather_near(picked_t).reshape(-1, D))
    else:
        mentor_picked = lax.all_gather(picked_t, "vocab", axis=0, tiled=True)
    final_s, saved = feed_forward(student, middle, saved)

    token_total = jnp.sum(all_facts[:, :, LEN]).astype(jnp.float32)
    masked_total = jnp.sum(all_facts[:, :, LEN + 1]).astype(jnp.float32)
    teacher_logit = (
        trailing_array_multiply(mentor_picked, mentor_lexicon_weights) / smoothing_heat_scale
    )
    peak_t = jnp.max(teacher_logit, axis=1)
    picked_s = final_s[offsets].astype(jnp.bfloat16)
    if near:
        learner_picked = gather_split(picked_s).reshape(-1, D)
        learner_picked, teacher_logit, peak_t = together(learner_picked, teacher_logit, peak_t)
    else:
        learner_picked = lax.all_gather(picked_s, "vocab", axis=0, tiled=True)
    live_weighting = (
        (jnp.arange(SLOTS)[None] < plane_facts[:, LEN + 1, None]).astype(jnp.float32).reshape(-1)
    )
    learner_energy = array_multiply(learner_picked, table_low) / smoothing_heat_scale
    peak_s = jnp.max(learner_energy, axis=1)
    teacher_exps = jnp.exp(teacher_logit - peak_t[:, None])
    stats = jnp.stack(
        [
            peak_s,
            jnp.sum(jnp.exp(learner_energy - peak_s[:, None]), axis=1),
            peak_t,
            jnp.sum(teacher_exps, axis=1),
            jnp.sum(teacher_exps * (teacher_logit - learner_energy), axis=1),
        ]
    )
    if near:
        stats = stats.reshape(5, 2, 2, 2, SLOTS)
        for axis, bit in ((1, CORE), (2, DEEP), (3, ACROSS)):
            stats = combine_stats(stats, jnp.flip(swap(stats, bit), axis))
        stats = stats.reshape(5, -1)
    else:
        everything = lax.all_gather(stats, "vocab", axis=0)
        stats = everything[0]
        for k in range(1, group):
            stats = combine_stats(stats, everything[k])
    logsum_s = stats[0] + jnp.log(stats[1])
    logsum_t = stats[2] + jnp.log(stats[3])
    diverge = stats[4] / stats[3] - logsum_t + logsum_s
    mine = 0 if near else here * SLOTS
    divergence_part = jnp.sum(lax.dynamic_slice_in_dim(diverge * live_weighting, mine, SLOTS))
    student_probs = jnp.exp(learner_energy - logsum_s[:, None])
    teacher_probs = jnp.exp(teacher_logit - logsum_t[:, None])
    grad_logit = (
        mixing_coefficient
        * smoothing_heat_scale
        / masked_total
        * live_weighting[:, None]
        * (student_probs - teacher_probs)
    ).astype(jnp.bfloat16)
    if near:
        half = grad_logit.shape[0] // 2
        far = trailing_array_multiply(grad_logit[half:], table_low).reshape(2, 2, SLOTS, D)
        close = trailing_array_multiply(grad_logit[:half], table_low).reshape(2, 2, SLOTS, D)
        grad_rows = plane_end(*plane_hop(close + swap(far, CORE)))
    else:
        grad_rows = lax.psum_scatter(
            trailing_array_multiply(grad_logit, table_low), "vocab", scatter_dimension=0, tiled=True
        )
    head_grad = matmul_left(learner_picked, grad_logit)
    head_grad, grad_rows = together(head_grad, grad_rows)
    head_part = lax.psum_scatter(head_grad, "dp", scatter_dimension=0, tiled=True)
    products = jnp.sum(final_s * final_t, axis=1)
    inverse_s = lax.rsqrt(jnp.sum(final_s * final_s, axis=1) + cosine_eps)
    inverse_t = lax.rsqrt(jnp.sum(final_t * final_t, axis=1) + cosine_eps)
    live_rows = (jnp.arange(LEN)[None, :] < lengths[:, None]).reshape(-1)
    cosine = products * inverse_s * inverse_t
    cosine_term = jnp.sum(jnp.where(live_rows, 1.0 - cosine, 0.0))
    weighting = jnp.where(live_rows, -cosine_weight / token_total, 0.0) * inverse_s * inverse_t
    grad_final = weighting[:, None] * (
        final_t - (products * inverse_s * inverse_s)[:, None] * final_s
    )
    grad_final = grad_final.at[offsets].add(grad_rows)
    flow = Flow() if near else PlainFlow(devices)
    grad_sum_one, grad_small, grad_upbias = feed_backward(student, saved, grad_final, flow)
    grad_embedded, head_part = attention_backward(
        student, saved, grad_sum_one, grad_small, grad_upbias, lengths, tiles_all - TAIL, flow, head_part
    )

    shares = grad_embedded.astype(jnp.bfloat16).reshape(LEN, planes, width_share).transpose(1, 0, 2)
    if near:
        own = upward(shares)
        shares = jnp.stack([own[0]] + [shift(own[k], k) for k in (1, 2, 3)])
        ids = all_facts[:, :, :LEN].reshape(2, 2, 2, planes, LEN)
        for axis, bit in ((0, CORE), (1, DEEP), (2, ACROSS)):
            ids = jnp.where((here & bit) != 0, jnp.flip(ids, axis), ids)
        ids = ids.transpose(1, 2, 0, 3, 4)
    else:
        shares = lax.all_to_all(shares, "dp", 0, 0)
        ids = all_facts[:, :, :LEN]
    token_grads = lax.all_gather(shares.reshape(-1, width_share), "vocab", axis=0, tiled=True)
    (shares,) = flow.advance(shares)
    token_grads = lax.all_gather(shares.reshape(-1, width_share), "vocab", axis=0, tiled=True)
    flow.advance()
    flow.advance()
    flow.advance()
    sum_down, sum_up, sum_qkv, sum_rest = flow.sums
    if near:
        home_grads = share_lines(sum_up, sum_down, sum_qkv, sum_rest, per, starts)
    else:
        home_grads = jnp.concatenate([sum_up, sum_down, sum_qkv, sum_rest])
    returned = pick_tiles(jnp.minimum(home_line, per - 1), home_grads, slot_count)
    returned = lax.all_to_all(returned.reshape(devices, capacity, TILE), everywhere, 0, 0)
    token_part = matmul_left(token_grads, chosen(ids))
    returned, token_part = together(returned, token_part)
    flat_grad = pick_tiles(jnp.minimum(slots, slot_count - 1), returned.reshape(slot_count, TILE), per)
    flat_grad = lax.cond(
        crowded,
        lambda grads: from_everywhere(home_grads)[own_homes],
        lambda grads: grads,
        flat_grad,
    )
    table_grad = (head_part + token_part).T
    loss_term = (
        mixing_coefficient * smoothing_heat_scale**2 * divergence_part / masked_total
        + cosine_weight * cosine_term / token_total
    )
    squares = jnp.sum(flat_grad * flat_grad) + jnp.sum(table_grad * table_grad)
    if near:
        squares, loss_value = sum_everywhere(jnp.stack([squares, loss_term]))
    else:
        squares, loss_value = lax.psum((squares, loss_term), ("dp", "vocab"))
    grad_norm = jnp.sqrt(squares)
    factor = clip_norm / jnp.maximum(grad_norm, clip_norm)
    step_float = step_count[0].astype(jnp.float32)
    new_flat, new_flat_first, new_flat_second = adam_step(
        student_flat, flat_first, flat_second, flat_grad * factor, step_float
    )
    new_embed, new_embed_first, new_embed_second = adam_step(
        student_embed, embed_first, embed_second, table_grad * factor, step_float
    )
    return (
        loss_value,
        grad_norm,
        new_flat,
        new_flat_first,
        new_flat_second,
        new_embed,
        new_embed_first,
        new_embed_second,
    )


def solution(mesh):
    near = mesh.shape["dp"] == 4 and mesh.shape["vocab"] == 8
    return jax.shard_map(
        functools.partial(on_device, near),
        mesh=mesh,
        in_specs=(
            P(("dp", "vocab"), None),
            P(("dp", "vocab")),
            P(("dp", "vocab"), None),
            P(("dp", "vocab")),
            P(),
            P(),
            P(("dp", "vocab"), None),
            P("vocab", None),
            P(("dp", "vocab"), None),
            P(("dp", "vocab"), None),
            P(("dp", "vocab"), None),
            P("vocab", "dp"),
            P("vocab", "dp"),
            P("vocab", "dp"),
        ),
        out_specs=(
            P(),
            P(),
            P(("dp", "vocab"), None),
            P(("dp", "vocab"), None),
            P(("dp", "vocab"), None),
            P("vocab", "dp"),
            P("vocab", "dp"),
            P("vocab", "dp"),
        ),
        check_vma=False,
    )
```

```python
import functools

import jax
import jax.numpy as jnp
from jax import lax
from jax.experimental import pallas as pl
from jax.experimental.pallas import tpu as pltpu
from jax.sharding import PartitionSpec as P

D = 768
HEADS = 12
HEAD_DIM = 64
FF = 3072
LEN = 512
CAP = 120
SLOTS = 128
TILE = 128

QKV = (0, D, 18)
OUT = (13824, D, 6)
UP = (18432, D, 24)
DOWN = (36864, FF, 6)
PLACE = (55296, LEN, 6)
MATRICES = (QKV, OUT, UP, DOWN, PLACE)
TAIL = 58368
TAIL_TILES = 88
HOME_ORDER = (UP, DOWN, QKV, OUT, PLACE)

VMEM_LIMIT = 60 * 1024 * 1024

smoothing_heat_scale = 2.0
mixing_coefficient = 5.0
cosine_weight = 20.0
clip_norm = 0.01
beta_first = 0.9
beta_second = 0.98
adam_eps = 1e-08
weight_decay = 0.01
learn_rate = 0.1
norm_eps = 1e-12
cosine_eps = 1e-06

CHIPS = 16
SLABS = ((0, 48, 1, 12, 0), (48, 48, 4, 3, 0), (96, 48, 1, 9, 0), (96, 48, 1, 3, 9), (144, 16, 2, 3, 0))
SHARE = (160, 1536)
TAIL_AT = (144, 6)
CORE, ACROSS, DEEP = 1, 2, 4


def swap(value, bit):
    return lax.ppermute(value, "vocab", [(i, i ^ bit) for i in range(8)])


def shift(value, steps):
    size = lax.axis_size("dp")
    return lax.ppermute(value, "dp", [(i, (i + steps) % size) for i in range(size)])


def gather_near(value):
    value = value[None]
    for bit in (ACROSS, DEEP, CORE):
        value = jnp.concatenate([value, swap(value, bit)])
    return value


def gather_split(value):
    half = value.shape[0] // 2
    across, deep = swap(value, ACROSS), swap(value, DEEP)
    diagonal = [swap(across[:half], DEEP), swap(deep[half:], ACROSS)]
    plane = jnp.concatenate([value, across, deep, *diagonal])
    return jnp.concatenate([plane, swap(plane, CORE)])


def plane_hop(value):
    half = value.shape[2] // 2
    upper, lower = value[:, :, :half], value[:, :, half:]
    return upper[:, 0] + swap(upper[:, 1], ACROSS), lower[0] + swap(lower[1], DEEP)


def plane_end(upper, lower):
    return jnp.concatenate([upper[0] + swap(upper[1], DEEP), lower[0] + swap(lower[1], ACROSS)])


def together(*values):
    return lax.optimization_barrier(values)


def sum_everywhere(value):
    value = value + swap(value, CORE)
    across, deep, both = (swap(value, bits) for bits in (ACROSS, DEEP, ACROSS | DEEP))
    value = (value + across) + (deep + both)
    near, far, farthest = (
        lax.ppermute(value, "dp", [(i, i ^ step) for i in range(4)]) for step in (1, 2, 3)
    )
    return (value + near) + (far + farthest)


def upward(table):
    z = lax.axis_index("dp")
    return [lax.dynamic_index_in_dim(table, (z + k) % 4, keepdims=False) for k in range(4)]


def shares_of(tiles_all, devices):
    sizes = [height * across // devices for _, height, across in HOME_ORDER]
    sizes.append((tiles_all - TAIL) // devices)
    starts = [sum(sizes[:n]) for n in range(len(sizes))]
    return sizes, starts


def homes_of(tiles, tiles_all, devices, near):
    per = tiles_all // devices
    sizes, starts = shares_of(tiles_all, devices)
    homes = ((tiles - TAIL) // sizes[-1]) * per + starts[-1] + (tiles - TAIL) % sizes[-1]
    for (first, height, across), size, start in zip(HOME_ORDER, sizes, starts):
        at = tiles - first
        inside = (at >= 0) & (at < height * across)
        if near:
            row, column = at // across, at % across
            slab, half = height // CHIPS, across // 2
            owner = row // slab * 2 + column // half
            line = column % half * slab + row % slab
        else:
            owner, line = at // size, at % size
        homes = jnp.where(inside, owner * per + start + line, homes)
    return homes


def room(per, devices):
    mean = per / devices
    return int(-(-(mean + 5.0 * mean**0.5) // 8) * 8)


def row_steps(total, size, step):
    whole, rest = divmod(total, size)

    def body(i, carry):
        step(i * size, size)
        return carry

    lax.fori_loop(0, whole, body, 0)
    if rest:
        step(whole * size, rest)


def send_kernel(slots, lines, tiles, packed, index, stage, *, per):
    slot_count = packed.shape[0]

    def clear(start, size):
        for u in range(size):
            index[start + u] = per

    row_steps(slot_count + 8, 64, clear)
    stage[...] = jnp.zeros_like(stage)

    def place(start, size):
        for u in range(size):
            slot = slots[start + u]
            stage[pl.ds(slot, 1), :] = tiles[pl.ds(start + u, 1), :]
            index[slot] = lines[start + u]

    row_steps(per, 64, place)
    packed[...] = stage[pl.ds(0, slot_count), :].astype(packed.dtype)


def send_tiles(slots, lines, tiles, slot_count):
    per = tiles.shape[0]
    return pl.pallas_call(
        functools.partial(send_kernel, per=per),
        in_specs=[pl.BlockSpec(memory_space=pltpu.SMEM)] * 2 + [pl.BlockSpec(memory_space=pltpu.VMEM)],
        out_specs=[pl.BlockSpec(memory_space=pltpu.VMEM), pl.BlockSpec(memory_space=pltpu.SMEM)],
        out_shape=[
            jax.ShapeDtypeStruct((slot_count, TILE), jnp.bfloat16),
            jax.ShapeDtypeStruct((slot_count + 8,), jnp.int32),
        ],
        scratch_shapes=[pltpu.VMEM((slot_count + 8, TILE), jnp.float32)],
        name="send_tiles",
    )(slots, lines, tiles)


def slab_pieces(starts):
    for (row, lines, groups, columns, offset), start in zip(SLABS, starts):
        for column in range(columns):
            for part in range(groups):
                yield row, offset + part * columns + column, lines, start + (column * groups + part) * lines


def land_kernel(index, packed, tiles, stage, full, *, starts):
    stage[...] = packed[...].astype(jnp.float32)

    def place(start, size):
        for u in range(size):
            full[pl.ds(index[start + u], 1), :] = stage[pl.ds(start + u, 1), :]

    row_steps(packed.shape[0], 128, place)
    if starts is None:
        tiles[...] = full[pl.ds(0, tiles.shape[0]), :].astype(tiles.dtype)
    else:
        tiles[...] = jnp.zeros_like(tiles)
        for row, column, lines, line in (*slab_pieces(starts), (*TAIL_AT, 16, starts[-1])):
            tiles[pl.ds(row, lines), column * TILE : (column + 1) * TILE] = full[pl.ds(line, lines), :].astype(
                tiles.dtype
            )


def land_tiles(index, packed, per, starts):
    slot_count = packed.shape[0]
    return pl.pallas_call(
        functools.partial(land_kernel, starts=starts),
        in_specs=[pl.BlockSpec(memory_space=pltpu.SMEM), pl.BlockSpec(memory_space=pltpu.VMEM)],
        out_specs=pl.BlockSpec(memory_space=pltpu.VMEM),
        out_shape=jax.ShapeDtypeStruct((per, TILE) if starts is None else SHARE, jnp.bfloat16),
        scratch_shapes=[pltpu.VMEM((slot_count, TILE), jnp.float32), pltpu.VMEM((per + 8, TILE), jnp.float32)],
        name="land_tiles",
    )(index, packed)


def share_lines_kernel(up, down, qkv, rest, lines, *, starts):
    slabs = (up, down, qkv, rest, rest)
    first = (0, 0, 0, 0, 48)
    for n, (source, (_, _, _, columns, _), begin, start) in enumerate(zip(slabs, SLABS, first, starts)):
        height = HOME_ORDER[n][1] // CHIPS
        for column in range(columns):
            lines[pl.ds(start + column * height, height), :] = source[
                pl.ds(begin, height), column * TILE : (column + 1) * TILE
            ]
    lines[pl.ds(starts[-1], 8), :] = rest[pl.ds(80, 8), :TILE]


def share_lines(up, down, qkv, rest, per, starts):
    return pl.pallas_call(
        functools.partial(share_lines_kernel, starts=starts),
        in_specs=[pl.BlockSpec(memory_space=pltpu.VMEM)] * 4,
        out_specs=pl.BlockSpec(memory_space=pltpu.VMEM),
        out_shape=jax.ShapeDtypeStruct((per, TILE), jnp.float32),
        name="share_lines",
    )(up, down, qkv, rest)


def pick_kernel(index, source, target, *, count):
    def pick(start, size):
        for u in range(size):
            target[pl.ds(start + u, 1), :] = source[pl.ds(index[start + u], 1), :]

    row_steps(count, 128, pick)


def pick_tiles(index, source, count):
    return pl.pallas_call(
        functools.partial(pick_kernel, count=count),
        in_specs=[pl.BlockSpec(memory_space=pltpu.SMEM), pl.BlockSpec(memory_space=pltpu.VMEM)],
        out_specs=pl.BlockSpec(memory_space=pltpu.VMEM),
        out_shape=jax.ShapeDtypeStruct((count, TILE), source.dtype),
        name="pick_tiles",
    )(index, source)


def assemble_kernel(arrived, up, down, qkv, out, place, tail, landed, sem):
    copy = pltpu.make_async_copy(arrived, landed, sem)
    copy.start()
    copy.wait()

    def one_device(block, carry):
        chip, core = block // 2, block % 2

        def put(target, row, lines, width, source_row, source_column):
            target[
                pl.ds(pl.multiple_of(row, 16), lines), pl.ds(pl.multiple_of(core * width, TILE), width)
            ] = landed[block, pl.ds(source_row, lines), source_column : source_column + width]

        put(up, chip * 48, 48, 1536, 0, 0)
        for part in range(4):
            put(down, chip * 192 + part * 48, 48, 384, 48, part * 384)
        put(qkv, chip * 48, 48, 1152, 96, 0)
        put(out, chip * 48, 48, 384, 96, 1152)
        for part in range(2):
            put(place, chip * 32 + part * 16, 16, 384, 144, part * 384)
        tail[block] = landed[block, pl.ds(TAIL_AT[0], 16), TAIL_AT[1] * TILE : (TAIL_AT[1] + 1) * TILE].astype(
            jnp.float32
        )[:8]
        return carry

    lax.fori_loop(0, landed.shape[0], one_device, 0)


def assemble_layer(arrived):
    devices = arrived.shape[0]
    return pl.pallas_call(
        assemble_kernel,
        in_specs=[pl.BlockSpec(memory_space=pl.ANY)],
        out_specs=[pl.BlockSpec(memory_space=pltpu.VMEM)] * 6,
        out_shape=[jax.ShapeDtypeStruct((h, a * TILE), jnp.bfloat16) for _, h, a in HOME_ORDER]
        + [jax.ShapeDtypeStruct((devices, 8, TILE), jnp.float32)],
        scratch_shapes=[
            pltpu.VMEM((devices, *SHARE), jnp.bfloat16),
            pltpu.SemaphoreType.DMA,
        ],
        compiler_params=pltpu.CompilerParams(vmem_limit_bytes=VMEM_LIMIT),
        cost_estimate=pl.CostEstimate(flops=0, bytes_accessed=60_000_000, transcendentals=0),
        name="assemble_layer",
    )(arrived)


def unpack_kernel(source, target, stage, *, across):
    stage[...] = source[...].astype(jnp.float32)

    def step(g, carry):
        for column in range(across):
            lines = stage[pl.ds(g * 16 * across + column, 16, stride=across), :]
            target[pl.ds(pl.multiple_of(g * 16, 16), 16), column * TILE : (column + 1) * TILE] = lines.astype(
                jnp.bfloat16
            )
        return carry

    lax.fori_loop(0, target.shape[0] // 16, step, 0)


def unpack_matrix(tiles, piece):
    first, height, across = piece
    lines = min(height, 384 if across > 6 else 768)
    block = lines * across
    return pl.pallas_call(
        functools.partial(unpack_kernel, across=across),
        grid=(height // lines,),
        in_specs=[pl.BlockSpec((block, TILE), lambda i: (first // block + i, 0))],
        out_specs=pl.BlockSpec((lines, across * TILE), lambda i: (i, 0)),
        out_shape=jax.ShapeDtypeStruct((height, across * TILE), jnp.bfloat16),
        scratch_shapes=[pltpu.VMEM((block, TILE), jnp.float32)],
        name="unpack_matrix",
    )(tiles)


def array_multiply(left_side, right_side):
    return jnp.dot(left_side, right_side, preferred_element_type=jnp.float32)


def matmul_left(left_side, right_side):
    return lax.dot_general(
        left_side, right_side, (((0,), (0,)), ((), ())), preferred_element_type=jnp.float32
    )


def trailing_array_multiply(left_side, right_side):
    return lax.dot_general(
        left_side, right_side, (((1,), (1,)), ((), ())), preferred_element_type=jnp.float32
    )


def pieces_of(matrices, tail):
    qkv, out, up, down, place = matrices
    return {
        "qkv": qkv,
        "out": out,
        "up": up,
        "down": down,
        "place": place,
        "small": tail[:60].reshape(10, D),
        "upbias": tail[60:84].reshape(FF),
    }


def norm_forward(values, gain_row, shift_row):
    center = values - jnp.mean(values, axis=-1, keepdims=True)
    inverse = lax.rsqrt(jnp.mean(center * center, axis=-1, keepdims=True) + norm_eps)
    normed = center * inverse
    return (normed * gain_row + shift_row, normed, inverse)


def norm_backward(grad_out, normed, inverse, gain_row):
    scaled = grad_out * gain_row
    grad_in = inverse * (
        scaled
        - jnp.mean(scaled, axis=-1, keepdims=True)
        - normed * jnp.mean(scaled * normed, axis=-1, keepdims=True)
    )
    return (grad_in, jnp.sum(grad_out * normed, axis=0), jnp.sum(grad_out, axis=0))


def gelu_slope(values):
    return (
        0.5 * (1.0 + lax.erf(values * 0.7071067811865476))
        + values * jnp.exp(-0.5 * values * values) * 0.3989422804014327
    )


def key_scores(projected, lengths):
    seqs_count = lengths.shape[0]
    split_heads = projected.reshape(seqs_count, LEN, 3, HEADS, HEAD_DIM)
    scores = jnp.einsum(
        "sqhd,skhd->shqk",
        split_heads[:, :, 0],
        split_heads[:, :, 1],
        preferred_element_type=jnp.float32,
    ) * HEAD_DIM ** (-0.5)
    live_keys = jnp.arange(LEN)[None, :] < lengths[:, None]
    return (jnp.where(live_keys[:, None, None, :], scores, -1000000000.0), split_heads)


def attention_forward(pieces, looked, lengths):
    small_rows = pieces["small"].astype(jnp.float32)
    seqs_count = lengths.shape[0]
    rows_here = seqs_count * LEN
    summed = (
        looked.reshape(seqs_count, LEN, D) + pieces["place"].astype(jnp.float32)[None]
    ).reshape(rows_here, D)
    first_norm, normed_zero, inverse_zero = norm_forward(summed, small_rows[4], small_rows[5])
    inputs = first_norm.astype(jnp.bfloat16)
    qkv_bias = jnp.concatenate([small_rows[0], jnp.zeros((D,), jnp.float32), small_rows[1]])
    projected = (array_multiply(inputs, pieces["qkv"]) + qkv_bias).astype(jnp.bfloat16)
    scores, split_heads = key_scores(projected, lengths)
    peak = jnp.max(scores, axis=-1, keepdims=True)
    exps = jnp.exp(scores - peak)
    totals = jnp.sum(exps, axis=-1, keepdims=True)
    probabilities = (exps / totals).astype(jnp.bfloat16)
    logsum = peak + jnp.log(totals)
    context = jnp.einsum(
        "shqk,skhd->sqhd", probabilities, split_heads[:, :, 2], preferred_element_type=jnp.float32
    )
    context = context.reshape(rows_here, D).astype(jnp.bfloat16)
    attended = array_multiply(context, pieces["out"]) + small_rows[2]
    middle, normed_one, inverse_one = norm_forward(
        first_norm + attended, small_rows[6], small_rows[7]
    )
    saved = {
        "inputs": inputs,
        "projected": projected,
        "logsum": logsum,
        "context": context,
        "normed_zero": normed_zero,
        "inverse_zero": inverse_zero,
        "normed_one": normed_one,
        "inverse_one": inverse_one,
    }
    return middle, saved


def feed_forward(pieces, middle, saved):
    small_rows = pieces["small"]
    middle_low = middle.astype(jnp.bfloat16)
    hidden = array_multiply(middle_low, pieces["up"]) + pieces["upbias"].astype(jnp.float32)
    activated = jax.nn.gelu(hidden, approximate=False).astype(jnp.bfloat16)
    output = array_multiply(activated, pieces["down"]) + small_rows[3]
    final_lines, normed_two, inverse_two = norm_forward(
        middle + output, small_rows[8], small_rows[9]
    )
    saved = {
        **saved,
        "middle_low": middle_low,
        "hidden": hidden,
        "activated": activated,
        "normed_two": normed_two,
        "inverse_two": inverse_two,
    }
    return (final_lines, saved)


def feed_backward(pieces, saved, grad_final, flow):
    small_rows = pieces["small"]
    grad_sum_two, grad_gain_two, grad_shift_two = norm_backward(
        grad_final, saved["normed_two"], saved["inverse_two"], small_rows[8]
    )
    grad_out = grad_sum_two.astype(jnp.bfloat16)
    flow.add_product(saved["activated"], grad_out, offload=True)
    grad_act = trailing_array_multiply(grad_out, pieces["down"])
    grad_hidden = (grad_act * gelu_slope(saved["hidden"])).astype(jnp.bfloat16)
    flow.add_product(saved["middle_low"], grad_hidden, offload=True)
    grad_middle = grad_sum_two + trailing_array_multiply(grad_hidden, pieces["up"])
    grad_sum_one, grad_gain_one, grad_shift_one = norm_backward(
        grad_middle, saved["normed_one"], saved["inverse_one"], small_rows[6]
    )
    grad_upbias = jnp.sum(grad_hidden.astype(jnp.float32), axis=0)
    (grad_sum_one,) = flow.advance(grad_sum_one)
    return (
        grad_sum_one,
        [jnp.sum(grad_out.astype(jnp.float32), axis=0), grad_gain_one, grad_shift_one, grad_gain_two, grad_shift_two],
        grad_upbias,
    )


def attention_backward(pieces, saved, grad_sum_one, grad_small, grad_upbias, lengths, tail_rows, flow, head_part):
    small_rows = pieces["small"]
    seqs_count = lengths.shape[0]
    rows_here = seqs_count * LEN
    grad_att = grad_sum_one.astype(jnp.bfloat16)
    grad_outw = matmul_left(saved["context"], grad_att)
    grad_context = (
        trailing_array_multiply(grad_att, pieces["out"])
        .astype(jnp.bfloat16)
        .reshape(seqs_count, LEN, HEADS, HEAD_DIM)
    )
    scores, split_heads = key_scores(saved["projected"], lengths)
    probabilities = jnp.exp(scores - saved["logsum"])
    grad_probs = jnp.einsum(
        "sqhd,skhd->shqk", grad_context, split_heads[:, :, 2], preferred_element_type=jnp.float32
    )
    grad_values = jnp.einsum(
        "shqk,sqhd->skhd",
        probabilities.astype(jnp.bfloat16),
        grad_context,
        preferred_element_type=jnp.float32,
    )
    grad_values, grad_probs = flow.advance(grad_values, grad_probs)
    grad_scores = probabilities * (
        grad_probs - jnp.sum(grad_probs * probabilities, axis=-1, keepdims=True)
    )
    grad_scores, head_part = flow.advance(grad_scores.astype(jnp.bfloat16), head_part)
    grad_queries = jnp.einsum(
        "shqk,skhd->sqhd", grad_scores, split_heads[:, :, 1], preferred_element_type=jnp.float32
    ) * HEAD_DIM ** (-0.5)
    grad_keys = jnp.einsum(
        "shqk,sqhd->skhd", grad_scores, split_heads[:, :, 0], preferred_element_type=jnp.float32
    ) * HEAD_DIM ** (-0.5)
    grad_proj = (
        jnp.stack([grad_queries, grad_keys, grad_values], axis=2)
        .reshape(rows_here, 3 * D)
        .astype(jnp.bfloat16)
    )
    flow.add_product(saved["inputs"], grad_proj)
    grad_bias_all = jnp.sum(grad_proj.astype(jnp.float32), axis=0)
    grad_first = grad_sum_one + trailing_array_multiply(grad_proj, pieces["qkv"])
    grad_embedded, grad_gain_zero, grad_shift_zero = norm_backward(
        grad_first, saved["normed_zero"], saved["inverse_zero"], small_rows[4]
    )
    grad_place = jnp.sum(grad_embedded.reshape(seqs_count, LEN, D), axis=0)
    grad_small = jnp.stack(
        [
            grad_bias_all[:D],
            grad_bias_all[2 * D :],
            jnp.sum(grad_att.astype(jnp.float32), axis=0),
            grad_small[0],
            grad_gain_zero,
            grad_shift_zero,
            *grad_small[1:],
        ]
    )
    tail = jnp.concatenate(
        [
            grad_small.reshape(60, TILE),
            grad_upbias.reshape(24, TILE),
            jnp.zeros((tail_rows - 84, TILE), jnp.float32),
        ]
    )
    (grad_embedded,) = flow.advance(grad_embedded)
    flow.add_rest(grad_outw, grad_place, tail)
    return grad_embedded, head_part


def combine_stats(earlier, later):
    peak_s = jnp.maximum(earlier[0], later[0])
    peak_t = jnp.maximum(earlier[2], later[2])
    factor_early = jnp.exp(earlier[0] - peak_s)
    factor_late = jnp.exp(later[0] - peak_s)
    teacher_early = jnp.exp(earlier[2] - peak_t)
    teacher_late = jnp.exp(later[2] - peak_t)
    return jnp.stack(
        [
            peak_s,
            earlier[1] * factor_early + later[1] * factor_late,
            peak_t,
            earlier[3] * teacher_early + later[3] * teacher_late,
            earlier[4] * teacher_early + later[4] * teacher_late,
        ]
    )


def adam_step(weight, first_moment, second, gradient, step_float):
    new_first = beta_first * first_moment + (1.0 - beta_first) * gradient
    new_second = beta_second * second + (1.0 - beta_second) * gradient * gradient
    fix_first = 1.0 - jnp.power(beta_first, step_float)
    fix_second = 1.0 - jnp.power(beta_second, step_float)
    update = new_first / fix_first / (jnp.sqrt(new_second / fix_second) + adam_eps)
    return (weight - learn_rate * (update + weight_decay * weight), new_first, new_second)


def at(value, index, axis):
    return lax.dynamic_index_in_dim(value, index, axis, keepdims=False)


def sent_low(value, bit):
    return swap(value.astype(jnp.bfloat16), bit).astype(jnp.float32)


def bit_of(bit):
    return lax.axis_index("vocab") // bit % 2


def halved(value, axis, bit):
    mine = bit_of(bit)
    return at(value, mine, axis) + sent_low(at(value, 1 - mine, axis), bit)


def reduce_steps(near, far, offload):
    (chip,) = yield [near + swap(far, CORE)]
    chip = chip.reshape(4, 2, 2, chip.shape[0] // CHIPS, chip.shape[1])
    first, second = yield [halved(chip[:2], 2, ACROSS), halved(chip[2:], 1, DEEP)]
    first, second = yield [halved(first, 1, DEEP), halved(second, 1, ACROSS)]
    if offload:
        total = lax.psum_scatter(jnp.concatenate([first, second]), "dp", scatter_dimension=0, tiled=False)
        yield []
        (total,) = yield [total]
        return total
    z = lax.axis_index("dp")
    blocks = [
        jnp.where((z + k) % 4 < 2, at(first, (z + k) % 2, 0), at(second, (z + k) % 2, 0)) for k in range(4)
    ]
    blocks = yield [blocks[0], *(shift(blocks[k], k) for k in (1, 2, 3))]
    return blocks[0] + blocks[1] + blocks[2] + blocks[3]


class Flow:
    near = True

    def __init__(self):
        self.lines, self.waiting, self.sums = [], [], []

    def add(self, near, far, offload=False):
        self.lines.append(reduce_steps(near, far, offload))
        self.waiting.append(next(self.lines[-1]))
        self.sums.append(None)

    def add_product(self, left, right, offload=False):
        width = right.shape[1] // 2
        core = bit_of(CORE)
        far = matmul_left(left, lax.dynamic_slice_in_dim(right, (1 - core) * width, width, 1))
        near = matmul_left(left, lax.dynamic_slice_in_dim(right, core * width, width, 1))
        self.add(near, far, offload)

    def add_rest(self, out, place, tail):
        def half(core):
            columns = [
                lax.dynamic_slice_in_dim(whole, core * 384, 384, 1).reshape(CHIPS, -1, 384) for whole in (out, place)
            ]
            ends = jnp.pad(at(tail.reshape(CHIPS, 2, 8, TILE), core, 1), ((0, 0), (0, 0), (0, 256)))
            return jnp.concatenate([*columns, ends], axis=1).reshape(-1, 384)

        self.add(half(bit_of(CORE)), half(1 - bit_of(CORE)))

    def advance(self, *values):
        tied, values = together([moved for moved in self.waiting if moved is not None], list(values))
        tied = list(tied)
        for n, moved in enumerate(self.waiting):
            if moved is not None:
                try:
                    self.waiting[n] = self.lines[n].send(tied.pop(0))
                except StopIteration as stop:
                    self.waiting[n], self.sums[n] = None, stop.value
        return values


class PlainFlow:
    near = False

    def __init__(self, devices):
        self.devices, self.sums = devices, []

    def add_product(self, left, right, offload=False):
        parts = matmul_left(left, right).reshape(self.devices, -1, TILE)
        self.sums.append(lax.psum_scatter(parts, ("dp", "vocab"), scatter_dimension=0, tiled=False))

    def add_rest(self, out, place, tail):
        parts = [part.reshape(self.devices, -1, TILE) for part in (out, place, tail)]
        parts = jnp.concatenate(parts, axis=1)
        self.sums.append(lax.psum_scatter(parts, ("dp", "vocab"), scatter_dimension=0, tiled=False))

    def advance(self, *values):
        return values


def on_device(
    near,
    token_ids,
    lengths,
    mask_pos,
    mask_count,
    owner_order,
    step_count,
    teacher_flat,
    mentor_lexicon_weights,
    student_flat,
    flat_first,
    flat_second,
    student_embed,
    embed_first,
    embed_second,
):
    per = student_flat.shape[0]
    tiles_all = owner_order.shape[0]
    vocab_rows, width_share = student_embed.shape
    planes = lax.axis_size("dp")
    group = lax.axis_size("vocab")
    here = lax.axis_index("vocab")
    spot = jnp.stack([lax.axis_index("dp"), here]).astype(jnp.int32)
    devices = planes * group
    everywhere = ("dp", "vocab")
    device = lax.axis_index(everywhere)
    capacity = room(per, devices)
    slot_count = devices * capacity

    facts = jnp.concatenate([token_ids.reshape(LEN), lengths, mask_count, jnp.zeros((TILE - 2,), jnp.int32)])
    columns_low = student_embed.T.astype(jnp.bfloat16)
    words = jnp.arange(vocab_rows, dtype=jnp.int32)

    def chosen(ids):
        return (ids.reshape(-1, 1) - here * vocab_rows == words[None]).astype(jnp.bfloat16)

    def rows_t(ids):
        return array_multiply(chosen(ids), mentor_lexicon_weights).astype(jnp.bfloat16)

    def rows_s(ids, table):
        return trailing_array_multiply(chosen(ids), table).astype(jnp.bfloat16)

    def teacher_pieces(tiles):
        return pieces_of(
            [unpack_matrix(tiles, piece) for piece in MATRICES],
            tiles[TAIL : TAIL + TAIL_TILES].astype(jnp.float32),
        )

    homes = homes_of(owner_order, tiles_all, devices, near)
    sizes, starts = shares_of(tiles_all, devices)
    one_of = jnp.arange(devices, dtype=jnp.int32)
    pairs = jnp.sum((homes.reshape(devices, per, 1) // per == one_of).astype(jnp.int32), axis=1)
    crowded = jnp.max(pairs) > capacity
    own_homes = lax.dynamic_slice_in_dim(homes, device * per, per)
    own_target = own_homes // per
    chosen_target = (own_target[:, None] == one_of).astype(jnp.bfloat16)
    lines = jnp.arange(per, dtype=jnp.int32)
    earlier = (lines[None] < lines[:, None]).astype(jnp.bfloat16)
    rank = jnp.sum(array_multiply(earlier, chosen_target) * chosen_target.astype(jnp.float32), axis=1)
    rank = rank.astype(jnp.int32)
    slots = jnp.where(rank < capacity, own_target * capacity + rank, slot_count)
    packed, home_line = send_tiles(slots, own_homes % per, student_flat, slot_count)
    if near:
        teacher_tiles = lax.all_gather(teacher_flat, everywhere, axis=0, tiled=True)
        plane_facts = gather_near(facts)
        shape = (2, 2, LEN, D)
        far = rows_t(plane_facts[4:, :LEN]).reshape(shape)
        columns = [columns_low, shift(columns_low, 1)]
        packed, home_line, far, columns = together(packed, home_line, far, columns)
    packed = lax.all_to_all(packed.reshape(devices, capacity, TILE), everywhere, 0, 0)
    home_line = lax.all_to_all(home_line[:slot_count].reshape(devices, 1, capacity), everywhere, 0, 0)
    home_line = home_line.reshape(slot_count)
    if near:
        looked_t = rows_t(plane_facts[:4, :LEN]).reshape(shape) + swap(far, CORE)
        packed, home_line, looked_t, ahead = together(packed, home_line, looked_t, shift(columns[1], 1))
        columns = [*columns, ahead]
    home_tiles = land_tiles(home_line, packed.reshape(slot_count, TILE), per, starts if near else None)
    if near:
        home_tiles, looked_t, ahead = together(home_tiles, plane_hop(looked_t), shift(columns[2], 1))
        columns = [*columns, ahead]

    def from_everywhere(part):
        copies = jnp.broadcast_to(part[None], (devices, *part.shape))
        return lax.all_to_all(copies, everywhere, 0, 0).reshape(-1, TILE)

    def every_tile(tiles):
        stored = from_everywhere(student_flat.astype(jnp.bfloat16))
        sources = jnp.zeros((tiles_all,), jnp.int32).at[homes].set(jnp.arange(tiles_all, dtype=jnp.int32))
        stored = stored[lax.dynamic_slice_in_dim(sources, device * per, per)]
        if near:
            return land_tiles(lines, stored, per, starts)
        return stored

    home_tiles = lax.cond(crowded, every_tile, lambda tiles: tiles, home_tiles)

    if near:
        layer = lax.all_gather(home_tiles, everywhere, axis=0)
        z = lax.axis_index("dp")
        table_low = jnp.zeros((D, vocab_rows), jnp.bfloat16)
        for k, part in enumerate(columns):
            table_low = lax.dynamic_update_slice(table_low, part, ((z + 4 - k) % 4 * width_share, 0))
        far = rows_s(plane_facts[4:, :LEN], table_low).reshape(shape)
        looked_t, far = together(plane_end(*looked_t).astype(jnp.float32), far)
        close = rows_s(plane_facts[:4, :LEN], table_low).reshape(shape)
        other_facts = gather_near(jnp.stack([shift(facts, 1), shift(facts, 2), shift(facts, 3)]))
        all_facts = jnp.concatenate([plane_facts[:, None], other_facts], axis=1)
        looked_s, teacher_tiles, all_facts = together(close + swap(far, CORE), teacher_tiles, all_facts)
        teacher = teacher_pieces(teacher_tiles)
        teacher, looked_s = together(teacher, plane_hop(looked_s))
        middle, _ = attention_forward(teacher, looked_t, lengths)
        middle, looked_s = together(middle, plane_end(*looked_s).astype(jnp.float32))
        final_t = feed_forward(teacher, middle, {})[0]
        final_t, layer = together(final_t, layer)
        matrices = assemble_layer(layer)
    else:
        table_low = lax.all_gather(columns_low, "dp", axis=0, tiled=True)
        by_plane = lax.all_gather(facts, "dp", axis=0)
        all_facts = lax.all_gather(by_plane, "vocab", axis=0)
        plane_facts = lax.dynamic_index_in_dim(all_facts, lax.axis_index("dp"), 1, keepdims=False)
        teacher_tiles = lax.all_gather(teacher_flat, everywhere, axis=0, tiled=True)
        layer = lax.all_gather(home_tiles, everywhere, axis=0)
        matrices = [
            layer[:, start : start + size].reshape(height, across * TILE)
            for (_, height, across), size, start in zip(HOME_ORDER, sizes, starts)
        ]
        matrices.append(layer[:, starts[-1] :].astype(jnp.float32))
        plane_ids = plane_facts[:, :LEN]
        looked_t, looked_s = (
            lax.psum_scatter(rows, "vocab", scatter_dimension=0, tiled=True).astype(jnp.float32)
            for rows in (rows_t(plane_ids), rows_s(plane_ids, table_low))
        )
        teacher = teacher_pieces(teacher_tiles)
        middle, _ = attention_forward(teacher, looked_t, lengths)
        final_t = feed_forward(teacher, middle, {})[0]
    up, down, qkv, out, place = matrices[:5]
    student = pieces_of((qkv, out, up, down, place), matrices[5].reshape(-1, TILE))
    middle, saved = attention_forward(student, looked_s, lengths)
    offsets = jnp.concatenate([mask_pos.reshape(CAP), jnp.zeros((SLOTS - CAP,), jnp.int32)])
    picked_t = final_t[offsets].astype(jnp.bfloat16)
    if near:
        middle, mentor_picked = together(middle, gather_near(picked_t).reshape(-1, D))
    else:
        mentor_picked = lax.all_gather(picked_t, "vocab", axis=0, tiled=True)
    final_s, saved = feed_forward(student, middle, saved)

    token_total = jnp.sum(all_facts[:, :, LEN]).astype(jnp.float32)
    masked_total = jnp.sum(all_facts[:, :, LEN + 1]).astype(jnp.float32)
    teacher_logit = (
        trailing_array_multiply(mentor_picked, mentor_lexicon_weights) / smoothing_heat_scale
    )
    peak_t = jnp.max(teacher_logit, axis=1)
    picked_s = final_s[offsets].astype(jnp.bfloat16)
    if near:
        learner_picked = gather_split(picked_s).reshape(-1, D)
        learner_picked, teacher_logit, peak_t = together(learner_picked, teacher_logit, peak_t)
    else:
        learner_picked = lax.all_gather(picked_s, "vocab", axis=0, tiled=True)
    live_weighting = (
        (jnp.arange(SLOTS)[None] < plane_facts[:, LEN + 1, None]).astype(jnp.float32).reshape(-1)
    )
    learner_energy = array_multiply(learner_picked, table_low) / smoothing_heat_scale
    peak_s = jnp.max(learner_energy, axis=1)
    teacher_exps = jnp.exp(teacher_logit - peak_t[:, None])
    stats = jnp.stack(
        [
            peak_s,
            jnp.sum(jnp.exp(learner_energy - peak_s[:, None]), axis=1),
            peak_t,
            jnp.sum(teacher_exps, axis=1),
            jnp.sum(teacher_exps * (teacher_logit - learner_energy), axis=1),
        ]
    )
    if near:
        stats = stats.reshape(5, 2, 2, 2, SLOTS)
        stats = combine_stats(stats, jnp.flip(swap(stats, CORE), 1))
        across, deep, both = (
            jnp.flip(swap(stats, bits), axes)
            for bits, axes in ((ACROSS, 3), (DEEP, 2), (ACROSS | DEEP, (2, 3)))
        )
        stats = combine_stats(combine_stats(stats, across), combine_stats(deep, both))
        stats = stats.reshape(5, -1)
    else:
        everything = lax.all_gather(stats, "vocab", axis=0)
        stats = everything[0]
        for k in range(1, group):
            stats = combine_stats(stats, everything[k])
    logsum_s = stats[0] + jnp.log(stats[1])
    logsum_t = stats[2] + jnp.log(stats[3])
    diverge = stats[4] / stats[3] - logsum_t + logsum_s
    mine = 0 if near else here * SLOTS
    divergence_part = jnp.sum(lax.dynamic_slice_in_dim(diverge * live_weighting, mine, SLOTS))
    student_probs = jnp.exp(learner_energy - logsum_s[:, None])
    teacher_probs = jnp.exp(teacher_logit - logsum_t[:, None])
    grad_logit = (
        mixing_coefficient
        * smoothing_heat_scale
        / masked_total
        * live_weighting[:, None]
        * (student_probs - teacher_probs)
    ).astype(jnp.bfloat16)
    if near:
        half = grad_logit.shape[0] // 2
        far = trailing_array_multiply(grad_logit[half:], table_low).reshape(2, 2, SLOTS, D)
        close = trailing_array_multiply(grad_logit[:half], table_low).reshape(2, 2, SLOTS, D)
        grad_rows = plane_end(*plane_hop(close + swap(far, CORE)))
    else:
        grad_rows = lax.psum_scatter(
            trailing_array_multiply(grad_logit, table_low), "vocab", scatter_dimension=0, tiled=True
        )
    head_grad = matmul_left(learner_picked, grad_logit)
    head_grad, grad_rows = together(head_grad, grad_rows)
    head_part = lax.psum_scatter(head_grad, "dp", scatter_dimension=0, tiled=True)
    products = jnp.sum(final_s * final_t, axis=1)
    inverse_s = lax.rsqrt(jnp.sum(final_s * final_s, axis=1) + cosine_eps)
    inverse_t = lax.rsqrt(jnp.sum(final_t * final_t, axis=1) + cosine_eps)
    live_rows = (jnp.arange(LEN)[None, :] < lengths[:, None]).reshape(-1)
    cosine = products * inverse_s * inverse_t
    cosine_term = jnp.sum(jnp.where(live_rows, 1.0 - cosine, 0.0))
    weighting = jnp.where(live_rows, -cosine_weight / token_total, 0.0) * inverse_s * inverse_t
    grad_final = weighting[:, None] * (
        final_t - (products * inverse_s * inverse_s)[:, None] * final_s
    )
    grad_final = grad_final.at[offsets].add(grad_rows)
    flow = Flow() if near else PlainFlow(devices)
    grad_sum_one, grad_small, grad_upbias = feed_backward(student, saved, grad_final, flow)
    grad_embedded, head_part = attention_backward(
        student, saved, grad_sum_one, grad_small, grad_upbias, lengths, tiles_all - TAIL, flow, head_part
    )

    shares = grad_embedded.astype(jnp.bfloat16).reshape(LEN, planes, width_share).transpose(1, 0, 2)
    if near:
        own = upward(shares)
        shares = jnp.stack([own[0]] + [shift(own[k], k) for k in (1, 2, 3)])
        ids = all_facts[:, :, :LEN].reshape(2, 2, 2, planes, LEN)
        for axis, bit in ((0, CORE), (1, DEEP), (2, ACROSS)):
            ids = jnp.where((here & bit) != 0, jnp.flip(ids, axis), ids)
        ids = ids.transpose(1, 2, 0, 3, 4)
    else:
        shares = lax.all_to_all(shares, "dp", 0, 0)
        ids = all_facts[:, :, :LEN]
    token_grads = lax.all_gather(shares.reshape(-1, width_share), "vocab", axis=0, tiled=True)
    (shares,) = flow.advance(shares)
    token_grads = lax.all_gather(shares.reshape(-1, width_share), "vocab", axis=0, tiled=True)
    flow.advance()
    flow.advance()
    flow.advance()
    sum_down, sum_up, sum_qkv, sum_rest = flow.sums
    if near:
        home_grads = share_lines(sum_up, sum_down, sum_qkv, sum_rest, per, starts)
    else:
        home_grads = jnp.concatenate([sum_up, sum_down, sum_qkv, sum_rest])
    returned = pick_tiles(jnp.minimum(home_line, per - 1), home_grads, slot_count)
    returned = lax.all_to_all(returned.reshape(devices, capacity, TILE), everywhere, 0, 0)
    token_part = matmul_left(token_grads, chosen(ids))
    returned, token_part = together(returned, token_part)
    flat_grad = pick_tiles(jnp.minimum(slots, slot_count - 1), returned.reshape(slot_count, TILE), per)
    flat_grad = lax.cond(
        crowded,
        lambda grads: from_everywhere(home_grads)[own_homes],
        lambda grads: grads,
        flat_grad,
    )
    table_grad = (head_part + token_part).T
    loss_term = (
        mixing_coefficient * smoothing_heat_scale**2 * divergence_part / masked_total
        + cosine_weight * cosine_term / token_total
    )
    squares = jnp.sum(flat_grad * flat_grad) + jnp.sum(table_grad * table_grad)
    if near:
        squares, loss_value = sum_everywhere(jnp.stack([squares, loss_term]))
    else:
        squares, loss_value = lax.psum((squares, loss_term), ("dp", "vocab"))
    grad_norm = jnp.sqrt(squares)
    factor = clip_norm / jnp.maximum(grad_norm, clip_norm)
    step_float = step_count[0].astype(jnp.float32)
    new_flat, new_flat_first, new_flat_second = adam_step(
        student_flat, flat_first, flat_second, flat_grad * factor, step_float
    )
    new_embed, new_embed_first, new_embed_second = adam_step(
        student_embed, embed_first, embed_second, table_grad * factor, step_float
    )
    return (
        loss_value,
        grad_norm,
        new_flat,
        new_flat_first,
        new_flat_second,
        new_embed,
        new_embed_first,
        new_embed_second,
    )


def solution(mesh):
    near = mesh.shape["dp"] == 4 and mesh.shape["vocab"] == 8
    return jax.shard_map(
        functools.partial(on_device, near),
        mesh=mesh,
        in_specs=(
            P(("dp", "vocab"), None),
            P(("dp", "vocab")),
            P(("dp", "vocab"), None),
            P(("dp", "vocab")),
            P(),
            P(),
            P(("dp", "vocab"), None),
            P("vocab", None),
            P(("dp", "vocab"), None),
            P(("dp", "vocab"), None),
            P(("dp", "vocab"), None),
            P("vocab", "dp"),
            P("vocab", "dp"),
            P("vocab", "dp"),
        ),
        out_specs=(
            P(),
            P(),
            P(("dp", "vocab"), None),
            P(("dp", "vocab"), None),
            P(("dp", "vocab"), None),
            P("vocab", "dp"),
            P("vocab", "dp"),
            P("vocab", "dp"),
        ),
        check_vma=False,
    )
```

```python
import functools

import jax
import jax.numpy as jnp
from jax import lax
from jax.experimental import pallas as pl
from jax.experimental.pallas import tpu as pltpu
from jax.sharding import PartitionSpec as P

D = 768
HEADS = 12
HEAD_DIM = 64
FF = 3072
LEN = 512
CAP = 120
SLOTS = 128
TILE = 128

QKV = (0, D, 18)
OUT = (13824, D, 6)
UP = (18432, D, 24)
DOWN = (36864, FF, 6)
PLACE = (55296, LEN, 6)
MATRICES = (QKV, OUT, UP, DOWN, PLACE)
TAIL = 58368
TAIL_TILES = 88
HOME_ORDER = (UP, DOWN, QKV, OUT, PLACE)

VMEM_LIMIT = 60 * 1024 * 1024

smoothing_heat_scale = 2.0
mixing_coefficient = 5.0
cosine_weight = 20.0
clip_norm = 0.01
beta_first = 0.9
beta_second = 0.98
adam_eps = 1e-08
weight_decay = 0.01
learn_rate = 0.1
norm_eps = 1e-12
cosine_eps = 1e-06

CHIPS = 16
SLABS = ((0, 48, 1, 12, 0), (48, 48, 4, 3, 0), (96, 48, 1, 9, 0), (96, 48, 1, 3, 9), (144, 16, 2, 3, 0))
SHARE = (160, 1536)
TAIL_AT = (144, 6)
CORE, ACROSS, DEEP = 1, 2, 4


def swap(value, bit):
    return lax.ppermute(value, "vocab", [(i, i ^ bit) for i in range(8)])


def shift(value, steps):
    size = lax.axis_size("dp")
    return lax.ppermute(value, "dp", [(i, (i + steps) % size) for i in range(size)])


def gather_near(value):
    value = value[None]
    for bit in (ACROSS, DEEP, CORE):
        value = jnp.concatenate([value, swap(value, bit)])
    return value


def gather_split(value):
    half = value.shape[0] // 2
    across, deep = swap(value, ACROSS), swap(value, DEEP)
    diagonal = [swap(across[:half], DEEP), swap(deep[half:], ACROSS)]
    plane = jnp.concatenate([value, across, deep, *diagonal])
    return jnp.concatenate([plane, swap(plane, CORE)])


def plane_hop(value):
    half = value.shape[2] // 2
    upper, lower = value[:, :, :half], value[:, :, half:]
    return upper[:, 0] + swap(upper[:, 1], ACROSS), lower[0] + swap(lower[1], DEEP)


def plane_end(upper, lower):
    return jnp.concatenate([upper[0] + swap(upper[1], DEEP), lower[0] + swap(lower[1], ACROSS)])


def together(*values):
    return lax.optimization_barrier(values)


def sum_everywhere(value):
    value = value + swap(value, CORE)
    across, deep, both = (swap(value, bits) for bits in (ACROSS, DEEP, ACROSS | DEEP))
    value = (value + across) + (deep + both)
    near, far, farthest = (
        lax.ppermute(value, "dp", [(i, i ^ step) for i in range(4)]) for step in (1, 2, 3)
    )
    return (value + near) + (far + farthest)


def upward(table):
    z = lax.axis_index("dp")
    return [lax.dynamic_index_in_dim(table, (z + k) % 4, keepdims=False) for k in range(4)]


def shares_of(tiles_all, devices):
    sizes = [height * across // devices for _, height, across in HOME_ORDER]
    sizes.append((tiles_all - TAIL) // devices)
    starts = [sum(sizes[:n]) for n in range(len(sizes))]
    return sizes, starts


def homes_of(tiles, tiles_all, devices, near):
    per = tiles_all // devices
    sizes, starts = shares_of(tiles_all, devices)
    homes = ((tiles - TAIL) // sizes[-1]) * per + starts[-1] + (tiles - TAIL) % sizes[-1]
    for (first, height, across), size, start in zip(HOME_ORDER, sizes, starts):
        at = tiles - first
        inside = (at >= 0) & (at < height * across)
        if near:
            row, column = at // across, at % across
            slab, half = height // CHIPS, across // 2
            owner = row // slab * 2 + column // half
            line = column % half * slab + row % slab
        else:
            owner, line = at // size, at % size
        homes = jnp.where(inside, owner * per + start + line, homes)
    return homes


def room(per, devices):
    mean = per / devices
    return int(-(-(mean + 5.0 * mean**0.5) // 8) * 8)


def row_steps(total, size, step):
    whole, rest = divmod(total, size)

    def body(i, carry):
        step(i * size, size)
        return carry

    lax.fori_loop(0, whole, body, 0)
    if rest:
        step(whole * size, rest)


def send_kernel(slots, lines, tiles, packed, index, stage, *, per):
    slot_count = packed.shape[0]

    def clear(start, size):
        for u in range(size):
            index[start + u] = per

    row_steps(slot_count + 8, 64, clear)
    stage[...] = jnp.zeros_like(stage)

    def place(start, size):
        for u in range(size):
            slot = slots[start + u]
            stage[pl.ds(slot, 1), :] = tiles[pl.ds(start + u, 1), :]
            index[slot] = lines[start + u]

    row_steps(per, 64, place)
    packed[...] = stage[pl.ds(0, slot_count), :].astype(packed.dtype)


def send_tiles(slots, lines, tiles, slot_count):
    per = tiles.shape[0]
    return pl.pallas_call(
        functools.partial(send_kernel, per=per),
        in_specs=[pl.BlockSpec(memory_space=pltpu.SMEM)] * 2 + [pl.BlockSpec(memory_space=pltpu.VMEM)],
        out_specs=[pl.BlockSpec(memory_space=pltpu.VMEM), pl.BlockSpec(memory_space=pltpu.SMEM)],
        out_shape=[
            jax.ShapeDtypeStruct((slot_count, TILE), jnp.bfloat16),
            jax.ShapeDtypeStruct((slot_count + 8,), jnp.int32),
        ],
        scratch_shapes=[pltpu.VMEM((slot_count + 8, TILE), jnp.float32)],
        name="send_tiles",
    )(slots, lines, tiles)


def slab_pieces(starts):
    for (row, lines, groups, columns, offset), start in zip(SLABS, starts):
        for column in range(columns):
            for part in range(groups):
                yield row, offset + part * columns + column, lines, start + (column * groups + part) * lines


def land_kernel(index, packed, tiles, stage, full, *, starts):
    stage[...] = packed[...].astype(jnp.float32)

    def place(start, size):
        for u in range(size):
            full[pl.ds(index[start + u], 1), :] = stage[pl.ds(start + u, 1), :]

    row_steps(packed.shape[0], 128, place)
    if starts is None:
        tiles[...] = full[pl.ds(0, tiles.shape[0]), :].astype(tiles.dtype)
    else:
        tiles[...] = jnp.zeros_like(tiles)
        for row, column, lines, line in (*slab_pieces(starts), (*TAIL_AT, 16, starts[-1])):
            tiles[pl.ds(row, lines), column * TILE : (column + 1) * TILE] = full[pl.ds(line, lines), :].astype(
                tiles.dtype
            )


def land_tiles(index, packed, per, starts):
    slot_count = packed.shape[0]
    return pl.pallas_call(
        functools.partial(land_kernel, starts=starts),
        in_specs=[pl.BlockSpec(memory_space=pltpu.SMEM), pl.BlockSpec(memory_space=pltpu.VMEM)],
        out_specs=pl.BlockSpec(memory_space=pltpu.VMEM),
        out_shape=jax.ShapeDtypeStruct((per, TILE) if starts is None else SHARE, jnp.bfloat16),
        scratch_shapes=[pltpu.VMEM((slot_count, TILE), jnp.float32), pltpu.VMEM((per + 8, TILE), jnp.float32)],
        name="land_tiles",
    )(index, packed)


def share_lines_kernel(up, down, qkv, rest, lines, *, starts):
    slabs = (up, down, qkv, rest, rest)
    first = (0, 0, 0, 0, 48)
    for n, (source, (_, _, _, columns, _), begin, start) in enumerate(zip(slabs, SLABS, first, starts)):
        height = HOME_ORDER[n][1] // CHIPS
        for column in range(columns):
            lines[pl.ds(start + column * height, height), :] = source[
                pl.ds(begin, height), column * TILE : (column + 1) * TILE
            ]
    lines[pl.ds(starts[-1], 8), :] = rest[pl.ds(80, 8), :TILE]


def share_lines(up, down, qkv, rest, per, starts):
    return pl.pallas_call(
        functools.partial(share_lines_kernel, starts=starts),
        in_specs=[pl.BlockSpec(memory_space=pltpu.VMEM)] * 4,
        out_specs=pl.BlockSpec(memory_space=pltpu.VMEM),
        out_shape=jax.ShapeDtypeStruct((per, TILE), jnp.float32),
        name="share_lines",
    )(up, down, qkv, rest)


def pick_kernel(index, source, target, *, count):
    def pick(start, size):
        for u in range(size):
            target[pl.ds(start + u, 1), :] = source[pl.ds(index[start + u], 1), :]

    row_steps(count, 128, pick)


def pick_tiles(index, source, count):
    return pl.pallas_call(
        functools.partial(pick_kernel, count=count),
        in_specs=[pl.BlockSpec(memory_space=pltpu.SMEM), pl.BlockSpec(memory_space=pltpu.VMEM)],
        out_specs=pl.BlockSpec(memory_space=pltpu.VMEM),
        out_shape=jax.ShapeDtypeStruct((count, TILE), source.dtype),
        name="pick_tiles",
    )(index, source)


def assemble_kernel(arrived, up, down, qkv, out, place, tail, landed, sem):
    copy = pltpu.make_async_copy(arrived, landed, sem)
    copy.start()
    copy.wait()

    def one_device(block, carry):
        chip, core = block // 2, block % 2

        def put(target, row, lines, width, source_row, source_column):
            target[
                pl.ds(pl.multiple_of(row, 16), lines), pl.ds(pl.multiple_of(core * width, TILE), width)
            ] = landed[block, pl.ds(source_row, lines), source_column : source_column + width]

        put(up, chip * 48, 48, 1536, 0, 0)
        for part in range(4):
            put(down, chip * 192 + part * 48, 48, 384, 48, part * 384)
        put(qkv, chip * 48, 48, 1152, 96, 0)
        put(out, chip * 48, 48, 384, 96, 1152)
        for part in range(2):
            put(place, chip * 32 + part * 16, 16, 384, 144, part * 384)
        tail[block] = landed[block, pl.ds(TAIL_AT[0], 16), TAIL_AT[1] * TILE : (TAIL_AT[1] + 1) * TILE].astype(
            jnp.float32
        )[:8]
        return carry

    lax.fori_loop(0, landed.shape[0], one_device, 0)


def assemble_layer(arrived):
    devices = arrived.shape[0]
    return pl.pallas_call(
        assemble_kernel,
        in_specs=[pl.BlockSpec(memory_space=pl.ANY)],
        out_specs=[pl.BlockSpec(memory_space=pltpu.VMEM)] * 6,
        out_shape=[jax.ShapeDtypeStruct((h, a * TILE), jnp.bfloat16) for _, h, a in HOME_ORDER]
        + [jax.ShapeDtypeStruct((devices, 8, TILE), jnp.float32)],
        scratch_shapes=[
            pltpu.VMEM((devices, *SHARE), jnp.bfloat16),
            pltpu.SemaphoreType.DMA,
        ],
        compiler_params=pltpu.CompilerParams(vmem_limit_bytes=VMEM_LIMIT),
        cost_estimate=pl.CostEstimate(flops=0, bytes_accessed=60_000_000, transcendentals=0),
        name="assemble_layer",
    )(arrived)


def unpack_kernel(source, target, stage, *, across):
    stage[...] = source[...].astype(jnp.float32)

    def step(g, carry):
        for column in range(across):
            lines = stage[pl.ds(g * 16 * across + column, 16, stride=across), :]
            target[pl.ds(pl.multiple_of(g * 16, 16), 16), column * TILE : (column + 1) * TILE] = lines.astype(
                jnp.bfloat16
            )
        return carry

    lax.fori_loop(0, target.shape[0] // 16, step, 0)


def unpack_matrix(tiles, piece):
    first, height, across = piece
    lines = min(height, 384 if across > 6 else 768)
    block = lines * across
    return pl.pallas_call(
        functools.partial(unpack_kernel, across=across),
        grid=(height // lines,),
        in_specs=[pl.BlockSpec((block, TILE), lambda i: (first // block + i, 0))],
        out_specs=pl.BlockSpec((lines, across * TILE), lambda i: (i, 0)),
        out_shape=jax.ShapeDtypeStruct((height, across * TILE), jnp.bfloat16),
        scratch_shapes=[pltpu.VMEM((block, TILE), jnp.float32)],
        name="unpack_matrix",
    )(tiles)


def array_multiply(left_side, right_side):
    return jnp.dot(left_side, right_side, preferred_element_type=jnp.float32)


def matmul_left(left_side, right_side):
    return lax.dot_general(
        left_side, right_side, (((0,), (0,)), ((), ())), preferred_element_type=jnp.float32
    )


def trailing_array_multiply(left_side, right_side):
    return lax.dot_general(
        left_side, right_side, (((1,), (1,)), ((), ())), preferred_element_type=jnp.float32
    )


def pieces_of(matrices, tail):
    qkv, out, up, down, place = matrices
    return {
        "qkv": qkv,
        "out": out,
        "up": up,
        "down": down,
        "place": place,
        "small": tail[:60].reshape(10, D),
        "upbias": tail[60:84].reshape(FF),
    }


def norm_forward(values, gain_row, shift_row):
    center = values - jnp.mean(values, axis=-1, keepdims=True)
    inverse = lax.rsqrt(jnp.mean(center * center, axis=-1, keepdims=True) + norm_eps)
    normed = center * inverse
    return (normed * gain_row + shift_row, normed, inverse)


def norm_backward(grad_out, normed, inverse, gain_row):
    scaled = grad_out * gain_row
    grad_in = inverse * (
        scaled
        - jnp.mean(scaled, axis=-1, keepdims=True)
        - normed * jnp.mean(scaled * normed, axis=-1, keepdims=True)
    )
    return (grad_in, jnp.sum(grad_out * normed, axis=0), jnp.sum(grad_out, axis=0))


def gelu_slope(values):
    return (
        0.5 * (1.0 + lax.erf(values * 0.7071067811865476))
        + values * jnp.exp(-0.5 * values * values) * 0.3989422804014327
    )


def key_scores(projected, lengths):
    seqs_count = lengths.shape[0]
    split_heads = projected.reshape(seqs_count, LEN, 3, HEADS, HEAD_DIM)
    scores = jnp.einsum(
        "sqhd,skhd->shqk",
        split_heads[:, :, 0],
        split_heads[:, :, 1],
        preferred_element_type=jnp.float32,
    ) * HEAD_DIM ** (-0.5)
    live_keys = jnp.arange(LEN)[None, :] < lengths[:, None]
    return (jnp.where(live_keys[:, None, None, :], scores, -1000000000.0), split_heads)


def attention_forward(pieces, looked, lengths):
    small_rows = pieces["small"].astype(jnp.float32)
    seqs_count = lengths.shape[0]
    rows_here = seqs_count * LEN
    summed = (
        looked.reshape(seqs_count, LEN, D) + pieces["place"].astype(jnp.float32)[None]
    ).reshape(rows_here, D)
    first_norm, normed_zero, inverse_zero = norm_forward(summed, small_rows[4], small_rows[5])
    inputs = first_norm.astype(jnp.bfloat16)
    qkv_bias = jnp.concatenate([small_rows[0], jnp.zeros((D,), jnp.float32), small_rows[1]])
    projected = (array_multiply(inputs, pieces["qkv"]) + qkv_bias).astype(jnp.bfloat16)
    scores, split_heads = key_scores(projected, lengths)
    peak = jnp.max(scores, axis=-1, keepdims=True)
    exps = jnp.exp(scores - peak)
    totals = jnp.sum(exps, axis=-1, keepdims=True)
    probabilities = (exps / totals).astype(jnp.bfloat16)
    logsum = peak + jnp.log(totals)
    context = jnp.einsum(
        "shqk,skhd->sqhd", probabilities, split_heads[:, :, 2], preferred_element_type=jnp.float32
    )
    context = context.reshape(rows_here, D).astype(jnp.bfloat16)
    attended = array_multiply(context, pieces["out"]) + small_rows[2]
    middle, normed_one, inverse_one = norm_forward(
        first_norm + attended, small_rows[6], small_rows[7]
    )
    saved = {
        "inputs": inputs,
        "projected": projected,
        "logsum": logsum,
        "context": context,
        "normed_zero": normed_zero,
        "inverse_zero": inverse_zero,
        "normed_one": normed_one,
        "inverse_one": inverse_one,
    }
    return middle, saved


def feed_forward(pieces, middle, saved):
    small_rows = pieces["small"]
    middle_low = middle.astype(jnp.bfloat16)
    hidden = array_multiply(middle_low, pieces["up"]) + pieces["upbias"].astype(jnp.float32)
    activated = jax.nn.gelu(hidden, approximate=False).astype(jnp.bfloat16)
    output = array_multiply(activated, pieces["down"]) + small_rows[3]
    final_lines, normed_two, inverse_two = norm_forward(
        middle + output, small_rows[8], small_rows[9]
    )
    saved = {
        **saved,
        "middle_low": middle_low,
        "hidden": hidden,
        "activated": activated,
        "normed_two": normed_two,
        "inverse_two": inverse_two,
    }
    return (final_lines, saved)


def feed_backward(pieces, saved, grad_final, flow):
    small_rows = pieces["small"]
    grad_sum_two, grad_gain_two, grad_shift_two = norm_backward(
        grad_final, saved["normed_two"], saved["inverse_two"], small_rows[8]
    )
    grad_out = grad_sum_two.astype(jnp.bfloat16)
    flow.add_product(saved["activated"], grad_out, offload=True)
    grad_act = trailing_array_multiply(grad_out, pieces["down"])
    grad_hidden = (grad_act * gelu_slope(saved["hidden"])).astype(jnp.bfloat16)
    flow.add_product(saved["middle_low"], grad_hidden, late=2)
    grad_middle = grad_sum_two + trailing_array_multiply(grad_hidden, pieces["up"])
    grad_sum_one, grad_gain_one, grad_shift_one = norm_backward(
        grad_middle, saved["normed_one"], saved["inverse_one"], small_rows[6]
    )
    grad_upbias = jnp.sum(grad_hidden.astype(jnp.float32), axis=0)
    (grad_sum_one,) = flow.advance(grad_sum_one)
    return (
        grad_sum_one,
        [jnp.sum(grad_out.astype(jnp.float32), axis=0), grad_gain_one, grad_shift_one, grad_gain_two, grad_shift_two],
        grad_upbias,
    )


def attention_backward(pieces, saved, grad_sum_one, grad_small, grad_upbias, lengths, tail_rows, flow, head_part):
    small_rows = pieces["small"]
    seqs_count = lengths.shape[0]
    rows_here = seqs_count * LEN
    grad_att = grad_sum_one.astype(jnp.bfloat16)
    grad_outw = matmul_left(saved["context"], grad_att)
    grad_context = (
        trailing_array_multiply(grad_att, pieces["out"])
        .astype(jnp.bfloat16)
        .reshape(seqs_count, LEN, HEADS, HEAD_DIM)
    )
    scores, split_heads = key_scores(saved["projected"], lengths)
    probabilities = jnp.exp(scores - saved["logsum"])
    grad_probs = jnp.einsum(
        "sqhd,skhd->shqk", grad_context, split_heads[:, :, 2], preferred_element_type=jnp.float32
    )
    grad_values = jnp.einsum(
        "shqk,sqhd->skhd",
        probabilities.astype(jnp.bfloat16),
        grad_context,
        preferred_element_type=jnp.float32,
    )
    grad_values, grad_probs = flow.advance(grad_values, grad_probs)
    grad_scores = probabilities * (
        grad_probs - jnp.sum(grad_probs * probabilities, axis=-1, keepdims=True)
    )
    grad_scores, head_part = flow.advance(grad_scores.astype(jnp.bfloat16), head_part)
    grad_queries = jnp.einsum(
        "shqk,skhd->sqhd", grad_scores, split_heads[:, :, 1], preferred_element_type=jnp.float32
    ) * HEAD_DIM ** (-0.5)
    grad_keys = jnp.einsum(
        "shqk,sqhd->skhd", grad_scores, split_heads[:, :, 0], preferred_element_type=jnp.float32
    ) * HEAD_DIM ** (-0.5)
    grad_proj = (
        jnp.stack([grad_queries, grad_keys, grad_values], axis=2)
        .reshape(rows_here, 3 * D)
        .astype(jnp.bfloat16)
    )
    flow.add_product(saved["inputs"], grad_proj)
    grad_bias_all = jnp.sum(grad_proj.astype(jnp.float32), axis=0)
    grad_first = grad_sum_one + trailing_array_multiply(grad_proj, pieces["qkv"])
    grad_embedded, grad_gain_zero, grad_shift_zero = norm_backward(
        grad_first, saved["normed_zero"], saved["inverse_zero"], small_rows[4]
    )
    grad_place = jnp.sum(grad_embedded.reshape(seqs_count, LEN, D), axis=0)
    grad_small = jnp.stack(
        [
            grad_bias_all[:D],
            grad_bias_all[2 * D :],
            jnp.sum(grad_att.astype(jnp.float32), axis=0),
            grad_small[0],
            grad_gain_zero,
            grad_shift_zero,
            *grad_small[1:],
        ]
    )
    tail = jnp.concatenate(
        [
            grad_small.reshape(60, TILE),
            grad_upbias.reshape(24, TILE),
            jnp.zeros((tail_rows - 84, TILE), jnp.float32),
        ]
    )
    (grad_embedded,) = flow.advance(grad_embedded)
    flow.add_rest(grad_outw, grad_place, tail)
    return grad_embedded, head_part


def combine_stats(earlier, later):
    peak_s = jnp.maximum(earlier[0], later[0])
    peak_t = jnp.maximum(earlier[2], later[2])
    factor_early = jnp.exp(earlier[0] - peak_s)
    factor_late = jnp.exp(later[0] - peak_s)
    teacher_early = jnp.exp(earlier[2] - peak_t)
    teacher_late = jnp.exp(later[2] - peak_t)
    return jnp.stack(
        [
            peak_s,
            earlier[1] * factor_early + later[1] * factor_late,
            peak_t,
            earlier[3] * teacher_early + later[3] * teacher_late,
            earlier[4] * teacher_early + later[4] * teacher_late,
        ]
    )


def adam_step(weight, first_moment, second, gradient, step_float):
    new_first = beta_first * first_moment + (1.0 - beta_first) * gradient
    new_second = beta_second * second + (1.0 - beta_second) * gradient * gradient
    fix_first = 1.0 - jnp.power(beta_first, step_float)
    fix_second = 1.0 - jnp.power(beta_second, step_float)
    update = new_first / fix_first / (jnp.sqrt(new_second / fix_second) + adam_eps)
    return (weight - learn_rate * (update + weight_decay * weight), new_first, new_second)


def at(value, index, axis):
    return lax.dynamic_index_in_dim(value, index, axis, keepdims=False)


def sent_low(value, bit):
    return swap(value.astype(jnp.bfloat16), bit).astype(jnp.float32)


def bit_of(bit):
    return lax.axis_index("vocab") // bit % 2


def halved(value, axis, bit):
    mine = bit_of(bit)
    return at(value, mine, axis) + sent_low(at(value, 1 - mine, axis), bit)


def reduce_steps(near, far, offload, late):
    (chip,) = yield [near + swap(far, CORE)]
    chip = chip.reshape(4, 2, 2, chip.shape[0] // CHIPS, chip.shape[1])
    first, second = yield [halved(chip[:2], 2, ACROSS), halved(chip[2:], 1, DEEP)]
    first, second = yield [halved(first, 1, DEEP), halved(second, 1, ACROSS)]
    if offload:
        total = lax.psum_scatter(jnp.concatenate([first, second]), "dp", scatter_dimension=0, tiled=False)
        yield []
        (total,) = yield [total]
        return total
    z = lax.axis_index("dp")
    blocks = [
        jnp.where((z + k) % 4 < 2, at(first, (z + k) % 2, 0), at(second, (z + k) % 2, 0)) for k in range(4)
    ]
    for _ in range(late):
        yield []
    blocks = yield [blocks[0], *(shift(blocks[k], k) for k in (1, 2, 3))]
    return blocks[0] + blocks[1] + blocks[2] + blocks[3]


class Flow:
    near = True

    def __init__(self):
        self.lines, self.waiting, self.sums = [], [], []

    def add(self, near, far, offload=False, late=0):
        self.lines.append(reduce_steps(near, far, offload, late))
        self.waiting.append(next(self.lines[-1]))
        self.sums.append(None)

    def add_product(self, left, right, offload=False, late=0):
        width = right.shape[1] // 2
        core = bit_of(CORE)
        far = matmul_left(left, lax.dynamic_slice_in_dim(right, (1 - core) * width, width, 1))
        near = matmul_left(left, lax.dynamic_slice_in_dim(right, core * width, width, 1))
        self.add(near, far, offload, late)

    def add_rest(self, out, place, tail):
        def half(core):
            columns = [
                lax.dynamic_slice_in_dim(whole, core * 384, 384, 1).reshape(CHIPS, -1, 384) for whole in (out, place)
            ]
            ends = jnp.pad(at(tail.reshape(CHIPS, 2, 8, TILE), core, 1), ((0, 0), (0, 0), (0, 256)))
            return jnp.concatenate([*columns, ends], axis=1).reshape(-1, 384)

        self.add(half(bit_of(CORE)), half(1 - bit_of(CORE)))

    def advance(self, *values):
        tied, values = together([moved for moved in self.waiting if moved is not None], list(values))
        tied = list(tied)
        for n, moved in enumerate(self.waiting):
            if moved is not None:
                try:
                    self.waiting[n] = self.lines[n].send(tied.pop(0))
                except StopIteration as stop:
                    self.waiting[n], self.sums[n] = None, stop.value
        return values


class PlainFlow:
    near = False

    def __init__(self, devices):
        self.devices, self.sums = devices, []

    def add_product(self, left, right, offload=False, late=0):
        parts = matmul_left(left, right).reshape(self.devices, -1, TILE)
        self.sums.append(lax.psum_scatter(parts, ("dp", "vocab"), scatter_dimension=0, tiled=False))

    def add_rest(self, out, place, tail):
        parts = [part.reshape(self.devices, -1, TILE) for part in (out, place, tail)]
        parts = jnp.concatenate(parts, axis=1)
        self.sums.append(lax.psum_scatter(parts, ("dp", "vocab"), scatter_dimension=0, tiled=False))

    def advance(self, *values):
        return values


def on_device(
    near,
    token_ids,
    lengths,
    mask_pos,
    mask_count,
    owner_order,
    step_count,
    teacher_flat,
    mentor_lexicon_weights,
    student_flat,
    flat_first,
    flat_second,
    student_embed,
    embed_first,
    embed_second,
):
    per = student_flat.shape[0]
    tiles_all = owner_order.shape[0]
    vocab_rows, width_share = student_embed.shape
    planes = lax.axis_size("dp")
    group = lax.axis_size("vocab")
    here = lax.axis_index("vocab")
    spot = jnp.stack([lax.axis_index("dp"), here]).astype(jnp.int32)
    devices = planes * group
    everywhere = ("dp", "vocab")
    device = lax.axis_index(everywhere)
    capacity = room(per, devices)
    slot_count = devices * capacity

    facts = jnp.concatenate([token_ids.reshape(LEN), lengths, mask_count, jnp.zeros((TILE - 2,), jnp.int32)])
    columns_low = student_embed.T.astype(jnp.bfloat16)
    words = jnp.arange(vocab_rows, dtype=jnp.int32)

    def chosen(ids):
        return (ids.reshape(-1, 1) - here * vocab_rows == words[None]).astype(jnp.bfloat16)

    def rows_t(ids):
        return array_multiply(chosen(ids), mentor_lexicon_weights).astype(jnp.bfloat16)

    def rows_s(ids, table):
        return trailing_array_multiply(chosen(ids), table).astype(jnp.bfloat16)

    def teacher_pieces(tiles):
        return pieces_of(
            [unpack_matrix(tiles, piece) for piece in MATRICES],
            tiles[TAIL : TAIL + TAIL_TILES].astype(jnp.float32),
        )

    homes = homes_of(owner_order, tiles_all, devices, near)
    sizes, starts = shares_of(tiles_all, devices)
    one_of = jnp.arange(devices, dtype=jnp.int32)
    pairs = jnp.sum((homes.reshape(devices, per, 1) // per == one_of).astype(jnp.int32), axis=1)
    crowded = jnp.max(pairs) > capacity
    own_homes = lax.dynamic_slice_in_dim(homes, device * per, per)
    own_target = own_homes // per
    chosen_target = (own_target[:, None] == one_of).astype(jnp.bfloat16)
    lines = jnp.arange(per, dtype=jnp.int32)
    earlier = (lines[None] < lines[:, None]).astype(jnp.bfloat16)
    rank = jnp.sum(array_multiply(earlier, chosen_target) * chosen_target.astype(jnp.float32), axis=1)
    rank = rank.astype(jnp.int32)
    slots = jnp.where(rank < capacity, own_target * capacity + rank, slot_count)
    packed, home_line = send_tiles(slots, own_homes % per, student_flat, slot_count)
    if near:
        teacher_tiles = lax.all_gather(teacher_flat, everywhere, axis=0, tiled=True)
        plane_facts = gather_near(facts)
        shape = (2, 2, LEN, D)
        far = rows_t(plane_facts[4:, :LEN]).reshape(shape)
        columns = [columns_low, shift(columns_low, 1)]
        packed, home_line, far, columns = together(packed, home_line, far, columns)
    packed = lax.all_to_all(packed.reshape(devices, capacity, TILE), everywhere, 0, 0)
    home_line = lax.all_to_all(home_line[:slot_count].reshape(devices, 1, capacity), everywhere, 0, 0)
    home_line = home_line.reshape(slot_count)
    if near:
        looked_t = rows_t(plane_facts[:4, :LEN]).reshape(shape) + swap(far, CORE)
        packed, home_line, looked_t, ahead = together(packed, home_line, looked_t, shift(columns[1], 1))
        columns = [*columns, ahead]
    home_tiles = land_tiles(home_line, packed.reshape(slot_count, TILE), per, starts if near else None)
    if near:
        home_tiles, looked_t, ahead = together(home_tiles, plane_hop(looked_t), shift(columns[2], 1))
        columns = [*columns, ahead]

    def from_everywhere(part):
        copies = jnp.broadcast_to(part[None], (devices, *part.shape))
        return lax.all_to_all(copies, everywhere, 0, 0).reshape(-1, TILE)

    def every_tile(tiles):
        stored = from_everywhere(student_flat.astype(jnp.bfloat16))
        sources = jnp.zeros((tiles_all,), jnp.int32).at[homes].set(jnp.arange(tiles_all, dtype=jnp.int32))
        stored = stored[lax.dynamic_slice_in_dim(sources, device * per, per)]
        if near:
            return land_tiles(lines, stored, per, starts)
        return stored

    home_tiles = lax.cond(crowded, every_tile, lambda tiles: tiles, home_tiles)

    if near:
        layer = lax.all_gather(home_tiles, everywhere, axis=0)
        z = lax.axis_index("dp")
        table_low = jnp.zeros((D, vocab_rows), jnp.bfloat16)
        for k, part in enumerate(columns):
            table_low = lax.dynamic_update_slice(table_low, part, ((z + 4 - k) % 4 * width_share, 0))
        far = rows_s(plane_facts[4:, :LEN], table_low).reshape(shape)
        looked_t, far = together(plane_end(*looked_t).astype(jnp.float32), far)
        close = rows_s(plane_facts[:4, :LEN], table_low).reshape(shape)
        other_facts = gather_near(jnp.stack([shift(facts, 1), shift(facts, 2), shift(facts, 3)]))
        all_facts = jnp.concatenate([plane_facts[:, None], other_facts], axis=1)
        looked_s, teacher_tiles, all_facts = together(close + swap(far, CORE), teacher_tiles, all_facts)
        teacher = teacher_pieces(teacher_tiles)
        teacher, looked_s = together(teacher, plane_hop(looked_s))
        middle, _ = attention_forward(teacher, looked_t, lengths)
        middle, looked_s = together(middle, plane_end(*looked_s).astype(jnp.float32))
        final_t = feed_forward(teacher, middle, {})[0]
        final_t, layer = together(final_t, layer)
        matrices = assemble_layer(layer)
    else:
        table_low = lax.all_gather(columns_low, "dp", axis=0, tiled=True)
        by_plane = lax.all_gather(facts, "dp", axis=0)
        all_facts = lax.all_gather(by_plane, "vocab", axis=0)
        plane_facts = lax.dynamic_index_in_dim(all_facts, lax.axis_index("dp"), 1, keepdims=False)
        teacher_tiles = lax.all_gather(teacher_flat, everywhere, axis=0, tiled=True)
        layer = lax.all_gather(home_tiles, everywhere, axis=0)
        matrices = [
            layer[:, start : start + size].reshape(height, across * TILE)
            for (_, height, across), size, start in zip(HOME_ORDER, sizes, starts)
        ]
        matrices.append(layer[:, starts[-1] :].astype(jnp.float32))
        plane_ids = plane_facts[:, :LEN]
        looked_t, looked_s = (
            lax.psum_scatter(rows, "vocab", scatter_dimension=0, tiled=True).astype(jnp.float32)
            for rows in (rows_t(plane_ids), rows_s(plane_ids, table_low))
        )
        teacher = teacher_pieces(teacher_tiles)
        middle, _ = attention_forward(teacher, looked_t, lengths)
        final_t = feed_forward(teacher, middle, {})[0]
    up, down, qkv, out, place = matrices[:5]
    student = pieces_of((qkv, out, up, down, place), matrices[5].reshape(-1, TILE))
    middle, saved = attention_forward(student, looked_s, lengths)
    offsets = jnp.concatenate([mask_pos.reshape(CAP), jnp.zeros((SLOTS - CAP,), jnp.int32)])
    picked_t = final_t[offsets].astype(jnp.bfloat16)
    if near:
        middle, mentor_picked = together(middle, gather_near(picked_t).reshape(-1, D))
    else:
        mentor_picked = lax.all_gather(picked_t, "vocab", axis=0, tiled=True)
    final_s, saved = feed_forward(student, middle, saved)

    token_total = jnp.sum(all_facts[:, :, LEN]).astype(jnp.float32)
    masked_total = jnp.sum(all_facts[:, :, LEN + 1]).astype(jnp.float32)
    teacher_logit = (
        trailing_array_multiply(mentor_picked, mentor_lexicon_weights) / smoothing_heat_scale
    )
    peak_t = jnp.max(teacher_logit, axis=1)
    picked_s = final_s[offsets].astype(jnp.bfloat16)
    if near:
        learner_picked = gather_split(picked_s).reshape(-1, D)
        learner_picked, teacher_logit, peak_t = together(learner_picked, teacher_logit, peak_t)
    else:
        learner_picked = lax.all_gather(picked_s, "vocab", axis=0, tiled=True)
    live_weighting = (
        (jnp.arange(SLOTS)[None] < plane_facts[:, LEN + 1, None]).astype(jnp.float32).reshape(-1)
    )
    learner_energy = array_multiply(learner_picked, table_low) / smoothing_heat_scale
    peak_s = jnp.max(learner_energy, axis=1)
    teacher_exps = jnp.exp(teacher_logit - peak_t[:, None])
    stats = jnp.stack(
        [
            peak_s,
            jnp.sum(jnp.exp(learner_energy - peak_s[:, None]), axis=1),
            peak_t,
            jnp.sum(teacher_exps, axis=1),
            jnp.sum(teacher_exps * (teacher_logit - learner_energy), axis=1),
        ]
    )
    if near:
        stats = stats.reshape(5, 2, 2, 2, SLOTS)
        stats = combine_stats(stats, jnp.flip(swap(stats, CORE), 1))
        across, deep, both = (
            jnp.flip(swap(stats, bits), axes)
            for bits, axes in ((ACROSS, 3), (DEEP, 2), (ACROSS | DEEP, (2, 3)))
        )
        stats = combine_stats(combine_stats(stats, across), combine_stats(deep, both))
        stats = stats.reshape(5, -1)
    else:
        everything = lax.all_gather(stats, "vocab", axis=0)
        stats = everything[0]
        for k in range(1, group):
            stats = combine_stats(stats, everything[k])
    logsum_s = stats[0] + jnp.log(stats[1])
    logsum_t = stats[2] + jnp.log(stats[3])
    diverge = stats[4] / stats[3] - logsum_t + logsum_s
    mine = 0 if near else here * SLOTS
    divergence_part = jnp.sum(lax.dynamic_slice_in_dim(diverge * live_weighting, mine, SLOTS))
    student_probs = jnp.exp(learner_energy - logsum_s[:, None])
    teacher_probs = jnp.exp(teacher_logit - logsum_t[:, None])
    grad_logit = (
        mixing_coefficient
        * smoothing_heat_scale
        / masked_total
        * live_weighting[:, None]
        * (student_probs - teacher_probs)
    ).astype(jnp.bfloat16)
    if near:
        half = grad_logit.shape[0] // 2
        far = trailing_array_multiply(grad_logit[half:], table_low).reshape(2, 2, SLOTS, D)
        close = trailing_array_multiply(grad_logit[:half], table_low).reshape(2, 2, SLOTS, D)
        grad_rows = plane_end(*plane_hop(close + swap(far, CORE)))
    else:
        grad_rows = lax.psum_scatter(
            trailing_array_multiply(grad_logit, table_low), "vocab", scatter_dimension=0, tiled=True
        )
    head_grad = matmul_left(learner_picked, grad_logit)
    head_grad, grad_rows = together(head_grad, grad_rows)
    head_part = lax.psum_scatter(head_grad, "dp", scatter_dimension=0, tiled=True)
    products = jnp.sum(final_s * final_t, axis=1)
    inverse_s = lax.rsqrt(jnp.sum(final_s * final_s, axis=1) + cosine_eps)
    inverse_t = lax.rsqrt(jnp.sum(final_t * final_t, axis=1) + cosine_eps)
    live_rows = (jnp.arange(LEN)[None, :] < lengths[:, None]).reshape(-1)
    cosine = products * inverse_s * inverse_t
    cosine_term = jnp.sum(jnp.where(live_rows, 1.0 - cosine, 0.0))
    weighting = jnp.where(live_rows, -cosine_weight / token_total, 0.0) * inverse_s * inverse_t
    grad_final = weighting[:, None] * (
        final_t - (products * inverse_s * inverse_s)[:, None] * final_s
    )
    grad_final = grad_final.at[offsets].add(grad_rows)
    flow = Flow() if near else PlainFlow(devices)
    grad_sum_one, grad_small, grad_upbias = feed_backward(student, saved, grad_final, flow)
    grad_embedded, head_part = attention_backward(
        student, saved, grad_sum_one, grad_small, grad_upbias, lengths, tiles_all - TAIL, flow, head_part
    )

    shares = grad_embedded.astype(jnp.bfloat16).reshape(LEN, planes, width_share).transpose(1, 0, 2)
    if near:
        own = upward(shares)
        shares = jnp.stack([own[0]] + [shift(own[k], k) for k in (1, 2, 3)])
        ids = all_facts[:, :, :LEN].reshape(2, 2, 2, planes, LEN)
        for axis, bit in ((0, CORE), (1, DEEP), (2, ACROSS)):
            ids = jnp.where((here & bit) != 0, jnp.flip(ids, axis), ids)
        ids = ids.transpose(1, 2, 0, 3, 4)
    else:
        shares = lax.all_to_all(shares, "dp", 0, 0)
        ids = all_facts[:, :, :LEN]
    token_grads = lax.all_gather(shares.reshape(-1, width_share), "vocab", axis=0, tiled=True)
    (shares,) = flow.advance(shares)
    token_grads = lax.all_gather(shares.reshape(-1, width_share), "vocab", axis=0, tiled=True)
    flow.advance()
    flow.advance()
    flow.advance()
    sum_down, sum_up, sum_qkv, sum_rest = flow.sums
    if near:
        home_grads = share_lines(sum_up, sum_down, sum_qkv, sum_rest, per, starts)
    else:
        home_grads = jnp.concatenate([sum_up, sum_down, sum_qkv, sum_rest])
    returned = pick_tiles(jnp.minimum(home_line, per - 1), home_grads, slot_count)
    returned = lax.all_to_all(returned.reshape(devices, capacity, TILE), everywhere, 0, 0)
    token_part = matmul_left(token_grads, chosen(ids))
    returned, token_part = together(returned, token_part)
    flat_grad = pick_tiles(jnp.minimum(slots, slot_count - 1), returned.reshape(slot_count, TILE), per)
    flat_grad = lax.cond(
        crowded,
        lambda grads: from_everywhere(home_grads)[own_homes],
        lambda grads: grads,
        flat_grad,
    )
    table_grad = (head_part + token_part).T
    loss_term = (
        mixing_coefficient * smoothing_heat_scale**2 * divergence_part / masked_total
        + cosine_weight * cosine_term / token_total
    )
    squares = jnp.sum(flat_grad * flat_grad) + jnp.sum(table_grad * table_grad)
    if near:
        squares, loss_value = sum_everywhere(jnp.stack([squares, loss_term]))
    else:
        squares, loss_value = lax.psum((squares, loss_term), ("dp", "vocab"))
    grad_norm = jnp.sqrt(squares)
    factor = clip_norm / jnp.maximum(grad_norm, clip_norm)
    step_float = step_count[0].astype(jnp.float32)
    new_flat, new_flat_first, new_flat_second = adam_step(
        student_flat, flat_first, flat_second, flat_grad * factor, step_float
    )
    new_embed, new_embed_first, new_embed_second = adam_step(
        student_embed, embed_first, embed_second, table_grad * factor, step_float
    )
    return (
        loss_value,
        grad_norm,
        new_flat,
        new_flat_first,
        new_flat_second,
        new_embed,
        new_embed_first,
        new_embed_second,
    )


def solution(mesh):
    near = mesh.shape["dp"] == 4 and mesh.shape["vocab"] == 8
    return jax.shard_map(
        functools.partial(on_device, near),
        mesh=mesh,
        in_specs=(
            P(("dp", "vocab"), None),
            P(("dp", "vocab")),
            P(("dp", "vocab"), None),
            P(("dp", "vocab")),
            P(),
            P(),
            P(("dp", "vocab"), None),
            P("vocab", None),
            P(("dp", "vocab"), None),
            P(("dp", "vocab"), None),
            P(("dp", "vocab"), None),
            P("vocab", "dp"),
            P("vocab", "dp"),
            P("vocab", "dp"),
        ),
        out_specs=(
            P(),
            P(),
            P(("dp", "vocab"), None),
            P(("dp", "vocab"), None),
            P(("dp", "vocab"), None),
            P("vocab", "dp"),
            P("vocab", "dp"),
            P("vocab", "dp"),
        ),
        check_vma=False,
    )
```

```python
import functools

import jax
import jax.numpy as jnp
from jax import lax
from jax.experimental import pallas as pl
from jax.experimental.pallas import tpu as pltpu
from jax.sharding import PartitionSpec as P

D = 768
HEADS = 12
HEAD_DIM = 64
FF = 3072
LEN = 512
CAP = 120
SLOTS = 128
TILE = 128

QKV = (0, D, 18)
OUT = (13824, D, 6)
UP = (18432, D, 24)
DOWN = (36864, FF, 6)
PLACE = (55296, LEN, 6)
MATRICES = (QKV, OUT, UP, DOWN, PLACE)
TAIL = 58368
TAIL_TILES = 88
HOME_ORDER = (UP, DOWN, QKV, OUT, PLACE)

VMEM_LIMIT = 60 * 1024 * 1024

smoothing_heat_scale = 2.0
mixing_coefficient = 5.0
cosine_weight = 20.0
clip_norm = 0.01
beta_first = 0.9
beta_second = 0.98
adam_eps = 1e-08
weight_decay = 0.01
learn_rate = 0.1
norm_eps = 1e-12
cosine_eps = 1e-06

CHIPS = 16
SLABS = ((0, 48, 1, 12, 0), (48, 48, 4, 3, 0), (96, 48, 1, 9, 0), (96, 48, 1, 3, 9), (144, 16, 2, 3, 0))
SHARE = (160, 1536)
TAIL_AT = (144, 6)
CORE, ACROSS, DEEP = 1, 2, 4


def swap(value, bit):
    return lax.ppermute(value, "vocab", [(i, i ^ bit) for i in range(8)])


def shift(value, steps):
    size = lax.axis_size("dp")
    return lax.ppermute(value, "dp", [(i, (i + steps) % size) for i in range(size)])


def gather_near(value):
    value = value[None]
    for bit in (ACROSS, DEEP, CORE):
        value = jnp.concatenate([value, swap(value, bit)])
    return value


def gather_split(value):
    half = value.shape[0] // 2
    across, deep = swap(value, ACROSS), swap(value, DEEP)
    diagonal = [swap(across[:half], DEEP), swap(deep[half:], ACROSS)]
    plane = jnp.concatenate([value, across, deep, *diagonal])
    return jnp.concatenate([plane, swap(plane, CORE)])


def plane_hop(value):
    half = value.shape[2] // 2
    upper, lower = value[:, :, :half], value[:, :, half:]
    return upper[:, 0] + swap(upper[:, 1], ACROSS), lower[0] + swap(lower[1], DEEP)


def plane_end(upper, lower):
    return jnp.concatenate([upper[0] + swap(upper[1], DEEP), lower[0] + swap(lower[1], ACROSS)])


def together(*values):
    return lax.optimization_barrier(values)


def sum_everywhere(value):
    value = value + swap(value, CORE)
    across, deep, both = (swap(value, bits) for bits in (ACROSS, DEEP, ACROSS | DEEP))
    value = (value + across) + (deep + both)
    near, far, farthest = (
        lax.ppermute(value, "dp", [(i, i ^ step) for i in range(4)]) for step in (1, 2, 3)
    )
    return (value + near) + (far + farthest)


def upward(table):
    z = lax.axis_index("dp")
    return [lax.dynamic_index_in_dim(table, (z + k) % 4, keepdims=False) for k in range(4)]


def shares_of(tiles_all, devices):
    sizes = [height * across // devices for _, height, across in HOME_ORDER]
    sizes.append((tiles_all - TAIL) // devices)
    starts = [sum(sizes[:n]) for n in range(len(sizes))]
    return sizes, starts


def homes_of(tiles, tiles_all, devices, near):
    per = tiles_all // devices
    sizes, starts = shares_of(tiles_all, devices)
    homes = ((tiles - TAIL) // sizes[-1]) * per + starts[-1] + (tiles - TAIL) % sizes[-1]
    for (first, height, across), size, start in zip(HOME_ORDER, sizes, starts):
        at = tiles - first
        inside = (at >= 0) & (at < height * across)
        if near:
            row, column = at // across, at % across
            slab, half = height // CHIPS, across // 2
            owner = row // slab * 2 + column // half
            line = column % half * slab + row % slab
        else:
            owner, line = at // size, at % size
        homes = jnp.where(inside, owner * per + start + line, homes)
    return homes


def room(per, devices):
    mean = per / devices
    return int(-(-(mean + 5.0 * mean**0.5) // 8) * 8)


def row_steps(total, size, step):
    whole, rest = divmod(total, size)

    def body(i, carry):
        step(i * size, size)
        return carry

    lax.fori_loop(0, whole, body, 0)
    if rest:
        step(whole * size, rest)


def send_kernel(slots, lines, tiles, packed, index, stage, *, per):
    slot_count = packed.shape[0]

    def clear(start, size):
        for u in range(size):
            index[start + u] = per

    row_steps(slot_count + 8, 64, clear)
    stage[...] = jnp.zeros_like(stage)

    def place(start, size):
        for u in range(size):
            slot = slots[start + u]
            stage[pl.ds(slot, 1), :] = tiles[pl.ds(start + u, 1), :]
            index[slot] = lines[start + u]

    row_steps(per, 64, place)
    packed[...] = stage[pl.ds(0, slot_count), :].astype(packed.dtype)


def send_tiles(slots, lines, tiles, slot_count):
    per = tiles.shape[0]
    return pl.pallas_call(
        functools.partial(send_kernel, per=per),
        in_specs=[pl.BlockSpec(memory_space=pltpu.SMEM)] * 2 + [pl.BlockSpec(memory_space=pltpu.VMEM)],
        out_specs=[pl.BlockSpec(memory_space=pltpu.VMEM), pl.BlockSpec(memory_space=pltpu.SMEM)],
        out_shape=[
            jax.ShapeDtypeStruct((slot_count, TILE), jnp.bfloat16),
            jax.ShapeDtypeStruct((slot_count + 8,), jnp.int32),
        ],
        scratch_shapes=[pltpu.VMEM((slot_count + 8, TILE), jnp.float32)],
        name="send_tiles",
    )(slots, lines, tiles)


def slab_pieces(starts):
    for (row, lines, groups, columns, offset), start in zip(SLABS, starts):
        for column in range(columns):
            for part in range(groups):
                yield row, offset + part * columns + column, lines, start + (column * groups + part) * lines


def land_kernel(index, packed, tiles, stage, full, *, starts):
    stage[...] = packed[...].astype(jnp.float32)

    def place(start, size):
        for u in range(size):
            full[pl.ds(index[start + u], 1), :] = stage[pl.ds(start + u, 1), :]

    row_steps(packed.shape[0], 128, place)
    if starts is None:
        tiles[...] = full[pl.ds(0, tiles.shape[0]), :].astype(tiles.dtype)
    else:
        tiles[...] = jnp.zeros_like(tiles)
        for row, column, lines, line in (*slab_pieces(starts), (*TAIL_AT, 16, starts[-1])):
            tiles[pl.ds(row, lines), column * TILE : (column + 1) * TILE] = full[pl.ds(line, lines), :].astype(
                tiles.dtype
            )


def land_tiles(index, packed, per, starts):
    slot_count = packed.shape[0]
    return pl.pallas_call(
        functools.partial(land_kernel, starts=starts),
        in_specs=[pl.BlockSpec(memory_space=pltpu.SMEM), pl.BlockSpec(memory_space=pltpu.VMEM)],
        out_specs=pl.BlockSpec(memory_space=pltpu.VMEM),
        out_shape=jax.ShapeDtypeStruct((per, TILE) if starts is None else SHARE, jnp.bfloat16),
        scratch_shapes=[pltpu.VMEM((slot_count, TILE), jnp.float32), pltpu.VMEM((per + 8, TILE), jnp.float32)],
        name="land_tiles",
    )(index, packed)


def share_lines_kernel(up, down, qkv, rest, lines, *, starts):
    slabs = (up, down, qkv, rest, rest)
    first = (0, 0, 0, 0, 48)
    for n, (source, (_, _, _, columns, _), begin, start) in enumerate(zip(slabs, SLABS, first, starts)):
        height = HOME_ORDER[n][1] // CHIPS
        for column in range(columns):
            lines[pl.ds(start + column * height, height), :] = source[
                pl.ds(begin, height), column * TILE : (column + 1) * TILE
            ]
    lines[pl.ds(starts[-1], 8), :] = rest[pl.ds(80, 8), :TILE]


def share_lines(up, down, qkv, rest, per, starts):
    return pl.pallas_call(
        functools.partial(share_lines_kernel, starts=starts),
        in_specs=[pl.BlockSpec(memory_space=pltpu.VMEM)] * 4,
        out_specs=pl.BlockSpec(memory_space=pltpu.VMEM),
        out_shape=jax.ShapeDtypeStruct((per, TILE), jnp.float32),
        name="share_lines",
    )(up, down, qkv, rest)


def pick_kernel(index, source, target, *, count):
    def pick(start, size):
        for u in range(size):
            target[pl.ds(start + u, 1), :] = source[pl.ds(index[start + u], 1), :]

    row_steps(count, 128, pick)


def pick_tiles(index, source, count):
    return pl.pallas_call(
        functools.partial(pick_kernel, count=count),
        in_specs=[pl.BlockSpec(memory_space=pltpu.SMEM), pl.BlockSpec(memory_space=pltpu.VMEM)],
        out_specs=pl.BlockSpec(memory_space=pltpu.VMEM),
        out_shape=jax.ShapeDtypeStruct((count, TILE), source.dtype),
        name="pick_tiles",
    )(index, source)


def assemble_kernel(arrived, up, down, qkv, out, place, tail, landed, sems):
    def arrival(block):
        return pltpu.make_async_copy(arrived.at[block], landed.at[block], sems.at[block])

    def begin(block, carry):
        arrival(block).start()
        return carry

    lax.fori_loop(0, landed.shape[0], begin, 0)

    def one_device(block, carry):
        arrival(block).wait()
        chip, core = block // 2, block % 2

        def put(target, row, lines, width, source_row, source_column):
            target[
                pl.ds(pl.multiple_of(row, 16), lines), pl.ds(pl.multiple_of(core * width, TILE), width)
            ] = landed[block, pl.ds(source_row, lines), source_column : source_column + width]

        put(up, chip * 48, 48, 1536, 0, 0)
        for part in range(4):
            put(down, chip * 192 + part * 48, 48, 384, 48, part * 384)
        put(qkv, chip * 48, 48, 1152, 96, 0)
        put(out, chip * 48, 48, 384, 96, 1152)
        for part in range(2):
            put(place, chip * 32 + part * 16, 16, 384, 144, part * 384)
        tail[block] = landed[block, pl.ds(TAIL_AT[0], 16), TAIL_AT[1] * TILE : (TAIL_AT[1] + 1) * TILE].astype(
            jnp.float32
        )[:8]
        return carry

    lax.fori_loop(0, landed.shape[0], one_device, 0)


def assemble_layer(arrived):
    devices = arrived.shape[0]
    return pl.pallas_call(
        assemble_kernel,
        in_specs=[pl.BlockSpec(memory_space=pl.ANY)],
        out_specs=[pl.BlockSpec(memory_space=pltpu.VMEM)] * 6,
        out_shape=[jax.ShapeDtypeStruct((h, a * TILE), jnp.bfloat16) for _, h, a in HOME_ORDER]
        + [jax.ShapeDtypeStruct((devices, 8, TILE), jnp.float32)],
        scratch_shapes=[
            pltpu.VMEM((devices, *SHARE), jnp.bfloat16),
            pltpu.SemaphoreType.DMA((devices,)),
        ],
        compiler_params=pltpu.CompilerParams(vmem_limit_bytes=VMEM_LIMIT),
        cost_estimate=pl.CostEstimate(flops=0, bytes_accessed=60_000_000, transcendentals=0),
        name="assemble_layer",
    )(arrived)


def unpack_kernel(source, target, stage, *, across):
    stage[...] = source[...].astype(jnp.float32)

    def step(g, carry):
        for column in range(across):
            lines = stage[pl.ds(g * 16 * across + column, 16, stride=across), :]
            target[pl.ds(pl.multiple_of(g * 16, 16), 16), column * TILE : (column + 1) * TILE] = lines.astype(
                jnp.bfloat16
            )
        return carry

    lax.fori_loop(0, target.shape[0] // 16, step, 0)


def unpack_matrix(tiles, piece):
    first, height, across = piece
    lines = min(height, 384 if across > 6 else 768)
    block = lines * across
    return pl.pallas_call(
        functools.partial(unpack_kernel, across=across),
        grid=(height // lines,),
        in_specs=[pl.BlockSpec((block, TILE), lambda i: (first // block + i, 0))],
        out_specs=pl.BlockSpec((lines, across * TILE), lambda i: (i, 0)),
        out_shape=jax.ShapeDtypeStruct((height, across * TILE), jnp.bfloat16),
        scratch_shapes=[pltpu.VMEM((block, TILE), jnp.float32)],
        name="unpack_matrix",
    )(tiles)


def array_multiply(left_side, right_side):
    return jnp.dot(left_side, right_side, preferred_element_type=jnp.float32)


def matmul_left(left_side, right_side):
    return lax.dot_general(
        left_side, right_side, (((0,), (0,)), ((), ())), preferred_element_type=jnp.float32
    )


def trailing_array_multiply(left_side, right_side):
    return lax.dot_general(
        left_side, right_side, (((1,), (1,)), ((), ())), preferred_element_type=jnp.float32
    )


def pieces_of(matrices, tail):
    qkv, out, up, down, place = matrices
    return {
        "qkv": qkv,
        "out": out,
        "up": up,
        "down": down,
        "place": place,
        "small": tail[:60].reshape(10, D),
        "upbias": tail[60:84].reshape(FF),
    }


def norm_forward(values, gain_row, shift_row):
    center = values - jnp.mean(values, axis=-1, keepdims=True)
    inverse = lax.rsqrt(jnp.mean(center * center, axis=-1, keepdims=True) + norm_eps)
    normed = center * inverse
    return (normed * gain_row + shift_row, normed, inverse)


def norm_backward(grad_out, normed, inverse, gain_row):
    scaled = grad_out * gain_row
    grad_in = inverse * (
        scaled
        - jnp.mean(scaled, axis=-1, keepdims=True)
        - normed * jnp.mean(scaled * normed, axis=-1, keepdims=True)
    )
    return (grad_in, jnp.sum(grad_out * normed, axis=0), jnp.sum(grad_out, axis=0))


def gelu_slope(values):
    return (
        0.5 * (1.0 + lax.erf(values * 0.7071067811865476))
        + values * jnp.exp(-0.5 * values * values) * 0.3989422804014327
    )


def key_scores(projected, lengths):
    seqs_count = lengths.shape[0]
    split_heads = projected.reshape(seqs_count, LEN, 3, HEADS, HEAD_DIM)
    scores = jnp.einsum(
        "sqhd,skhd->shqk",
        split_heads[:, :, 0],
        split_heads[:, :, 1],
        preferred_element_type=jnp.float32,
    ) * HEAD_DIM ** (-0.5)
    live_keys = jnp.arange(LEN)[None, :] < lengths[:, None]
    return (jnp.where(live_keys[:, None, None, :], scores, -1000000000.0), split_heads)


def attention_forward(pieces, looked, lengths):
    small_rows = pieces["small"].astype(jnp.float32)
    seqs_count = lengths.shape[0]
    rows_here = seqs_count * LEN
    summed = (
        looked.reshape(seqs_count, LEN, D) + pieces["place"].astype(jnp.float32)[None]
    ).reshape(rows_here, D)
    first_norm, normed_zero, inverse_zero = norm_forward(summed, small_rows[4], small_rows[5])
    inputs = first_norm.astype(jnp.bfloat16)
    qkv_bias = jnp.concatenate([small_rows[0], jnp.zeros((D,), jnp.float32), small_rows[1]])
    projected = (array_multiply(inputs, pieces["qkv"]) + qkv_bias).astype(jnp.bfloat16)
    scores, split_heads = key_scores(projected, lengths)
    peak = jnp.max(scores, axis=-1, keepdims=True)
    exps = jnp.exp(scores - peak)
    totals = jnp.sum(exps, axis=-1, keepdims=True)
    probabilities = (exps / totals).astype(jnp.bfloat16)
    logsum = peak + jnp.log(totals)
    context = jnp.einsum(
        "shqk,skhd->sqhd", probabilities, split_heads[:, :, 2], preferred_element_type=jnp.float32
    )
    context = context.reshape(rows_here, D).astype(jnp.bfloat16)
    attended = array_multiply(context, pieces["out"]) + small_rows[2]
    middle, normed_one, inverse_one = norm_forward(
        first_norm + attended, small_rows[6], small_rows[7]
    )
    saved = {
        "inputs": inputs,
        "projected": projected,
        "logsum": logsum,
        "context": context,
        "normed_zero": normed_zero,
        "inverse_zero": inverse_zero,
        "normed_one": normed_one,
        "inverse_one": inverse_one,
    }
    return middle, saved


def feed_forward(pieces, middle, saved):
    small_rows = pieces["small"]
    middle_low = middle.astype(jnp.bfloat16)
    hidden = array_multiply(middle_low, pieces["up"]) + pieces["upbias"].astype(jnp.float32)
    activated = jax.nn.gelu(hidden, approximate=False).astype(jnp.bfloat16)
    output = array_multiply(activated, pieces["down"]) + small_rows[3]
    final_lines, normed_two, inverse_two = norm_forward(
        middle + output, small_rows[8], small_rows[9]
    )
    saved = {
        **saved,
        "middle_low": middle_low,
        "hidden": hidden,
        "activated": activated,
        "normed_two": normed_two,
        "inverse_two": inverse_two,
    }
    return (final_lines, saved)


def feed_backward(pieces, saved, grad_final, flow):
    small_rows = pieces["small"]
    grad_sum_two, grad_gain_two, grad_shift_two = norm_backward(
        grad_final, saved["normed_two"], saved["inverse_two"], small_rows[8]
    )
    grad_out = grad_sum_two.astype(jnp.bfloat16)
    flow.add_product(saved["activated"], grad_out, offload=True)
    grad_act = trailing_array_multiply(grad_out, pieces["down"])
    grad_hidden = (grad_act * gelu_slope(saved["hidden"])).astype(jnp.bfloat16)
    flow.add_product(saved["middle_low"], grad_hidden, late=2)
    grad_middle = grad_sum_two + trailing_array_multiply(grad_hidden, pieces["up"])
    grad_sum_one, grad_gain_one, grad_shift_one = norm_backward(
        grad_middle, saved["normed_one"], saved["inverse_one"], small_rows[6]
    )
    grad_upbias = jnp.sum(grad_hidden.astype(jnp.float32), axis=0)
    (grad_sum_one,) = flow.advance(grad_sum_one)
    return (
        grad_sum_one,
        [jnp.sum(grad_out.astype(jnp.float32), axis=0), grad_gain_one, grad_shift_one, grad_gain_two, grad_shift_two],
        grad_upbias,
    )


def attention_backward(pieces, saved, grad_sum_one, grad_small, grad_upbias, lengths, tail_rows, flow, head_part):
    small_rows = pieces["small"]
    seqs_count = lengths.shape[0]
    rows_here = seqs_count * LEN
    grad_att = grad_sum_one.astype(jnp.bfloat16)
    grad_outw = matmul_left(saved["context"], grad_att)
    grad_context = (
        trailing_array_multiply(grad_att, pieces["out"])
        .astype(jnp.bfloat16)
        .reshape(seqs_count, LEN, HEADS, HEAD_DIM)
    )
    scores, split_heads = key_scores(saved["projected"], lengths)
    probabilities = jnp.exp(scores - saved["logsum"])
    grad_probs = jnp.einsum(
        "sqhd,skhd->shqk", grad_context, split_heads[:, :, 2], preferred_element_type=jnp.float32
    )
    grad_values = jnp.einsum(
        "shqk,sqhd->skhd",
        probabilities.astype(jnp.bfloat16),
        grad_context,
        preferred_element_type=jnp.float32,
    )
    grad_values, grad_probs = flow.advance(grad_values, grad_probs)
    grad_scores = probabilities * (
        grad_probs - jnp.sum(grad_probs * probabilities, axis=-1, keepdims=True)
    )
    grad_scores, head_part = flow.advance(grad_scores.astype(jnp.bfloat16), head_part)
    grad_queries = jnp.einsum(
        "shqk,skhd->sqhd", grad_scores, split_heads[:, :, 1], preferred_element_type=jnp.float32
    ) * HEAD_DIM ** (-0.5)
    grad_keys = jnp.einsum(
        "shqk,sqhd->skhd", grad_scores, split_heads[:, :, 0], preferred_element_type=jnp.float32
    ) * HEAD_DIM ** (-0.5)
    grad_proj = (
        jnp.stack([grad_queries, grad_keys, grad_values], axis=2)
        .reshape(rows_here, 3 * D)
        .astype(jnp.bfloat16)
    )
    flow.add_product(saved["inputs"], grad_proj)
    grad_bias_all = jnp.sum(grad_proj.astype(jnp.float32), axis=0)
    grad_first = grad_sum_one + trailing_array_multiply(grad_proj, pieces["qkv"])
    grad_embedded, grad_gain_zero, grad_shift_zero = norm_backward(
        grad_first, saved["normed_zero"], saved["inverse_zero"], small_rows[4]
    )
    grad_place = jnp.sum(grad_embedded.reshape(seqs_count, LEN, D), axis=0)
    grad_small = jnp.stack(
        [
            grad_bias_all[:D],
            grad_bias_all[2 * D :],
            jnp.sum(grad_att.astype(jnp.float32), axis=0),
            grad_small[0],
            grad_gain_zero,
            grad_shift_zero,
            *grad_small[1:],
        ]
    )
    tail = jnp.concatenate(
        [
            grad_small.reshape(60, TILE),
            grad_upbias.reshape(24, TILE),
            jnp.zeros((tail_rows - 84, TILE), jnp.float32),
        ]
    )
    (grad_embedded,) = flow.advance(grad_embedded)
    flow.add_rest(grad_outw, grad_place, tail)
    return grad_embedded, head_part


def combine_stats(earlier, later):
    peak_s = jnp.maximum(earlier[0], later[0])
    peak_t = jnp.maximum(earlier[2], later[2])
    factor_early = jnp.exp(earlier[0] - peak_s)
    factor_late = jnp.exp(later[0] - peak_s)
    teacher_early = jnp.exp(earlier[2] - peak_t)
    teacher_late = jnp.exp(later[2] - peak_t)
    return jnp.stack(
        [
            peak_s,
            earlier[1] * factor_early + later[1] * factor_late,
            peak_t,
            earlier[3] * teacher_early + later[3] * teacher_late,
            earlier[4] * teacher_early + later[4] * teacher_late,
        ]
    )


def adam_step(weight, first_moment, second, gradient, step_float):
    new_first = beta_first * first_moment + (1.0 - beta_first) * gradient
    new_second = beta_second * second + (1.0 - beta_second) * gradient * gradient
    fix_first = 1.0 - jnp.power(beta_first, step_float)
    fix_second = 1.0 - jnp.power(beta_second, step_float)
    update = new_first / fix_first / (jnp.sqrt(new_second / fix_second) + adam_eps)
    return (weight - learn_rate * (update + weight_decay * weight), new_first, new_second)


def at(value, index, axis):
    return lax.dynamic_index_in_dim(value, index, axis, keepdims=False)


def sent_low(value, bit):
    return swap(value.astype(jnp.bfloat16), bit).astype(jnp.float32)


def bit_of(bit):
    return lax.axis_index("vocab") // bit % 2


def halved(value, axis, bit):
    mine = bit_of(bit)
    return at(value, mine, axis) + sent_low(at(value, 1 - mine, axis), bit)


def reduce_steps(near, far, offload, late):
    (chip,) = yield [near + swap(far, CORE)]
    chip = chip.reshape(4, 2, 2, chip.shape[0] // CHIPS, chip.shape[1])
    first, second = yield [halved(chip[:2], 2, ACROSS), halved(chip[2:], 1, DEEP)]
    first, second = yield [halved(first, 1, DEEP), halved(second, 1, ACROSS)]
    if offload:
        total = lax.psum_scatter(jnp.concatenate([first, second]), "dp", scatter_dimension=0, tiled=False)
        yield []
        (total,) = yield [total]
        return total
    z = lax.axis_index("dp")
    blocks = [
        jnp.where((z + k) % 4 < 2, at(first, (z + k) % 2, 0), at(second, (z + k) % 2, 0)) for k in range(4)
    ]
    for _ in range(late):
        yield []
    blocks = yield [blocks[0], *(shift(blocks[k], k) for k in (1, 2, 3))]
    return blocks[0] + blocks[1] + blocks[2] + blocks[3]


class Flow:
    near = True

    def __init__(self):
        self.lines, self.waiting, self.sums = [], [], []

    def add(self, near, far, offload=False, late=0):
        self.lines.append(reduce_steps(near, far, offload, late))
        self.waiting.append(next(self.lines[-1]))
        self.sums.append(None)

    def add_product(self, left, right, offload=False, late=0):
        width = right.shape[1] // 2
        core = bit_of(CORE)
        far = matmul_left(left, lax.dynamic_slice_in_dim(right, (1 - core) * width, width, 1))
        near = matmul_left(left, lax.dynamic_slice_in_dim(right, core * width, width, 1))
        self.add(near, far, offload, late)

    def add_rest(self, out, place, tail):
        def half(core):
            columns = [
                lax.dynamic_slice_in_dim(whole, core * 384, 384, 1).reshape(CHIPS, -1, 384) for whole in (out, place)
            ]
            ends = jnp.pad(at(tail.reshape(CHIPS, 2, 8, TILE), core, 1), ((0, 0), (0, 0), (0, 256)))
            return jnp.concatenate([*columns, ends], axis=1).reshape(-1, 384)

        self.add(half(bit_of(CORE)), half(1 - bit_of(CORE)))

    def advance(self, *values):
        tied, values = together([moved for moved in self.waiting if moved is not None], list(values))
        tied = list(tied)
        for n, moved in enumerate(self.waiting):
            if moved is not None:
                try:
                    self.waiting[n] = self.lines[n].send(tied.pop(0))
                except StopIteration as stop:
                    self.waiting[n], self.sums[n] = None, stop.value
        return values


class PlainFlow:
    near = False

    def __init__(self, devices):
        self.devices, self.sums = devices, []

    def add_product(self, left, right, offload=False, late=0):
        parts = matmul_left(left, right).reshape(self.devices, -1, TILE)
        self.sums.append(lax.psum_scatter(parts, ("dp", "vocab"), scatter_dimension=0, tiled=False))

    def add_rest(self, out, place, tail):
        parts = [part.reshape(self.devices, -1, TILE) for part in (out, place, tail)]
        parts = jnp.concatenate(parts, axis=1)
        self.sums.append(lax.psum_scatter(parts, ("dp", "vocab"), scatter_dimension=0, tiled=False))

    def advance(self, *values):
        return values


def on_device(
    near,
    token_ids,
    lengths,
    mask_pos,
    mask_count,
    owner_order,
    step_count,
    teacher_flat,
    mentor_lexicon_weights,
    student_flat,
    flat_first,
    flat_second,
    student_embed,
    embed_first,
    embed_second,
):
    per = student_flat.shape[0]
    tiles_all = owner_order.shape[0]
    vocab_rows, width_share = student_embed.shape
    planes = lax.axis_size("dp")
    group = lax.axis_size("vocab")
    here = lax.axis_index("vocab")
    spot = jnp.stack([lax.axis_index("dp"), here]).astype(jnp.int32)
    devices = planes * group
    everywhere = ("dp", "vocab")
    device = lax.axis_index(everywhere)
    capacity = room(per, devices)
    slot_count = devices * capacity

    facts = jnp.concatenate([token_ids.reshape(LEN), lengths, mask_count, jnp.zeros((TILE - 2,), jnp.int32)])
    columns_low = student_embed.T.astype(jnp.bfloat16)
    words = jnp.arange(vocab_rows, dtype=jnp.int32)

    def chosen(ids):
        return (ids.reshape(-1, 1) - here * vocab_rows == words[None]).astype(jnp.bfloat16)

    def rows_t(ids):
        return array_multiply(chosen(ids), mentor_lexicon_weights).astype(jnp.bfloat16)

    def rows_s(ids, table):
        return trailing_array_multiply(chosen(ids), table).astype(jnp.bfloat16)

    def teacher_pieces(tiles):
        return pieces_of(
            [unpack_matrix(tiles, piece) for piece in MATRICES],
            tiles[TAIL : TAIL + TAIL_TILES].astype(jnp.float32),
        )

    homes = homes_of(owner_order, tiles_all, devices, near)
    sizes, starts = shares_of(tiles_all, devices)
    one_of = jnp.arange(devices, dtype=jnp.int32)
    pairs = jnp.sum((homes.reshape(devices, per, 1) // per == one_of).astype(jnp.int32), axis=1)
    crowded = jnp.max(pairs) > capacity
    own_homes = lax.dynamic_slice_in_dim(homes, device * per, per)
    own_target = own_homes // per
    chosen_target = (own_target[:, None] == one_of).astype(jnp.bfloat16)
    lines = jnp.arange(per, dtype=jnp.int32)
    earlier = (lines[None] < lines[:, None]).astype(jnp.bfloat16)
    rank = jnp.sum(array_multiply(earlier, chosen_target) * chosen_target.astype(jnp.float32), axis=1)
    rank = rank.astype(jnp.int32)
    slots = jnp.where(rank < capacity, own_target * capacity + rank, slot_count)
    packed, home_line = send_tiles(slots, own_homes % per, student_flat, slot_count)
    if near:
        teacher_tiles = lax.all_gather(teacher_flat, everywhere, axis=0, tiled=True)
        plane_facts = gather_near(facts)
        shape = (2, 2, LEN, D)
        far = rows_t(plane_facts[4:, :LEN]).reshape(shape)
        columns = [columns_low, shift(columns_low, 1)]
        packed, home_line, far, columns = together(packed, home_line, far, columns)
    packed = lax.all_to_all(packed.reshape(devices, capacity, TILE), everywhere, 0, 0)
    home_line = lax.all_to_all(home_line[:slot_count].reshape(devices, 1, capacity), everywhere, 0, 0)
    home_line = home_line.reshape(slot_count)
    if near:
        looked_t = rows_t(plane_facts[:4, :LEN]).reshape(shape) + swap(far, CORE)
        packed, home_line, looked_t, ahead = together(packed, home_line, looked_t, shift(columns[1], 1))
        columns = [*columns, ahead]
    home_tiles = land_tiles(home_line, packed.reshape(slot_count, TILE), per, starts if near else None)
    if near:
        home_tiles, looked_t, ahead = together(home_tiles, plane_hop(looked_t), shift(columns[2], 1))
        columns = [*columns, ahead]

    def from_everywhere(part):
        copies = jnp.broadcast_to(part[None], (devices, *part.shape))
        return lax.all_to_all(copies, everywhere, 0, 0).reshape(-1, TILE)

    def every_tile(tiles):
        stored = from_everywhere(student_flat.astype(jnp.bfloat16))
        sources = jnp.zeros((tiles_all,), jnp.int32).at[homes].set(jnp.arange(tiles_all, dtype=jnp.int32))
        stored = stored[lax.dynamic_slice_in_dim(sources, device * per, per)]
        if near:
            return land_tiles(lines, stored, per, starts)
        return stored

    home_tiles = lax.cond(crowded, every_tile, lambda tiles: tiles, home_tiles)

    if near:
        layer = lax.all_gather(home_tiles, everywhere, axis=0)
        z = lax.axis_index("dp")
        table_low = jnp.zeros((D, vocab_rows), jnp.bfloat16)
        for k, part in enumerate(columns):
            table_low = lax.dynamic_update_slice(table_low, part, ((z + 4 - k) % 4 * width_share, 0))
        far = rows_s(plane_facts[4:, :LEN], table_low).reshape(shape)
        looked_t, far = together(plane_end(*looked_t).astype(jnp.float32), far)
        close = rows_s(plane_facts[:4, :LEN], table_low).reshape(shape)
        other_facts = gather_near(jnp.stack([shift(facts, 1), shift(facts, 2), shift(facts, 3)]))
        all_facts = jnp.concatenate([plane_facts[:, None], other_facts], axis=1)
        looked_s, teacher_tiles, all_facts = together(close + swap(far, CORE), teacher_tiles, all_facts)
        teacher = teacher_pieces(teacher_tiles)
        teacher, looked_s = together(teacher, plane_hop(looked_s))
        middle, _ = attention_forward(teacher, looked_t, lengths)
        middle, looked_s = together(middle, plane_end(*looked_s).astype(jnp.float32))
        final_t = feed_forward(teacher, middle, {})[0]
        final_t, layer = together(final_t, layer)
        matrices = assemble_layer(layer)
    else:
        table_low = lax.all_gather(columns_low, "dp", axis=0, tiled=True)
        by_plane = lax.all_gather(facts, "dp", axis=0)
        all_facts = lax.all_gather(by_plane, "vocab", axis=0)
        plane_facts = lax.dynamic_index_in_dim(all_facts, lax.axis_index("dp"), 1, keepdims=False)
        teacher_tiles = lax.all_gather(teacher_flat, everywhere, axis=0, tiled=True)
        layer = lax.all_gather(home_tiles, everywhere, axis=0)
        matrices = [
            layer[:, start : start + size].reshape(height, across * TILE)
            for (_, height, across), size, start in zip(HOME_ORDER, sizes, starts)
        ]
        matrices.append(layer[:, starts[-1] :].astype(jnp.float32))
        plane_ids = plane_facts[:, :LEN]
        looked_t, looked_s = (
            lax.psum_scatter(rows, "vocab", scatter_dimension=0, tiled=True).astype(jnp.float32)
            for rows in (rows_t(plane_ids), rows_s(plane_ids, table_low))
        )
        teacher = teacher_pieces(teacher_tiles)
        middle, _ = attention_forward(teacher, looked_t, lengths)
        final_t = feed_forward(teacher, middle, {})[0]
    up, down, qkv, out, place = matrices[:5]
    student = pieces_of((qkv, out, up, down, place), matrices[5].reshape(-1, TILE))
    middle, saved = attention_forward(student, looked_s, lengths)
    offsets = jnp.concatenate([mask_pos.reshape(CAP), jnp.zeros((SLOTS - CAP,), jnp.int32)])
    picked_t = final_t[offsets].astype(jnp.bfloat16)
    if near:
        middle, mentor_picked = together(middle, gather_near(picked_t).reshape(-1, D))
    else:
        mentor_picked = lax.all_gather(picked_t, "vocab", axis=0, tiled=True)
    final_s, saved = feed_forward(student, middle, saved)

    token_total = jnp.sum(all_facts[:, :, LEN]).astype(jnp.float32)
    masked_total = jnp.sum(all_facts[:, :, LEN + 1]).astype(jnp.float32)
    teacher_logit = (
        trailing_array_multiply(mentor_picked, mentor_lexicon_weights) / smoothing_heat_scale
    )
    peak_t = jnp.max(teacher_logit, axis=1)
    picked_s = final_s[offsets].astype(jnp.bfloat16)
    if near:
        learner_picked = gather_split(picked_s).reshape(-1, D)
        learner_picked, teacher_logit, peak_t = together(learner_picked, teacher_logit, peak_t)
    else:
        learner_picked = lax.all_gather(picked_s, "vocab", axis=0, tiled=True)
    live_weighting = (
        (jnp.arange(SLOTS)[None] < plane_facts[:, LEN + 1, None]).astype(jnp.float32).reshape(-1)
    )
    learner_energy = array_multiply(learner_picked, table_low) / smoothing_heat_scale
    peak_s = jnp.max(learner_energy, axis=1)
    teacher_exps = jnp.exp(teacher_logit - peak_t[:, None])
    stats = jnp.stack(
        [
            peak_s,
            jnp.sum(jnp.exp(learner_energy - peak_s[:, None]), axis=1),
            peak_t,
            jnp.sum(teacher_exps, axis=1),
            jnp.sum(teacher_exps * (teacher_logit - learner_energy), axis=1),
        ]
    )
    if near:
        stats = stats.reshape(5, 2, 2, 2, SLOTS)
        stats = combine_stats(stats, jnp.flip(swap(stats, CORE), 1))
        across, deep, both = (
            jnp.flip(swap(stats, bits), axes)
            for bits, axes in ((ACROSS, 3), (DEEP, 2), (ACROSS | DEEP, (2, 3)))
        )
        stats = combine_stats(combine_stats(stats, across), combine_stats(deep, both))
        stats = stats.reshape(5, -1)
    else:
        everything = lax.all_gather(stats, "vocab", axis=0)
        stats = everything[0]
        for k in range(1, group):
            stats = combine_stats(stats, everything[k])
    logsum_s = stats[0] + jnp.log(stats[1])
    logsum_t = stats[2] + jnp.log(stats[3])
    diverge = stats[4] / stats[3] - logsum_t + logsum_s
    mine = 0 if near else here * SLOTS
    divergence_part = jnp.sum(lax.dynamic_slice_in_dim(diverge * live_weighting, mine, SLOTS))
    student_probs = jnp.exp(learner_energy - logsum_s[:, None])
    teacher_probs = jnp.exp(teacher_logit - logsum_t[:, None])
    grad_logit = (
        mixing_coefficient
        * smoothing_heat_scale
        / masked_total
        * live_weighting[:, None]
        * (student_probs - teacher_probs)
    ).astype(jnp.bfloat16)
    if near:
        half = grad_logit.shape[0] // 2
        far = trailing_array_multiply(grad_logit[half:], table_low).reshape(2, 2, SLOTS, D)
        close = trailing_array_multiply(grad_logit[:half], table_low).reshape(2, 2, SLOTS, D)
        grad_rows = plane_end(*plane_hop(close + swap(far, CORE)))
    else:
        grad_rows = lax.psum_scatter(
            trailing_array_multiply(grad_logit, table_low), "vocab", scatter_dimension=0, tiled=True
        )
    head_grad = matmul_left(learner_picked, grad_logit)
    head_grad, grad_rows = together(head_grad, grad_rows)
    head_part = lax.psum_scatter(head_grad, "dp", scatter_dimension=0, tiled=True)
    products = jnp.sum(final_s * final_t, axis=1)
    inverse_s = lax.rsqrt(jnp.sum(final_s * final_s, axis=1) + cosine_eps)
    inverse_t = lax.rsqrt(jnp.sum(final_t * final_t, axis=1) + cosine_eps)
    live_rows = (jnp.arange(LEN)[None, :] < lengths[:, None]).reshape(-1)
    cosine = products * inverse_s * inverse_t
    cosine_term = jnp.sum(jnp.where(live_rows, 1.0 - cosine, 0.0))
    weighting = jnp.where(live_rows, -cosine_weight / token_total, 0.0) * inverse_s * inverse_t
    grad_final = weighting[:, None] * (
        final_t - (products * inverse_s * inverse_s)[:, None] * final_s
    )
    grad_final = grad_final.at[offsets].add(grad_rows)
    flow = Flow() if near else PlainFlow(devices)
    grad_sum_one, grad_small, grad_upbias = feed_backward(student, saved, grad_final, flow)
    grad_embedded, head_part = attention_backward(
        student, saved, grad_sum_one, grad_small, grad_upbias, lengths, tiles_all - TAIL, flow, head_part
    )

    shares = grad_embedded.astype(jnp.bfloat16).reshape(LEN, planes, width_share).transpose(1, 0, 2)
    if near:
        own = upward(shares)
        shares = jnp.stack([own[0]] + [shift(own[k], k) for k in (1, 2, 3)])
        ids = all_facts[:, :, :LEN].reshape(2, 2, 2, planes, LEN)
        for axis, bit in ((0, CORE), (1, DEEP), (2, ACROSS)):
            ids = jnp.where((here & bit) != 0, jnp.flip(ids, axis), ids)
        ids = ids.transpose(1, 2, 0, 3, 4)
    else:
        shares = lax.all_to_all(shares, "dp", 0, 0)
        ids = all_facts[:, :, :LEN]
    token_grads = lax.all_gather(shares.reshape(-1, width_share), "vocab", axis=0, tiled=True)
    (shares,) = flow.advance(shares)
    token_grads = lax.all_gather(shares.reshape(-1, width_share), "vocab", axis=0, tiled=True)
    flow.advance()
    flow.advance()
    flow.advance()
    sum_down, sum_up, sum_qkv, sum_rest = flow.sums
    if near:
        home_grads = share_lines(sum_up, sum_down, sum_qkv, sum_rest, per, starts)
    else:
        home_grads = jnp.concatenate([sum_up, sum_down, sum_qkv, sum_rest])
    returned = pick_tiles(jnp.minimum(home_line, per - 1), home_grads, slot_count)
    returned = lax.all_to_all(returned.reshape(devices, capacity, TILE), everywhere, 0, 0)
    token_part = matmul_left(token_grads, chosen(ids))
    returned, token_part = together(returned, token_part)
    flat_grad = pick_tiles(jnp.minimum(slots, slot_count - 1), returned.reshape(slot_count, TILE), per)
    flat_grad = lax.cond(
        crowded,
        lambda grads: from_everywhere(home_grads)[own_homes],
        lambda grads: grads,
        flat_grad,
    )
    table_grad = (head_part + token_part).T
    loss_term = (
        mixing_coefficient * smoothing_heat_scale**2 * divergence_part / masked_total
        + cosine_weight * cosine_term / token_total
    )
    squares = jnp.sum(flat_grad * flat_grad) + jnp.sum(table_grad * table_grad)
    if near:
        squares, loss_value = sum_everywhere(jnp.stack([squares, loss_term]))
    else:
        squares, loss_value = lax.psum((squares, loss_term), ("dp", "vocab"))
    grad_norm = jnp.sqrt(squares)
    factor = clip_norm / jnp.maximum(grad_norm, clip_norm)
    step_float = step_count[0].astype(jnp.float32)
    new_flat, new_flat_first, new_flat_second = adam_step(
        student_flat, flat_first, flat_second, flat_grad * factor, step_float
    )
    new_embed, new_embed_first, new_embed_second = adam_step(
        student_embed, embed_first, embed_second, table_grad * factor, step_float
    )
    return (
        loss_value,
        grad_norm,
        new_flat,
        new_flat_first,
        new_flat_second,
        new_embed,
        new_embed_first,
        new_embed_second,
    )


def solution(mesh):
    near = mesh.shape["dp"] == 4 and mesh.shape["vocab"] == 8
    return jax.shard_map(
        functools.partial(on_device, near),
        mesh=mesh,
        in_specs=(
            P(("dp", "vocab"), None),
            P(("dp", "vocab")),
            P(("dp", "vocab"), None),
            P(("dp", "vocab")),
            P(),
            P(),
            P(("dp", "vocab"), None),
            P("vocab", None),
            P(("dp", "vocab"), None),
            P(("dp", "vocab"), None),
            P(("dp", "vocab"), None),
            P("vocab", "dp"),
            P("vocab", "dp"),
            P("vocab", "dp"),
        ),
        out_specs=(
            P(),
            P(),
            P(("dp", "vocab"), None),
            P(("dp", "vocab"), None),
            P(("dp", "vocab"), None),
            P("vocab", "dp"),
            P("vocab", "dp"),
            P("vocab", "dp"),
        ),
        check_vma=False,
    )
```
